32 devices in a mesh: batch: 8 (over z, y), fsdp: 4 (over x, core).
Axes of the slice: x: 2, y: 2, z: 4, core: 2. Of those that a mesh axis runs over, the one named last changes fastest.
Arguments:
- tokens: bfloat16 [128, 256, 768], P(('batch', 'fsdp')), may hold values from -6 to 6
- cotangent: bfloat16 [128, 256, 768], P(('batch', 'fsdp')), may hold values from -6 to 6
- mask_pos: int32 [128, 128], P(('batch', 'fsdp')), may hold values from 0 to 255, as said below
- mask_count: int32 [128], P(('batch', 'fsdp')), may hold values from 8 to 128, as said below
- w_qkv: float32 [768, 2304], P('fsdp'), may hold values from -0.21875 to 0.21875
- m_qkv: float32 [768, 2304], P(('fsdp', 'batch')), may hold values from -217.2232 to 217.2232
- v_qkv: float32 [768, 2304], P(('fsdp', 'batch')), may hold values from 1474.56 to 23592.96
- w_out: float32 [768, 768], P('fsdp'), may hold values from -0.875 to 0.875
- m_out: float32 [768, 768], P(('fsdp', 'batch')), may hold values from -50.685413 to 50.685413
- v_out: float32 [768, 768], P(('fsdp', 'batch')), may hold values from 80.2816 to 1284.5056
- w_fc1: float32 [768, 3072], P('fsdp'), may hold values from -0.21875 to 0.21875
- m_fc1: float32 [768, 3072], P(('fsdp', 'batch')), may hold values from -86.88928 to 86.88928
- v_fc1: float32 [768, 3072], P(('fsdp', 'batch')), may hold values from 235.9296 to 3774.8735
- w_fc2: float32 [3072, 768], P('fsdp'), may hold values from -0.109375 to 0.109375
- m_fc2: float32 [3072, 768], P(('fsdp', 'batch')), may hold values from -181.01933 to 181.01933
- v_fc2: float32 [3072, 768], P(('fsdp', 'batch')), may hold values from 1024 to 16384
- vectors: float32 [14, 768], P(None, 'fsdp'), may hold values from -1.2 to 1.6
- m_vec: float32 [14, 768], P(None, ('fsdp', 'batch')), may hold values from -217.2232 to 217.2232
- v_vec: float32 [14, 768], P(None, ('fsdp', 'batch')), may hold values from 1474.56 to 23592.96
Outputs:
- layer_out: bfloat16 [128, 256, 768], P(('batch', 'fsdp'))
- grad_tokens: float32 [128, 256, 768], P(('batch', 'fsdp'))
- new_w_qkv: float32 [768, 2304], P('fsdp')
- new_m_qkv: float32 [768, 2304], P(('fsdp', 'batch'))
- new_v_qkv: float32 [768, 2304], P(('fsdp', 'batch'))
- new_w_out: float32 [768, 768], P('fsdp')
- new_m_out: float32 [768, 768], P(('fsdp', 'batch'))
- new_v_out: float32 [768, 768], P(('fsdp', 'batch'))
- new_w_fc1: float32 [768, 3072], P('fsdp')
- new_m_fc1: float32 [768, 3072], P(('fsdp', 'batch'))
- new_v_fc1: float32 [768, 3072], P(('fsdp', 'batch'))
- new_w_fc2: float32 [3072, 768], P('fsdp')
- new_m_fc2: float32 [3072, 768], P(('fsdp', 'batch'))
- new_v_fc2: float32 [3072, 768], P(('fsdp', 'batch'))
- new_vectors: float32 [14, 768], P(None, 'fsdp')
- new_m_vec: float32 [14, 768], P(None, ('fsdp', 'batch'))
- new_v_vec: float32 [14, 768], P(None, ('fsdp', 'batch'))
The draws below stay inside these ranges and needn't reach their ends.
Inputs may be any that keep to these rules, and one draw needn't show every extreme that they name: `mask_pos`: each row holds 128 different positions of the pair; its first mask_count entries are the masked tokens. `mask_count`: some pair has 128 masked tokens.
All inputs are finite; a program needn't handle non-finite values.
Results may differ from the reference program's by a relative error of at most 0.015.
Values may be sent and summed in bfloat16 or wider, within the bound.
No kernel may reach another device: no remote copies, remote signals or barrier semaphores. Data moves between devices by JAX's collectives and lax.ppermute only.
A program may use at most 192 MiB of HBM per device.

```python
import math
import jax
import jax.numpy as jnp
from jax import lax

D = 768
HEADS = 12
HDIM = 64
FF = 3072
TEXT = 40
STEP = 3
LEN = 256
MAXM = 128
NVEC = 14
PAIRS = 128


def draw_mask_pos(key, part):
    pair_keys = jax.random.split(key, PAIRS)
    orders = jax.vmap(lambda pair_key: jax.random.permutation(pair_key, LEN))(pair_keys)
    return orders[:, :MAXM].astype(jnp.int32)


def draw_mask_count(key, part):
    key_base, key_shift, key_full = jax.random.split(key, 3)
    least = max(MAXM // 16, 1)
    base_draw = jax.random.randint(key_base, (PAIRS,), 0, MAXM - least + 1)
    shifter = jax.random.randint(key_shift, (PAIRS,), 0, 4)
    counts = least + jnp.right_shift(base_draw, shifter)
    fullest = jax.random.randint(key_full, (), 0, PAIRS)
    counts = counts.at[fullest].set(MAXM)
    return counts.astype(jnp.int32)


def draw_vectors(key, part):
    noise = jnp.clip(jax.random.normal(key, (NVEC, D), jnp.float32), -4.0, 4.0)
    row_index = lax.broadcasted_iota(jnp.int32, (NVEC, D), 0)
    gain_rows = (row_index == 2) | (row_index == 7)
    return jnp.where(gain_rows, 1.0 + 0.15 * noise, 0.3 * noise)


def level_of(own_key, shape, pieces, smallest, largest):
    def one(position, shards_of):
        draws = jax.random.uniform(jax.random.fold_in(jax.random.fold_in(own_key, 6), position), (shards_of,), jnp.float32, smallest / len(pieces), largest / len(pieces))
        return jnp.repeat(jnp.exp(draws), shape[position] // shards_of).reshape((-1,) + (1,) * (len(shape) - position - 1))

    factor_of = one(*pieces[0])
    for cut in pieces[1:]:
        factor_of = factor_of * one(*cut)
    return factor_of


def gaussian(stream_key, dims, spread, most, shards=(), kind=jnp.bfloat16):
    drawn = jax.random.normal(stream_key, dims, jnp.float32) * spread
    if len(shards) > 0:
        drawn = level_of(stream_key, dims, shards, -0.22, 0.18) * drawn
    return jnp.clip(drawn, min=-most, max=most).astype(kind)


def setup_inputs(seed: int = 0) -> dict:
    splits = jax.random.split(jax.random.key(seed), 20)
    return {
        "tokens": gaussian(splits[0], (PAIRS, LEN, D), 1.0, 6.0, ((0, 32),)),
        "cotangent": gaussian(splits[1], (PAIRS, LEN, D), 1.0, 6.0, ((0, 32),)),
        "mask_pos": draw_mask_pos(jax.random.fold_in(splits[19], 71), 0),
        "mask_count": draw_mask_count(jax.random.fold_in(splits[19], 71), 0),
        "w_qkv": gaussian(splits[4], (D, 3 * D), D ** -0.5, 0.21875, ((0, 4),), jnp.float32),
        "m_qkv": gaussian(splits[5], (D, 3 * D), (0.3 * (PAIRS * LEN) ** 0.5), 217.2232, ((0, 32),), jnp.float32),
        "v_qkv": jnp.clip(jnp.exp(math.log(23592.96) - 2.7725887 * jax.random.uniform(splits[6], (D, 3 * D), jnp.float32) ** level_of(splits[6], (D, 3 * D), ((0, 32),), -0.2, 0.2)), 1474.56, 23592.96),
        "w_out": gaussian(splits[7], (D, D), (D // 16) ** -0.5, 0.875, ((0, 4),), jnp.float32),
        "m_out": gaussian(splits[8], (D, D), (0.07 * (PAIRS * LEN) ** 0.5), 50.685413, ((0, 32),), jnp.float32),
        "v_out": jnp.clip(jnp.exp(math.log(1284.5056) - 2.7725887 * jax.random.uniform(splits[9], (D, D), jnp.float32) ** level_of(splits[9], (D, D), ((0, 32),), -0.2, 0.2)), 80.2816, 1284.5056),
        "w_fc1": gaussian(splits[10], (D, FF), D ** -0.5, 0.21875, ((0, 4),), jnp.float32),
        "m_fc1": gaussian(splits[11], (D, FF), (0.12 * (PAIRS * LEN) ** 0.5), 86.88928, ((0, 32),), jnp.float32),
        "v_fc1": jnp.clip(jnp.exp(math.log(3774.8735) - 2.7725887 * jax.random.uniform(splits[12], (D, FF), jnp.float32) ** level_of(splits[12], (D, FF), ((0, 32),), -0.2, 0.2)), 235.9296, 3774.8735),
        "w_fc2": gaussian(splits[13], (FF, D), FF ** -0.5, 0.109375, ((0, 4),), jnp.float32),
        "m_fc2": gaussian(splits[14], (FF, D), (0.25 * (PAIRS * LEN) ** 0.5), 181.01933, ((0, 32),), jnp.float32),
        "v_fc2": jnp.clip(jnp.exp(math.log(16384.0) - 2.7725887 * jax.random.uniform(splits[15], (FF, D), jnp.float32) ** level_of(splits[15], (FF, D), ((0, 32),), -0.2, 0.2)), 1024.0, 16384.0),
        "vectors": draw_vectors(jax.random.fold_in(splits[19], 71), 0),
        "m_vec": gaussian(splits[17], (NVEC, D), (0.3 * (PAIRS * LEN) ** 0.5), 217.2232, ((1, 32),), jnp.float32),
        "v_vec": jnp.clip(jnp.exp(math.log(23592.96) - 2.7725887 * jax.random.uniform(splits[18], (NVEC, D), jnp.float32) ** level_of(splits[18], (NVEC, D), ((1, 32),), -0.2, 0.2)), 1474.56, 23592.96),
    }


HIGHEST_PREC = lax.Precision.HIGHEST
BETA_ONE = 0.5
BETA_TWO = 0.5
EPS_ADAM = 1e-08
STEP_RATES = (0.03, 0.1, 0.03, 0.015, 0.3)
DECAY_RATES = (0.01, 0.01, 0.01, 0.01, 0.0)

@jax.custom_vjp
def low(v):
    return lax.optimization_barrier(v.astype(jnp.bfloat16)).astype(jnp.float32)

@jax.custom_vjp
def low_back(v):
    return v

def low_keep(v):
    return (low(v), None)

def low_pass(kept, grad):
    return (grad,)

def back_keep(v):
    return (v, None)

def back_low(kept, grad):
    return (low(grad),)
low.defvjp(low_keep, low_pass)
low_back.defvjp(back_keep, back_low)

def layer_norm(hidden, gain_row, shift_row):
    row_mean = lax.optimization_barrier(jnp.mean(hidden, axis=-1, keepdims=True))
    centred = hidden - row_mean
    variance = lax.optimization_barrier(jnp.mean(centred * centred, axis=-1, keepdims=True))
    return centred * lax.rsqrt(variance + 1e-06) * gain_row + shift_row

def project(left_mat, right_mat):
    return jnp.einsum('gtd,de->gte', left_mat, right_mat, precision=HIGHEST_PREC)

def forward(inputs, vectors, w_qkv, w_out, w_fc1, w_fc2):
    vectors = low(vectors)
    w_qkv = low(w_qkv)
    w_out = low(w_out)
    w_fc1 = low(w_fc1)
    w_fc2 = low(w_fc2)
    group_pairs, seq_len, model_width = inputs.shape
    fc1_parts = FF // D
    is_image = (jnp.arange(seq_len) >= TEXT)[:, None]
    stream_zero = inputs + jnp.where(is_image, vectors[1], vectors[0])
    normed_one = low(layer_norm(stream_zero, vectors[2], vectors[3]))
    qkv_bias = jnp.concatenate([vectors[4], jnp.zeros((model_width,), jnp.float32), vectors[5]])
    qkv_all = low(low_back(project(normed_one, w_qkv)) + qkv_bias)
    head_view = qkv_all.reshape(group_pairs, seq_len, 3, HEADS, HDIM)
    queries = head_view[:, :, 0]
    keys_all = head_view[:, :, 1]
    values_all = head_view[:, :, 2]
    scores = low_back(jnp.einsum('gqhe,gkhe->gqhk', queries, keys_all, precision=HIGHEST_PREC) * HDIM ** (-0.5))
    attn_weights = low(jax.nn.softmax(scores, axis=-1))
    mixed_heads = jnp.einsum('gqhk,gkhe->gqhe', attn_weights, values_all, precision=HIGHEST_PREC)
    mixed_heads = low(low_back(mixed_heads)).reshape(group_pairs, seq_len, model_width)
    stream_one = stream_zero + low_back(project(mixed_heads, w_out)) + vectors[6]
    normed_two = low(layer_norm(stream_one, vectors[7], vectors[8]))
    fc1_bias = vectors[9:9 + fc1_parts].reshape(FF)
    preact = low_back(project(normed_two, w_fc1)) + fc1_bias
    activated = low(jax.nn.gelu(preact, approximate=False))
    return stream_one + low_back(project(activated, w_fc2)) + vectors[9 + fc1_parts]

def adamw(weight, gradient, moment_one, moment_two, step_rate, decay_rate):
    new_first = BETA_ONE * moment_one + (1.0 - BETA_ONE) * gradient
    new_second = BETA_TWO * moment_two + (1.0 - BETA_TWO) * gradient * gradient
    correct_one = 1.0 - BETA_ONE ** STEP
    correct_two = 1.0 - BETA_TWO ** STEP
    update = new_first / correct_one / (jnp.sqrt(new_second / correct_two) + EPS_ADAM) + decay_rate * weight
    return (weight - step_rate * update, new_first, new_second)

def reference(tokens, cotangent, mask_pos, mask_count, w_qkv, m_qkv, v_qkv, w_out, m_out, v_out, w_fc1, m_fc1, v_fc1, w_fc2, m_fc2, v_fc2, vectors, m_vec, v_vec):
    slot_live = jnp.arange(MAXM)[None, :] < mask_count[:, None]
    slot_hits = (mask_pos[:, :, None] == jnp.arange(LEN)[None, None, :]) & slot_live[:, :, None]
    masked = jnp.any(slot_hits, axis=1)
    cot_masked = cotangent.astype(jnp.float32) * masked[:, :, None].astype(jnp.float32)
    group_pairs = math.gcd(PAIRS, 16)
    blocks = PAIRS // group_pairs
    scanned = (tokens.astype(jnp.float32).reshape(blocks, group_pairs, LEN, D), cot_masked.reshape(blocks, group_pairs, LEN, D))
    weights = (vectors, w_qkv, w_out, w_fc1, w_fc2)

    def one_group(totals, group_data):
        inputs, cot_group = group_data
        result, pull_back = jax.vjp(forward, inputs, *weights)
        gradients = pull_back(cot_group)
        totals = tuple((total_sum + piece_grad for total_sum, piece_grad in zip(totals, gradients[1:])))
        return (totals, (result.astype(jnp.bfloat16), gradients[0]))
    zeros_init = tuple((jnp.zeros(weight.shape, jnp.float32) for weight in weights))
    totals, (outputs, input_grads) = lax.scan(one_group, zeros_init, scanned)
    layer_out = outputs.reshape(PAIRS, LEN, D)
    grad_tokens = input_grads.reshape(PAIRS, LEN, D)
    vec_new = adamw(vectors, totals[0], m_vec, v_vec, STEP_RATES[4], DECAY_RATES[4])
    qkv_new = adamw(w_qkv, totals[1], m_qkv, v_qkv, STEP_RATES[0], DECAY_RATES[0])
    out_new = adamw(w_out, totals[2], m_out, v_out, STEP_RATES[1], DECAY_RATES[1])
    fc1_new = adamw(w_fc1, totals[3], m_fc1, v_fc1, STEP_RATES[2], DECAY_RATES[2])
    fc2_new = adamw(w_fc2, totals[4], m_fc2, v_fc2, STEP_RATES[3], DECAY_RATES[3])
    return (layer_out, grad_tokens, qkv_new[0], qkv_new[1], qkv_new[2], out_new[0], out_new[1], out_new[2], fc1_new[0], fc1_new[1], fc1_new[2], fc2_new[0], fc2_new[1], fc2_new[2], vec_new[0], vec_new[1], vec_new[2])
```

```python
import functools
import math

import jax
import jax.numpy as jnp
import numpy as np
from jax import lax
from jax.experimental import pallas as pl
from jax.experimental.pallas import tpu as pltpu
from jax.sharding import PartitionSpec as P

D = 768
HEADS = 12
HDIM = 64
FF = 3072
TEXT = 40
STEP = 3
MAXM = 128
NVEC = 14
PARTS = FF // D
LANES = 128
SLABS = D // LANES

BETA_ONE = 0.5
BETA_TWO = 0.5
EPS_ADAM = 1e-08
STEP_RATES = (0.03, 0.1, 0.03, 0.015, 0.3)
DECAY_RATES = (0.01, 0.01, 0.01, 0.01, 0.0)
INV_ROOT_TWO = 1.0 / math.sqrt(2.0)
INV_ROOT_TWOPI = 1.0 / math.sqrt(2.0 * math.pi)

F32 = jnp.float32
BF16 = jnp.bfloat16


def dot(a, b):
    return lax.dot_general(a, b, (((1,), (0,)), ((), ())), preferred_element_type=F32)


def dot_first(a, b):
    return lax.dot_general(a, b, (((0,), (0,)), ((), ())), preferred_element_type=F32)


def dot_last(a, b):
    return lax.dot_general(a, b, (((1,), (1,)), ((), ())), preferred_element_type=F32)


def normalize(hidden):
    row_mean = jnp.mean(hidden, axis=-1, keepdims=True)
    centred = hidden - row_mean
    inv_scale = lax.rsqrt(jnp.mean(centred * centred, axis=-1, keepdims=True) + 1e-06)
    return centred * inv_scale, inv_scale


def norm_back(gradient, normed, inv_scale, gain_row):
    scaled = gradient * gain_row
    return inv_scale * (
        scaled
        - jnp.mean(scaled, axis=-1, keepdims=True)
        - normed * jnp.mean(scaled * normed, axis=-1, keepdims=True)
    )


def adamw(weight, gradient, moment_one, moment_two, step_rate, decay_rate):
    new_first = BETA_ONE * moment_one + (1.0 - BETA_ONE) * gradient
    new_second = BETA_TWO * moment_two + (1.0 - BETA_TWO) * gradient * gradient
    correct_one = 1.0 - BETA_ONE**STEP
    correct_two = 1.0 - BETA_TWO**STEP
    update = (
        new_first / correct_one / (jnp.sqrt(new_second / correct_two) + EPS_ADAM)
        + decay_rate * weight
    )
    return (weight - step_rate * update, new_first, new_second)


def cost(flops, moved, trans=0):
    return pl.CostEstimate(flops=int(flops), bytes_accessed=int(moved), transcendentals=int(trans))


def full(shape):
    zeros = (0,) * len(shape)
    return pl.BlockSpec(shape, lambda *_: zeros)


ANYWHERE = pl.BlockSpec(memory_space=pl.ANY)


def swap(value, axis, bit, size):
    return lax.ppermute(value, axis, [(i, i ^ (1 << bit)) for i in range(size)])


class Plan:
    def __init__(self, mesh):
        self.nf = mesh.shape["fsdp"]
        self.nb = mesh.shape["batch"]
        self.nd = self.nf * self.nb
        self.fbits = self.nf.bit_length() - 1
        self.bbits = self.nb.bit_length() - 1
        assert self.nf == 1 << self.fbits and self.nb == 1 << self.bbits
        core = [("fsdp", 0)]
        rest = [("fsdp", k) for k in range(1, self.fbits)]
        near = [("batch", 0)]
        far = [("batch", k) for k in range(1, self.bbits)]
        self.orders = {"x": core + rest + near + far, "y": core + near + rest + far}

    def size(self, axis):
        return self.nf if axis == "fsdp" else self.nb

    def masks(self, order):
        rank = len(order)
        index = np.arange(1 << rank)
        out = {"fsdp": np.zeros_like(index), "batch": np.zeros_like(index)}
        for place, (axis, bit) in enumerate(order):
            out[axis] |= ((index >> (rank - 1 - place)) & 1) << bit
        return out

    def owners(self, order, findex, bindex):
        m = self.masks(order)
        fm = jnp.asarray(m["fsdp"], jnp.int32)
        bm = jnp.asarray(m["batch"], jnp.int32)
        return (findex ^ fm) * self.nb + (bindex ^ bm)


def scatter_sum(plan, order, send, keep):
    parts = [keep]
    count = keep.shape[0]
    for place, (axis, bit) in enumerate(order):
        got = swap(send, axis, bit, plan.size(axis))
        parts.append(got)
        count //= 2
        if count == 0:
            break
        total = parts[0][count : 2 * count].astype(F32)
        for part in parts[1:]:
            total = total + part[count : 2 * count].astype(F32)
        send = total.astype(BF16)
        parts = [part[:count] for part in parts]
    total = parts[0].astype(F32)
    for part in parts[1:]:
        total = total + part.astype(F32)
    return total[0]


def gather_blocks(plan, value):
    blocks = value[None]
    for bit in reversed(range(plan.bbits)):
        got = swap(blocks, "batch", bit, plan.nb)
        blocks = jnp.concatenate([blocks, got], axis=0)
    return blocks


def gather_pieces(plan, shard, low_bit):
    rows = shard.shape[0]
    half = rows // 2
    pieces = [(0, None, shard)]
    if plan.fbits >= 1:
        pieces.append((1, None, swap(shard, "fsdp", 0, plan.nf)))
    for bit in range(1, plan.fbits):
        mask = 1 << bit
        mine = lax.dynamic_slice_in_dim(shard, low_bit * half, half, 0)
        near = swap(mine, "fsdp", bit, plan.nf)
        other = swap(near, "batch", 0, plan.nb)
        pieces.append((mask, 0, near))
        pieces.append((mask, 1, other))
        pieces.append((mask | 1, 0, swap(near, "fsdp", 0, plan.nf)))
        pieces.append((mask | 1, 1, swap(other, "fsdp", 0, plan.nf)))
        assert plan.fbits <= 2
    return pieces


def piece_arrays(pieces):
    return [p[2] for p in pieces]


def piece_copies(meta, refs, target, sems, findex, low_bit, rows):
    copies = []
    for number, ((mask, half, _), ref) in enumerate(zip(meta, refs)):
        start = (findex ^ mask) * rows
        if half is not None:
            start = start + (low_bit if half == 0 else 1 - low_bit) * (rows // 2)
        length = rows if half is None else rows // 2
        copies.append(
            pltpu.make_async_copy(
                ref, target.at[pl.ds(pl.multiple_of(start, 8), length)], sems.at[number]
            )
        )
    return copies


def piece_meta(pieces):
    return [(m, h, None) for m, h, _ in pieces]


def order_kernel(count_ref, pos_ref, tok_ref, cot_ref, perm_ref, tokp_ref, img_ref, dy_ref):
    pair = pl.program_id(0)
    length = tok_ref.shape[1]
    slots = pos_ref.shape[2]
    token = lax.broadcasted_iota(jnp.int32, (length, slots), 0)
    slot = lax.broadcasted_iota(jnp.int32, (length, slots), 1)
    hit = jnp.where(token == pos_ref[0], 1.0, 0.0)
    free = 1.0 - jnp.sum(hit, axis=1, keepdims=True)
    below = lax.broadcasted_iota(jnp.int32, (length, length), 1) < lax.broadcasted_iota(
        jnp.int32, (length, length), 0
    )
    rank = dot(
        jnp.where(below, 1.0, 0.0).astype(BF16),
        jnp.broadcast_to(free, (length, slots)).astype(BF16),
    )
    rest = jnp.where(rank == slot.astype(F32), jnp.broadcast_to(free, (length, slots)), 0.0)
    perm = jnp.concatenate([hit, rest], axis=1).astype(BF16)
    perm_ref[0] = perm
    tokp_ref[0] = dot_first(perm, tok_ref[0]).astype(BF16)
    image = jnp.where(lax.broadcasted_iota(jnp.int32, (length, LANES), 0) >= TEXT, 1.0, 0.0)
    img_ref[0] = dot_first(perm, image.astype(BF16))
    chosen = dot_first(perm[:, :slots], cot_ref[0])
    live = lax.broadcasted_iota(jnp.int32, (slots, 1), 0) < count_ref[pair]
    dy_ref[0] = jnp.where(live, chosen, 0.0).astype(BF16)


def start_row(tok_ref, img_ref, vec_ref):
    return tok_ref[0].astype(F32) + jnp.where(
        img_ref[0][:, :1] > 0.5, vec_ref[1:2, :], vec_ref[0:1, :]
    )


def attn_kernel(meta, rows, place_ref, tok_ref, img_ref, vec_ref, *refs):
    pieces = refs[: len(meta)]
    n1_ref, qkv_ref, a_ref, w_ref, sems = refs[len(meta) :]
    first = pl.program_id(0) == 0
    copies = piece_copies(meta, pieces, w_ref, sems, place_ref[0], place_ref[1], rows)

    @pl.when(first)
    def _():
        for copy in copies:
            copy.start()

    normed, _ = normalize(start_row(tok_ref, img_ref, vec_ref))
    n1 = (normed * vec_ref[2:3, :] + vec_ref[3:4, :]).astype(BF16)
    n1_ref[0] = n1

    @pl.when(first)
    def _():
        for copy in copies:
            copy.wait()

    qkv_ref[0, :, :D] = (dot(n1, w_ref[:, :D]) + vec_ref[4:5, :]).astype(BF16)
    qkv_ref[0, :, D : 2 * D] = dot(n1, w_ref[:, D : 2 * D]).astype(BF16)
    qkv_ref[0, :, 2 * D :] = (dot(n1, w_ref[:, 2 * D :]) + vec_ref[5:6, :]).astype(BF16)
    low = lax.broadcasted_iota(jnp.int32, (1, LANES), 1) < HDIM
    for slab in range(SLABS):
        cols = slice(slab * LANES, (slab + 1) * LANES)
        q = qkv_ref[0, :, cols] * jnp.asarray(HDIM**-0.5, BF16)
        k = qkv_ref[0, :, D + slab * LANES : D + (slab + 1) * LANES]
        v = qkv_ref[0, :, 2 * D + slab * LANES : 2 * D + (slab + 1) * LANES]
        outs = []
        for head in range(2):
            mine = low if head == 0 else jnp.logical_not(low)
            scores = dot_last(jnp.where(mine, q, jnp.zeros_like(q)), k)
            e = jnp.exp(scores - jnp.max(scores, axis=-1, keepdims=True))
            p = (e * (1.0 / jnp.sum(e, axis=-1, keepdims=True))).astype(BF16)
            outs.append(dot(p, v))
        a_ref[0, :, cols] = jnp.where(low, outs[0], outs[1]).astype(BF16)


def fc1_kernel(
    meta_o, rows_o, meta_1, rows_1, place_ref, tok_ref, img_ref, a_ref, vec_ref, *refs
):
    no, n1 = len(meta_o), len(meta_1)
    po, p1 = refs[:no], refs[no : no + n1]
    h1_ref, n2_ref, z_ref, slope_ref, wo_ref, w1_ref, sem_o, sem_1 = refs[no + n1 :]
    first = pl.program_id(0) == 0
    copies_o = piece_copies(meta_o, po, wo_ref, sem_o, place_ref[0], place_ref[1], rows_o)
    copies_1 = piece_copies(meta_1, p1, w1_ref, sem_1, place_ref[0], place_ref[1], rows_1)

    @pl.when(first)
    def _():
        for copy in copies_o:
            copy.start()
        for copy in copies_1:
            copy.start()
        for copy in copies_o:
            copy.wait()

    h1 = start_row(tok_ref, img_ref, vec_ref) + dot(a_ref[0], wo_ref[...]) + vec_ref[6:7, :]
    h1_ref[0] = h1
    normed, _ = normalize(h1)
    n2 = (normed * vec_ref[7:8, :] + vec_ref[8:9, :]).astype(BF16)
    n2_ref[0] = n2

    @pl.when(first)
    def _():
        for copy in copies_1:
            copy.wait()

    slots = slope_ref.shape[1]
    for part in range(PARTS):
        cols = slice(part * D, (part + 1) * D)
        f = dot(n2, w1_ref[:, cols]) + vec_ref[9 + part : 10 + part, :]
        phi = 0.5 * (1.0 + lax.erf(f * INV_ROOT_TWO))
        z_ref[0, :, cols] = (f * phi).astype(BF16)
        fs = f[:slots]
        slope = phi[:slots] + fs * jnp.exp(-0.5 * fs * fs) * INV_ROOT_TWOPI
        slope_ref[0, :, cols] = slope.astype(BF16)


def gw2_kernel(half, nb, bmask, place_ref, z_ref, dy_ref, out_ref, *more):
    acc_ref = more[-1]
    pairs, slots, width = z_ref.shape
    dy = dy_ref[...].reshape(pairs * slots, -1)
    acc_ref[...] = dot_first(z_ref[...].reshape(pairs * slots, width), dy)
    block = width // nb
    for spot in range(nb):
        start = pl.multiple_of((place_ref[2] ^ int(bmask[spot])) * block, 8)
        out_ref[0, spot] = acc_ref[pl.ds(start, block), :].astype(BF16)
    if half == 0:
        more[0][...] = jnp.sum(dy.astype(F32), axis=0, keepdims=True)


def spread(acc_ref, owners_ref, send_ref, keep_ref, block):
    half = send_ref.shape[0]
    for spot in range(half):
        start = pl.multiple_of(owners_ref[half + spot] * block, 8)
        send_ref[spot] = acc_ref[pl.ds(start, block), :].astype(BF16)
    for spot in range(half):
        start = pl.multiple_of(owners_ref[spot] * block, 8)
        keep_ref[spot] = acc_ref[pl.ds(start, block), :].astype(BF16)


def gw1_kernel(meta, rows, place_ref, owners_ref, dy_ref, slope_ref, n2_ref, *refs):
    pieces = refs[: len(meta)]
    df_ref, gb1_ref, send_ref, keep_ref, w2_ref, n2t_ref, acc_ref, sems = refs[len(meta) :]
    step = pl.program_id(0)
    pairs, slots, width = slope_ref.shape
    total = pairs * slots
    copies = piece_copies(meta, pieces, w2_ref, sems, place_ref[0], place_ref[1], rows)

    @pl.when(step == 0)
    def _():
        for copy in copies:
            copy.start()
        n2t_ref[...] = n2_ref[...].reshape(total, D).T
        for copy in copies:
            copy.wait()

    dz = dot_last(
        dy_ref[...].reshape(total, D), w2_ref[pl.ds(pl.multiple_of(step * width, 8), width), :]
    )
    df = dz * slope_ref[...].reshape(total, width).astype(F32)
    gb1_ref[...] = jnp.sum(df, axis=0, keepdims=True)
    low = df.astype(BF16)
    df_ref[...] = low
    acc_ref[...] = dot(n2t_ref[...], low)
    spread(acc_ref, owners_ref, send_ref, keep_ref, D // (2 * send_ref.shape[0]))


def mlp_back_kernel(
    meta_1, rows_1, meta_o, rows_o, place_ref, df_ref, dy_ref, h1_ref, vec_ref, *refs
):
    n1, no = len(meta_1), len(meta_o)
    p1, po = refs[:n1], refs[n1 : n1 + no]
    dh_ref, dhr_ref, da_ref, sum_ref, w1_ref, wo_ref, sem_1, sem_o = refs[n1 + no :]
    first = pl.program_id(0) == 0
    copies_1 = piece_copies(meta_1, p1, w1_ref, sem_1, place_ref[0], place_ref[1], rows_1)
    copies_o = piece_copies(meta_o, po, wo_ref, sem_o, place_ref[0], place_ref[1], rows_o)

    @pl.when(first)
    def _():
        for copy in copies_1:
            copy.start()
        for copy in copies_o:
            copy.start()
        sum_ref[...] = jnp.zeros_like(sum_ref)
        for copy in copies_1:
            copy.wait()
        for copy in copies_o:
            copy.wait()

    dn2 = dot_last(df_ref[...], w1_ref[...])
    normed, scale = normalize(h1_ref[0])
    dh = dy_ref[0].astype(F32) + norm_back(dn2, normed, scale, vec_ref[7:8, :])
    dh_ref[0] = dh
    sum_ref[0:1, :] += jnp.sum(dh, axis=0, keepdims=True)
    sum_ref[1:2, :] += jnp.sum(dn2 * normed, axis=0, keepdims=True)
    sum_ref[2:3, :] += jnp.sum(dn2, axis=0, keepdims=True)
    low = dh.astype(BF16)
    dhr_ref[0] = low
    da_ref[0] = dot_last(low, wo_ref[...]).astype(BF16)


def attn_back_kernel(qkv_ref, da_ref, dq_ref, dkv_ref, sum_ref):
    slots = da_ref.shape[1]

    @pl.when(pl.program_id(0) == 0)
    def _():
        sum_ref[...] = jnp.zeros_like(sum_ref)

    low = lax.broadcasted_iota(jnp.int32, (1, LANES), 1) < HDIM
    scale = jnp.asarray(HDIM**-0.5, BF16)
    for slab in range(SLABS):
        cols = slice(slab * LANES, (slab + 1) * LANES)
        q = qkv_ref[0, :slots, cols] * scale
        k = qkv_ref[0, :, D + slab * LANES : D + (slab + 1) * LANES]
        v = qkv_ref[0, :, 2 * D + slab * LANES : 2 * D + (slab + 1) * LANES]
        da = da_ref[0, :, cols]
        gqs, gks, gvs = [], [], []
        for head in range(2):
            mine = low if head == 0 else jnp.logical_not(low)
            zero = jnp.zeros_like(q)
            scores = dot_last(jnp.where(mine, q, zero), k)
            e = jnp.exp(scores - jnp.max(scores, axis=-1, keepdims=True))
            p = e * (1.0 / jnp.sum(e, axis=-1, keepdims=True))
            gvs.append(dot_first(p.astype(BF16), da))
            dp = dot_last(jnp.where(mine, da, zero), v)
            ds = (p * (dp - jnp.sum(p * dp, axis=-1, keepdims=True))).astype(BF16)
            gqs.append(dot(ds, k))
            gks.append(dot_first(ds, q))
        gq = jnp.where(low, gqs[0], gqs[1]) * (HDIM**-0.5)
        gk = jnp.where(low, gks[0], gks[1])
        gv = jnp.where(low, gvs[0], gvs[1])
        dq_ref[0, :, cols] = gq.astype(BF16)
        dkv_ref[0, :, cols] = gk.astype(BF16)
        dkv_ref[0, :, D + slab * LANES : D + (slab + 1) * LANES] = gv.astype(BF16)
        sum_ref[0:1, cols] += jnp.sum(gq, axis=0, keepdims=True)
        sum_ref[1:2, cols] += jnp.sum(gv, axis=0, keepdims=True)


def gqkv_kernel(
    owners_ref, n1_ref, dq_ref, dkv_ref, a_ref, dhr_ref, send_ref, keep_ref, n1t_ref, acc_ref
):
    step = pl.program_id(0)
    pairs, length, _ = n1_ref.shape
    slots = dq_ref.shape[1]

    @pl.when(step == 0)
    def _():
        n1t_ref[...] = n1_ref[...].reshape(pairs * length, D).T
        total = dot(n1t_ref[:, :slots], dq_ref[0])
        for pair in range(1, pairs):
            total += dot(n1t_ref[:, pair * length : pair * length + slots], dq_ref[pair])
        acc_ref[...] = total

    @pl.when(jnp.logical_or(step == 1, step == 2))
    def _():
        acc_ref[...] = dot(n1t_ref[...], dkv_ref[...].reshape(pairs * length, D))

    @pl.when(step == 3)
    def _():
        acc_ref[...] = dot_first(
            a_ref[...].reshape(pairs * slots, D), dhr_ref[...].reshape(pairs * slots, D)
        )

    spread(acc_ref, owners_ref, send_ref, keep_ref, D // (2 * send_ref.shape[0]))


def split_three(value):
    one = value.astype(BF16)
    left = value - one.astype(F32)
    two = left.astype(BF16)
    return one, two, (left - two.astype(F32)).astype(BF16)


def grad_in_kernel(
    meta, rows, place_ref, tok_ref, img_ref, vec_ref, dq_ref, dkv_ref, dh_ref, perm_ref, *refs
):
    pieces = refs[: len(meta)]
    out_ref, sum_ref, w_ref, sems = refs[len(meta) :]
    first = pl.program_id(0) == 0
    slots = dq_ref.shape[1]
    copies = piece_copies(meta, pieces, w_ref, sems, place_ref[0], place_ref[1], rows)

    @pl.when(first)
    def _():
        for copy in copies:
            copy.start()
        sum_ref[...] = jnp.zeros_like(sum_ref)
        for copy in copies:
            copy.wait()

    dn_all = dot_last(dkv_ref[0], w_ref[:, D:])
    dn_top = dn_all[:slots] + dot_last(dq_ref[0], w_ref[:, :D])
    dn = jnp.concatenate([dn_top, dn_all[slots:]], axis=0)
    normed, scale = normalize(start_row(tok_ref, img_ref, vec_ref))
    grad = norm_back(dn, normed, scale, vec_ref[2:3, :])
    grad = jnp.concatenate([grad[:slots] + dh_ref[0], grad[slots:]], axis=0)
    image = img_ref[0][:, :1] > 0.5
    sum_ref[0:1, :] += jnp.sum(jnp.where(image, 0.0, grad), axis=0, keepdims=True)
    sum_ref[1:2, :] += jnp.sum(jnp.where(image, grad, 0.0), axis=0, keepdims=True)
    sum_ref[2:3, :] += jnp.sum(dn * normed, axis=0, keepdims=True)
    sum_ref[3:4, :] += jnp.sum(dn, axis=0, keepdims=True)
    one, two, three = split_three(grad)
    perm = perm_ref[0]
    out_ref[0] = dot(perm, one) + dot(perm, two) + dot(perm, three)


def out_kernel(meta, rows, place_ref, z_ref, h1_ref, vec_ref, perm_ref, *refs):
    pieces = refs[: len(meta)]
    out_ref, w_ref, sems = refs[len(meta) :]
    first = pl.program_id(0) == 0
    copies = piece_copies(meta, pieces, w_ref, sems, place_ref[0], place_ref[1], rows)

    @pl.when(first)
    def _():
        for copy in copies:
            copy.start()
        for copy in copies:
            copy.wait()

    y = h1_ref[0] + dot(z_ref[0], w_ref[...]) + vec_ref[9 + PARTS : 10 + PARTS, :]
    out_ref[0] = dot(perm_ref[0], y.astype(BF16)).astype(BF16)


def place_kernel(place_ref, blocks_ref, out_ref):
    nb, rows, _ = blocks_ref.shape
    bits = nb.bit_length() - 1
    for spot in range(nb):
        mask = sum(((spot >> (bits - 1 - k)) & 1) << k for k in range(bits))
        start = pl.multiple_of((place_ref[2] ^ mask) * rows, 8)
        out_ref[pl.ds(start, rows), :] = blocks_ref[spot].astype(F32)


def shards(
    plan,
    tokens,
    cotangent,
    mask_pos,
    mask_count,
    w_qkv,
    m_qkv,
    v_qkv,
    w_out,
    m_out,
    v_out,
    w_fc1,
    m_fc1,
    v_fc1,
    w_fc2,
    m_fc2,
    v_fc2,
    vectors,
    m_vec,
    v_vec,
):
    pairs, length, _ = tokens.shape
    slots = mask_pos.shape[1]
    nf, nb, nd = plan.nf, plan.nb, plan.nd
    fi = lax.axis_index("fsdp")
    bi = lax.axis_index("batch")
    low_bit = bi & 1
    place = jnp.stack([fi, low_bit, bi]).astype(jnp.int32)
    prefetch = functools.partial(pltpu.PrefetchScalarGridSpec, num_scalar_prefetch=1)

    def call(kernel, grid, in_specs, out_specs, out_shape, scratch, estimate, name, scalars=1):
        return pl.pallas_call(
            kernel,
            grid_spec=pltpu.PrefetchScalarGridSpec(
                num_scalar_prefetch=scalars,
                grid=grid,
                in_specs=in_specs,
                out_specs=out_specs,
                scratch_shapes=scratch,
            ),
            out_shape=out_shape,
            cost_estimate=estimate,
            name=name,
        )

    def shape(dims, kind):
        return jax.ShapeDtypeStruct(dims, kind)

    def pair_spec(rows, cols):
        return pl.BlockSpec((1, rows, cols), lambda i, *_: (i, 0, 0))

    low_vec = vectors.astype(BF16)
    vec_parts = [low_vec]
    for bit in range(plan.fbits):
        vec_parts += [swap(part, "fsdp", bit, nf) for part in vec_parts]
    low_qkv = w_qkv.astype(BF16)
    qkv_pieces = gather_pieces(plan, low_qkv, low_bit)
    low_out = w_out.astype(BF16)
    out_pieces = gather_pieces(plan, low_out, low_bit)
    low_1 = w_fc1.astype(BF16)
    fc1_pieces = gather_pieces(plan, low_1, low_bit)
    low_2 = w_fc2.astype(BF16)
    fc2_pieces = gather_pieces(plan, low_2, low_bit)
    columns = []
    for spot in range(nf):
        chosen = vec_parts[0]
        for mask in range(1, nf):
            chosen = jnp.where((fi ^ mask) == spot, vec_parts[mask], chosen)
        columns.append(chosen)
    vec = jnp.concatenate(columns, axis=1).astype(F32)
    vec = jnp.pad(vec, ((0, 16 - NVEC), (0, 0)))
    vec_spec = full(vec.shape)

    rows_d, rows_f = D // nf, FF // nf
    meta_qkv, meta_out = piece_meta(qkv_pieces), piece_meta(out_pieces)
    meta_1, meta_2 = piece_meta(fc1_pieces), piece_meta(fc2_pieces)
    sems = lambda meta: pltpu.SemaphoreType.DMA((len(meta),))

    perm, tokp, img, dy = call(
        order_kernel,
        (pairs,),
        [
            pl.BlockSpec((1, 1, slots), lambda i, *_: (i, 0, 0)),
            pair_spec(length, D),
            pair_spec(length, D),
        ],
        [pair_spec(length, length), pair_spec(length, D), pair_spec(length, LANES), pair_spec(slots, D)],
        [
            shape((pairs, length, length), BF16),
            shape((pairs, length, D), BF16),
            shape((pairs, length, LANES), F32),
            shape((pairs, slots, D), BF16),
        ],
        [],
        cost(pairs * length * length * D * 4, pairs * length * D * 8),
        "order",
    )(mask_count, mask_pos.reshape(pairs, 1, slots), tokens, cotangent)

    n1, qkv, mixed = call(
        functools.partial(attn_kernel, meta_qkv, rows_d),
        (pairs,),
        [pair_spec(length, D), pair_spec(length, LANES), vec_spec] + [ANYWHERE] * len(meta_qkv),
        [pair_spec(length, D), pair_spec(length, 3 * D), pair_spec(length, D)],
        [
            shape((pairs, length, D), BF16),
            shape((pairs, length, 3 * D), BF16),
            shape((pairs, length, D), BF16),
        ],
        [pltpu.VMEM((D, 3 * D), BF16), sems(meta_qkv)],
        cost(pairs * length * (6 * D * D + 8 * length * D), pairs * length * D * 12, pairs * HEADS * length * length),
        "attn",
    )(place, tokp, img, vec, *piece_arrays(qkv_pieces))

    h1, n2, z, slope = call(
        functools.partial(fc1_kernel, meta_out, rows_d, meta_1, rows_d),
        (pairs,),
        [pair_spec(length, D), pair_spec(length, LANES), pair_spec(length, D), vec_spec]
        + [ANYWHERE] * (len(meta_out) + len(meta_1)),
        [pair_spec(length, D), pair_spec(length, D), pair_spec(length, FF), pair_spec(slots, FF)],
        [
            shape((pairs, length, D), F32),
            shape((pairs, length, D), BF16),
            shape((pairs, length, FF), BF16),
            shape((pairs, slots, FF), BF16),
        ],
        [pltpu.VMEM((D, D), BF16), pltpu.VMEM((D, FF), BF16), sems(meta_out), sems(meta_1)],
        cost(pairs * length * (2 * D * D + 2 * D * FF), pairs * length * D * 22, pairs * length * FF),
        "fc1",
    )(place, tokp, img, mixed, vec, *piece_arrays(out_pieces), *piece_arrays(fc1_pieces))

    order_2 = plan.orders["x"]
    masks_2 = plan.masks(order_2)
    halves = nf // 2
    bmask = masks_2["batch"][:nb]

    def gw2(half):
        def lhs_map(i, place_ref):
            flip = (1 - half) + 2 * i
            return (0, 0, place_ref[0] ^ flip)

        outs = [pl.BlockSpec((1, nb, FF // nd, D), lambda i, *_: (i, 0, 0, 0))]
        shapes = [shape((halves, nb, FF // nd, D), BF16)]
        if half == 0:
            outs.append(full((1, D)))
            shapes.append(shape((1, D), F32))
        return call(
            functools.partial(gw2_kernel, half, nb, bmask),
            (halves,),
            [pl.BlockSpec((pairs, slots, FF // nf), lhs_map), full((pairs, slots, D))],
            outs,
            shapes,
            [pltpu.VMEM((FF // nf, D), F32)],
            cost(pairs * slots * D * FF, pairs * slots * (FF + D) + FF * D),
            "gw2",
        )(place, z, dy)

    send_2, gb2 = gw2(0)
    (keep_2,) = gw2(1)
    rows_2 = FF // nd
    sum_2 = scatter_sum(
        plan, order_2, send_2.reshape(nd // 2, rows_2, D), keep_2.reshape(nd // 2, rows_2, D)
    )

    rows_1 = D // nd
    order_1 = plan.orders["y"]
    owners_1 = plan.owners(order_1, fi, bi)
    chunk = D
    top_rows = lambda cols, idx: pl.BlockSpec((pairs, slots, cols), idx)
    df, gb1, send_1, keep_1 = call(
        functools.partial(gw1_kernel, meta_2, rows_f),
        (FF // chunk,),
        [
            full((pairs, slots, D)),
            top_rows(chunk, lambda i, *_: (0, 0, i)),
            top_rows(D, lambda i, *_: (0, 0, 0)),
        ]
        + [ANYWHERE] * len(meta_2),
        [
            pl.BlockSpec((pairs * slots, chunk), lambda i, *_: (0, i)),
            pl.BlockSpec((1, chunk), lambda i, *_: (0, i)),
            pl.BlockSpec((nd // 2, rows_1, chunk), lambda i, *_: (0, 0, i)),
            pl.BlockSpec((nd // 2, rows_1, chunk), lambda i, *_: (0, 0, i)),
        ],
        [
            shape((pairs * slots, FF), BF16),
            shape((1, FF), F32),
            shape((nd // 2, rows_1, FF), BF16),
            shape((nd // 2, rows_1, FF), BF16),
        ],
        [
            pltpu.VMEM((FF, D), BF16),
            pltpu.VMEM((D, pairs * slots), BF16),
            pltpu.VMEM((D, chunk), F32),
            sems(meta_2),
        ],
        cost(pairs * slots * D * FF * 4, pairs * slots * FF * 4 + FF * D * 4),
        "gw1",
        scalars=2,
    )(place, owners_1, dy, slope, n2, *piece_arrays(fc2_pieces))
    sum_1 = scatter_sum(plan, order_1, send_1, keep_1)

    dh, dhr, da, sums_two = call(
        functools.partial(mlp_back_kernel, meta_1, rows_d, meta_out, rows_d),
        (pairs,),
        [
            pl.BlockSpec((slots, FF), lambda i, *_: (i, 0)),
            pair_spec(slots, D),
            pair_spec(slots, D),
            vec_spec,
        ]
        + [ANYWHERE] * (len(meta_1) + len(meta_out)),
        [pair_spec(slots, D), pair_spec(slots, D), pair_spec(slots, D), full((8, D))],
        [
            shape((pairs, slots, D), F32),
            shape((pairs, slots, D), BF16),
            shape((pairs, slots, D), BF16),
            shape((8, D), F32),
        ],
        [pltpu.VMEM((D, FF), BF16), pltpu.VMEM((D, D), BF16), sems(meta_1), sems(meta_out)],
        cost(pairs * slots * (2 * D * FF + 2 * D * D), pairs * slots * (FF * 2 + D * 14) + D * FF * 2),
        "mlp_back",
    )(place, df, dy, h1, vec, *piece_arrays(fc1_pieces), *piece_arrays(out_pieces))

    dq, dkv, sums_attn = pl.pallas_call(
        attn_back_kernel,
        grid=(pairs,),
        in_specs=[pair_spec(length, 3 * D), pair_spec(slots, D)],
        out_specs=[pair_spec(slots, D), pair_spec(length, 2 * D), full((8, D))],
        out_shape=[
            shape((pairs, slots, D), BF16),
            shape((pairs, length, 2 * D), BF16),
            shape((8, D), F32),
        ],
        cost_estimate=cost(
            pairs * slots * length * D * 20, pairs * length * D * 12, pairs * HEADS * slots * length
        ),
        name="attn_back",
    )(qkv, da)

    owners_3 = owners_1
    wide = 4 * D
    send_3, keep_3 = call(
        gqkv_kernel,
        (4,),
        [
            full((pairs, length, D)),
            full((pairs, slots, D)),
            pl.BlockSpec((pairs, length, D), lambda i, *_: (0, 0, jnp.where(i == 2, 1, 0))),
            top_rows(D, lambda i, *_: (0, 0, 0)),
            full((pairs, slots, D)),
        ],
        [
            pl.BlockSpec((nd // 2, rows_1, D), lambda i, *_: (0, 0, i)),
            pl.BlockSpec((nd // 2, rows_1, D), lambda i, *_: (0, 0, i)),
        ],
        [shape((nd // 2, rows_1, wide), BF16)] * 2,
        [pltpu.VMEM((D, pairs * length), BF16), pltpu.VMEM((D, D), F32)],
        cost(pairs * length * D * D * 6, pairs * length * D * 8 + D * D * 8),
        "gqkv",
    )(owners_3, n1, dq, dkv, mixed, dhr)
    sum_3 = scatter_sum(plan, order_1, send_3, keep_3)

    grad_tokens, sums_one = call(
        functools.partial(grad_in_kernel, meta_qkv, rows_d),
        (pairs,),
        [
            pair_spec(length, D),
            pair_spec(length, LANES),
            vec_spec,
            pair_spec(slots, D),
            pair_spec(length, 2 * D),
            pair_spec(slots, D),
            pair_spec(length, length),
        ]
        + [ANYWHERE] * len(meta_qkv),
        [pair_spec(length, D), full((8, D))],
        [shape((pairs, length, D), F32), shape((8, D), F32)],
        [pltpu.VMEM((D, 3 * D), BF16), sems(meta_qkv)],
        cost(pairs * length * (6 * D * D + 6 * length * D), pairs * length * D * 14 + D * D * 6),
        "grad_in",
    )(place, tokp, img, vec, dq, dkv, dh, perm, *piece_arrays(qkv_pieces))

    layer_out = call(
        functools.partial(out_kernel, meta_2, rows_f),
        (pairs,),
        [pair_spec(length, FF), pair_spec(length, D), vec_spec, pair_spec(length, length)]
        + [ANYWHERE] * len(meta_2),
        pair_spec(length, D),
        shape((pairs, length, D), BF16),
        [pltpu.VMEM((FF, D), BF16), sems(meta_2)],
        cost(pairs * length * (2 * D * FF + 2 * length * D), pairs * length * (FF * 2 + D * 6) + D * FF * 2),
        "out",
    )(place, z, h1, vec, perm, *piece_arrays(fc2_pieces))

    grad_vec = jnp.concatenate(
        [
            sums_one[0:4],
            sums_attn[0:2],
            sums_two[0:3],
            gb1.reshape(PARTS, D),
            gb2,
        ],
        axis=0,
    )
    for axis, bit in order_1:
        got = swap(grad_vec.astype(BF16), axis, bit, plan.size(axis))
        grad_vec = grad_vec + got.astype(F32)
    own_cols = D // nd
    grad_vec = lax.dynamic_slice_in_dim(grad_vec, (fi * nb + bi) * own_cols, own_cols, 1)

    def finish(master, gradient, moment_one, moment_two, which):
        rows = gradient.shape[0]
        own = lax.dynamic_slice_in_dim(master, bi * rows, rows, 0)
        new_w, new_m, new_v = adamw(
            own, gradient, moment_one, moment_two, STEP_RATES[which], DECAY_RATES[which]
        )
        return new_w.astype(BF16), new_m, new_v

    def place_blocks(blocks, width, start):
        rows = blocks.shape[1]
        if rows % 8 == 0:
            step = min(width, D)
            return call(
                place_kernel,
                (width // step,),
                [pl.BlockSpec((nb, rows, step), lambda i, *_: (0, 0, i + start // step))],
                pl.BlockSpec((nb * rows, step), lambda i, *_: (0, i)),
                shape((nb * rows, width), F32),
                [],
                cost(0, nb * rows * width * 6),
                "place",
            )(place, blocks)
        bits = plan.bbits
        spots = np.arange(nb)
        mask = sum(((spots >> (bits - 1 - k)) & 1) << k for k in range(bits))
        inverse = np.argsort(mask)
        picked = jnp.take(blocks, jnp.asarray(inverse)[spots ^ bi], axis=0)
        return picked[:, :, start : start + width].reshape(nb * rows, width).astype(F32)

    new_2, new_m2, new_v2 = finish(w_fc2, sum_2, m_fc2, v_fc2, 3)
    w2_all = gather_blocks(plan, new_2)
    new_1, new_m1, new_v1 = finish(w_fc1, sum_1, m_fc1, v_fc1, 2)
    w1_all = gather_blocks(plan, new_1)
    new_q, new_mq, new_vq = finish(w_qkv, sum_3[:, : 3 * D], m_qkv, v_qkv, 0)
    new_o, new_mo, new_vo = finish(w_out, sum_3[:, 3 * D :], m_out, v_out, 1)
    w3_all = gather_blocks(plan, jnp.concatenate([new_q, new_o], axis=1))
    own_vec = lax.dynamic_slice_in_dim(vectors, bi * own_cols, own_cols, 1)
    new_vec, new_mv, new_vv = adamw(
        own_vec, grad_vec, m_vec, v_vec, STEP_RATES[4], DECAY_RATES[4]
    )
    vec_all = gather_blocks(plan, new_vec.astype(BF16))
    bits = plan.bbits
    spots = np.arange(nb)
    mask = sum(((spots >> (bits - 1 - k)) & 1) << k for k in range(bits))
    inverse = np.argsort(mask)
    vec_nat = jnp.take(vec_all, jnp.asarray(inverse)[spots ^ bi], axis=0)
    vec_new = jnp.transpose(vec_nat, (1, 0, 2)).reshape(NVEC, nb * own_cols).astype(F32)

    return (
        layer_out,
        grad_tokens,
        place_blocks(w3_all, 3 * D, 0),
        new_mq,
        new_vq,
        place_blocks(w3_all, D, 3 * D),
        new_mo,
        new_vo,
        place_blocks(w1_all, FF, 0),
        new_m1,
        new_v1,
        place_blocks(w2_all, D, 0),
        new_m2,
        new_v2,
        vec_new,
        new_mv,
        new_vv,
    )


def solution(mesh):
    pairs = P(("batch", "fsdp"), None, None)
    weight = P("fsdp", None)
    state = P(("fsdp", "batch"), None)
    vec_state = P(None, ("fsdp", "batch"))
    matrix = (weight, state, state)
    return jax.shard_map(
        functools.partial(shards, Plan(mesh)),
        mesh=mesh,
        in_specs=(pairs, pairs, P(("batch", "fsdp"), None), P(("batch", "fsdp")))
        + matrix * 4
        + (P(None, "fsdp"), vec_state, vec_state),
        out_specs=(pairs, pairs) + matrix * 4 + (P(None, "fsdp"), vec_state, vec_state),
        check_vma=False,
    )
```

```python
import functools
import math

import jax
import jax.numpy as jnp
import numpy as np
from jax import lax
from jax.experimental import pallas as pl
from jax.experimental.pallas import tpu as pltpu
from jax.sharding import PartitionSpec as P

D = 768
HEADS = 12
HDIM = 64
FF = 3072
TEXT = 40
STEP = 3
MAXM = 128
NVEC = 14
PARTS = FF // D
LANES = 128
SLABS = D // LANES

BETA_ONE = 0.5
BETA_TWO = 0.5
EPS_ADAM = 1e-08
STEP_RATES = (0.03, 0.1, 0.03, 0.015, 0.3)
DECAY_RATES = (0.01, 0.01, 0.01, 0.01, 0.0)
INV_ROOT_TWO = 1.0 / math.sqrt(2.0)
INV_ROOT_TWOPI = 1.0 / math.sqrt(2.0 * math.pi)

FLOPS_SCALE = 3e9
BYTES_SCALE = 1e7
F32 = jnp.float32
BF16 = jnp.bfloat16


def dot(a, b):
    return lax.dot_general(a, b, (((1,), (0,)), ((), ())), preferred_element_type=F32)


def dot_first(a, b):
    return lax.dot_general(a, b, (((0,), (0,)), ((), ())), preferred_element_type=F32)


def dot_last(a, b):
    return lax.dot_general(a, b, (((1,), (1,)), ((), ())), preferred_element_type=F32)


def normalize(hidden):
    row_mean = jnp.mean(hidden, axis=-1, keepdims=True)
    centred = hidden - row_mean
    inv_scale = lax.rsqrt(jnp.mean(centred * centred, axis=-1, keepdims=True) + 1e-06)
    return centred * inv_scale, inv_scale


def norm_back(gradient, normed, inv_scale, gain_row):
    scaled = gradient * gain_row
    return inv_scale * (
        scaled
        - jnp.mean(scaled, axis=-1, keepdims=True)
        - normed * jnp.mean(scaled * normed, axis=-1, keepdims=True)
    )


def adamw(weight, gradient, moment_one, moment_two, step_rate, decay_rate):
    new_first = BETA_ONE * moment_one + (1.0 - BETA_ONE) * gradient
    new_second = BETA_TWO * moment_two + (1.0 - BETA_TWO) * gradient * gradient
    correct_one = 1.0 - BETA_ONE**STEP
    correct_two = 1.0 - BETA_TWO**STEP
    update = (
        new_first / correct_one / (jnp.sqrt(new_second / correct_two) + EPS_ADAM)
        + decay_rate * weight
    )
    return (weight - step_rate * update, new_first, new_second)


def spent(micros):
    return pl.CostEstimate(
        flops=int(micros * FLOPS_SCALE), bytes_accessed=int(micros * BYTES_SCALE), transcendentals=0
    )


def full(shape):
    zeros = (0,) * len(shape)
    return pl.BlockSpec(shape, lambda *_: zeros)


ANYWHERE = pl.BlockSpec(memory_space=pl.ANY)


class Plan:
    def __init__(self, mesh):
        self.nf = mesh.shape["fsdp"]
        self.nb = mesh.shape["batch"]
        self.nd = self.nf * self.nb
        self.fbits = self.nf.bit_length() - 1
        self.bbits = self.nb.bit_length() - 1
        assert self.nf == 1 << self.fbits and self.nb == 1 << self.bbits
        assert self.fbits == 2 and self.bbits >= 2
        near = [1, 2, 6] if self.bbits == 3 else [1 << k for k in range(self.bbits)]
        self.batch = [mask * self.nf for mask in near]
        first, second, *rest = self.batch
        self.scatter = ([1, 2, second, first] + rest, [1, first, 2, second] + rest)
        self.gather = (rest[::-1] + [second, first], rest[::-1] + [first, second])
        self.helper = (first, second)

    def exchange(self, value, even, odd=None):
        odd = even if odd is None else odd
        pairs = [(i, i ^ (odd if i & 1 else even)) for i in range(self.nd)]
        return lax.ppermute(value, ("batch", "fsdp"), pairs)

    def spans(self, gens):
        masks = np.zeros(1, np.int32)
        for mask in reversed(gens):
            masks = np.concatenate([masks, masks ^ mask])
        return masks

    def owners(self, fi, bi):
        mine = bi * self.nf + fi
        even, odd = (jnp.asarray(self.spans(order[1:]), jnp.int32) for order in self.scatter)
        is_even = (fi & 1) == 0
        keep = mine ^ jnp.where(is_even, even, odd)
        send = (mine ^ 1) ^ jnp.where(is_even, odd, even)
        index = jnp.concatenate([keep, send])
        return (index & (self.nf - 1)) * self.nb + (index >> self.fbits)

    def gathered(self, fi, bi):
        even, odd = (
            jnp.asarray(self.spans(gens[::-1]) >> self.fbits, jnp.int32) for gens in self.gather
        )
        return bi ^ jnp.where((fi & 1) == 0, even, odd)


PIECES = ((0, None), (1, None), (2, 0), (2, 1), (3, 2), (3, 3))


def piece_copies(refs, target, sems, place_ref, rows, start=0):
    copies = []
    cols = target.shape[1]
    for number, ((mask, kind), ref) in enumerate(zip(PIECES, refs)):
        row = (place_ref[0] ^ mask) * rows
        length = rows
        if kind is not None:
            length = rows // 2
            low = place_ref[1 + kind // 2]
            row = row + (low if kind % 2 == 0 else 1 - low) * length
        copies.append(
            pltpu.make_async_copy(
                ref.at[:, pl.ds(start, cols)],
                target.at[pl.ds(pl.multiple_of(row, 8), length)],
                sems.at[number],
            )
        )
    return copies


def start_all(copies):
    for copy in copies:
        copy.start()


def wait_all(copies):
    for copy in copies:
        copy.wait()


def cast_kernel(place_ref, *refs):
    parts, (shard_ref, mine_ref) = refs[:-2], refs[-2:]
    start = 0
    for part in parts:
        cols = slice(start, start + part.shape[1])
        low = part[...].astype(BF16)
        shard_ref[:, cols] = low

        @pl.when(pl.program_id(0) == 0)
        def _(low=low, cols=cols):
            mine_ref[:, cols] = low

        start += part.shape[1]


def order_kernel(count_ref, pos_ref, tok_ref, cot_ref, perm_ref, tokp_ref, img_ref, dy_ref):
    pair = pl.program_id(0)
    length = tok_ref.shape[1]
    slots = pos_ref.shape[2]
    token = lax.broadcasted_iota(jnp.int32, (length, slots), 0)
    slot = lax.broadcasted_iota(jnp.int32, (length, slots), 1)
    hit = jnp.where(token == pos_ref[0], 1.0, 0.0)
    free = 1.0 - jnp.sum(hit, axis=1, keepdims=True)
    below = lax.broadcasted_iota(jnp.int32, (length, length), 1) < lax.broadcasted_iota(
        jnp.int32, (length, length), 0
    )
    rank = dot(
        jnp.where(below, 1.0, 0.0).astype(BF16),
        jnp.broadcast_to(free, (length, slots)).astype(BF16),
    )
    rest = jnp.where(rank == slot.astype(F32), jnp.broadcast_to(free, (length, slots)), 0.0)
    perm = jnp.concatenate([hit, rest], axis=1).astype(BF16)
    perm_ref[0] = perm
    tokp_ref[0] = dot_first(perm, tok_ref[0]).astype(BF16)
    image = jnp.where(lax.broadcasted_iota(jnp.int32, (length, LANES), 0) >= TEXT, 1.0, 0.0)
    img_ref[0] = dot_first(perm, image.astype(BF16))
    chosen = dot_first(perm[:, :slots], cot_ref[0])
    live = lax.broadcasted_iota(jnp.int32, (slots, 1), 0) < count_ref[pair]
    dy_ref[0] = jnp.where(live, chosen, 0.0).astype(BF16)


def start_row(tok_ref, img_ref, vec_ref):
    return tok_ref[0].astype(F32) + jnp.where(
        img_ref[0][:, :1] > 0.5, vec_ref[1:2, :], vec_ref[0:1, :]
    )


def qkv_kernel(rows, place_ref, tok_ref, img_ref, vec_ref, *refs):
    pieces = refs[: len(PIECES)]
    n1_ref, qkv_ref, w_ref, sems = refs[len(PIECES) :]
    first = pl.program_id(0) == 0
    copies = piece_copies(pieces, w_ref, sems, place_ref, rows)

    @pl.when(first)
    def _():
        start_all(copies)

    normed, _ = normalize(start_row(tok_ref, img_ref, vec_ref))
    n1 = (normed * vec_ref[2:3, :] + vec_ref[3:4, :]).astype(BF16)
    n1_ref[0] = n1

    @pl.when(first)
    def _():
        wait_all(copies)

    qkv_ref[0, :, :D] = (dot(n1, w_ref[:, :D]) + vec_ref[4:5, :]).astype(BF16)
    qkv_ref[0, :, D : 2 * D] = dot(n1, w_ref[:, D : 2 * D]).astype(BF16)
    qkv_ref[0, :, 2 * D :] = (dot(n1, w_ref[:, 2 * D :]) + vec_ref[5:6, :]).astype(BF16)


def mix_kernel(qkv_ref, a_ref):
    low = lax.broadcasted_iota(jnp.int32, (1, LANES), 1) < HDIM
    for slab in range(SLABS):
        cols = slice(slab * LANES, (slab + 1) * LANES)
        q = qkv_ref[0, :, cols] * jnp.asarray(HDIM**-0.5, BF16)
        k = qkv_ref[0, :, D + slab * LANES : D + (slab + 1) * LANES]
        v = qkv_ref[0, :, 2 * D + slab * LANES : 2 * D + (slab + 1) * LANES]
        outs = []
        for head in range(2):
            mine = low if head == 0 else jnp.logical_not(low)
            scores = dot_last(jnp.where(mine, q, jnp.zeros_like(q)), k)
            e = jnp.exp(scores - jnp.max(scores, axis=-1, keepdims=True))
            p = (e * (1.0 / jnp.sum(e, axis=-1, keepdims=True))).astype(BF16)
            outs.append(dot(p, v))
        a_ref[0, :, cols] = jnp.where(low, outs[0], outs[1]).astype(BF16)


def fc1_kernel(rows, place_ref, tok_ref, img_ref, a_ref, vec_ref, *refs):
    pieces = refs[: len(PIECES)]
    h1_ref, n2_ref, z_ref, slope_ref, wo_ref, w1_ref, sem_o, sem_1 = refs[len(PIECES) :]
    first = pl.program_id(0) == 0
    copies_o = piece_copies(pieces, wo_ref, sem_o, place_ref, rows)
    copies_1 = piece_copies(pieces, w1_ref, sem_1, place_ref, rows, D)

    @pl.when(first)
    def _():
        start_all(copies_o)
        start_all(copies_1)
        wait_all(copies_o)

    h1 = start_row(tok_ref, img_ref, vec_ref) + dot(a_ref[0], wo_ref[...]) + vec_ref[6:7, :]
    h1_ref[0] = h1
    normed, _ = normalize(h1)
    n2 = (normed * vec_ref[7:8, :] + vec_ref[8:9, :]).astype(BF16)
    n2_ref[0] = n2

    @pl.when(first)
    def _():
        wait_all(copies_1)

    slots = slope_ref.shape[1]
    for part in range(PARTS):
        cols = slice(part * D, (part + 1) * D)
        f = dot(n2, w1_ref[:, cols]) + vec_ref[9 + part : 10 + part, :]
        phi = 0.5 * (1.0 + lax.erf(f * INV_ROOT_TWO))
        z_ref[0, :, cols] = (f * phi).astype(BF16)
        fs = f[:slots]
        slope = phi[:slots] + fs * jnp.exp(-0.5 * fs * fs) * INV_ROOT_TWOPI
        slope_ref[0, :, cols] = slope.astype(BF16)


def spread(acc_ref, owners_ref, outs):
    if len(outs) == 1:
        outs[0][...] = acc_ref[...].astype(BF16)
        return
    keep_ref, send_ref = outs
    half, block, _ = send_ref.shape
    for out_ref, base in ((send_ref, half), (keep_ref, 0)):
        for spot in range(half):
            start = pl.multiple_of(owners_ref[base + spot] * block, 8)
            out_ref[spot] = acc_ref[pl.ds(start, block), :].astype(BF16)


def gw2_kernel(owners_ref, z_ref, dy_ref, *refs):
    outs, (sum_ref, zt_ref, acc_ref) = refs[:-3], refs[-3:]
    pairs, slots, width = z_ref.shape

    @pl.when(pl.program_id(0) == 0)
    def _():
        zt_ref[...] = z_ref[...].reshape(pairs * slots, width).T

    dy = dy_ref[...].reshape(pairs * slots, -1)
    acc_ref[...] = dot(zt_ref[...], dy)
    sum_ref[...] = jnp.sum(dy.astype(F32), axis=0, keepdims=True)
    spread(acc_ref, owners_ref, outs)


def df_kernel(rows, place_ref, dy_ref, slope_ref, *refs):
    pieces = refs[: len(PIECES)]
    df_ref, gb1_ref, w2_ref, sems = refs[len(PIECES) :]
    step = pl.program_id(0)
    pairs, slots, width = slope_ref.shape
    total = pairs * slots
    copies = piece_copies(pieces, w2_ref, sems, place_ref, rows)

    @pl.when(step == 0)
    def _():
        start_all(copies)
        wait_all(copies)

    dz = dot_last(
        dy_ref[...].reshape(total, D), w2_ref[pl.ds(pl.multiple_of(step * width, 8), width), :]
    )
    df = dz * slope_ref[...].reshape(total, width).astype(F32)
    gb1_ref[...] = jnp.sum(df, axis=0, keepdims=True)
    df_ref[...] = df.astype(BF16)


def mlp_back_kernel(rows, place_ref, df_ref, dy_ref, h1_ref, vec_ref, *refs):
    pieces = refs[: len(PIECES)]
    dh_ref, dhr_ref, da_ref, sum_ref, w1_ref, wo_ref, sem_1, sem_o = refs[len(PIECES) :]
    first = pl.program_id(0) == 0
    copies_1 = piece_copies(pieces, w1_ref, sem_1, place_ref, rows, D)
    copies_o = piece_copies(pieces, wo_ref, sem_o, place_ref, rows)

    @pl.when(first)
    def _():
        start_all(copies_1)
        start_all(copies_o)
        sum_ref[...] = jnp.zeros_like(sum_ref)
        wait_all(copies_1)
        wait_all(copies_o)

    some, slots, _ = dy_ref.shape
    total = some * slots
    dn2 = dot_last(df_ref[...], w1_ref[...])
    normed, scale = normalize(h1_ref[...].reshape(total, D))
    dh = dy_ref[...].reshape(total, D).astype(F32) + norm_back(dn2, normed, scale, vec_ref[7:8, :])
    dh_ref[...] = dh.reshape(some, slots, D)
    sum_ref[0:1, :] += jnp.sum(dh, axis=0, keepdims=True)
    sum_ref[1:2, :] += jnp.sum(dn2 * normed, axis=0, keepdims=True)
    sum_ref[2:3, :] += jnp.sum(dn2, axis=0, keepdims=True)
    low = dh.astype(BF16)
    dhr_ref[...] = low.reshape(some, slots, D)
    da_ref[...] = dot_last(low, wo_ref[...]).astype(BF16).reshape(some, slots, D)


def gw1o_kernel(owners_ref, n2_ref, df_ref, a_ref, dhr_ref, *refs):
    outs, (n2t_ref, acc_ref) = refs[:-2], refs[-2:]
    step = pl.program_id(0)
    pairs, slots, _ = n2_ref.shape
    total = pairs * slots

    @pl.when(step == 0)
    def _():
        n2t_ref[...] = n2_ref[...].reshape(total, D).T

    @pl.when(step < PARTS)
    def _():
        acc_ref[...] = dot(n2t_ref[...], df_ref[...])

    @pl.when(step == PARTS)
    def _():
        acc_ref[...] = dot_first(a_ref[...].reshape(total, D), dhr_ref[...].reshape(total, D))

    spread(acc_ref, owners_ref, outs)


def attn_back_kernel(more, qkv_ref, da_ref, *refs):
    if more:
        _, _, before_ref, dq_ref, dkv_ref, sum_ref = refs
    else:
        dq_ref, dkv_ref, sum_ref = refs
    slots = da_ref.shape[1]

    @pl.when(pl.program_id(0) == 0)
    def _():
        sum_ref[...] = before_ref[...] if more else jnp.zeros_like(sum_ref)

    low = lax.broadcasted_iota(jnp.int32, (1, LANES), 1) < HDIM
    scale = jnp.asarray(HDIM**-0.5, BF16)
    for slab in range(SLABS):
        cols = slice(slab * LANES, (slab + 1) * LANES)
        q = qkv_ref[0, :slots, cols] * scale
        k = qkv_ref[0, :, D + slab * LANES : D + (slab + 1) * LANES]
        v = qkv_ref[0, :, 2 * D + slab * LANES : 2 * D + (slab + 1) * LANES]
        da = da_ref[0, :, cols]
        gqs, gks, gvs = [], [], []
        for head in range(2):
            mine = low if head == 0 else jnp.logical_not(low)
            zero = jnp.zeros_like(q)
            scores = dot_last(jnp.where(mine, q, zero), k)
            e = jnp.exp(scores - jnp.max(scores, axis=-1, keepdims=True))
            p = e * (1.0 / jnp.sum(e, axis=-1, keepdims=True))
            gvs.append(dot_first(p.astype(BF16), da))
            dp = dot_last(jnp.where(mine, da, zero), v)
            ds = (p * (dp - jnp.sum(p * dp, axis=-1, keepdims=True))).astype(BF16)
            gqs.append(dot(ds, k))
            gks.append(dot_first(ds, q))
        gq = jnp.where(low, gqs[0], gqs[1]) * (HDIM**-0.5)
        gk = jnp.where(low, gks[0], gks[1])
        gv = jnp.where(low, gvs[0], gvs[1])
        dq_ref[0, :, cols] = gq.astype(BF16)
        dkv_ref[0, :, cols] = gk.astype(BF16)
        dkv_ref[0, :, D + slab * LANES : D + (slab + 1) * LANES] = gv.astype(BF16)
        sum_ref[0:1, cols] += jnp.sum(gq, axis=0, keepdims=True)
        sum_ref[1:2, cols] += jnp.sum(gv, axis=0, keepdims=True)


def gqkv_kernel(owners_ref, n1_ref, dq_ref, dkv_ref, *refs):
    outs, (n1t_ref, acc_ref) = refs[:-2], refs[-2:]
    step = pl.program_id(0)
    pairs, length, _ = n1_ref.shape
    slots = dq_ref.shape[1]

    @pl.when(step == 0)
    def _():
        n1t_ref[...] = n1_ref[...].reshape(pairs * length, D).T
        total = dot(n1t_ref[:, :slots], dq_ref[0])
        for pair in range(1, pairs):
            total += dot(n1t_ref[:, pair * length : pair * length + slots], dq_ref[pair])
        acc_ref[...] = total

    @pl.when(step > 0)
    def _():
        acc_ref[...] = dot(n1t_ref[...], dkv_ref[...].reshape(pairs * length, D))

    spread(acc_ref, owners_ref, outs)


def split_three(value):
    one = value.astype(BF16)
    left = value - one.astype(F32)
    two = left.astype(BF16)
    return one, two, (left - two.astype(F32)).astype(BF16)


def grad_in_kernel(
    rows,
    place_ref,
    tok_ref,
    img_ref,
    vec_ref,
    dq_ref,
    dkv_ref,
    dh_ref,
    perm_ref,
    attn_sum_ref,
    mlp_sum_ref,
    gb1_ref,
    gb2_ref,
    *refs,
):
    pieces = refs[: len(PIECES)]
    out_ref, sum_ref, w_ref, sems = refs[len(PIECES) :]
    first = pl.program_id(0) == 0
    slots = dq_ref.shape[1]
    copies = piece_copies(pieces, w_ref, sems, place_ref, rows)

    @pl.when(first)
    def _():
        start_all(copies)
        sum_ref[...] = jnp.zeros_like(sum_ref)
        sum_ref[4:6, :] = attn_sum_ref[0:2, :]
        sum_ref[6:9, :] = mlp_sum_ref[0:3, :]
        for part in range(PARTS):
            sum_ref[9 + part : 10 + part, :] = gb1_ref[:, part * D : (part + 1) * D]
        sum_ref[9 + PARTS : 10 + PARTS, :] = gb2_ref[...]
        wait_all(copies)

    dn_all = dot_last(dkv_ref[0], w_ref[:, D:])
    dn_top = dn_all[:slots] + dot_last(dq_ref[0], w_ref[:, :D])
    dn = jnp.concatenate([dn_top, dn_all[slots:]], axis=0)
    normed, scale = normalize(start_row(tok_ref, img_ref, vec_ref))
    grad = norm_back(dn, normed, scale, vec_ref[2:3, :])
    grad = jnp.concatenate([grad[:slots] + dh_ref[0], grad[slots:]], axis=0)
    image = img_ref[0][:, :1] > 0.5
    sum_ref[0:1, :] += jnp.sum(jnp.where(image, 0.0, grad), axis=0, keepdims=True)
    sum_ref[1:2, :] += jnp.sum(jnp.where(image, grad, 0.0), axis=0, keepdims=True)
    sum_ref[2:3, :] += jnp.sum(dn * normed, axis=0, keepdims=True)
    sum_ref[3:4, :] += jnp.sum(dn, axis=0, keepdims=True)
    one, two, three = split_three(grad)
    perm = perm_ref[0]
    out_ref[0] = dot(perm, one) + dot(perm, two) + dot(perm, three)


def out_kernel(rows, place_ref, z_ref, h1_ref, vec_ref, perm_ref, *refs):
    pieces = refs[: len(PIECES)]
    out_ref, w_ref, sems = refs[len(PIECES) :]
    first = pl.program_id(0) == 0
    copies = piece_copies(pieces, w_ref, sems, place_ref, rows)

    @pl.when(first)
    def _():
        start_all(copies)
        wait_all(copies)

    y = h1_ref[0] + dot(z_ref[0], w_ref[...]) + vec_ref[9 + PARTS : 10 + PARTS, :]
    out_ref[0] = dot(perm_ref[0], y.astype(BF16)).astype(BF16)


def add_kernel(count, *refs):
    ins, outs = refs[: -1 - (len(refs) > count + 1)], refs[-1 - (len(refs) > count + 1) :]
    total = ins[0][...].astype(F32)
    for ref in ins[1:count]:
        total = total + ref[...].astype(F32)
    outs[0][...] = total.astype(BF16)
    if len(outs) > 1:
        outs[1][...] = ins[count][...] + ins[count + 1][...]


def finish_kernel(count, which, place_ref, *refs):
    parts = refs[:count]
    number = len(which)
    states = refs[count : count + 3 * number]
    new_ref = refs[count + 3 * number]
    moments = refs[count + 3 * number + 1 :]
    total = parts[0][0].astype(F32)
    for ref in parts[1:]:
        total = total + ref[0].astype(F32)
    start = 0
    for spot, kind in enumerate(which):
        master, first, second = states[3 * spot : 3 * spot + 3]
        cols = slice(start, start + master.shape[1])
        new_w, new_m, new_v = adamw(
            master[...], total[:, cols], first[...], second[...], STEP_RATES[kind], DECAY_RATES[kind]
        )
        new_ref[0, :, cols] = new_w.astype(BF16)
        moments[2 * spot][...] = new_m
        moments[2 * spot + 1][...] = new_v
        start += master.shape[1]


def join_kernel(one_ref, two_ref, out_ref):
    count = one_ref.shape[0]
    out_ref[:count] = one_ref[...]
    out_ref[count:] = two_ref[...]


def place_kernel(number, spots_ref, blocks_ref, *refs):
    start = 0
    for out_ref in refs[-number:]:
        width = out_ref.shape[1]
        out_ref[...] = blocks_ref[0, :, start : start + width].astype(F32)
        start += width


def later(value, dep):
    return lax.optimization_barrier((value, dep))[0]


class Chain:
    def __init__(self):
        self.last = None

    def __call__(
        self, kernel, grid, scalars, ins, outs, scratch, estimate, name, after=(), aliases=None
    ):
        deps = list(after)
        if self.last is not None:
            deps.append(self.last)
        fixed = len(scalars) + len(ins)
        extra = len(deps)

        def body(*refs):
            kernel(*refs[:fixed], *refs[fixed + extra :])

        got = pl.pallas_call(
            body,
            grid_spec=pltpu.PrefetchScalarGridSpec(
                num_scalar_prefetch=len(scalars),
                grid=grid,
                in_specs=[spec for _, spec in ins] + [ANYWHERE] * extra,
                out_specs=[spec for spec, _, _ in outs],
                scratch_shapes=scratch,
            ),
            out_shape=[jax.ShapeDtypeStruct(dims, kind) for _, dims, kind in outs],
            input_output_aliases={
                len(scalars) + k: v for k, v in (aliases or {}).items()
            },
            cost_estimate=estimate,
            name=name,
        )(*scalars, *[value for value, _ in ins], *deps)
        self.last = got[-1]
        return got


class Sum:
    def __init__(self, plan, call, keep, send):
        self.plan, self.call = plan, call
        self.parts, self.count, self.place = [keep], keep.shape[0], 0
        self.move(send)

    def move(self, send):
        got = self.plan.exchange(send, *(order[self.place] for order in self.plan.scatter))
        self.parts.append(got)
        self.place += 1

    def add(self, vec=None):
        self.count //= 2
        count = self.count
        _, rows, cols = self.parts[0].shape
        block = max(1, count // 4)
        base = count // block
        spec = pl.BlockSpec((block, rows, cols), lambda i, *_: (base + i, 0, 0))
        ins = [(part, spec) for part in self.parts]
        outs = [
            (pl.BlockSpec((block, rows, cols), lambda i, *_: (i, 0, 0)), (count, rows, cols), BF16)
        ]
        if vec is not None:
            ins += [(value, full(value.shape)) for value in vec]
            outs.append((full(vec[0].shape), vec[0].shape, F32))
        size = count * rows * cols
        got = self.call(
            functools.partial(add_kernel, len(self.parts)),
            (count // block,),
            [],
            ins,
            outs,
            [],
            spent(1.5),
            "add",
        )
        self.move(got[0])
        return got[1] if vec is not None else None


class Spread:
    def __init__(self, plan, call, block):
        self.plan, self.call, self.blocks, self.place = plan, call, block, 0
        self.move()

    def move(self):
        self.got = self.plan.exchange(self.blocks, *(order[self.place] for order in self.plan.gather))
        self.place += 1

    def join(self):
        shape = self.blocks.shape
        self.blocks = self.call(
            join_kernel,
            (1,),
            [],
            [(self.blocks, full(shape)), (self.got, full(shape))],
            [(full((2 * shape[0],) + shape[1:]), (2 * shape[0],) + shape[1:], BF16)],
            [],
            spent(0.3),
            "join",
        )[0]
        self.move()

    def put(self, spots, widths, before=None):
        blocks = self.blocks if before is None else self.got
        count, rows, cols = blocks.shape
        base = 0 if before is None else count
        nb = self.plan.nb
        ins = [(blocks, pl.BlockSpec((1, rows, cols), lambda i, *_: (i, 0, 0)))]
        aliases = None
        if before is not None:
            ins += [(value, ANYWHERE) for value in before]
            aliases = {1 + k: k for k in range(len(widths))}
        return self.call(
            functools.partial(place_kernel, len(widths)),
            (count,),
            [spots],
            ins,
            [
                (
                    pl.BlockSpec((rows, width), lambda i, spots_ref: (spots_ref[base + i], 0)),
                    (nb * rows, width),
                    F32,
                )
                for width in widths
            ],
            [],
            spent(0.1),
            "place",
            aliases=aliases,
        )


def shards(
    plan,
    tokens,
    cotangent,
    mask_pos,
    mask_count,
    w_qkv,
    m_qkv,
    v_qkv,
    w_out,
    m_out,
    v_out,
    w_fc1,
    m_fc1,
    v_fc1,
    w_fc2,
    m_fc2,
    v_fc2,
    vectors,
    m_vec,
    v_vec,
):
    pairs, length, _ = tokens.shape
    slots = mask_pos.shape[1]
    nf, nb, nd = plan.nf, plan.nb, plan.nd
    fi = lax.axis_index("fsdp").astype(jnp.int32)
    bi = lax.axis_index("batch").astype(jnp.int32)
    halves = jnp.stack([bi & 1, (bi >> 1) & 1])
    place = jnp.stack([fi, halves[fi & 1], halves[1 - (fi & 1)], bi])
    owners = plan.owners(fi, bi)
    spots = plan.gathered(fi, bi)
    call = Chain()

    def pair_spec(rows, cols):
        return pl.BlockSpec((1, rows, cols), lambda i, *_: (i, 0, 0))

    def piece_ins(pieces):
        return [(value, ANYWHERE) for value in pieces]

    sems = pltpu.SemaphoreType.DMA((len(PIECES),))
    rows_d, rows_f = D // nf, FF // nf

    low_vec = vectors.astype(BF16)
    vec_parts = [low_vec, plan.exchange(low_vec, 1)]
    vec_parts += [plan.exchange(part, 2) for part in vec_parts]
    columns = []
    for spot in range(nf):
        chosen = vec_parts[0]
        for mask in range(1, nf):
            chosen = jnp.where((fi ^ mask) == spot, vec_parts[mask], chosen)
        columns.append(chosen)
    vec = jnp.concatenate(columns, axis=1).astype(F32)
    vec = jnp.pad(vec, ((0, 16 - NVEC), (0, 0)))
    vec_in = (vec, full(vec.shape))

    def cast(shard_list, after=()):
        rows = shard_list[0].shape[0]
        half = rows // 2
        cols = sum(value.shape[1] for value in shard_list)
        row = lambda i, place_ref: (i ^ place_ref[1], 0)
        shard, mine = call(
            cast_kernel,
            (2,),
            [place],
            [(value, pl.BlockSpec((half, value.shape[1]), row)) for value in shard_list],
            [
                (pl.BlockSpec((half, cols), row), (rows, cols), BF16),
                (pl.BlockSpec((half, cols), lambda i, *_: (0, 0)), (half, cols), BF16),
            ],
            [],
            spent(rows * cols / 2e5),
            "cast",
            after,
        )
        return [shard, plan.exchange(shard, 1), plan.exchange(mine, 2)]

    def spread_pieces(pieces, dep=None):
        near = pieces[2]
        ready = near if dep is None else later(near, dep)
        other = plan.exchange(ready, *plan.helper)
        return pieces[:2] + [near, other, plan.exchange(ready, 1)]

    def last_piece(pieces, dep=None):
        other = pieces[3]
        return pieces + [plan.exchange(other if dep is None else later(other, dep), 1)]

    set_a = cast([w_qkv])

    perm, tokp, img, dy = call(
        order_kernel,
        (pairs,),
        [mask_count],
        [
            (mask_pos.reshape(pairs, 1, slots), pl.BlockSpec((1, 1, slots), lambda i, *_: (i, 0, 0))),
            (tokens, pair_spec(length, D)),
            (cotangent, pair_spec(length, D)),
        ],
        [
            (pair_spec(length, length), (pairs, length, length), BF16),
            (pair_spec(length, D), (pairs, length, D), BF16),
            (pair_spec(length, LANES), (pairs, length, LANES), F32),
            (pair_spec(slots, D), (pairs, slots, D), BF16),
        ],
        [],
        spent(6),
        "order",
    )

    set_b = cast([w_out, w_fc1])
    near_a = set_a[2]
    set_a = last_piece(spread_pieces(set_a))
    set_c = cast([w_fc2], [near_a])

    n1, qkv = call(
        functools.partial(qkv_kernel, rows_d),
        (pairs,),
        [place],
        [(tokp, pair_spec(length, D)), (img, pair_spec(length, LANES)), vec_in] + piece_ins(set_a),
        [
            (pair_spec(length, D), (pairs, length, D), BF16),
            (pair_spec(length, 3 * D), (pairs, length, 3 * D), BF16),
        ],
        [pltpu.VMEM((D, 3 * D), BF16), sems],
        spent(1),
        "qkv",
    )

    near_b = set_b[2]
    set_b = spread_pieces(set_b, n1)
    (mixed,) = call(
        mix_kernel,
        (pairs,),
        [],
        [(qkv, pair_spec(length, 3 * D))],
        [(pair_spec(length, D), (pairs, length, D), BF16)],
        [],
        spent(1),
        "mix",
        [near_b],
    )

    set_b = last_piece(set_b, mixed)
    h1, n2, z, slope = call(
        functools.partial(fc1_kernel, rows_d),
        (pairs,),
        [place],
        [
            (tokp, pair_spec(length, D)),
            (img, pair_spec(length, LANES)),
            (mixed, pair_spec(length, D)),
            vec_in,
        ]
        + piece_ins(set_b),
        [
            (pair_spec(length, D), (pairs, length, D), F32),
            (pair_spec(length, D), (pairs, length, D), BF16),
            (pair_spec(length, FF), (pairs, length, FF), BF16),
            (pair_spec(slots, FF), (pairs, slots, FF), BF16),
        ],
        [pltpu.VMEM((D, D), BF16), pltpu.VMEM((D, FF), BF16), sems, sems],
        spent(18),
        "fc1",
    )

    def top_rows(cols, idx=lambda i, *_: (0, 0, 0)):
        return pl.BlockSpec((pairs, slots, cols), idx)

    def grad_outs(rows, cols, chunk):
        block = rows // nd
        if block % 8:
            return [(pl.BlockSpec((rows, chunk), lambda i, *_: (0, i)), (rows, cols), BF16)]
        spec = pl.BlockSpec((nd // 2, block, chunk), lambda i, *_: (0, 0, i))
        return [(spec, (nd // 2, block, cols), BF16)] * 2

    def grad_sum(outs):
        if len(outs) == 1:
            rows, cols = outs[0].shape
            blocks = jnp.take(outs[0].reshape(nd, rows // nd, cols), owners, axis=0)
            outs = [blocks[: nd // 2], blocks[nd // 2 :]]
        return Sum(plan, call, *outs)

    set_c = spread_pieces(set_c, n2)

    chunk = 2 * LANES
    *got, gb2 = call(
        gw2_kernel,
        (D // chunk,),
        [owners],
        [
            (z, top_rows(FF)),
            (dy, top_rows(chunk, lambda i, *_: (0, 0, i))),
        ],
        grad_outs(FF, D, chunk) + [(pl.BlockSpec((1, chunk), lambda i, *_: (0, i)), (1, D), F32)],
        [pltpu.VMEM((FF, pairs * slots), BF16), pltpu.VMEM((FF, chunk), F32)],
        spent(8),
        "gw2",
    )
    sum_2 = grad_sum(got)
    set_c = last_piece(set_c, gb2)

    df, gb1 = call(
        functools.partial(df_kernel, rows_f),
        (PARTS,),
        [place],
        [(dy, top_rows(D)), (slope, top_rows(D, lambda i, *_: (0, 0, i)))] + piece_ins(set_c),
        [
            (pl.BlockSpec((pairs * slots, D), lambda i, *_: (0, i)), (pairs * slots, FF), BF16),
            (pl.BlockSpec((1, D), lambda i, *_: (0, i)), (1, FF), F32),
        ],
        [pltpu.VMEM((FF, D), BF16), sems],
        spent(7),
        "df",
    )
    sum_2.add()

    some = 2 if pairs % 2 == 0 else 1
    some_spec = pl.BlockSpec((some, slots, D), lambda i, *_: (i, 0, 0))
    dh, dhr, da, mlp_sum = call(
        functools.partial(mlp_back_kernel, rows_d),
        (pairs // some,),
        [place],
        [
            (df, pl.BlockSpec((some * slots, FF), lambda i, *_: (i, 0))),
            (dy, some_spec),
            (h1, some_spec),
            vec_in,
        ]
        + piece_ins(set_b),
        [
            (some_spec, (pairs, slots, D), F32),
            (some_spec, (pairs, slots, D), BF16),
            (some_spec, (pairs, slots, D), BF16),
            (full((8, D)), (8, D), F32),
        ],
        [pltpu.VMEM((D, FF), BF16), pltpu.VMEM((D, D), BF16), sems, sems],
        spent(10),
        "mlp_back",
    )

    got = call(
        gw1o_kernel,
        (PARTS + 1,),
        [owners],
        [
            (n2, top_rows(D)),
            (
                df,
                pl.BlockSpec((pairs * slots, D), lambda i, *_: (0, jnp.minimum(i, PARTS - 1))),
            ),
            (mixed, top_rows(D)),
            (dhr, top_rows(D)),
        ],
        grad_outs(D, FF + D, D),
        [pltpu.VMEM((D, pairs * slots), BF16), pltpu.VMEM((D, D), F32)],
        spent(9),
        "gw1o",
    )
    sum_1 = grad_sum(got)
    sum_2.add()

    part_pairs = pairs // 2 if pairs % 2 == 0 else pairs
    back = None
    for number in range(pairs // part_pairs):
        base = number * part_pairs
        at = lambda rows, cols, base=base: pl.BlockSpec(
            (1, rows, cols), lambda i, *_: (base + i, 0, 0)
        )
        ins = [(qkv, at(length, 3 * D)), (da, at(slots, D))]
        if back is not None:
            ins += [(back[0], ANYWHERE), (back[1], ANYWHERE), (back[2], full((8, D)))]
        back = call(
            functools.partial(attn_back_kernel, back is not None),
            (part_pairs,),
            [],
            ins,
            [
                (at(slots, D), (pairs, slots, D), BF16),
                (at(length, 2 * D), (pairs, length, 2 * D), BF16),
                (full((8, D)), (8, D), F32),
            ],
            [],
            spent(12),
            "attn_back",
            aliases=None if back is None else {2: 0, 3: 1},
        )
        if number == 0:
            sum_1.add()
        sum_2.add()
    dq, dkv, attn_sum = back

    got = call(
        gqkv_kernel,
        (3,),
        [owners],
        [
            (n1, full((pairs, length, D))),
            (dq, full((pairs, slots, D))),
            (
                dkv,
                pl.BlockSpec((pairs, length, D), lambda i, *_: (0, 0, jnp.where(i == 2, 1, 0))),
            ),
        ],
        grad_outs(D, 3 * D, D),
        [pltpu.VMEM((D, pairs * length), BF16), pltpu.VMEM((D, D), F32)],
        spent(9),
        "gqkv",
    )
    sum_3 = grad_sum(got)
    while sum_2.count > 1:
        sum_2.add()
    sum_1.add()

    fallback = (D // nd) % 8 != 0 or (FF // nd) % 8 != 0

    def finish(total, which, masters, moments):
        _, rows, cols = total.parts[0].shape
        if fallback:
            grad = sum(part[0].astype(F32) for part in total.parts)
            start, news, states = 0, [], []
            for kind, master, (first, second) in zip(which, masters, moments):
                width = master.shape[1]
                own = lax.dynamic_slice_in_dim(master, bi * rows, rows, 0)
                new_w, new_m, new_v = adamw(
                    own,
                    grad[:, start : start + width],
                    first,
                    second,
                    STEP_RATES[kind],
                    DECAY_RATES[kind],
                )
                news.append(new_w.astype(BF16))
                states += [new_m, new_v]
                start += width
            block = jnp.concatenate(news, axis=1)[None]
        else:
            own = pl.BlockSpec((1, rows, cols), lambda i, *_: (0, 0, 0))
            ins = [(part, own) for part in total.parts]
            outs = [(full((1, rows, cols)), (1, rows, cols), BF16)]
            for master, pair in zip(masters, moments):
                width = master.shape[1]
                ins.append((master, pl.BlockSpec((rows, width), lambda i, place_ref: (place_ref[3], 0))))
                ins += [(value, full(value.shape)) for value in pair]
                outs += [(full((rows, width)), (rows, width), F32)] * 2
            block, *states = call(
                functools.partial(finish_kernel, len(total.parts), which),
                (1,),
                [place],
                ins,
                outs,
                [],
                spent(2),
                "finish",
            )
        return Spread(plan, call, block), states

    def put(moved, widths, before=None):
        if not fallback:
            return moved.put(spots, widths, before)
        if before is None:
            return moved.blocks
        blocks = jnp.concatenate([before, moved.got], axis=0)
        count, rows, cols = blocks.shape
        order = jnp.zeros(count, jnp.int32).at[spots].set(jnp.arange(count, dtype=jnp.int32))
        blocks = jnp.take(blocks, order, axis=0).reshape(count * rows, cols).astype(F32)
        cuts = np.cumsum([0] + list(widths))
        return [blocks[:, a:b] for a, b in zip(cuts[:-1], cuts[1:])]

    last = plan.bbits
    moved_2, (new_m2, new_v2) = finish(sum_2, (3,), (w_fc2,), ((m_fc2, v_fc2),))
    sum_3.add()

    grad_tokens, vec_sum = call(
        functools.partial(grad_in_kernel, rows_d),
        (pairs,),
        [place],
        [
            (tokp, pair_spec(length, D)),
            (img, pair_spec(length, LANES)),
            vec_in,
            (dq, pair_spec(slots, D)),
            (dkv, pair_spec(length, 2 * D)),
            (dh, pair_spec(slots, D)),
            (perm, pair_spec(length, length)),
            (attn_sum, full((8, D))),
            (mlp_sum, full((8, D))),
            (gb1, full((1, FF))),
            (gb2, full((1, D))),
        ]
        + piece_ins(set_a),
        [
            (pair_spec(length, D), (pairs, length, D), F32),
            (full((16, D)), (16, D), F32),
        ],
        [pltpu.VMEM((D, 3 * D), BF16), sems],
        spent(15),
        "grad_in",
    )

    vec_gens = [1, 2] + plan.batch
    vec_got = plan.exchange(vec_sum, vec_gens[0])
    vec_place = 1

    def vec_step(total):
        nonlocal vec_sum, vec_got, vec_place
        if vec_place > len(vec_gens):
            total.add()
            return
        vec_sum = total.add((vec_sum, vec_got))
        vec_got = plan.exchange(vec_sum, vec_gens[vec_place]) if vec_place < len(vec_gens) else None
        vec_place += 1

    moved_2.join()
    sum_1.add()
    vec_step(sum_3)

    (layer_out,) = call(
        functools.partial(out_kernel, rows_f),
        (pairs,),
        [place],
        [
            (z, pair_spec(length, FF)),
            (h1, pair_spec(length, D)),
            vec_in,
            (perm, pair_spec(length, length)),
        ]
        + piece_ins(set_c),
        [(pair_spec(length, D), (pairs, length, D), BF16)],
        [pltpu.VMEM((FF, D), BF16), sems],
        spent(13),
        "out",
    )

    while sum_1.count > 1:
        sum_1.add()
    vec_step(sum_3)
    while moved_2.place < last:
        moved_2.join()
    put_2 = put(moved_2, (D,))
    while sum_3.count > 1:
        vec_step(sum_3)
    moved_1, (new_m1, new_v1, new_mo, new_vo) = finish(
        sum_1, (2, 1), (w_fc1, w_out), ((m_fc1, v_fc1), (m_out, v_out))
    )
    moved_3, (new_mq, new_vq) = finish(sum_3, (0,), (w_qkv,), ((m_qkv, v_qkv),))
    (new_2,) = put(moved_2, (D,), put_2)
    while moved_3.place < last:
        moved_1.join()
        moved_3.join()
    put_1 = put(moved_1, (FF, D))
    put_3 = put(moved_3, (3 * D,))
    new_1, new_o = put(moved_1, (FF, D), put_1)
    (new_q,) = put(moved_3, (3 * D,), put_3)

    while vec_place <= len(vec_gens):
        vec_sum = vec_sum + vec_got
        vec_got = plan.exchange(vec_sum, vec_gens[vec_place]) if vec_place < len(vec_gens) else None
        vec_place += 1
    states = jnp.concatenate([m_vec, v_vec], axis=0)[None]
    for rank in range(plan.bbits):
        got = plan.exchange(states, *(order[rank] for order in plan.gather))
        states = jnp.concatenate([states, got], axis=0)
    order = jnp.zeros(nb, jnp.int32).at[spots].set(jnp.arange(nb, dtype=jnp.int32))
    own_cols = D // nd
    states = jnp.transpose(jnp.take(states, order, axis=0), (1, 0, 2)).reshape(2 * NVEC, nb * own_cols)
    grad_vec = lax.dynamic_slice_in_dim(vec_sum[:NVEC], fi * nb * own_cols, nb * own_cols, 1)
    vec_new, all_m, all_v = adamw(
        vectors, grad_vec, states[:NVEC], states[NVEC:], STEP_RATES[4], DECAY_RATES[4]
    )
    new_mv = lax.dynamic_slice_in_dim(all_m, bi * own_cols, own_cols, 1)
    new_vv = lax.dynamic_slice_in_dim(all_v, bi * own_cols, own_cols, 1)

    return (
        layer_out,
        grad_tokens,
        new_q,
        new_mq,
        new_vq,
        new_o,
        new_mo,
        new_vo,
        new_1,
        new_m1,
        new_v1,
        new_2,
        new_m2,
        new_v2,
        vec_new,
        new_mv,
        new_vv,
    )


def solution(mesh):
    pairs = P(("batch", "fsdp"), None, None)
    weight = P("fsdp", None)
    state = P(("fsdp", "batch"), None)
    vec_state = P(None, ("fsdp", "batch"))
    matrix = (weight, state, state)
    return jax.shard_map(
        functools.partial(shards, Plan(mesh)),
        mesh=mesh,
        in_specs=(pairs, pairs, P(("batch", "fsdp"), None), P(("batch", "fsdp")))
        + matrix * 4
        + (P(None, "fsdp"), vec_state, vec_state),
        out_specs=(pairs, pairs) + matrix * 4 + (P(None, "fsdp"), vec_state, vec_state),
        check_vma=False,
    )
```

```python
import functools
import math

import jax
import jax.numpy as jnp
import numpy as np
from jax import lax
from jax.experimental import pallas as pl
from jax.experimental.pallas import tpu as pltpu
from jax.sharding import PartitionSpec as P

D = 768
HEADS = 12
HDIM = 64
FF = 3072
TEXT = 40
STEP = 3
MAXM = 128
NVEC = 14
PARTS = FF // D
LANES = 128
SLABS = D // LANES

BETA_ONE = 0.5
BETA_TWO = 0.5
EPS_ADAM = 1e-08
STEP_RATES = (0.03, 0.1, 0.03, 0.015, 0.3)
DECAY_RATES = (0.01, 0.01, 0.01, 0.01, 0.0)
INV_ROOT_TWO = 1.0 / math.sqrt(2.0)
INV_ROOT_TWOPI = 1.0 / math.sqrt(2.0 * math.pi)

FLOPS_SCALE = 3e9
BYTES_SCALE = 1e7
F32 = jnp.float32
BF16 = jnp.bfloat16


def dot(a, b):
    return lax.dot_general(a, b, (((1,), (0,)), ((), ())), preferred_element_type=F32)


def dot_first(a, b):
    return lax.dot_general(a, b, (((0,), (0,)), ((), ())), preferred_element_type=F32)


def dot_last(a, b):
    return lax.dot_general(a, b, (((1,), (1,)), ((), ())), preferred_element_type=F32)


def normalize(hidden):
    row_mean = jnp.mean(hidden, axis=-1, keepdims=True)
    centred = hidden - row_mean
    inv_scale = lax.rsqrt(jnp.mean(centred * centred, axis=-1, keepdims=True) + 1e-06)
    return centred * inv_scale, inv_scale


def norm_back(gradient, normed, inv_scale, gain_row):
    scaled = gradient * gain_row
    return inv_scale * (
        scaled
        - jnp.mean(scaled, axis=-1, keepdims=True)
        - normed * jnp.mean(scaled * normed, axis=-1, keepdims=True)
    )


def adamw(weight, gradient, moment_one, moment_two, step_rate, decay_rate):
    new_first = BETA_ONE * moment_one + (1.0 - BETA_ONE) * gradient
    new_second = BETA_TWO * moment_two + (1.0 - BETA_TWO) * gradient * gradient
    correct_one = 1.0 - BETA_ONE**STEP
    correct_two = 1.0 - BETA_TWO**STEP
    update = (
        new_first / correct_one / (jnp.sqrt(new_second / correct_two) + EPS_ADAM)
        + decay_rate * weight
    )
    return (weight - step_rate * update, new_first, new_second)


def spent(micros):
    return pl.CostEstimate(
        flops=int(micros * FLOPS_SCALE), bytes_accessed=int(micros * BYTES_SCALE), transcendentals=0
    )


def full(shape):
    zeros = (0,) * len(shape)
    return pl.BlockSpec(shape, lambda *_: zeros)


ANYWHERE = pl.BlockSpec(memory_space=pl.ANY)


class Plan:
    def __init__(self, mesh):
        self.nf = mesh.shape["fsdp"]
        self.nb = mesh.shape["batch"]
        self.nd = self.nf * self.nb
        self.fbits = self.nf.bit_length() - 1
        self.bbits = self.nb.bit_length() - 1
        assert self.nf == 1 << self.fbits and self.nb == 1 << self.bbits
        assert self.fbits == 2 and self.bbits >= 2
        near = [1, 2, 6] if self.bbits == 3 else [1 << k for k in range(self.bbits)]
        self.batch = [mask * self.nf for mask in near]
        first, second, *rest = self.batch
        self.scatter = ([1, 2, second, first] + rest, [1, first, 2, second] + rest)
        self.gather = (rest[::-1] + [second, first], rest[::-1] + [first, second])
        self.helper = (first, second)

    def exchange(self, value, even, odd=None):
        odd = even if odd is None else odd
        pairs = [(i, i ^ (odd if i & 1 else even)) for i in range(self.nd)]
        return lax.ppermute(value, ("batch", "fsdp"), pairs)

    def spans(self, gens):
        masks = np.zeros(1, np.int32)
        for mask in reversed(gens):
            masks = np.concatenate([masks, masks ^ mask])
        return masks

    def table(self):
        rows = []
        for index in range(self.nd):
            core, fi, bi = index & 1, index & (self.nf - 1), index >> self.fbits
            halves = (bi & 1, (bi >> 1) & 1)
            keep = index ^ self.spans(self.scatter[core][1:])
            send = (index ^ 1) ^ self.spans(self.scatter[1 - core][1:])
            order = np.concatenate([keep, send])
            owners = (order & (self.nf - 1)) * self.nb + (order >> self.fbits)
            places = bi ^ (self.spans(self.gather[core][::-1]) >> self.fbits)
            own = np.asarray([fi, halves[core], halves[1 - core], bi])
            rows.append(np.concatenate([own, owners, places]))
        return np.stack(rows).astype(np.int32)


OWN = 4


PIECES = ((0, None), (1, None), (2, 0), (2, 1), (3, 2), (3, 3))


def piece_copies(refs, target, sems, place_ref, rows, start=0):
    copies = []
    cols = target.shape[1]
    for number, ((mask, kind), ref) in enumerate(zip(PIECES, refs)):
        row = (place_ref[0] ^ mask) * rows
        length = rows
        if kind is not None:
            length = rows // 2
            low = place_ref[1 + kind // 2]
            row = row + (low if kind % 2 == 0 else 1 - low) * length
        copies.append(
            pltpu.make_async_copy(
                ref.at[:, pl.ds(start, cols)],
                target.at[pl.ds(pl.multiple_of(row, 8), length)],
                sems.at[number],
            )
        )
    return copies


def start_all(copies):
    for copy in copies:
        copy.start()


def wait_all(copies):
    for copy in copies:
        copy.wait()


def cast_kernel(place_ref, *refs):
    parts, (shard_ref, mine_ref) = refs[:-2], refs[-2:]
    start = 0
    for part in parts:
        cols = slice(start, start + part.shape[1])
        low = part[...].astype(BF16)
        shard_ref[:, cols] = low

        @pl.when(pl.program_id(0) == 0)
        def _(low=low, cols=cols):
            mine_ref[:, cols] = low

        start += part.shape[1]


def order_kernel(count_ref, pos_ref, tok_ref, cot_ref, perm_ref, tokp_ref, img_ref, dy_ref):
    pair = pl.program_id(0)
    length = tok_ref.shape[1]
    slots = pos_ref.shape[2]
    token = lax.broadcasted_iota(jnp.int32, (length, slots), 0)
    slot = lax.broadcasted_iota(jnp.int32, (length, slots), 1)
    hit = jnp.where(token == pos_ref[0], 1.0, 0.0)
    free = 1.0 - jnp.sum(hit, axis=1, keepdims=True)
    below = lax.broadcasted_iota(jnp.int32, (length, length), 1) < lax.broadcasted_iota(
        jnp.int32, (length, length), 0
    )
    rank = dot(
        jnp.where(below, 1.0, 0.0).astype(BF16),
        jnp.broadcast_to(free, (length, slots)).astype(BF16),
    )
    rest = jnp.where(rank == slot.astype(F32), jnp.broadcast_to(free, (length, slots)), 0.0)
    perm = jnp.concatenate([hit, rest], axis=1).astype(BF16)
    perm_ref[0] = perm
    tokp_ref[0] = dot_first(perm, tok_ref[0]).astype(BF16)
    image = jnp.where(lax.broadcasted_iota(jnp.int32, (length, LANES), 0) >= TEXT, 1.0, 0.0)
    img_ref[0] = dot_first(perm, image.astype(BF16))
    chosen = dot_first(perm[:, :slots], cot_ref[0])
    live = lax.broadcasted_iota(jnp.int32, (slots, 1), 0) < count_ref[pair]
    dy_ref[0] = jnp.where(live, chosen, 0.0).astype(BF16)


def start_row(tok_ref, img_ref, vec_ref):
    return tok_ref[0].astype(F32) + jnp.where(
        img_ref[0][:, :1] > 0.5, vec_ref[1:2, :], vec_ref[0:1, :]
    )


def qkv_kernel(rows, place_ref, tok_ref, img_ref, vec_ref, *refs):
    pieces = refs[: len(PIECES)]
    n1_ref, qkv_ref, w_ref, sems = refs[len(PIECES) :]
    first = pl.program_id(0) == 0
    copies = piece_copies(pieces, w_ref, sems, place_ref, rows)

    @pl.when(first)
    def _():
        start_all(copies)

    normed, _ = normalize(start_row(tok_ref, img_ref, vec_ref))
    n1 = (normed * vec_ref[2:3, :] + vec_ref[3:4, :]).astype(BF16)
    n1_ref[0] = n1

    @pl.when(first)
    def _():
        wait_all(copies)

    qkv_ref[0, :, :D] = (dot(n1, w_ref[:, :D]) + vec_ref[4:5, :]).astype(BF16)
    qkv_ref[0, :, D : 2 * D] = dot(n1, w_ref[:, D : 2 * D]).astype(BF16)
    qkv_ref[0, :, 2 * D :] = (dot(n1, w_ref[:, 2 * D :]) + vec_ref[5:6, :]).astype(BF16)


def lane_slab(slab):
    return pl.ds(pl.multiple_of(slab * LANES, LANES), LANES)


def mix_kernel(qkv_ref, a_ref):
    low = lax.broadcasted_iota(jnp.int32, (1, LANES), 1) < HDIM
    def some_slabs(turn, _):
        for slab in (2 * turn, 2 * turn + 1):
            cols = lane_slab(slab)
            q = qkv_ref[0, :, cols] * jnp.asarray(HDIM**-0.5, BF16)
            k = qkv_ref[0, :, lane_slab(slab + SLABS)]
            v = qkv_ref[0, :, lane_slab(slab + 2 * SLABS)]
            outs = []
            for head in range(2):
                mine = low if head == 0 else jnp.logical_not(low)
                scores = dot_last(jnp.where(mine, q, jnp.zeros_like(q)), k)
                e = jnp.exp(scores - jnp.max(scores, axis=-1, keepdims=True))
                p = (e * (1.0 / jnp.sum(e, axis=-1, keepdims=True))).astype(BF16)
                outs.append(dot(p, v))
            a_ref[0, :, cols] = jnp.where(low, outs[0], outs[1]).astype(BF16)
        return 0

    lax.fori_loop(0, SLABS // 2, some_slabs, 0)


def fc1_kernel(rows, place_ref, tok_ref, img_ref, a_ref, vec_ref, *refs):
    pieces = refs[: len(PIECES)]
    h1_ref, n2_ref, z_ref, slope_ref, wo_ref, w1_ref, sem_o, sem_1 = refs[len(PIECES) :]
    first = pl.program_id(0) == 0
    copies_o = piece_copies(pieces, wo_ref, sem_o, place_ref, rows)
    copies_1 = piece_copies(pieces, w1_ref, sem_1, place_ref, rows, D)

    @pl.when(first)
    def _():
        start_all(copies_o)
        start_all(copies_1)
        wait_all(copies_o)

    h1 = start_row(tok_ref, img_ref, vec_ref) + dot(a_ref[0], wo_ref[...]) + vec_ref[6:7, :]
    h1_ref[0] = h1
    normed, _ = normalize(h1)
    n2 = (normed * vec_ref[7:8, :] + vec_ref[8:9, :]).astype(BF16)
    n2_ref[0] = n2

    @pl.when(first)
    def _():
        wait_all(copies_1)

    slots = slope_ref.shape[1]
    for part in range(PARTS):
        cols = slice(part * D, (part + 1) * D)
        f = dot(n2, w1_ref[:, cols]) + vec_ref[9 + part : 10 + part, :]
        phi = 0.5 * (1.0 + lax.erf(f * INV_ROOT_TWO))
        z_ref[0, :, cols] = (f * phi).astype(BF16)
        fs = f[:slots]
        slope = phi[:slots] + fs * jnp.exp(-0.5 * fs * fs) * INV_ROOT_TWOPI
        slope_ref[0, :, cols] = slope.astype(BF16)


def spread(acc_ref, owners_ref, outs):
    if len(outs) == 1:
        outs[0][...] = acc_ref[...].astype(BF16)
        return
    keep_ref, send_ref = outs
    half, block, _ = send_ref.shape

    def one(spot, _):
        for out_ref, base in ((send_ref, half), (keep_ref, 0)):
            start = pl.multiple_of(owners_ref[OWN + base + spot] * block, 8)
            out_ref[spot] = acc_ref[pl.ds(start, block), :].astype(BF16)
        return 0

    lax.fori_loop(0, half, one, 0)


def gw2_kernel(owners_ref, z_ref, dy_ref, *refs):
    outs, (sum_ref, zt_ref, acc_ref) = refs[:-3], refs[-3:]
    pairs, slots, width = z_ref.shape

    @pl.when(pl.program_id(0) == 0)
    def _():
        zt_ref[...] = z_ref[...].reshape(pairs * slots, width).T

    dy = dy_ref[...].reshape(pairs * slots, -1)
    acc_ref[...] = dot(zt_ref[...], dy)
    sum_ref[...] = jnp.sum(dy.astype(F32), axis=0, keepdims=True)
    spread(acc_ref, owners_ref, outs)


def df_kernel(rows, place_ref, dy_ref, slope_ref, *refs):
    pieces = refs[: len(PIECES)]
    df_ref, gb1_ref, w2_ref, sems = refs[len(PIECES) :]
    step = pl.program_id(0)
    pairs, slots, width = slope_ref.shape
    total = pairs * slots
    copies = piece_copies(pieces, w2_ref, sems, place_ref, rows)

    @pl.when(step == 0)
    def _():
        start_all(copies)
        wait_all(copies)

    dz = dot_last(
        dy_ref[...].reshape(total, D), w2_ref[pl.ds(pl.multiple_of(step * width, 8), width), :]
    )
    df = dz * slope_ref[...].reshape(total, width).astype(F32)
    gb1_ref[...] = jnp.sum(df, axis=0, keepdims=True)
    df_ref[...] = df.astype(BF16)


def mlp_back_kernel(rows, place_ref, df_ref, dy_ref, h1_ref, vec_ref, *refs):
    pieces = refs[: len(PIECES)]
    dh_ref, dhr_ref, da_ref, sum_ref, w1_ref, wo_ref, sem_1, sem_o = refs[len(PIECES) :]
    first = pl.program_id(0) == 0
    copies_1 = piece_copies(pieces, w1_ref, sem_1, place_ref, rows, D)
    copies_o = piece_copies(pieces, wo_ref, sem_o, place_ref, rows)

    @pl.when(first)
    def _():
        start_all(copies_1)
        start_all(copies_o)
        sum_ref[...] = jnp.zeros_like(sum_ref)
        wait_all(copies_1)
        wait_all(copies_o)

    some, slots, _ = dy_ref.shape
    total = some * slots
    dn2 = dot_last(df_ref[...], w1_ref[...])
    normed, scale = normalize(h1_ref[...].reshape(total, D))
    dh = dy_ref[...].reshape(total, D).astype(F32) + norm_back(dn2, normed, scale, vec_ref[7:8, :])
    dh_ref[...] = dh.reshape(some, slots, D)
    sum_ref[0:1, :] += jnp.sum(dh, axis=0, keepdims=True)
    sum_ref[1:2, :] += jnp.sum(dn2 * normed, axis=0, keepdims=True)
    sum_ref[2:3, :] += jnp.sum(dn2, axis=0, keepdims=True)
    low = dh.astype(BF16)
    dhr_ref[...] = low.reshape(some, slots, D)
    da_ref[...] = dot_last(low, wo_ref[...]).astype(BF16).reshape(some, slots, D)


def gw1o_kernel(owners_ref, n2_ref, df_ref, a_ref, dhr_ref, *refs):
    outs, (n2t_ref, acc_ref) = refs[:-2], refs[-2:]
    step = pl.program_id(0)
    pairs, slots, _ = n2_ref.shape
    total = pairs * slots

    @pl.when(step == 0)
    def _():
        n2t_ref[...] = n2_ref[...].reshape(total, D).T

    @pl.when(step < PARTS)
    def _():
        acc_ref[...] = dot(n2t_ref[...], df_ref[...])

    @pl.when(step == PARTS)
    def _():
        acc_ref[...] = dot_first(a_ref[...].reshape(total, D), dhr_ref[...].reshape(total, D))

    spread(acc_ref, owners_ref, outs)


def attn_back_kernel(more, qkv_ref, da_ref, *refs):
    if more:
        _, _, before_ref, dq_ref, dkv_ref, sum_ref = refs
    else:
        dq_ref, dkv_ref, sum_ref = refs
    slots = da_ref.shape[1]

    @pl.when(pl.program_id(0) == 0)
    def _():
        sum_ref[...] = before_ref[...] if more else jnp.zeros_like(sum_ref)

    low = lax.broadcasted_iota(jnp.int32, (1, LANES), 1) < HDIM
    scale = jnp.asarray(HDIM**-0.5, BF16)
    def some_slabs(turn, _):
        for slab in (2 * turn, 2 * turn + 1):
            cols = lane_slab(slab)
            q = qkv_ref[0, :slots, cols] * scale
            k = qkv_ref[0, :, lane_slab(slab + SLABS)]
            v = qkv_ref[0, :, lane_slab(slab + 2 * SLABS)]
            da = da_ref[0, :, cols]
            gqs, gks, gvs = [], [], []
            for head in range(2):
                mine = low if head == 0 else jnp.logical_not(low)
                zero = jnp.zeros_like(q)
                scores = dot_last(jnp.where(mine, q, zero), k)
                e = jnp.exp(scores - jnp.max(scores, axis=-1, keepdims=True))
                p = e * (1.0 / jnp.sum(e, axis=-1, keepdims=True))
                gvs.append(dot_first(p.astype(BF16), da))
                dp = dot_last(jnp.where(mine, da, zero), v)
                ds = (p * (dp - jnp.sum(p * dp, axis=-1, keepdims=True))).astype(BF16)
                gqs.append(dot(ds, k))
                gks.append(dot_first(ds, q))
            gq = jnp.where(low, gqs[0], gqs[1]) * (HDIM**-0.5)
            gk = jnp.where(low, gks[0], gks[1])
            gv = jnp.where(low, gvs[0], gvs[1])
            dq_ref[0, :, cols] = gq.astype(BF16)
            dkv_ref[0, :, cols] = gk.astype(BF16)
            dkv_ref[0, :, lane_slab(slab + SLABS)] = gv.astype(BF16)
            sum_ref[0:1, cols] += jnp.sum(gq, axis=0, keepdims=True)
            sum_ref[1:2, cols] += jnp.sum(gv, axis=0, keepdims=True)
        return 0

    lax.fori_loop(0, SLABS // 2, some_slabs, 0)


def gqkv_kernel(owners_ref, n1_ref, dq_ref, dkv_ref, *refs):
    outs, (n1t_ref, acc_ref) = refs[:-2], refs[-2:]
    step = pl.program_id(0)
    pairs, length, _ = n1_ref.shape
    slots = dq_ref.shape[1]

    @pl.when(step == 0)
    def _():
        n1t_ref[...] = n1_ref[...].reshape(pairs * length, D).T
        total = dot(n1t_ref[:, :slots], dq_ref[0])
        for pair in range(1, pairs):
            total += dot(n1t_ref[:, pair * length : pair * length + slots], dq_ref[pair])
        acc_ref[...] = total

    @pl.when(step > 0)
    def _():
        acc_ref[...] = dot(n1t_ref[...], dkv_ref[...].reshape(pairs * length, D))

    spread(acc_ref, owners_ref, outs)


def split_three(value):
    one = value.astype(BF16)
    left = value - one.astype(F32)
    two = left.astype(BF16)
    return one, two, (left - two.astype(F32)).astype(BF16)


def grad_in_kernel(
    rows,
    place_ref,
    tok_ref,
    img_ref,
    vec_ref,
    dq_ref,
    dkv_ref,
    dh_ref,
    perm_ref,
    attn_sum_ref,
    mlp_sum_ref,
    gb1_ref,
    gb2_ref,
    *refs,
):
    pieces = refs[: len(PIECES)]
    out_ref, sum_ref, w_ref, sems = refs[len(PIECES) :]
    first = pl.program_id(0) == 0
    slots = dq_ref.shape[1]
    copies = piece_copies(pieces, w_ref, sems, place_ref, rows)

    @pl.when(first)
    def _():
        start_all(copies)
        sum_ref[...] = jnp.zeros_like(sum_ref)
        sum_ref[4:6, :] = attn_sum_ref[0:2, :]
        sum_ref[6:9, :] = mlp_sum_ref[0:3, :]
        for part in range(PARTS):
            sum_ref[9 + part : 10 + part, :] = gb1_ref[:, part * D : (part + 1) * D]
        sum_ref[9 + PARTS : 10 + PARTS, :] = gb2_ref[...]
        wait_all(copies)

    dn_all = dot_last(dkv_ref[0], w_ref[:, D:])
    dn_top = dn_all[:slots] + dot_last(dq_ref[0], w_ref[:, :D])
    dn = jnp.concatenate([dn_top, dn_all[slots:]], axis=0)
    normed, scale = normalize(start_row(tok_ref, img_ref, vec_ref))
    grad = norm_back(dn, normed, scale, vec_ref[2:3, :])
    grad = jnp.concatenate([grad[:slots] + dh_ref[0], grad[slots:]], axis=0)
    image = img_ref[0][:, :1] > 0.5
    sum_ref[0:1, :] += jnp.sum(jnp.where(image, 0.0, grad), axis=0, keepdims=True)
    sum_ref[1:2, :] += jnp.sum(jnp.where(image, grad, 0.0), axis=0, keepdims=True)
    sum_ref[2:3, :] += jnp.sum(dn * normed, axis=0, keepdims=True)
    sum_ref[3:4, :] += jnp.sum(dn, axis=0, keepdims=True)
    one, two, three = split_three(grad)
    perm = perm_ref[0]
    out_ref[0] = dot(perm, one) + dot(perm, two) + dot(perm, three)


def out_kernel(rows, place_ref, z_ref, h1_ref, vec_ref, perm_ref, *refs):
    pieces = refs[: len(PIECES)]
    out_ref, w_ref, sems = refs[len(PIECES) :]
    first = pl.program_id(0) == 0
    copies = piece_copies(pieces, w_ref, sems, place_ref, rows)

    @pl.when(first)
    def _():
        start_all(copies)
        wait_all(copies)

    y = h1_ref[0] + dot(z_ref[0], w_ref[...]) + vec_ref[9 + PARTS : 10 + PARTS, :]
    out_ref[0] = dot(perm_ref[0], y.astype(BF16)).astype(BF16)


HBM = pl.BlockSpec(memory_space=pltpu.HBM)


class Job:
    def __init__(self, ins, outs, scratch, plan, then):
        self.ins, self.outs, self.scratch, self.plan, self.then = ins, outs, scratch, plan, then


def run_kernel(jobs, tab_ref, *refs):
    refs = list(refs)
    ins = [[refs.pop(0) for _ in job.ins] for job in jobs]
    outs = [[refs.pop(0) for _ in job.outs] for job in jobs]
    bufs = [[refs.pop(0) for _ in job.scratch] for job in jobs]
    sems = refs.pop(0)
    used = 0
    plans = [job.plan(tab_ref, *args) for job, *args in zip(jobs, ins, outs, bufs)]
    ready, late = [], []

    def copies_of(pairs):
        nonlocal used
        made = []
        for source, target in pairs:
            made.append(pltpu.make_async_copy(source, target, sems.at[used]))
            made[-1].start()
            used += 1
        return made

    for straight, steps in plans:
        late += copies_of(straight)
        ready.append([copies_of(needs) for needs, _ in steps])
    for (_, steps), waits in zip(plans, ready):
        for (_, work), copies in zip(steps, waits):
            wait_all(copies)
            late += copies_of(work())
    wait_all(late)


def add_job(parts, count, then):
    _, rows, cols = parts[0].shape
    number = len(parts)
    chunks = min(count, 2)
    size = count // chunks

    def plan(tab_ref, ins, outs, bufs):
        def step(chunk):
            at = pl.ds(chunk * size, size)

            def work():
                def one(k, _):
                    total = bufs[0][k].astype(F32)
                    for buf in bufs[1:number]:
                        total = total + buf[k].astype(F32)
                    bufs[number][k] = total.astype(BF16)
                    return 0

                lax.fori_loop(chunk * size, (chunk + 1) * size, one, 0)
                return [(bufs[number].at[at], outs[0].at[at])]

            return [(ref.at[pl.ds(count + chunk * size, size)], buf.at[at]) for ref, buf in zip(ins, bufs)], work

        return [], [step(chunk) for chunk in range(chunks)]

    return Job(
        parts,
        [((count, rows, cols), BF16)],
        [pltpu.VMEM((count, rows, cols), BF16)] * (number + 1),
        plan,
        then,
    )


def plus_job(one, two, then):
    def plan(tab_ref, ins, outs, bufs):
        def work():
            bufs[2][...] = bufs[0][...] + bufs[1][...]
            return [(bufs[2], outs[0])]

        return [], [(list(zip(ins, bufs)), work)]

    return Job([one, two], [(one.shape, F32)], [pltpu.VMEM(one.shape, F32)] * 3, plan, then)


def join_job(one, two, then):
    count = one.shape[0]

    def plan(tab_ref, ins, outs, bufs):
        return [
            (ins[0], outs[0].at[pl.ds(0, count)]),
            (ins[1], outs[0].at[pl.ds(count, count)]),
        ], []

    return Job([one, two], [((2 * count,) + one.shape[1:], BF16)], [], plan, then)


def finish_job(parts, which, masters, moments, then):
    _, rows, cols = parts[0].shape
    number = len(parts)
    widths = [value.shape[1] for value in masters]
    states = [value for pair in moments for value in pair]

    def plan(tab_ref, ins, outs, bufs):
        own = pl.ds(pl.multiple_of(tab_ref[3] * rows, 8), rows)
        needs = [(ref.at[0], buf) for ref, buf in zip(ins[:number], bufs)]
        kinds = len(which)
        for spot in range(kinds):
            needs.append((ins[number + spot].at[own], bufs[number + spot]))
        for spot in range(2 * kinds):
            needs.append((ins[number + kinds + spot], bufs[number + kinds + spot]))
        new = bufs[number + 3 * kinds]

        def work():
            start, copies = 0, []
            for spot, kind in enumerate(which):
                width = widths[spot]
                for low in range(start, start + width, D):
                    cols = slice(low, low + D)
                    here = slice(low - start, low - start + D)
                    total = bufs[0][:, cols].astype(F32)
                    for buf in bufs[1:number]:
                        total = total + buf[:, cols].astype(F32)
                    first, second = bufs[number + kinds + 2 * spot : number + kinds + 2 * spot + 2]
                    new_w, new_m, new_v = adamw(
                        bufs[number + spot][:, here],
                        total,
                        first[:, here],
                        second[:, here],
                        STEP_RATES[kind],
                        DECAY_RATES[kind],
                    )
                    new[:, cols] = new_w.astype(BF16)
                    first[:, here] = new_m
                    second[:, here] = new_v
                copies += [(first, outs[1 + 2 * spot]), (second, outs[2 + 2 * spot])]
                start += width
            return [(new, outs[0].at[0])] + copies

        return [], [(needs, work)]

    return Job(
        list(parts) + list(masters) + states,
        [((1, rows, cols), BF16)] + [(value.shape, F32) for value in states],
        [pltpu.VMEM((rows, cols), BF16)] * number
        + [pltpu.VMEM((rows, width), F32) for width in widths]
        + [pltpu.VMEM(value.shape, F32) for value in states]
        + [pltpu.VMEM((rows, cols), BF16)],
        plan,
        then,
    )


def place_job(one, two, base, widths, then):
    count, rows, cols = one.shape
    nb = 2 * count

    def plan(tab_ref, ins, outs, bufs):
        def step(part):
            spots = range(part * count, part * count + count)

            def work():
                def one(spot, _):
                    start = 0
                    for number, width in enumerate(widths):
                        bufs[1 + number][spot] = bufs[0][spot, :, start : start + width].astype(F32)
                        start += width
                    return 0

                lax.fori_loop(part * count, part * count + count, one, 0)
                copies = []
                for spot in spots:
                    at = pl.ds(pl.multiple_of(tab_ref[base + spot] * rows, 8), rows)
                    for number in range(len(widths)):
                        copies.append((bufs[1 + number].at[spot], outs[number].at[at]))
                return copies

            return [(ins[part], bufs[0].at[pl.ds(part * count, count)])], work

        return [], [step(part) for part in range(2)]

    return Job(
        [one, two],
        [((nb * rows, width), F32) for width in widths],
        [pltpu.VMEM((nb, rows, cols), BF16)]
        + [pltpu.VMEM((nb, rows, width), F32) for width in widths],
        plan,
        then,
    )


def later(value, dep):
    return lax.optimization_barrier((value, dep))[0]


class Chain:
    def __init__(self):
        self.last = None

    def __call__(
        self, kernel, grid, scalars, ins, outs, scratch, estimate, name, after=(), aliases=None
    ):
        deps = list(after)
        if self.last is not None:
            deps.append(self.last)
        fixed = len(scalars) + len(ins)
        extra = len(deps)

        def body(*refs):
            kernel(*refs[:fixed], *refs[fixed + extra :])

        got = pl.pallas_call(
            body,
            grid_spec=pltpu.PrefetchScalarGridSpec(
                num_scalar_prefetch=len(scalars),
                grid=grid,
                in_specs=[spec for _, spec in ins] + [ANYWHERE] * extra,
                out_specs=[spec for spec, _, _ in outs],
                scratch_shapes=scratch,
            ),
            out_shape=[jax.ShapeDtypeStruct(dims, kind) for _, dims, kind in outs],
            input_output_aliases={
                len(scalars) + k: v for k, v in (aliases or {}).items()
            },
            cost_estimate=estimate,
            name=name,
        )(*scalars, *[value for value, _ in ins], *deps)
        self.last = got[-1]
        return got


class Sum:
    def __init__(self, plan, keep, send):
        self.plan = plan
        self.parts, self.count, self.place = [keep], keep.shape[0], 0
        self.move(send)

    def move(self, send):
        got = self.plan.exchange(send, *(order[self.place] for order in self.plan.scatter))
        self.parts.append(got)
        self.place += 1

    def add(self):
        self.count //= 2
        return add_job(list(self.parts), self.count, self.move)


class Spread:
    def __init__(self, plan, block):
        self.plan, self.blocks, self.place, self.age = plan, block, 0, 0
        self.move(block)

    def move(self, blocks):
        self.blocks = blocks
        self.got = self.plan.exchange(blocks, *(order[self.place] for order in self.plan.gather))
        self.place += 1

    def join(self):
        return join_job(self.blocks, self.got, self.move)


def shards(
    plan,
    tokens,
    cotangent,
    mask_pos,
    mask_count,
    w_qkv,
    m_qkv,
    v_qkv,
    w_out,
    m_out,
    v_out,
    w_fc1,
    m_fc1,
    v_fc1,
    w_fc2,
    m_fc2,
    v_fc2,
    vectors,
    m_vec,
    v_vec,
):
    pairs, length, _ = tokens.shape
    slots = mask_pos.shape[1]
    nf, nb, nd = plan.nf, plan.nb, plan.nd
    fi = lax.axis_index("fsdp").astype(jnp.int32)
    bi = lax.axis_index("batch").astype(jnp.int32)
    tab = lax.dynamic_index_in_dim(jnp.asarray(plan.table()), bi * nf + fi, 0, keepdims=False)
    place = owners = tab
    call = Chain()

    def run(micros, *jobs):
        jobs = [job for job in jobs if job is not None]
        if not jobs:
            return
        got = call(
            functools.partial(run_kernel, jobs),
            (),
            [tab],
            [(value, HBM) for job in jobs for value in job.ins],
            [(HBM, dims, kind) for job in jobs for dims, kind in job.outs],
            [buf for job in jobs for buf in job.scratch] + [pltpu.SemaphoreType.DMA((256,))],
            spent(micros),
            "turn",
        )
        for job in jobs:
            job.then(*got[: len(job.outs)])
            got = got[len(job.outs) :]

    def pair_spec(rows, cols):
        return pl.BlockSpec((1, rows, cols), lambda i, *_: (i, 0, 0))

    def piece_ins(pieces):
        return [(value, ANYWHERE) for value in pieces]

    sems = pltpu.SemaphoreType.DMA((len(PIECES),))
    rows_d, rows_f = D // nf, FF // nf

    low_vec = vectors.astype(BF16)
    vec_parts = [low_vec, plan.exchange(low_vec, 1)]
    vec_parts += [plan.exchange(part, 2) for part in vec_parts]
    columns = []
    for spot in range(nf):
        chosen = vec_parts[0]
        for mask in range(1, nf):
            chosen = jnp.where((fi ^ mask) == spot, vec_parts[mask], chosen)
        columns.append(chosen)
    vec = jnp.concatenate(columns, axis=1).astype(F32)
    vec = jnp.pad(vec, ((0, 16 - NVEC), (0, 0)))
    vec_in = (vec, full(vec.shape))

    def cast(shard_list, after=()):
        rows = shard_list[0].shape[0]
        half = rows // 2
        cols = sum(value.shape[1] for value in shard_list)
        row = lambda i, place_ref: (i ^ place_ref[1], 0)
        shard, mine = call(
            cast_kernel,
            (2,),
            [place],
            [(value, pl.BlockSpec((half, value.shape[1]), row)) for value in shard_list],
            [
                (pl.BlockSpec((half, cols), row), (rows, cols), BF16),
                (pl.BlockSpec((half, cols), lambda i, *_: (0, 0)), (half, cols), BF16),
            ],
            [],
            spent(rows * cols / 2e5),
            "cast",
            after,
        )
        return [shard, plan.exchange(shard, 1), plan.exchange(mine, 2)]

    def spread_pieces(pieces, dep=None):
        near = pieces[2]
        ready = near if dep is None else later(near, dep)
        other = plan.exchange(ready, *plan.helper)
        return pieces[:2] + [near, other, plan.exchange(ready, 1)]

    def last_piece(pieces, dep=None):
        other = pieces[3]
        return pieces + [plan.exchange(other if dep is None else later(other, dep), 1)]

    set_a = cast([w_qkv])

    perm, tokp, img, dy = call(
        order_kernel,
        (pairs,),
        [mask_count],
        [
            (mask_pos.reshape(pairs, 1, slots), pl.BlockSpec((1, 1, slots), lambda i, *_: (i, 0, 0))),
            (tokens, pair_spec(length, D)),
            (cotangent, pair_spec(length, D)),
        ],
        [
            (pair_spec(length, length), (pairs, length, length), BF16),
            (pair_spec(length, D), (pairs, length, D), BF16),
            (pair_spec(length, LANES), (pairs, length, LANES), F32),
            (pair_spec(slots, D), (pairs, slots, D), BF16),
        ],
        [],
        spent(6),
        "order",
    )

    set_b = cast([w_out, w_fc1])
    near_a = set_a[2]
    set_a = last_piece(spread_pieces(set_a, set_b[0]))
    set_c = cast([w_fc2], [near_a])

    n1, qkv = call(
        functools.partial(qkv_kernel, rows_d),
        (pairs,),
        [place],
        [(tokp, pair_spec(length, D)), (img, pair_spec(length, LANES)), vec_in] + piece_ins(set_a),
        [
            (pair_spec(length, D), (pairs, length, D), BF16),
            (pair_spec(length, 3 * D), (pairs, length, 3 * D), BF16),
        ],
        [pltpu.VMEM((D, 3 * D), BF16), sems],
        spent(1),
        "qkv",
    )

    near_b = set_b[2]
    set_b = spread_pieces(set_b, n1)
    (mixed,) = call(
        mix_kernel,
        (pairs,),
        [],
        [(qkv, pair_spec(length, 3 * D))],
        [(pair_spec(length, D), (pairs, length, D), BF16)],
        [],
        spent(1),
        "mix",
        [near_b],
    )

    set_b = last_piece(set_b, mixed)
    h1, n2, z, slope = call(
        functools.partial(fc1_kernel, rows_d),
        (pairs,),
        [place],
        [
            (tokp, pair_spec(length, D)),
            (img, pair_spec(length, LANES)),
            (mixed, pair_spec(length, D)),
            vec_in,
        ]
        + piece_ins(set_b),
        [
            (pair_spec(length, D), (pairs, length, D), F32),
            (pair_spec(length, D), (pairs, length, D), BF16),
            (pair_spec(length, FF), (pairs, length, FF), BF16),
            (pair_spec(slots, FF), (pairs, slots, FF), BF16),
        ],
        [pltpu.VMEM((D, D), BF16), pltpu.VMEM((D, FF), BF16), sems, sems],
        spent(18),
        "fc1",
    )

    def top_rows(cols, idx=lambda i, *_: (0, 0, 0)):
        return pl.BlockSpec((pairs, slots, cols), idx)

    def grad_outs(rows, cols, chunk):
        block = rows // nd
        if block % 8:
            return [(pl.BlockSpec((rows, chunk), lambda i, *_: (0, i)), (rows, cols), BF16)]
        spec = pl.BlockSpec((nd // 2, block, chunk), lambda i, *_: (0, 0, i))
        return [(spec, (nd // 2, block, cols), BF16)] * 2

    def grad_sum(outs):
        if len(outs) == 1:
            rows, cols = outs[0].shape
            blocks = jnp.take(outs[0].reshape(nd, rows // nd, cols), tab[OWN : OWN + nd], axis=0)
            outs = [blocks[: nd // 2], blocks[nd // 2 :]]
        return Sum(plan, *outs)

    set_c = spread_pieces(set_c, n2)

    chunk = 2 * LANES
    *got, gb2 = call(
        gw2_kernel,
        (D // chunk,),
        [owners],
        [
            (z, top_rows(FF)),
            (dy, top_rows(chunk, lambda i, *_: (0, 0, i))),
        ],
        grad_outs(FF, D, chunk) + [(pl.BlockSpec((1, chunk), lambda i, *_: (0, i)), (1, D), F32)],
        [pltpu.VMEM((FF, pairs * slots), BF16), pltpu.VMEM((FF, chunk), F32)],
        spent(8),
        "gw2",
    )
    sum_2 = grad_sum(got)
    set_c = last_piece(set_c, gb2)

    df, gb1 = call(
        functools.partial(df_kernel, rows_f),
        (PARTS,),
        [place],
        [(dy, top_rows(D)), (slope, top_rows(D, lambda i, *_: (0, 0, i)))] + piece_ins(set_c),
        [
            (pl.BlockSpec((pairs * slots, D), lambda i, *_: (0, i)), (pairs * slots, FF), BF16),
            (pl.BlockSpec((1, D), lambda i, *_: (0, i)), (1, FF), F32),
        ],
        [pltpu.VMEM((FF, D), BF16), sems],
        spent(7),
        "df",
    )
    run(3, sum_2.add())

    some = 2 if pairs % 2 == 0 else 1
    some_spec = pl.BlockSpec((some, slots, D), lambda i, *_: (i, 0, 0))
    dh, dhr, da, mlp_sum = call(
        functools.partial(mlp_back_kernel, rows_d),
        (pairs // some,),
        [place],
        [
            (df, pl.BlockSpec((some * slots, FF), lambda i, *_: (i, 0))),
            (dy, some_spec),
            (h1, some_spec),
            vec_in,
        ]
        + piece_ins(set_b),
        [
            (some_spec, (pairs, slots, D), F32),
            (some_spec, (pairs, slots, D), BF16),
            (some_spec, (pairs, slots, D), BF16),
            (full((8, D)), (8, D), F32),
        ],
        [pltpu.VMEM((D, FF), BF16), pltpu.VMEM((D, D), BF16), sems, sems],
        spent(10),
        "mlp_back",
    )

    got = call(
        gw1o_kernel,
        (PARTS + 1,),
        [owners],
        [
            (n2, top_rows(D)),
            (
                df,
                pl.BlockSpec((pairs * slots, D), lambda i, *_: (0, jnp.minimum(i, PARTS - 1))),
            ),
            (mixed, top_rows(D)),
            (dhr, top_rows(D)),
        ],
        grad_outs(D, FF + D, D),
        [pltpu.VMEM((D, pairs * slots), BF16), pltpu.VMEM((D, D), F32)],
        spent(9),
        "gw1o",
    )
    sum_1 = grad_sum(got)
    run(2, sum_2.add())

    part_pairs = pairs // 2 if pairs % 2 == 0 else pairs
    back = None
    for number in range(pairs // part_pairs):
        base = number * part_pairs
        at = lambda rows, cols, base=base: pl.BlockSpec(
            (1, rows, cols), lambda i, *_: (base + i, 0, 0)
        )
        ins = [(qkv, at(length, 3 * D)), (da, at(slots, D))]
        if back is not None:
            ins += [(back[0], ANYWHERE), (back[1], ANYWHERE), (back[2], full((8, D)))]
        back = call(
            functools.partial(attn_back_kernel, back is not None),
            (part_pairs,),
            [],
            ins,
            [
                (at(slots, D), (pairs, slots, D), BF16),
                (at(length, 2 * D), (pairs, length, 2 * D), BF16),
                (full((8, D)), (8, D), F32),
            ],
            [],
            spent(12),
            "attn_back",
            aliases=None if back is None else {2: 0, 3: 1},
        )
        if number == 0:
            run(3, sum_1.add(), sum_2.add())
    dq, dkv, attn_sum = back

    got = call(
        gqkv_kernel,
        (3,),
        [owners],
        [
            (n1, full((pairs, length, D))),
            (dq, full((pairs, slots, D))),
            (
                dkv,
                pl.BlockSpec((pairs, length, D), lambda i, *_: (0, 0, jnp.where(i == 2, 1, 0))),
            ),
        ],
        grad_outs(D, 3 * D, D),
        [pltpu.VMEM((D, pairs * length), BF16), pltpu.VMEM((D, D), F32)],
        spent(9),
        "gqkv",
    )
    sum_3 = grad_sum(got)
    run(8, sum_1.add(), sum_2.add())
    run(3, sum_3.add())

    fallback = (D // nd) % 8 != 0 or (FF // nd) % 8 != 0
    places = OWN + nd
    moved, states = {}, {}

    def finish(name, total, which, masters, moments):
        def then(block, *new_states):
            moved[name] = Spread(plan, block)
            states[name] = new_states

        if not fallback:
            return finish_job(total.parts, which, masters, moments, then)
        _, rows, cols = total.parts[0].shape
        grad = sum(part[0].astype(F32) for part in total.parts)
        start, news, made = 0, [], []
        for kind, master, (first, second) in zip(which, masters, moments):
            width = master.shape[1]
            own = lax.dynamic_slice_in_dim(master, bi * rows, rows, 0)
            new_w, new_m, new_v = adamw(
                own,
                grad[:, start : start + width],
                first,
                second,
                STEP_RATES[kind],
                DECAY_RATES[kind],
            )
            news.append(new_w.astype(BF16))
            made += [new_m, new_v]
            start += width
        then(jnp.concatenate(news, axis=1)[None], *made)
        return None

    news = {}

    def put(name, widths):
        blocks, got = moved[name].blocks, moved[name].got

        def then(*outs):
            news[name] = outs

        if not fallback:
            return place_job(blocks, got, places, widths, then)
        blocks = jnp.concatenate([blocks, got], axis=0)
        count, rows, cols = blocks.shape
        order = jnp.zeros(count, jnp.int32).at[tab[places:]].set(jnp.arange(count, dtype=jnp.int32))
        blocks = jnp.take(blocks, order, axis=0).reshape(count * rows, cols).astype(F32)
        cuts = np.cumsum([0] + list(widths))
        then(*[blocks[:, a:b] for a, b in zip(cuts[:-1], cuts[1:])])
        return None

    grad_tokens, vec_sum = call(
        functools.partial(grad_in_kernel, rows_d),
        (pairs,),
        [place],
        [
            (tokp, pair_spec(length, D)),
            (img, pair_spec(length, LANES)),
            vec_in,
            (dq, pair_spec(slots, D)),
            (dkv, pair_spec(length, 2 * D)),
            (dh, pair_spec(slots, D)),
            (perm, pair_spec(length, length)),
            (attn_sum, full((8, D))),
            (mlp_sum, full((8, D))),
            (gb1, full((1, FF))),
            (gb2, full((1, D))),
        ]
        + piece_ins(set_a),
        [
            (pair_spec(length, D), (pairs, length, D), F32),
            (full((16, D)), (16, D), F32),
        ],
        [pltpu.VMEM((D, 3 * D), BF16), sems],
        spent(15),
        "grad_in",
    )

    vec_gens = [1, 2] + plan.batch
    vec_got = plan.exchange(vec_sum, vec_gens[0])
    vec_place = 1

    def vec_step():
        if vec_place >= len(vec_gens):
            return None

        def then(total):
            nonlocal vec_sum, vec_got, vec_place
            vec_sum = total
            vec_got = plan.exchange(total, vec_gens[vec_place])
            vec_place += 1

        return plus_job(vec_sum, vec_got, then)

    def step_of(name, total, *rest):
        if total.count > 1:
            return total.add()
        if name not in moved:
            return finish(name, total, *rest)
        if moved[name].place < plan.bbits:
            return moved[name].join()
        return None

    args_2 = ("2", sum_2, (3,), (w_fc2,), ((m_fc2, v_fc2),))
    args_1 = ("1", sum_1, (2, 1), (w_fc1, w_out), ((m_fc1, v_fc1), (m_out, v_out)))
    args_3 = ("3", sum_3, (0,), (w_qkv,), ((m_qkv, v_qkv),))

    def is_done(name):
        return name in moved and moved[name].place >= plan.bbits

    run(4, step_of(*args_3), step_of(*args_1), step_of(*args_2))

    (layer_out,) = call(
        functools.partial(out_kernel, rows_f),
        (pairs,),
        [place],
        [
            (z, pair_spec(length, FF)),
            (h1, pair_spec(length, D)),
            vec_in,
            (perm, pair_spec(length, length)),
        ]
        + piece_ins(set_c),
        [(pair_spec(length, D), (pairs, length, D), BF16)],
        [pltpu.VMEM((FF, D), BF16), sems],
        spent(13),
        "out",
    )

    placed = set()
    widths = {"2": (D,), "1": (FF, D), "3": (3 * D,)}
    while not is_done("3"):
        puts = []
        for name in ("2", "1"):
            if is_done(name) and name not in placed and moved[name].age > 0:
                placed.add(name)
                puts.append(put(name, widths[name]))
        for one in moved.values():
            one.age += one.place >= plan.bbits
        run(2, step_of(*args_3), step_of(*args_1), step_of(*args_2), vec_step(), *puts)
    for name in ("2", "1"):
        if name not in placed:
            while not is_done(name):
                run(1, step_of(*{"2": args_2, "1": args_1}[name]))
            run(0.2, put(name, widths[name]))
    run(1, put("3", widths["3"]))

    while vec_place <= len(vec_gens):
        vec_sum = vec_sum + vec_got
        vec_got = plan.exchange(vec_sum, vec_gens[vec_place]) if vec_place < len(vec_gens) else None
        vec_place += 1
    held = jnp.concatenate([m_vec, v_vec], axis=0)[None]
    for rank in range(plan.bbits):
        got = plan.exchange(held, *(order[rank] for order in plan.gather))
        held = jnp.concatenate([held, got], axis=0)
    order = jnp.zeros(nb, jnp.int32).at[tab[places:]].set(jnp.arange(nb, dtype=jnp.int32))
    own_cols = D // nd
    held = jnp.transpose(jnp.take(held, order, axis=0), (1, 0, 2)).reshape(2 * NVEC, nb * own_cols)
    grad_vec = lax.dynamic_slice_in_dim(vec_sum[:NVEC], fi * nb * own_cols, nb * own_cols, 1)
    vec_new, all_m, all_v = adamw(
        vectors, grad_vec, held[:NVEC], held[NVEC:], STEP_RATES[4], DECAY_RATES[4]
    )
    new_mv = lax.dynamic_slice_in_dim(all_m, bi * own_cols, own_cols, 1)
    new_vv = lax.dynamic_slice_in_dim(all_v, bi * own_cols, own_cols, 1)

    (new_2,), (new_1, new_o), (new_q,) = news["2"], news["1"], news["3"]
    new_m2, new_v2 = states["2"]
    new_m1, new_v1, new_mo, new_vo = states["1"]
    new_mq, new_vq = states["3"]
    return (
        layer_out,
        grad_tokens,
        new_q,
        new_mq,
        new_vq,
        new_o,
        new_mo,
        new_vo,
        new_1,
        new_m1,
        new_v1,
        new_2,
        new_m2,
        new_v2,
        vec_new,
        new_mv,
        new_vv,
    )


def solution(mesh):
    pairs = P(("batch", "fsdp"), None, None)
    weight = P("fsdp", None)
    state = P(("fsdp", "batch"), None)
    vec_state = P(None, ("fsdp", "batch"))
    matrix = (weight, state, state)
    return jax.shard_map(
        functools.partial(shards, Plan(mesh)),
        mesh=mesh,
        in_specs=(pairs, pairs, P(("batch", "fsdp"), None), P(("batch", "fsdp")))
        + matrix * 4
        + (P(None, "fsdp"), vec_state, vec_state),
        out_specs=(pairs, pairs) + matrix * 4 + (P(None, "fsdp"), vec_state, vec_state),
        check_vma=False,
    )
```

```python
import functools
import math

import jax
import jax.numpy as jnp
import numpy as np
from jax import lax
from jax.experimental import pallas as pl
from jax.experimental.pallas import tpu as pltpu
from jax.sharding import PartitionSpec as P

D = 768
HEADS = 12
HDIM = 64
FF = 3072
TEXT = 40
STEP = 3
MAXM = 128
NVEC = 14
PARTS = FF // D
LANES = 128
SLABS = D // LANES

BETA_ONE = 0.5
BETA_TWO = 0.5
EPS_ADAM = 1e-08
STEP_RATES = (0.03, 0.1, 0.03, 0.015, 0.3)
DECAY_RATES = (0.01, 0.01, 0.01, 0.01, 0.0)
INV_ROOT_TWO = 1.0 / math.sqrt(2.0)
INV_ROOT_TWOPI = 1.0 / math.sqrt(2.0 * math.pi)

FLOPS_SCALE = 3e9
BYTES_SCALE = 1e7
F32 = jnp.float32
BF16 = jnp.bfloat16


def dot(a, b):
    return lax.dot_general(a, b, (((1,), (0,)), ((), ())), preferred_element_type=F32)


def dot_first(a, b):
    return lax.dot_general(a, b, (((0,), (0,)), ((), ())), preferred_element_type=F32)


def dot_last(a, b):
    return lax.dot_general(a, b, (((1,), (1,)), ((), ())), preferred_element_type=F32)


def normalize(hidden):
    row_mean = jnp.mean(hidden, axis=-1, keepdims=True)
    centred = hidden - row_mean
    inv_scale = lax.rsqrt(jnp.mean(centred * centred, axis=-1, keepdims=True) + 1e-06)
    return centred * inv_scale, inv_scale


def norm_back(gradient, normed, inv_scale, gain_row):
    scaled = gradient * gain_row
    return inv_scale * (
        scaled
        - jnp.mean(scaled, axis=-1, keepdims=True)
        - normed * jnp.mean(scaled * normed, axis=-1, keepdims=True)
    )


def adamw(weight, gradient, moment_one, moment_two, step_rate, decay_rate):
    new_first = BETA_ONE * moment_one + (1.0 - BETA_ONE) * gradient
    new_second = BETA_TWO * moment_two + (1.0 - BETA_TWO) * gradient * gradient
    correct_one = 1.0 - BETA_ONE**STEP
    correct_two = 1.0 - BETA_TWO**STEP
    update = (
        new_first / correct_one / (jnp.sqrt(new_second / correct_two) + EPS_ADAM)
        + decay_rate * weight
    )
    return (weight - step_rate * update, new_first, new_second)


def spent(micros):
    return pl.CostEstimate(
        flops=int(micros * FLOPS_SCALE), bytes_accessed=int(micros * BYTES_SCALE), transcendentals=0
    )


def full(shape):
    zeros = (0,) * len(shape)
    return pl.BlockSpec(shape, lambda *_: zeros)


ANYWHERE = pl.BlockSpec(memory_space=pl.ANY)


class Plan:
    def __init__(self, mesh):
        self.nf = mesh.shape["fsdp"]
        self.nb = mesh.shape["batch"]
        self.nd = self.nf * self.nb
        self.fbits = self.nf.bit_length() - 1
        self.bbits = self.nb.bit_length() - 1
        assert self.nf == 1 << self.fbits and self.nb == 1 << self.bbits
        assert self.fbits == 2 and self.bbits >= 2
        near = [1, 2, 6] if self.bbits == 3 else [1 << k for k in range(self.bbits)]
        self.batch = [mask * self.nf for mask in near]
        first, second, *rest = self.batch
        self.scatter = ([1, 2, second, first] + rest, [1, first, 2, second] + rest)
        self.gather = (rest[::-1] + [second, first], rest[::-1] + [first, second])
        self.helper = (first, second)

    def exchange(self, value, even, odd=None):
        odd = even if odd is None else odd
        pairs = [(i, i ^ (odd if i & 1 else even)) for i in range(self.nd)]
        return lax.ppermute(value, ("batch", "fsdp"), pairs)

    def spans(self, gens):
        masks = np.zeros(1, np.int32)
        for mask in reversed(gens):
            masks = np.concatenate([masks, masks ^ mask])
        return masks

    def table(self):
        rows = []
        for index in range(self.nd):
            core, fi, bi = index & 1, index & (self.nf - 1), index >> self.fbits
            halves = (bi & 1, (bi >> 1) & 1)
            keep = index ^ self.spans(self.scatter[core][1:])
            send = (index ^ 1) ^ self.spans(self.scatter[1 - core][1:])
            order = np.concatenate([keep, send])
            owners = (order & (self.nf - 1)) * self.nb + (order >> self.fbits)
            places = bi ^ (self.spans(self.gather[core][::-1]) >> self.fbits)
            own = np.asarray([fi, halves[core], halves[1 - core], bi])
            rows.append(np.concatenate([own, owners, places]))
        return np.stack(rows).astype(np.int32)


OWN = 4


PIECES = ((0, None), (1, None), (2, 0), (2, 1), (3, 2), (3, 3))


def piece_copies(refs, target, sems, place_ref, rows, start=0):
    copies = []
    cols = target.shape[1]
    for number, ((mask, kind), ref) in enumerate(zip(PIECES, refs)):
        row = (place_ref[0] ^ mask) * rows
        length = rows
        if kind is not None:
            length = rows // 2
            low = place_ref[1 + kind // 2]
            row = row + (low if kind % 2 == 0 else 1 - low) * length
        copies.append(
            pltpu.make_async_copy(
                ref.at[:, pl.ds(start, cols)],
                target.at[pl.ds(pl.multiple_of(row, 8), length)],
                sems.at[number],
            )
        )
    return copies


def start_all(copies):
    for copy in copies:
        copy.start()


def wait_all(copies):
    for copy in copies:
        copy.wait()


def cast_kernel(place_ref, *refs):
    parts, (shard_ref, mine_ref) = refs[:-2], refs[-2:]
    start = 0
    for part in parts:
        cols = slice(start, start + part.shape[1])
        low = part[...].astype(BF16)
        shard_ref[:, cols] = low

        @pl.when(pl.program_id(0) == 0)
        def _(low=low, cols=cols):
            mine_ref[:, cols] = low

        start += part.shape[1]


def order_kernel(count_ref, pos_ref, tok_ref, cot_ref, perm_ref, tokp_ref, img_ref, dy_ref):
    pair = pl.program_id(0)
    length = tok_ref.shape[1]
    slots = pos_ref.shape[2]
    token = lax.broadcasted_iota(jnp.int32, (length, slots), 0)
    slot = lax.broadcasted_iota(jnp.int32, (length, slots), 1)
    hit = jnp.where(token == pos_ref[0], 1.0, 0.0)
    free = 1.0 - jnp.sum(hit, axis=1, keepdims=True)
    below = lax.broadcasted_iota(jnp.int32, (length, length), 1) < lax.broadcasted_iota(
        jnp.int32, (length, length), 0
    )
    rank = dot(
        jnp.where(below, 1.0, 0.0).astype(BF16),
        jnp.broadcast_to(free, (length, slots)).astype(BF16),
    )
    rest = jnp.where(rank == slot.astype(F32), jnp.broadcast_to(free, (length, slots)), 0.0)
    perm = jnp.concatenate([hit, rest], axis=1).astype(BF16)
    perm_ref[0] = perm
    tokp_ref[0] = dot_first(perm, tok_ref[0]).astype(BF16)
    image = jnp.where(lax.broadcasted_iota(jnp.int32, (length, LANES), 0) >= TEXT, 1.0, 0.0)
    img_ref[0] = dot_first(perm, image.astype(BF16))
    chosen = dot_first(perm[:, :slots], cot_ref[0])
    live = lax.broadcasted_iota(jnp.int32, (slots, 1), 0) < count_ref[pair]
    dy_ref[0] = jnp.where(live, chosen, 0.0).astype(BF16)


def start_row(tok_ref, img_ref, vec_ref):
    return tok_ref[0].astype(F32) + jnp.where(
        img_ref[0][:, :1] > 0.5, vec_ref[1:2, :], vec_ref[0:1, :]
    )


def qkv_kernel(rows, place_ref, tok_ref, img_ref, vec_ref, *refs):
    pieces = refs[: len(PIECES)]
    n1_ref, qkv_ref, w_ref, sems = refs[len(PIECES) :]
    first = pl.program_id(0) == 0
    copies = piece_copies(pieces, w_ref, sems, place_ref, rows)

    @pl.when(first)
    def _():
        start_all(copies)

    normed, _ = normalize(start_row(tok_ref, img_ref, vec_ref))
    n1 = (normed * vec_ref[2:3, :] + vec_ref[3:4, :]).astype(BF16)
    n1_ref[0] = n1

    @pl.when(first)
    def _():
        wait_all(copies)

    qkv_ref[0, :, :D] = (dot(n1, w_ref[:, :D]) + vec_ref[4:5, :]).astype(BF16)
    qkv_ref[0, :, D : 2 * D] = dot(n1, w_ref[:, D : 2 * D]).astype(BF16)
    qkv_ref[0, :, 2 * D :] = (dot(n1, w_ref[:, 2 * D :]) + vec_ref[5:6, :]).astype(BF16)


def mix_kernel(qkv_ref, a_ref):
    low = lax.broadcasted_iota(jnp.int32, (1, LANES), 1) < HDIM
    for slab in range(SLABS):
        cols = slice(slab * LANES, (slab + 1) * LANES)
        q = qkv_ref[0, :, cols] * jnp.asarray(HDIM**-0.5, BF16)
        k = qkv_ref[0, :, D + slab * LANES : D + (slab + 1) * LANES]
        v = qkv_ref[0, :, 2 * D + slab * LANES : 2 * D + (slab + 1) * LANES]
        outs = []
        for head in range(2):
            mine = low if head == 0 else jnp.logical_not(low)
            scores = dot_last(jnp.where(mine, q, jnp.zeros_like(q)), k)
            e = jnp.exp(scores - jnp.max(scores, axis=-1, keepdims=True))
            p = (e * (1.0 / jnp.sum(e, axis=-1, keepdims=True))).astype(BF16)
            outs.append(dot(p, v))
        a_ref[0, :, cols] = jnp.where(low, outs[0], outs[1]).astype(BF16)


def fc1_kernel(rows, place_ref, tok_ref, img_ref, a_ref, vec_ref, *refs):
    pieces = refs[: len(PIECES)]
    h1_ref, n2_ref, z_ref, slope_ref, wo_ref, w1_ref, sem_o, sem_1 = refs[len(PIECES) :]
    first = pl.program_id(0) == 0
    copies_o = piece_copies(pieces, wo_ref, sem_o, place_ref, rows)
    copies_1 = piece_copies(pieces, w1_ref, sem_1, place_ref, rows, D)

    @pl.when(first)
    def _():
        start_all(copies_o)
        start_all(copies_1)
        wait_all(copies_o)

    h1 = start_row(tok_ref, img_ref, vec_ref) + dot(a_ref[0], wo_ref[...]) + vec_ref[6:7, :]
    h1_ref[0] = h1
    normed, _ = normalize(h1)
    n2 = (normed * vec_ref[7:8, :] + vec_ref[8:9, :]).astype(BF16)
    n2_ref[0] = n2

    @pl.when(first)
    def _():
        wait_all(copies_1)

    slots = slope_ref.shape[1]
    for part in range(PARTS):
        cols = slice(part * D, (part + 1) * D)
        f = dot(n2, w1_ref[:, cols]) + vec_ref[9 + part : 10 + part, :]
        phi = 0.5 * (1.0 + lax.erf(f * INV_ROOT_TWO))
        z_ref[0, :, cols] = (f * phi).astype(BF16)
        fs = f[:slots]
        slope = phi[:slots] + fs * jnp.exp(-0.5 * fs * fs) * INV_ROOT_TWOPI
        slope_ref[0, :, cols] = slope.astype(BF16)


def spread(acc_ref, owners_ref, outs):
    if len(outs) == 1:
        outs[0][...] = acc_ref[...].astype(BF16)
        return
    keep_ref, send_ref = outs
    half, block, _ = send_ref.shape
    for out_ref, base in ((send_ref, half), (keep_ref, 0)):
        for spot in range(half):
            start = pl.multiple_of(owners_ref[OWN + base + spot] * block, 8)
            out_ref[spot] = acc_ref[pl.ds(start, block), :].astype(BF16)


def gw2_kernel(owners_ref, z_ref, dy_ref, *refs):
    outs, (sum_ref, zt_ref, acc_ref) = refs[:-3], refs[-3:]
    pairs, slots, width = z_ref.shape

    @pl.when(pl.program_id(0) == 0)
    def _():
        zt_ref[...] = z_ref[...].reshape(pairs * slots, width).T

    dy = dy_ref[...].reshape(pairs * slots, -1)
    acc_ref[...] = dot(zt_ref[...], dy)
    sum_ref[...] = jnp.sum(dy.astype(F32), axis=0, keepdims=True)
    spread(acc_ref, owners_ref, outs)


def df_kernel(rows, place_ref, dy_ref, slope_ref, *refs):
    pieces = refs[: len(PIECES)]
    df_ref, gb1_ref, w2_ref, sems = refs[len(PIECES) :]
    step = pl.program_id(0)
    pairs, slots, width = slope_ref.shape
    total = pairs * slots
    copies = piece_copies(pieces, w2_ref, sems, place_ref, rows)

    @pl.when(step == 0)
    def _():
        start_all(copies)
        wait_all(copies)

    dz = dot_last(
        dy_ref[...].reshape(total, D), w2_ref[pl.ds(pl.multiple_of(step * width, 8), width), :]
    )
    df = dz * slope_ref[...].reshape(total, width).astype(F32)
    gb1_ref[...] = jnp.sum(df, axis=0, keepdims=True)
    df_ref[...] = df.astype(BF16)


def mlp_back_kernel(rows, place_ref, df_ref, dy_ref, h1_ref, vec_ref, *refs):
    pieces = refs[: len(PIECES)]
    dh_ref, dhr_ref, da_ref, sum_ref, w1_ref, wo_ref, sem_1, sem_o = refs[len(PIECES) :]
    first = pl.program_id(0) == 0
    copies_1 = piece_copies(pieces, w1_ref, sem_1, place_ref, rows, D)
    copies_o = piece_copies(pieces, wo_ref, sem_o, place_ref, rows)

    @pl.when(first)
    def _():
        start_all(copies_1)
        start_all(copies_o)
        sum_ref[...] = jnp.zeros_like(sum_ref)
        wait_all(copies_1)
        wait_all(copies_o)

    some, slots, _ = dy_ref.shape
    total = some * slots
    dn2 = dot_last(df_ref[...], w1_ref[...])
    normed, scale = normalize(h1_ref[...].reshape(total, D))
    dh = dy_ref[...].reshape(total, D).astype(F32) + norm_back(dn2, normed, scale, vec_ref[7:8, :])
    dh_ref[...] = dh.reshape(some, slots, D)
    sum_ref[0:1, :] += jnp.sum(dh, axis=0, keepdims=True)
    sum_ref[1:2, :] += jnp.sum(dn2 * normed, axis=0, keepdims=True)
    sum_ref[2:3, :] += jnp.sum(dn2, axis=0, keepdims=True)
    low = dh.astype(BF16)
    dhr_ref[...] = low.reshape(some, slots, D)
    da_ref[...] = dot_last(low, wo_ref[...]).astype(BF16).reshape(some, slots, D)


def gw1o_kernel(owners_ref, n2_ref, df_ref, a_ref, dhr_ref, *refs):
    outs, (n2t_ref, acc_ref) = refs[:-2], refs[-2:]
    step = pl.program_id(0)
    pairs, slots, _ = n2_ref.shape
    total = pairs * slots

    @pl.when(step == 0)
    def _():
        n2t_ref[...] = n2_ref[...].reshape(total, D).T

    @pl.when(step < PARTS)
    def _():
        acc_ref[...] = dot(n2t_ref[...], df_ref[...])

    @pl.when(step == PARTS)
    def _():
        acc_ref[...] = dot_first(a_ref[...].reshape(total, D), dhr_ref[...].reshape(total, D))

    spread(acc_ref, owners_ref, outs)


def attn_back_kernel(more, qkv_ref, da_ref, *refs):
    if more:
        _, _, before_ref, dq_ref, dkv_ref, sum_ref = refs
    else:
        dq_ref, dkv_ref, sum_ref = refs
    slots = da_ref.shape[1]

    @pl.when(pl.program_id(0) == 0)
    def _():
        sum_ref[...] = before_ref[...] if more else jnp.zeros_like(sum_ref)

    low = lax.broadcasted_iota(jnp.int32, (1, LANES), 1) < HDIM
    scale = jnp.asarray(HDIM**-0.5, BF16)
    for slab in range(SLABS):
        cols = slice(slab * LANES, (slab + 1) * LANES)
        q = qkv_ref[0, :slots, cols] * scale
        k = qkv_ref[0, :, D + slab * LANES : D + (slab + 1) * LANES]
        v = qkv_ref[0, :, 2 * D + slab * LANES : 2 * D + (slab + 1) * LANES]
        da = da_ref[0, :, cols]
        gqs, gks, gvs = [], [], []
        for head in range(2):
            mine = low if head == 0 else jnp.logical_not(low)
            zero = jnp.zeros_like(q)
            scores = dot_last(jnp.where(mine, q, zero), k)
            e = jnp.exp(scores - jnp.max(scores, axis=-1, keepdims=True))
            p = e * (1.0 / jnp.sum(e, axis=-1, keepdims=True))
            gvs.append(dot_first(p.astype(BF16), da))
            dp = dot_last(jnp.where(mine, da, zero), v)
            ds = (p * (dp - jnp.sum(p * dp, axis=-1, keepdims=True))).astype(BF16)
            gqs.append(dot(ds, k))
            gks.append(dot_first(ds, q))
        gq = jnp.where(low, gqs[0], gqs[1]) * (HDIM**-0.5)
        gk = jnp.where(low, gks[0], gks[1])
        gv = jnp.where(low, gvs[0], gvs[1])
        dq_ref[0, :, cols] = gq.astype(BF16)
        dkv_ref[0, :, cols] = gk.astype(BF16)
        dkv_ref[0, :, D + slab * LANES : D + (slab + 1) * LANES] = gv.astype(BF16)
        sum_ref[0:1, cols] += jnp.sum(gq, axis=0, keepdims=True)
        sum_ref[1:2, cols] += jnp.sum(gv, axis=0, keepdims=True)


def gqkv_kernel(owners_ref, n1_ref, dq_ref, dkv_ref, *refs):
    outs, (n1t_ref, acc_ref) = refs[:-2], refs[-2:]
    step = pl.program_id(0)
    pairs, length, _ = n1_ref.shape
    slots = dq_ref.shape[1]

    @pl.when(step == 0)
    def _():
        n1t_ref[...] = n1_ref[...].reshape(pairs * length, D).T
        total = dot(n1t_ref[:, :slots], dq_ref[0])
        for pair in range(1, pairs):
            total += dot(n1t_ref[:, pair * length : pair * length + slots], dq_ref[pair])
        acc_ref[...] = total

    @pl.when(step > 0)
    def _():
        acc_ref[...] = dot(n1t_ref[...], dkv_ref[...].reshape(pairs * length, D))

    spread(acc_ref, owners_ref, outs)


def split_three(value):
    one = value.astype(BF16)
    left = value - one.astype(F32)
    two = left.astype(BF16)
    return one, two, (left - two.astype(F32)).astype(BF16)


def grad_in_kernel(
    rows,
    place_ref,
    tok_ref,
    img_ref,
    vec_ref,
    dq_ref,
    dkv_ref,
    dh_ref,
    perm_ref,
    attn_sum_ref,
    mlp_sum_ref,
    gb1_ref,
    gb2_ref,
    *refs,
):
    pieces = refs[: len(PIECES)]
    out_ref, sum_ref, w_ref, sems = refs[len(PIECES) :]
    first = pl.program_id(0) == 0
    slots = dq_ref.shape[1]
    copies = piece_copies(pieces, w_ref, sems, place_ref, rows)

    @pl.when(first)
    def _():
        start_all(copies)
        sum_ref[...] = jnp.zeros_like(sum_ref)
        sum_ref[4:6, :] = attn_sum_ref[0:2, :]
        sum_ref[6:9, :] = mlp_sum_ref[0:3, :]
        for part in range(PARTS):
            sum_ref[9 + part : 10 + part, :] = gb1_ref[:, part * D : (part + 1) * D]
        sum_ref[9 + PARTS : 10 + PARTS, :] = gb2_ref[...]
        wait_all(copies)

    dn_all = dot_last(dkv_ref[0], w_ref[:, D:])
    dn_top = dn_all[:slots] + dot_last(dq_ref[0], w_ref[:, :D])
    dn = jnp.concatenate([dn_top, dn_all[slots:]], axis=0)
    normed, scale = normalize(start_row(tok_ref, img_ref, vec_ref))
    grad = norm_back(dn, normed, scale, vec_ref[2:3, :])
    grad = jnp.concatenate([grad[:slots] + dh_ref[0], grad[slots:]], axis=0)
    image = img_ref[0][:, :1] > 0.5
    sum_ref[0:1, :] += jnp.sum(jnp.where(image, 0.0, grad), axis=0, keepdims=True)
    sum_ref[1:2, :] += jnp.sum(jnp.where(image, grad, 0.0), axis=0, keepdims=True)
    sum_ref[2:3, :] += jnp.sum(dn * normed, axis=0, keepdims=True)
    sum_ref[3:4, :] += jnp.sum(dn, axis=0, keepdims=True)
    one, two, three = split_three(grad)
    perm = perm_ref[0]
    out_ref[0] = dot(perm, one) + dot(perm, two) + dot(perm, three)


def out_kernel(rows, place_ref, z_ref, h1_ref, vec_ref, perm_ref, *refs):
    pieces = refs[: len(PIECES)]
    out_ref, w_ref, sems = refs[len(PIECES) :]
    first = pl.program_id(0) == 0
    copies = piece_copies(pieces, w_ref, sems, place_ref, rows)

    @pl.when(first)
    def _():
        start_all(copies)
        wait_all(copies)

    y = h1_ref[0] + dot(z_ref[0], w_ref[...]) + vec_ref[9 + PARTS : 10 + PARTS, :]
    out_ref[0] = dot(perm_ref[0], y.astype(BF16)).astype(BF16)


def place_kernel(number, base, spots_ref, one_ref, two_ref, *refs):
    step = pl.program_id(0)
    count, rows, _ = one_ref.shape

    def put(out_ref):
        for spot in range(2 * count):
            source = one_ref if spot < count else two_ref
            at = pl.ds(pl.multiple_of(spots_ref[base + spot] * rows, 8), rows)
            out_ref[at, :] = source[spot % count].astype(F32)

    if number == 1:
        put(refs[0])
        return
    last = pl.num_programs(0) - 1

    @pl.when(step < last)
    def _():
        put(refs[0])

    @pl.when(step == last)
    def _():
        put(refs[1])


def later(value, dep):
    return lax.optimization_barrier((value, dep))[0]


class Chain:
    def __init__(self):
        self.last, self.waiting = None, []

    def pin(self, values):
        return lax.optimization_barrier((list(values), self.last))[0]

    def hold(self, value):
        self.waiting.append(value)
        return value

    def __call__(
        self, kernel, grid, scalars, ins, outs, scratch, estimate, name, after=(), aliases=None
    ):
        deps = list(after) + self.waiting
        self.waiting = []
        if self.last is not None:
            deps.append(self.last)
        fixed = len(scalars) + len(ins)
        extra = len(deps)

        def body(*refs):
            kernel(*refs[:fixed], *refs[fixed + extra :])

        got = pl.pallas_call(
            body,
            grid_spec=pltpu.PrefetchScalarGridSpec(
                num_scalar_prefetch=len(scalars),
                grid=grid,
                in_specs=[spec for _, spec in ins] + [ANYWHERE] * extra,
                out_specs=[spec for spec, _, _ in outs],
                scratch_shapes=scratch,
            ),
            out_shape=[jax.ShapeDtypeStruct(dims, kind) for _, dims, kind in outs],
            input_output_aliases={
                len(scalars) + k: v for k, v in (aliases or {}).items()
            },
            cost_estimate=estimate,
            name=name,
        )(*scalars, *[value for value, _ in ins], *deps)
        self.last = got[-1]
        return got


class Sum:
    def __init__(self, plan, call, keep, send):
        self.plan, self.call = plan, call
        self.parts, self.count, self.place = [keep], keep.shape[0], 0
        self.move(send)

    def move(self, send):
        got = self.plan.exchange(send, *(order[self.place] for order in self.plan.scatter))
        self.parts.append(got)
        self.place += 1

    def total(self, low, high):
        parts = self.call.pin(self.parts)
        total = parts[0][low:high].astype(F32)
        for part in parts[1:]:
            total = total + part[low:high].astype(F32)
        return total

    def add(self):
        self.count //= 2
        total = self.total(self.count, 2 * self.count)
        self.sent = self.call.hold(total.astype(BF16))
        self.move(self.sent)


class Spread:
    def __init__(self, plan, call, block):
        self.plan, self.call, self.place = plan, call, 0
        self.move(block)

    def move(self, blocks):
        self.blocks = self.call.hold(blocks)
        self.got = self.plan.exchange(blocks, *(order[self.place] for order in self.plan.gather))
        self.place += 1

    def join(self):
        self.move(jnp.concatenate(self.call.pin([self.blocks, self.got]), axis=0))

    def put(self, base, tab, widths):
        count, rows, cols = self.blocks.shape
        step = D if len(widths) > 1 or cols > D else D // 3
        last = widths[0] // step - 1
        ins = [
            (value, pl.BlockSpec((count, rows, step), lambda i, *_: (0, 0, i)))
            for value in (self.blocks, self.got)
        ]
        maps = [lambda i, *_: (0, jnp.minimum(i, last)), lambda i, *_: (0, 0)]
        return self.call(
            functools.partial(place_kernel, len(widths), base),
            (cols // step,),
            [tab],
            ins,
            [
                (pl.BlockSpec((2 * count * rows, step), idx), (2 * count * rows, width), F32)
                for idx, width in zip(maps, widths)
            ],
            [],
            spent(1),
            "place",
        )


def shards(
    plan,
    tokens,
    cotangent,
    mask_pos,
    mask_count,
    w_qkv,
    m_qkv,
    v_qkv,
    w_out,
    m_out,
    v_out,
    w_fc1,
    m_fc1,
    v_fc1,
    w_fc2,
    m_fc2,
    v_fc2,
    vectors,
    m_vec,
    v_vec,
):
    pairs, length, _ = tokens.shape
    slots = mask_pos.shape[1]
    nf, nb, nd = plan.nf, plan.nb, plan.nd
    fi = lax.axis_index("fsdp").astype(jnp.int32)
    bi = lax.axis_index("batch").astype(jnp.int32)
    tab = lax.dynamic_index_in_dim(jnp.asarray(plan.table()), bi * nf + fi, 0, keepdims=False)
    place = owners = tab
    call = Chain()


    def pair_spec(rows, cols):
        return pl.BlockSpec((1, rows, cols), lambda i, *_: (i, 0, 0))

    def piece_ins(pieces):
        return [(value, ANYWHERE) for value in pieces]

    sems = pltpu.SemaphoreType.DMA((len(PIECES),))
    rows_d, rows_f = D // nf, FF // nf

    low_vec = vectors.astype(BF16)
    vec_parts = [low_vec, plan.exchange(low_vec, 1)]
    vec_parts += [plan.exchange(part, 2) for part in vec_parts]
    columns = []
    for spot in range(nf):
        chosen = vec_parts[0]
        for mask in range(1, nf):
            chosen = jnp.where((fi ^ mask) == spot, vec_parts[mask], chosen)
        columns.append(chosen)
    vec = jnp.concatenate(columns, axis=1).astype(F32)
    vec = jnp.pad(vec, ((0, 16 - NVEC), (0, 0)))
    vec_in = (vec, full(vec.shape))

    def cast(shard_list, after=()):
        rows = shard_list[0].shape[0]
        half = rows // 2
        cols = sum(value.shape[1] for value in shard_list)
        row = lambda i, place_ref: (i ^ place_ref[1], 0)
        shard, mine = call(
            cast_kernel,
            (2,),
            [place],
            [(value, pl.BlockSpec((half, value.shape[1]), row)) for value in shard_list],
            [
                (pl.BlockSpec((half, cols), row), (rows, cols), BF16),
                (pl.BlockSpec((half, cols), lambda i, *_: (0, 0)), (half, cols), BF16),
            ],
            [],
            spent(rows * cols / 2e5),
            "cast",
            after,
        )
        return [shard, plan.exchange(shard, 1), plan.exchange(mine, 2)]

    def spread_pieces(pieces, dep=None):
        near = pieces[2]
        ready = near if dep is None else later(near, dep)
        other = plan.exchange(ready, *plan.helper)
        return pieces[:2] + [near, other, plan.exchange(ready, 1)]

    def last_piece(pieces, dep=None):
        other = pieces[3]
        return pieces + [plan.exchange(other if dep is None else later(other, dep), 1)]

    set_a = cast([w_qkv])

    perm, tokp, img, dy = call(
        order_kernel,
        (pairs,),
        [mask_count],
        [
            (mask_pos.reshape(pairs, 1, slots), pl.BlockSpec((1, 1, slots), lambda i, *_: (i, 0, 0))),
            (tokens, pair_spec(length, D)),
            (cotangent, pair_spec(length, D)),
        ],
        [
            (pair_spec(length, length), (pairs, length, length), BF16),
            (pair_spec(length, D), (pairs, length, D), BF16),
            (pair_spec(length, LANES), (pairs, length, LANES), F32),
            (pair_spec(slots, D), (pairs, slots, D), BF16),
        ],
        [],
        spent(6),
        "order",
    )

    set_b = cast([w_out, w_fc1])
    near_a = set_a[2]
    set_a = last_piece(spread_pieces(set_a, set_b[0]))
    set_c = cast([w_fc2], [near_a])

    n1, qkv = call(
        functools.partial(qkv_kernel, rows_d),
        (pairs,),
        [place],
        [(tokp, pair_spec(length, D)), (img, pair_spec(length, LANES)), vec_in] + piece_ins(set_a),
        [
            (pair_spec(length, D), (pairs, length, D), BF16),
            (pair_spec(length, 3 * D), (pairs, length, 3 * D), BF16),
        ],
        [pltpu.VMEM((D, 3 * D), BF16), sems],
        spent(1),
        "qkv",
    )

    near_b = set_b[2]
    set_b = spread_pieces(set_b, n1)
    (mixed,) = call(
        mix_kernel,
        (pairs,),
        [],
        [(qkv, pair_spec(length, 3 * D))],
        [(pair_spec(length, D), (pairs, length, D), BF16)],
        [],
        spent(1),
        "mix",
        [near_b],
    )

    set_b = last_piece(set_b, mixed)
    h1, n2, z, slope = call(
        functools.partial(fc1_kernel, rows_d),
        (pairs,),
        [place],
        [
            (tokp, pair_spec(length, D)),
            (img, pair_spec(length, LANES)),
            (mixed, pair_spec(length, D)),
            vec_in,
        ]
        + piece_ins(set_b),
        [
            (pair_spec(length, D), (pairs, length, D), F32),
            (pair_spec(length, D), (pairs, length, D), BF16),
            (pair_spec(length, FF), (pairs, length, FF), BF16),
            (pair_spec(slots, FF), (pairs, slots, FF), BF16),
        ],
        [pltpu.VMEM((D, D), BF16), pltpu.VMEM((D, FF), BF16), sems, sems],
        spent(18),
        "fc1",
    )

    def top_rows(cols, idx=lambda i, *_: (0, 0, 0)):
        return pl.BlockSpec((pairs, slots, cols), idx)

    def grad_outs(rows, cols, chunk):
        block = rows // nd
        if block % 8:
            return [(pl.BlockSpec((rows, chunk), lambda i, *_: (0, i)), (rows, cols), BF16)]
        spec = pl.BlockSpec((nd // 2, block, chunk), lambda i, *_: (0, 0, i))
        return [(spec, (nd // 2, block, cols), BF16)] * 2

    def grad_sum(outs):
        if len(outs) == 1:
            rows, cols = outs[0].shape
            blocks = jnp.take(outs[0].reshape(nd, rows // nd, cols), tab[OWN : OWN + nd], axis=0)
            outs = [blocks[: nd // 2], blocks[nd // 2 :]]
        return Sum(plan, call, *outs)

    set_c = spread_pieces(set_c, n2)

    chunk = 2 * LANES
    *got, gb2 = call(
        gw2_kernel,
        (D // chunk,),
        [owners],
        [
            (z, top_rows(FF)),
            (dy, top_rows(chunk, lambda i, *_: (0, 0, i))),
        ],
        grad_outs(FF, D, chunk) + [(pl.BlockSpec((1, chunk), lambda i, *_: (0, i)), (1, D), F32)],
        [pltpu.VMEM((FF, pairs * slots), BF16), pltpu.VMEM((FF, chunk), F32)],
        spent(8),
        "gw2",
    )
    sum_2 = grad_sum(got)
    set_c = last_piece(set_c, gb2)

    df, gb1 = call(
        functools.partial(df_kernel, rows_f),
        (PARTS,),
        [place],
        [(dy, top_rows(D)), (slope, top_rows(D, lambda i, *_: (0, 0, i)))] + piece_ins(set_c),
        [
            (pl.BlockSpec((pairs * slots, D), lambda i, *_: (0, i)), (pairs * slots, FF), BF16),
            (pl.BlockSpec((1, D), lambda i, *_: (0, i)), (1, FF), F32),
        ],
        [pltpu.VMEM((FF, D), BF16), sems],
        spent(7),
        "df",
    )
    sum_2.add()

    some = 2 if pairs % 2 == 0 else 1
    some_spec = pl.BlockSpec((some, slots, D), lambda i, *_: (i, 0, 0))
    dh, dhr, da, mlp_sum = call(
        functools.partial(mlp_back_kernel, rows_d),
        (pairs // some,),
        [place],
        [
            (df, pl.BlockSpec((some * slots, FF), lambda i, *_: (i, 0))),
            (dy, some_spec),
            (h1, some_spec),
            vec_in,
        ]
        + piece_ins(set_b),
        [
            (some_spec, (pairs, slots, D), F32),
            (some_spec, (pairs, slots, D), BF16),
            (some_spec, (pairs, slots, D), BF16),
            (full((8, D)), (8, D), F32),
        ],
        [pltpu.VMEM((D, FF), BF16), pltpu.VMEM((D, D), BF16), sems, sems],
        spent(10),
        "mlp_back",
    )

    got = call(
        gw1o_kernel,
        (PARTS + 1,),
        [owners],
        [
            (n2, top_rows(D)),
            (
                df,
                pl.BlockSpec((pairs * slots, D), lambda i, *_: (0, jnp.minimum(i, PARTS - 1))),
            ),
            (mixed, top_rows(D)),
            (dhr, top_rows(D)),
        ],
        grad_outs(D, FF + D, D),
        [pltpu.VMEM((D, pairs * slots), BF16), pltpu.VMEM((D, D), F32)],
        spent(9),
        "gw1o",
    )
    sum_1 = grad_sum(got)
    sum_2.add()

    part_pairs = pairs // 2 if pairs % 2 == 0 else pairs
    back = None
    for number in range(pairs // part_pairs):
        base = number * part_pairs
        at = lambda rows, cols, base=base: pl.BlockSpec(
            (1, rows, cols), lambda i, *_: (base + i, 0, 0)
        )
        ins = [(qkv, at(length, 3 * D)), (da, at(slots, D))]
        if back is not None:
            ins += [(back[0], ANYWHERE), (back[1], ANYWHERE), (back[2], full((8, D)))]
        back = call(
            functools.partial(attn_back_kernel, back is not None),
            (part_pairs,),
            [],
            ins,
            [
                (at(slots, D), (pairs, slots, D), BF16),
                (at(length, 2 * D), (pairs, length, 2 * D), BF16),
                (full((8, D)), (8, D), F32),
            ],
            [],
            spent(12),
            "attn_back",
            aliases=None if back is None else {2: 0, 3: 1},
        )
        if number == 0:
            sum_1.add()
        sum_2.add()
    dq, dkv, attn_sum = back

    got = call(
        gqkv_kernel,
        (3,),
        [owners],
        [
            (n1, full((pairs, length, D))),
            (dq, full((pairs, slots, D))),
            (
                dkv,
                pl.BlockSpec((pairs, length, D), lambda i, *_: (0, 0, jnp.where(i == 2, 1, 0))),
            ),
        ],
        grad_outs(D, 3 * D, D),
        [pltpu.VMEM((D, pairs * length), BF16), pltpu.VMEM((D, D), F32)],
        spent(9),
        "gqkv",
    )
    sum_3 = grad_sum(got)
    sum_1.add()

    fallback = (D // nd) % 8 != 0 or (FF // nd) % 8 != 0
    places = OWN + nd

    def finish(total, which, masters, moments):
        _, rows, cols = total.parts[0].shape
        grad = total.total(0, 1)[0]
        start, news, made = 0, [], []
        for kind, master, (first, second) in zip(which, masters, moments):
            width = master.shape[1]
            own = lax.dynamic_slice_in_dim(master, bi * rows, rows, 0)
            new_w, new_m, new_v = adamw(
                own,
                grad[:, start : start + width],
                first,
                second,
                STEP_RATES[kind],
                DECAY_RATES[kind],
            )
            news.append(new_w.astype(BF16))
            made += [new_m, new_v]
            start += width
        return Spread(plan, call, jnp.concatenate(news, axis=1)[None]), made

    def put(moved, widths):
        if not fallback:
            return moved.put(places, tab, widths)
        blocks = jnp.concatenate([moved.blocks, moved.got], axis=0)
        count, rows, cols = blocks.shape
        order = jnp.zeros(count, jnp.int32).at[tab[places:]].set(jnp.arange(count, dtype=jnp.int32))
        blocks = jnp.take(blocks, order, axis=0).reshape(count * rows, cols).astype(F32)
        cuts = np.cumsum([0] + list(widths))
        return [blocks[:, a:b] for a, b in zip(cuts[:-1], cuts[1:])]

    sum_3.add()

    grad_tokens, vec_sum = call(
        functools.partial(grad_in_kernel, rows_d),
        (pairs,),
        [place],
        [
            (tokp, pair_spec(length, D)),
            (img, pair_spec(length, LANES)),
            vec_in,
            (dq, pair_spec(slots, D)),
            (dkv, pair_spec(length, 2 * D)),
            (dh, pair_spec(slots, D)),
            (perm, pair_spec(length, length)),
            (attn_sum, full((8, D))),
            (mlp_sum, full((8, D))),
            (gb1, full((1, FF))),
            (gb2, full((1, D))),
        ]
        + piece_ins(set_a),
        [
            (pair_spec(length, D), (pairs, length, D), F32),
            (full((16, D)), (16, D), F32),
        ],
        [pltpu.VMEM((D, 3 * D), BF16), sems],
        spent(15),
        "grad_in",
    )

    vec_gens = [1, 2] + plan.batch
    vec_got = plan.exchange(vec_sum, vec_gens[0])

    last = plan.bbits
    sum_3.add()
    sum_1.add()
    while sum_2.count > 1:
        sum_2.add()
    moved_2, (new_m2, new_v2) = finish(sum_2, (3,), (w_fc2,), ((m_fc2, v_fc2),))

    (layer_out,) = call(
        functools.partial(out_kernel, rows_f),
        (pairs,),
        [place],
        [
            (z, pair_spec(length, FF)),
            (h1, pair_spec(length, D)),
            vec_in,
            (perm, pair_spec(length, length)),
        ]
        + piece_ins(set_c),
        [(pair_spec(length, D), (pairs, length, D), BF16)],
        [pltpu.VMEM((FF, D), BF16), sems],
        spent(13),
        "out",
    )

    vec_place = 1

    def vec_step():
        nonlocal vec_sum, vec_got, vec_place
        if vec_place > len(vec_gens):
            return
        one, two = call.pin([vec_sum, vec_got])
        vec_sum = one + two
        if vec_place < len(vec_gens):
            vec_got = plan.exchange(vec_sum, vec_gens[vec_place])
        vec_place += 1

    moved_1 = moved_3 = None
    while moved_3 is None or moved_3.place < last:
        token = None
        if sum_3.count > 1:
            sum_3.add()
            token = sum_3.sent
        elif moved_3 is None:
            moved_3, (new_mq, new_vq) = finish(sum_3, (0,), (w_qkv,), ((m_qkv, v_qkv),))
            token = moved_3.blocks
        else:
            moved_3.join()
            token = moved_3.blocks
        if sum_1.count > 1:
            sum_1.add()
        elif moved_1 is None:
            moved_1, (new_m1, new_v1, new_mo, new_vo) = finish(
                sum_1, (2, 1), (w_fc1, w_out), ((m_fc1, v_fc1), (m_out, v_out))
            )
        elif moved_1.place < last:
            moved_1.join()
        if moved_2.place < last:
            moved_2.join()
        vec_step()
        call.last = token
    while len(vec_gens) >= vec_place:
        vec_step()
    while moved_1.place < last:
        moved_1.join()
    while moved_2.place < last:
        moved_2.join()
    call.waiting = []
    (new_2,) = put(moved_2, (D,))
    new_1, new_o = put(moved_1, (FF, D))
    (new_q,) = put(moved_3, (3 * D,))

    states = jnp.concatenate([m_vec, v_vec], axis=0)[None]
    for rank in range(plan.bbits):
        got = plan.exchange(states, *(order[rank] for order in plan.gather))
        states = jnp.concatenate([states, got], axis=0)
    order = jnp.zeros(nb, jnp.int32).at[tab[places:]].set(jnp.arange(nb, dtype=jnp.int32))
    own_cols = D // nd
    states = jnp.transpose(jnp.take(states, order, axis=0), (1, 0, 2)).reshape(2 * NVEC, nb * own_cols)
    grad_vec = lax.dynamic_slice_in_dim(vec_sum[:NVEC], fi * nb * own_cols, nb * own_cols, 1)
    vec_new, all_m, all_v = adamw(
        vectors, grad_vec, states[:NVEC], states[NVEC:], STEP_RATES[4], DECAY_RATES[4]
    )
    new_mv = lax.dynamic_slice_in_dim(all_m, bi * own_cols, own_cols, 1)
    new_vv = lax.dynamic_slice_in_dim(all_v, bi * own_cols, own_cols, 1)

    return (
        layer_out,
        grad_tokens,
        new_q,
        new_mq,
        new_vq,
        new_o,
        new_mo,
        new_vo,
        new_1,
        new_m1,
        new_v1,
        new_2,
        new_m2,
        new_v2,
        vec_new,
        new_mv,
        new_vv,
    )


def solution(mesh):
    pairs = P(("batch", "fsdp"), None, None)
    weight = P("fsdp", None)
    state = P(("fsdp", "batch"), None)
    vec_state = P(None, ("fsdp", "batch"))
    matrix = (weight, state, state)
    return jax.shard_map(
        functools.partial(shards, Plan(mesh)),
        mesh=mesh,
        in_specs=(pairs, pairs, P(("batch", "fsdp"), None), P(("batch", "fsdp")))
        + matrix * 4
        + (P(None, "fsdp"), vec_state, vec_state),
        out_specs=(pairs, pairs) + matrix * 4 + (P(None, "fsdp"), vec_state, vec_state),
        check_vma=False,
    )
```

```python
import functools
import math

import jax
import jax.numpy as jnp
import numpy as np
from jax import lax
from jax.experimental import pallas as pl
from jax.experimental.pallas import tpu as pltpu
from jax.sharding import PartitionSpec as P

D = 768
HEADS = 12
HDIM = 64
FF = 3072
TEXT = 40
STEP = 3
MAXM = 128
NVEC = 14
PARTS = FF // D
LANES = 128
SLABS = D // LANES

BETA_ONE = 0.5
BETA_TWO = 0.5
EPS_ADAM = 1e-08
STEP_RATES = (0.03, 0.1, 0.03, 0.015, 0.3)
DECAY_RATES = (0.01, 0.01, 0.01, 0.01, 0.0)
INV_ROOT_TWO = 1.0 / math.sqrt(2.0)
INV_ROOT_TWOPI = 1.0 / math.sqrt(2.0 * math.pi)

KERNEL_VMEM = 24 * 2**20
FLOPS_SCALE = 3e9
BYTES_SCALE = 1e7
F32 = jnp.float32
BF16 = jnp.bfloat16


def dot(a, b):
    return lax.dot_general(a, b, (((1,), (0,)), ((), ())), preferred_element_type=F32)


def dot_first(a, b):
    return lax.dot_general(a, b, (((0,), (0,)), ((), ())), preferred_element_type=F32)


def dot_last(a, b):
    return lax.dot_general(a, b, (((1,), (1,)), ((), ())), preferred_element_type=F32)


def normalize(hidden):
    row_mean = jnp.mean(hidden, axis=-1, keepdims=True)
    centred = hidden - row_mean
    inv_scale = lax.rsqrt(jnp.mean(centred * centred, axis=-1, keepdims=True) + 1e-06)
    return centred * inv_scale, inv_scale


def norm_back(gradient, normed, inv_scale, gain_row):
    scaled = gradient * gain_row
    return inv_scale * (
        scaled
        - jnp.mean(scaled, axis=-1, keepdims=True)
        - normed * jnp.mean(scaled * normed, axis=-1, keepdims=True)
    )


def adamw(weight, gradient, moment_one, moment_two, step_rate, decay_rate):
    new_first = BETA_ONE * moment_one + (1.0 - BETA_ONE) * gradient
    new_second = BETA_TWO * moment_two + (1.0 - BETA_TWO) * gradient * gradient
    correct_one = 1.0 - BETA_ONE**STEP
    correct_two = 1.0 - BETA_TWO**STEP
    update = (
        new_first / correct_one / (jnp.sqrt(new_second / correct_two) + EPS_ADAM)
        + decay_rate * weight
    )
    return (weight - step_rate * update, new_first, new_second)


def spent(micros):
    return pl.CostEstimate(
        flops=int(micros * FLOPS_SCALE), bytes_accessed=int(micros * BYTES_SCALE), transcendentals=0
    )


def full(shape):
    zeros = (0,) * len(shape)
    return pl.BlockSpec(shape, lambda *_: zeros)


ANYWHERE = pl.BlockSpec(memory_space=pl.ANY)


class Plan:
    def __init__(self, mesh):
        self.nf = mesh.shape["fsdp"]
        self.nb = mesh.shape["batch"]
        self.nd = self.nf * self.nb
        self.fbits = self.nf.bit_length() - 1
        self.bbits = self.nb.bit_length() - 1
        assert self.nf == 1 << self.fbits and self.nb == 1 << self.bbits
        assert self.fbits == 2 and self.bbits >= 2
        near = [1, 2, 6] if self.bbits == 3 else [1 << k for k in range(self.bbits)]
        self.batch = [mask * self.nf for mask in near]
        first, second, *rest = self.batch
        self.scatter = ([1, 2, second, first] + rest, [1, first, 2, second] + rest)
        self.gather = (rest[::-1] + [second, first], rest[::-1] + [first, second])
        self.helper = (first, second)

    def exchange(self, value, even, odd=None):
        odd = even if odd is None else odd
        pairs = [(i, i ^ (odd if i & 1 else even)) for i in range(self.nd)]
        return lax.ppermute(value, ("batch", "fsdp"), pairs)

    def spans(self, gens):
        masks = np.zeros(1, np.int32)
        for mask in reversed(gens):
            masks = np.concatenate([masks, masks ^ mask])
        return masks

    def table(self):
        rows = []
        for index in range(self.nd):
            core, fi, bi = index & 1, index & (self.nf - 1), index >> self.fbits
            halves = (bi & 1, (bi >> 1) & 1)
            keep = index ^ self.spans(self.scatter[core][1:])
            send = (index ^ 1) ^ self.spans(self.scatter[1 - core][1:])
            order = np.concatenate([keep, send])
            owners = (order & (self.nf - 1)) * self.nb + (order >> self.fbits)
            places = bi ^ (self.spans(self.gather[core][::-1]) >> self.fbits)
            own = np.asarray([fi, halves[core], halves[1 - core], bi])
            rows.append(np.concatenate([own, owners, places]))
        return np.stack(rows).astype(np.int32)


OWN = 4


PIECES = ((0, None), (1, None), (2, 0), (2, 1), (3, 2), (3, 3))


def piece_copies(refs, target, sems, place_ref, rows, start=0):
    copies = []
    cols = target.shape[1]
    for number, ((mask, kind), ref) in enumerate(zip(PIECES, refs)):
        row = (place_ref[0] ^ mask) * rows
        length = rows
        if kind is not None:
            length = rows // 2
            low = place_ref[1 + kind // 2]
            row = row + (low if kind % 2 == 0 else 1 - low) * length
        copies.append(
            pltpu.make_async_copy(
                ref.at[:, pl.ds(start, cols)],
                target.at[pl.ds(pl.multiple_of(row, 8), length)],
                sems.at[number],
            )
        )
    return copies


def start_all(copies):
    for copy in copies:
        copy.start()


def wait_all(copies):
    for copy in copies:
        copy.wait()


def cast_kernel(place_ref, *refs):
    parts, (shard_ref, mine_ref) = refs[:-2], refs[-2:]
    start = 0
    for part in parts:
        cols = slice(start, start + part.shape[1])
        low = part[...].astype(BF16)
        shard_ref[:, cols] = low

        @pl.when(pl.program_id(0) == 0)
        def _(low=low, cols=cols):
            mine_ref[:, cols] = low

        start += part.shape[1]


def order_kernel(count_ref, pos_ref, tok_ref, cot_ref, perm_ref, tokp_ref, img_ref, dy_ref):
    pair = pl.program_id(0)
    length = tok_ref.shape[1]
    slots = pos_ref.shape[2]
    token = lax.broadcasted_iota(jnp.int32, (length, slots), 0)
    slot = lax.broadcasted_iota(jnp.int32, (length, slots), 1)
    hit = jnp.where(token == pos_ref[0], 1.0, 0.0)
    free = 1.0 - jnp.sum(hit, axis=1, keepdims=True)
    below = lax.broadcasted_iota(jnp.int32, (length, length), 1) < lax.broadcasted_iota(
        jnp.int32, (length, length), 0
    )
    rank = dot(
        jnp.where(below, 1.0, 0.0).astype(BF16),
        jnp.broadcast_to(free, (length, slots)).astype(BF16),
    )
    rest = jnp.where(rank == slot.astype(F32), jnp.broadcast_to(free, (length, slots)), 0.0)
    perm = jnp.concatenate([hit, rest], axis=1).astype(BF16)
    perm_ref[0] = perm
    tokp_ref[0] = dot_first(perm, tok_ref[0]).astype(BF16)
    image = jnp.where(lax.broadcasted_iota(jnp.int32, (length, LANES), 0) >= TEXT, 1.0, 0.0)
    img_ref[0] = dot_first(perm, image.astype(BF16))
    chosen = dot_first(perm[:, :slots], cot_ref[0])
    live = lax.broadcasted_iota(jnp.int32, (slots, 1), 0) < count_ref[pair]
    dy_ref[0] = jnp.where(live, chosen, 0.0).astype(BF16)


def start_row(tok_ref, img_ref, vec_ref):
    return tok_ref[0].astype(F32) + jnp.where(
        img_ref[0][:, :1] > 0.5, vec_ref[1:2, :], vec_ref[0:1, :]
    )


def qkv_kernel(rows, place_ref, tok_ref, img_ref, vec_ref, *refs):
    pieces = refs[: len(PIECES)]
    n1_ref, qkv_ref, w_ref, sems = refs[len(PIECES) :]
    first = pl.program_id(0) == 0
    copies = piece_copies(pieces, w_ref, sems, place_ref, rows)

    @pl.when(first)
    def _():
        start_all(copies)

    normed, _ = normalize(start_row(tok_ref, img_ref, vec_ref))
    n1 = (normed * vec_ref[2:3, :] + vec_ref[3:4, :]).astype(BF16)
    n1_ref[0] = n1

    @pl.when(first)
    def _():
        wait_all(copies)

    qkv_ref[0, :, :D] = (dot(n1, w_ref[:, :D]) + vec_ref[4:5, :]).astype(BF16)
    qkv_ref[0, :, D : 2 * D] = dot(n1, w_ref[:, D : 2 * D]).astype(BF16)
    qkv_ref[0, :, 2 * D :] = (dot(n1, w_ref[:, 2 * D :]) + vec_ref[5:6, :]).astype(BF16)


def mix_kernel(qkv_ref, a_ref):
    low = lax.broadcasted_iota(jnp.int32, (1, LANES), 1) < HDIM
    for slab in range(SLABS):
        cols = slice(slab * LANES, (slab + 1) * LANES)
        q = qkv_ref[0, :, cols] * jnp.asarray(HDIM**-0.5, BF16)
        k = qkv_ref[0, :, D + slab * LANES : D + (slab + 1) * LANES]
        v = qkv_ref[0, :, 2 * D + slab * LANES : 2 * D + (slab + 1) * LANES]
        outs = []
        for head in range(2):
            mine = low if head == 0 else jnp.logical_not(low)
            scores = dot_last(jnp.where(mine, q, jnp.zeros_like(q)), k)
            e = jnp.exp(scores - jnp.max(scores, axis=-1, keepdims=True))
            p = (e * (1.0 / jnp.sum(e, axis=-1, keepdims=True))).astype(BF16)
            outs.append(dot(p, v))
        a_ref[0, :, cols] = jnp.where(low, outs[0], outs[1]).astype(BF16)


def fc1_kernel(rows, place_ref, tok_ref, img_ref, a_ref, vec_ref, *refs):
    pieces = refs[: len(PIECES)]
    h1_ref, n2_ref, z_ref, slope_ref, wo_ref, w1_ref, sem_o, sem_1 = refs[len(PIECES) :]
    first = pl.program_id(0) == 0
    copies_o = piece_copies(pieces, wo_ref, sem_o, place_ref, rows)
    copies_1 = piece_copies(pieces, w1_ref, sem_1, place_ref, rows, D)

    @pl.when(first)
    def _():
        start_all(copies_o)
        start_all(copies_1)
        wait_all(copies_o)

    h1 = start_row(tok_ref, img_ref, vec_ref) + dot(a_ref[0], wo_ref[...]) + vec_ref[6:7, :]
    h1_ref[0] = h1
    normed, _ = normalize(h1)
    n2 = (normed * vec_ref[7:8, :] + vec_ref[8:9, :]).astype(BF16)
    n2_ref[0] = n2

    @pl.when(first)
    def _():
        wait_all(copies_1)

    slots = slope_ref.shape[1]
    for part in range(PARTS):
        cols = slice(part * D, (part + 1) * D)
        f = dot(n2, w1_ref[:, cols]) + vec_ref[9 + part : 10 + part, :]
        phi = 0.5 * (1.0 + lax.erf(f * INV_ROOT_TWO))
        z_ref[0, :, cols] = (f * phi).astype(BF16)
        fs = f[:slots]
        slope = phi[:slots] + fs * jnp.exp(-0.5 * fs * fs) * INV_ROOT_TWOPI
        slope_ref[0, :, cols] = slope.astype(BF16)


def spread(acc_ref, owners_ref, outs):
    if len(outs) == 1:
        outs[0][...] = acc_ref[...].astype(BF16)
        return
    keep_ref, send_ref = outs
    half, block, _ = send_ref.shape

    def one(spot, _):
        for out_ref, base in ((send_ref, half), (keep_ref, 0)):
            start = pl.multiple_of(owners_ref[OWN + base + spot] * block, 8)
            out_ref[spot] = acc_ref[pl.ds(start, block), :].astype(BF16)
        return 0

    lax.fori_loop(0, half, one, 0)


def gw2_kernel(owners_ref, z_ref, dy_ref, *refs):
    outs, (sum_ref, zt_ref, acc_ref) = refs[:-3], refs[-3:]
    pairs, slots, width = z_ref.shape

    @pl.when(pl.program_id(0) == 0)
    def _():
        zt_ref[...] = z_ref[...].reshape(pairs * slots, width).T

    dy = dy_ref[...].reshape(pairs * slots, -1)
    acc_ref[...] = dot(zt_ref[...], dy)
    sum_ref[...] = jnp.sum(dy.astype(F32), axis=0, keepdims=True)
    spread(acc_ref, owners_ref, outs)


def df_kernel(rows, place_ref, dy_ref, slope_ref, *refs):
    pieces = refs[: len(PIECES)]
    df_ref, gb1_ref, w2_ref, sems = refs[len(PIECES) :]
    step = pl.program_id(0)
    pairs, slots, width = slope_ref.shape
    total = pairs * slots
    copies = piece_copies(pieces, w2_ref, sems, place_ref, rows)

    @pl.when(step == 0)
    def _():
        start_all(copies)
        wait_all(copies)

    dz = dot_last(
        dy_ref[...].reshape(total, D), w2_ref[pl.ds(pl.multiple_of(step * width, 8), width), :]
    )
    df = dz * slope_ref[...].reshape(total, width).astype(F32)
    gb1_ref[...] = jnp.sum(df, axis=0, keepdims=True)
    df_ref[...] = df.astype(BF16)


def mlp_back_kernel(rows, place_ref, df_ref, dy_ref, h1_ref, vec_ref, *refs):
    pieces = refs[: len(PIECES)]
    dh_ref, dhr_ref, da_ref, sum_ref, w1_ref, wo_ref, sem_1, sem_o = refs[len(PIECES) :]
    first = pl.program_id(0) == 0
    copies_1 = piece_copies(pieces, w1_ref, sem_1, place_ref, rows, D)
    copies_o = piece_copies(pieces, wo_ref, sem_o, place_ref, rows)

    @pl.when(first)
    def _():
        start_all(copies_1)
        start_all(copies_o)
        sum_ref[...] = jnp.zeros_like(sum_ref)
        wait_all(copies_1)
        wait_all(copies_o)

    some, slots, _ = dy_ref.shape
    total = some * slots
    dn2 = dot_last(df_ref[...], w1_ref[...])
    normed, scale = normalize(h1_ref[...].reshape(total, D))
    dh = dy_ref[...].reshape(total, D).astype(F32) + norm_back(dn2, normed, scale, vec_ref[7:8, :])
    dh_ref[...] = dh.reshape(some, slots, D)
    sum_ref[0:1, :] += jnp.sum(dh, axis=0, keepdims=True)
    sum_ref[1:2, :] += jnp.sum(dn2 * normed, axis=0, keepdims=True)
    sum_ref[2:3, :] += jnp.sum(dn2, axis=0, keepdims=True)
    low = dh.astype(BF16)
    dhr_ref[...] = low.reshape(some, slots, D)
    da_ref[...] = dot_last(low, wo_ref[...]).astype(BF16).reshape(some, slots, D)


def gw1o_kernel(owners_ref, n2_ref, df_ref, a_ref, dhr_ref, *refs):
    outs, (n2t_ref, acc_ref) = refs[:-2], refs[-2:]
    step = pl.program_id(0)
    pairs, slots, _ = n2_ref.shape
    total = pairs * slots

    @pl.when(step == 0)
    def _():
        n2t_ref[...] = n2_ref[...].reshape(total, D).T

    @pl.when(step < PARTS)
    def _():
        acc_ref[...] = dot(n2t_ref[...], df_ref[...])

    @pl.when(step == PARTS)
    def _():
        acc_ref[...] = dot_first(a_ref[...].reshape(total, D), dhr_ref[...].reshape(total, D))

    spread(acc_ref, owners_ref, outs)


def attn_back_kernel(more, qkv_ref, da_ref, *refs):
    if more:
        _, _, before_ref, dq_ref, dkv_ref, sum_ref = refs
    else:
        dq_ref, dkv_ref, sum_ref = refs
    slots = da_ref.shape[1]

    @pl.when(pl.program_id(0) == 0)
    def _():
        sum_ref[...] = before_ref[...] if more else jnp.zeros_like(sum_ref)

    low = lax.broadcasted_iota(jnp.int32, (1, LANES), 1) < HDIM
    scale = jnp.asarray(HDIM**-0.5, BF16)
    for slab in range(SLABS):
        cols = slice(slab * LANES, (slab + 1) * LANES)
        q = qkv_ref[0, :slots, cols] * scale
        k = qkv_ref[0, :, D + slab * LANES : D + (slab + 1) * LANES]
        v = qkv_ref[0, :, 2 * D + slab * LANES : 2 * D + (slab + 1) * LANES]
        da = da_ref[0, :, cols]
        gqs, gks, gvs = [], [], []
        for head in range(2):
            mine = low if head == 0 else jnp.logical_not(low)
            zero = jnp.zeros_like(q)
            scores = dot_last(jnp.where(mine, q, zero), k)
            e = jnp.exp(scores - jnp.max(scores, axis=-1, keepdims=True))
            p = e * (1.0 / jnp.sum(e, axis=-1, keepdims=True))
            gvs.append(dot_first(p.astype(BF16), da))
            dp = dot_last(jnp.where(mine, da, zero), v)
            ds = (p * (dp - jnp.sum(p * dp, axis=-1, keepdims=True))).astype(BF16)
            gqs.append(dot(ds, k))
            gks.append(dot_first(ds, q))
        gq = jnp.where(low, gqs[0], gqs[1]) * (HDIM**-0.5)
        gk = jnp.where(low, gks[0], gks[1])
        gv = jnp.where(low, gvs[0], gvs[1])
        dq_ref[0, :, cols] = gq.astype(BF16)
        dkv_ref[0, :, cols] = gk.astype(BF16)
        dkv_ref[0, :, D + slab * LANES : D + (slab + 1) * LANES] = gv.astype(BF16)
        sum_ref[0:1, cols] += jnp.sum(gq, axis=0, keepdims=True)
        sum_ref[1:2, cols] += jnp.sum(gv, axis=0, keepdims=True)


def gqkv_kernel(owners_ref, n1_ref, dq_ref, dkv_ref, *refs):
    outs, (n1t_ref, acc_ref) = refs[:-2], refs[-2:]
    step = pl.program_id(0)
    pairs, length, _ = n1_ref.shape
    slots = dq_ref.shape[1]

    @pl.when(step == 0)
    def _():
        n1t_ref[...] = n1_ref[...].reshape(pairs * length, D).T
        total = dot(n1t_ref[:, :slots], dq_ref[0])
        for pair in range(1, pairs):
            total += dot(n1t_ref[:, pair * length : pair * length + slots], dq_ref[pair])
        acc_ref[...] = total

    @pl.when(step > 0)
    def _():
        acc_ref[...] = dot(n1t_ref[...], dkv_ref[...].reshape(pairs * length, D))

    spread(acc_ref, owners_ref, outs)


def split_three(value):
    one = value.astype(BF16)
    left = value - one.astype(F32)
    two = left.astype(BF16)
    return one, two, (left - two.astype(F32)).astype(BF16)


def grad_in_kernel(
    rows,
    place_ref,
    tok_ref,
    img_ref,
    vec_ref,
    dq_ref,
    dkv_ref,
    dh_ref,
    perm_ref,
    attn_sum_ref,
    mlp_sum_ref,
    gb1_ref,
    gb2_ref,
    *refs,
):
    pieces = refs[: len(PIECES)]
    out_ref, sum_ref, w_ref, sems = refs[len(PIECES) :]
    first = pl.program_id(0) == 0
    slots = dq_ref.shape[1]
    copies = piece_copies(pieces, w_ref, sems, place_ref, rows)

    @pl.when(first)
    def _():
        start_all(copies)
        sum_ref[...] = jnp.zeros_like(sum_ref)
        sum_ref[4:6, :] = attn_sum_ref[0:2, :]
        sum_ref[6:9, :] = mlp_sum_ref[0:3, :]
        for part in range(PARTS):
            sum_ref[9 + part : 10 + part, :] = gb1_ref[:, part * D : (part + 1) * D]
        sum_ref[9 + PARTS : 10 + PARTS, :] = gb2_ref[...]
        wait_all(copies)

    dn_all = dot_last(dkv_ref[0], w_ref[:, D:])
    dn_top = dn_all[:slots] + dot_last(dq_ref[0], w_ref[:, :D])
    dn = jnp.concatenate([dn_top, dn_all[slots:]], axis=0)
    normed, scale = normalize(start_row(tok_ref, img_ref, vec_ref))
    grad = norm_back(dn, normed, scale, vec_ref[2:3, :])
    grad = jnp.concatenate([grad[:slots] + dh_ref[0], grad[slots:]], axis=0)
    image = img_ref[0][:, :1] > 0.5
    sum_ref[0:1, :] += jnp.sum(jnp.where(image, 0.0, grad), axis=0, keepdims=True)
    sum_ref[1:2, :] += jnp.sum(jnp.where(image, grad, 0.0), axis=0, keepdims=True)
    sum_ref[2:3, :] += jnp.sum(dn * normed, axis=0, keepdims=True)
    sum_ref[3:4, :] += jnp.sum(dn, axis=0, keepdims=True)
    one, two, three = split_three(grad)
    perm = perm_ref[0]
    out_ref[0] = dot(perm, one) + dot(perm, two) + dot(perm, three)


def out_kernel(rows, place_ref, z_ref, h1_ref, vec_ref, perm_ref, *refs):
    pieces = refs[: len(PIECES)]
    out_ref, w_ref, sems = refs[len(PIECES) :]
    first = pl.program_id(0) == 0
    copies = piece_copies(pieces, w_ref, sems, place_ref, rows)

    @pl.when(first)
    def _():
        start_all(copies)
        wait_all(copies)

    y = h1_ref[0] + dot(z_ref[0], w_ref[...]) + vec_ref[9 + PARTS : 10 + PARTS, :]
    out_ref[0] = dot(perm_ref[0], y.astype(BF16)).astype(BF16)


def place_kernel(number, base, spots_ref, one_ref, two_ref, *refs):
    step = pl.program_id(0)
    count, rows, _ = one_ref.shape

    def put(out_ref):
        def one(spot, _):
            for source, first in ((one_ref, base), (two_ref, base + count)):
                at = pl.ds(pl.multiple_of(spots_ref[first + spot] * rows, 8), rows)
                out_ref[at, :] = source[spot].astype(F32)
            return 0

        lax.fori_loop(0, count, one, 0)

    if number == 1:
        put(refs[0])
        return
    last = pl.num_programs(0) - 1

    @pl.when(step < last)
    def _():
        put(refs[0])

    @pl.when(step == last)
    def _():
        put(refs[1])


def later(value, dep):
    return lax.optimization_barrier((value, dep))[0]


class Chain:
    def __init__(self):
        self.last, self.waiting = None, []

    def pin(self, values):
        return lax.optimization_barrier((list(values), self.last))[0]

    def hold(self, value):
        self.waiting.append(value)
        return value

    def __call__(
        self, kernel, grid, scalars, ins, outs, scratch, estimate, name, after=(), aliases=None
    ):
        deps = list(after) + self.waiting
        self.waiting = []
        if self.last is not None:
            deps.append(self.last)
        fixed = len(scalars) + len(ins)
        extra = len(deps)

        def body(*refs):
            kernel(*refs[:fixed], *refs[fixed + extra :])

        got = pl.pallas_call(
            body,
            grid_spec=pltpu.PrefetchScalarGridSpec(
                num_scalar_prefetch=len(scalars),
                grid=grid,
                in_specs=[spec for _, spec in ins] + [ANYWHERE] * extra,
                out_specs=[spec for spec, _, _ in outs],
                scratch_shapes=scratch,
            ),
            out_shape=[jax.ShapeDtypeStruct(dims, kind) for _, dims, kind in outs],
            input_output_aliases={
                len(scalars) + k: v for k, v in (aliases or {}).items()
            },
            cost_estimate=estimate,
            compiler_params=pltpu.CompilerParams(vmem_limit_bytes=KERNEL_VMEM),
            name=name,
        )(*scalars, *[value for value, _ in ins], *deps)
        self.last = got[-1]
        return got


class Sum:
    def __init__(self, plan, call, keep, send):
        self.plan, self.call = plan, call
        self.parts, self.count, self.place = [keep], keep.shape[0], 0
        self.move(send)

    def move(self, send):
        got = self.plan.exchange(send, *(order[self.place] for order in self.plan.scatter))
        self.parts.append(got)
        self.place += 1

    def total(self, low, high):
        parts = self.call.pin(self.parts)
        total = parts[0][low:high].astype(F32)
        for part in parts[1:]:
            total = total + part[low:high].astype(F32)
        return total

    def add(self):
        self.count //= 2
        total = self.total(self.count, 2 * self.count)
        self.sent = self.call.hold(total.astype(BF16))
        self.move(self.sent)


class Spread:
    def __init__(self, plan, call, block):
        self.plan, self.call, self.place = plan, call, 0
        self.move(block)

    def move(self, blocks):
        self.blocks = self.call.hold(blocks)
        self.got = self.plan.exchange(blocks, *(order[self.place] for order in self.plan.gather))
        self.place += 1

    def join(self):
        self.move(jnp.concatenate(self.call.pin([self.blocks, self.got]), axis=0))

    def put(self, base, tab, widths):
        count, rows, cols = self.blocks.shape
        step = D if len(widths) > 1 or cols > D else D // 3
        last = widths[0] // step - 1
        ins = [
            (value, pl.BlockSpec((count, rows, step), lambda i, *_: (0, 0, i)))
            for value in (self.blocks, self.got)
        ]
        maps = [lambda i, *_: (0, jnp.minimum(i, last)), lambda i, *_: (0, 0)]
        return self.call(
            functools.partial(place_kernel, len(widths), base),
            (cols // step,),
            [tab],
            ins,
            [
                (pl.BlockSpec((2 * count * rows, step), idx), (2 * count * rows, width), F32)
                for idx, width in zip(maps, widths)
            ],
            [],
            spent(1),
            "place",
        )


def shards(
    plan,
    tokens,
    cotangent,
    mask_pos,
    mask_count,
    w_qkv,
    m_qkv,
    v_qkv,
    w_out,
    m_out,
    v_out,
    w_fc1,
    m_fc1,
    v_fc1,
    w_fc2,
    m_fc2,
    v_fc2,
    vectors,
    m_vec,
    v_vec,
):
    pairs, length, _ = tokens.shape
    slots = mask_pos.shape[1]
    nf, nb, nd = plan.nf, plan.nb, plan.nd
    fi = lax.axis_index("fsdp").astype(jnp.int32)
    bi = lax.axis_index("batch").astype(jnp.int32)
    tab = lax.dynamic_index_in_dim(jnp.asarray(plan.table()), bi * nf + fi, 0, keepdims=False)
    place = owners = tab
    call = Chain()


    def pair_spec(rows, cols):
        return pl.BlockSpec((1, rows, cols), lambda i, *_: (i, 0, 0))

    def piece_ins(pieces):
        return [(value, ANYWHERE) for value in pieces]

    sems = pltpu.SemaphoreType.DMA((len(PIECES),))
    rows_d, rows_f = D // nf, FF // nf

    low_vec = vectors.astype(BF16)
    vec_parts = [low_vec, plan.exchange(low_vec, 1)]
    vec_parts += [plan.exchange(part, 2) for part in vec_parts]
    columns = []
    for spot in range(nf):
        chosen = vec_parts[0]
        for mask in range(1, nf):
            chosen = jnp.where((fi ^ mask) == spot, vec_parts[mask], chosen)
        columns.append(chosen)
    vec = jnp.concatenate(columns, axis=1).astype(F32)
    vec = jnp.pad(vec, ((0, 16 - NVEC), (0, 0)))
    vec_in = (vec, full(vec.shape))

    def cast(shard_list, after=()):
        rows = shard_list[0].shape[0]
        half = rows // 2
        cols = sum(value.shape[1] for value in shard_list)
        row = lambda i, place_ref: (i ^ place_ref[1], 0)
        shard, mine = call(
            cast_kernel,
            (2,),
            [place],
            [(value, pl.BlockSpec((half, value.shape[1]), row)) for value in shard_list],
            [
                (pl.BlockSpec((half, cols), row), (rows, cols), BF16),
                (pl.BlockSpec((half, cols), lambda i, *_: (0, 0)), (half, cols), BF16),
            ],
            [],
            spent(rows * cols / 2e5),
            "cast",
            after,
        )
        return [shard, plan.exchange(shard, 1), plan.exchange(mine, 2)]

    def spread_pieces(pieces, dep=None):
        near = pieces[2]
        ready = near if dep is None else later(near, dep)
        other = plan.exchange(ready, *plan.helper)
        return pieces[:2] + [near, other, plan.exchange(ready, 1)]

    def last_piece(pieces, dep=None):
        other = pieces[3]
        return pieces + [plan.exchange(other if dep is None else later(other, dep), 1)]

    set_a = cast([w_qkv])

    perm, tokp, img, dy = call(
        order_kernel,
        (pairs,),
        [mask_count],
        [
            (mask_pos.reshape(pairs, 1, slots), pl.BlockSpec((1, 1, slots), lambda i, *_: (i, 0, 0))),
            (tokens, pair_spec(length, D)),
            (cotangent, pair_spec(length, D)),
        ],
        [
            (pair_spec(length, length), (pairs, length, length), BF16),
            (pair_spec(length, D), (pairs, length, D), BF16),
            (pair_spec(length, LANES), (pairs, length, LANES), F32),
            (pair_spec(slots, D), (pairs, slots, D), BF16),
        ],
        [],
        spent(6),
        "order",
    )

    set_b = cast([w_out, w_fc1])
    near_a = set_a[2]
    set_a = last_piece(spread_pieces(set_a, set_b[0]))
    set_c = cast([w_fc2], [near_a])

    n1, qkv = call(
        functools.partial(qkv_kernel, rows_d),
        (pairs,),
        [place],
        [(tokp, pair_spec(length, D)), (img, pair_spec(length, LANES)), vec_in] + piece_ins(set_a),
        [
            (pair_spec(length, D), (pairs, length, D), BF16),
            (pair_spec(length, 3 * D), (pairs, length, 3 * D), BF16),
        ],
        [pltpu.VMEM((D, 3 * D), BF16), sems],
        spent(1),
        "qkv",
    )

    near_b = set_b[2]
    set_b = spread_pieces(set_b, n1)
    (mixed,) = call(
        mix_kernel,
        (pairs,),
        [],
        [(qkv, pair_spec(length, 3 * D))],
        [(pair_spec(length, D), (pairs, length, D), BF16)],
        [],
        spent(1),
        "mix",
        [near_b],
    )

    set_b = last_piece(set_b, mixed)
    h1, n2, z, slope = call(
        functools.partial(fc1_kernel, rows_d),
        (pairs,),
        [place],
        [
            (tokp, pair_spec(length, D)),
            (img, pair_spec(length, LANES)),
            (mixed, pair_spec(length, D)),
            vec_in,
        ]
        + piece_ins(set_b),
        [
            (pair_spec(length, D), (pairs, length, D), F32),
            (pair_spec(length, D), (pairs, length, D), BF16),
            (pair_spec(length, FF), (pairs, length, FF), BF16),
            (pair_spec(slots, FF), (pairs, slots, FF), BF16),
        ],
        [pltpu.VMEM((D, D), BF16), pltpu.VMEM((D, FF), BF16), sems, sems],
        spent(18),
        "fc1",
    )

    def top_rows(cols, idx=lambda i, *_: (0, 0, 0)):
        return pl.BlockSpec((pairs, slots, cols), idx)

    def grad_outs(rows, cols, chunk):
        block = rows // nd
        if block % 8:
            return [(pl.BlockSpec((rows, chunk), lambda i, *_: (0, i)), (rows, cols), BF16)]
        spec = pl.BlockSpec((nd // 2, block, chunk), lambda i, *_: (0, 0, i))
        return [(spec, (nd // 2, block, cols), BF16)] * 2

    def grad_sum(outs):
        if len(outs) == 1:
            rows, cols = outs[0].shape
            blocks = jnp.take(outs[0].reshape(nd, rows // nd, cols), tab[OWN : OWN + nd], axis=0)
            outs = [blocks[: nd // 2], blocks[nd // 2 :]]
        return Sum(plan, call, *outs)

    set_c = spread_pieces(set_c, n2)

    chunk = 2 * LANES
    *got, gb2 = call(
        gw2_kernel,
        (D // chunk,),
        [owners],
        [
            (z, top_rows(FF)),
            (dy, top_rows(chunk, lambda i, *_: (0, 0, i))),
        ],
        grad_outs(FF, D, chunk) + [(pl.BlockSpec((1, chunk), lambda i, *_: (0, i)), (1, D), F32)],
        [pltpu.VMEM((FF, pairs * slots), BF16), pltpu.VMEM((FF, chunk), F32)],
        spent(8),
        "gw2",
    )
    sum_2 = grad_sum(got)
    set_c = last_piece(set_c, gb2)

    df, gb1 = call(
        functools.partial(df_kernel, rows_f),
        (PARTS,),
        [place],
        [(dy, top_rows(D)), (slope, top_rows(D, lambda i, *_: (0, 0, i)))] + piece_ins(set_c),
        [
            (pl.BlockSpec((pairs * slots, D), lambda i, *_: (0, i)), (pairs * slots, FF), BF16),
            (pl.BlockSpec((1, D), lambda i, *_: (0, i)), (1, FF), F32),
        ],
        [pltpu.VMEM((FF, D), BF16), sems],
        spent(7),
        "df",
    )
    sum_2.add()

    some = 2 if pairs % 2 == 0 else 1
    some_spec = pl.BlockSpec((some, slots, D), lambda i, *_: (i, 0, 0))
    dh, dhr, da, mlp_sum = call(
        functools.partial(mlp_back_kernel, rows_d),
        (pairs // some,),
        [place],
        [
            (df, pl.BlockSpec((some * slots, FF), lambda i, *_: (i, 0))),
            (dy, some_spec),
            (h1, some_spec),
            vec_in,
        ]
        + piece_ins(set_b),
        [
            (some_spec, (pairs, slots, D), F32),
            (some_spec, (pairs, slots, D), BF16),
            (some_spec, (pairs, slots, D), BF16),
            (full((8, D)), (8, D), F32),
        ],
        [pltpu.VMEM((D, FF), BF16), pltpu.VMEM((D, D), BF16), sems, sems],
        spent(10),
        "mlp_back",
    )

    got = call(
        gw1o_kernel,
        (PARTS + 1,),
        [owners],
        [
            (n2, top_rows(D)),
            (
                df,
                pl.BlockSpec((pairs * slots, D), lambda i, *_: (0, jnp.minimum(i, PARTS - 1))),
            ),
            (mixed, top_rows(D)),
            (dhr, top_rows(D)),
        ],
        grad_outs(D, FF + D, D),
        [pltpu.VMEM((D, pairs * slots), BF16), pltpu.VMEM((D, D), F32)],
        spent(9),
        "gw1o",
    )
    sum_1 = grad_sum(got)
    sum_2.add()

    part_pairs = pairs // 2 if pairs % 2 == 0 else pairs
    back = None
    for number in range(pairs // part_pairs):
        base = number * part_pairs
        at = lambda rows, cols, base=base: pl.BlockSpec(
            (1, rows, cols), lambda i, *_: (base + i, 0, 0)
        )
        ins = [(qkv, at(length, 3 * D)), (da, at(slots, D))]
        if back is not None:
            ins += [(back[0], ANYWHERE), (back[1], ANYWHERE), (back[2], full((8, D)))]
        back = call(
            functools.partial(attn_back_kernel, back is not None),
            (part_pairs,),
            [],
            ins,
            [
                (at(slots, D), (pairs, slots, D), BF16),
                (at(length, 2 * D), (pairs, length, 2 * D), BF16),
                (full((8, D)), (8, D), F32),
            ],
            [],
            spent(12),
            "attn_back",
            aliases=None if back is None else {2: 0, 3: 1},
        )
        if number == 0:
            sum_1.add()
        sum_2.add()
    dq, dkv, attn_sum = back

    got = call(
        gqkv_kernel,
        (3,),
        [owners],
        [
            (n1, full((pairs, length, D))),
            (dq, full((pairs, slots, D))),
            (
                dkv,
                pl.BlockSpec((pairs, length, D), lambda i, *_: (0, 0, jnp.where(i == 2, 1, 0))),
            ),
        ],
        grad_outs(D, 3 * D, D),
        [pltpu.VMEM((D, pairs * length), BF16), pltpu.VMEM((D, D), F32)],
        spent(9),
        "gqkv",
    )
    sum_3 = grad_sum(got)
    sum_1.add()

    fallback = (D // nd) % 8 != 0 or (FF // nd) % 8 != 0
    places = OWN + nd

    def finish(total, which, masters, moments):
        _, rows, cols = total.parts[0].shape
        grad = total.total(0, 1)[0]
        start, news, made = 0, [], []
        for kind, master, (first, second) in zip(which, masters, moments):
            width = master.shape[1]
            own = lax.dynamic_slice_in_dim(master, bi * rows, rows, 0)
            new_w, new_m, new_v = adamw(
                own,
                grad[:, start : start + width],
                first,
                second,
                STEP_RATES[kind],
                DECAY_RATES[kind],
            )
            news.append(new_w.astype(BF16))
            made += [new_m, new_v]
            start += width
        return Spread(plan, call, jnp.concatenate(news, axis=1)[None]), made

    def put(moved, widths):
        if not fallback:
            return moved.put(places, tab, widths)
        blocks = jnp.concatenate([moved.blocks, moved.got], axis=0)
        count, rows, cols = blocks.shape
        order = jnp.zeros(count, jnp.int32).at[tab[places:]].set(jnp.arange(count, dtype=jnp.int32))
        blocks = jnp.take(blocks, order, axis=0).reshape(count * rows, cols).astype(F32)
        cuts = np.cumsum([0] + list(widths))
        return [blocks[:, a:b] for a, b in zip(cuts[:-1], cuts[1:])]

    sum_3.add()

    grad_tokens, vec_sum = call(
        functools.partial(grad_in_kernel, rows_d),
        (pairs,),
        [place],
        [
            (tokp, pair_spec(length, D)),
            (img, pair_spec(length, LANES)),
            vec_in,
            (dq, pair_spec(slots, D)),
            (dkv, pair_spec(length, 2 * D)),
            (dh, pair_spec(slots, D)),
            (perm, pair_spec(length, length)),
            (attn_sum, full((8, D))),
            (mlp_sum, full((8, D))),
            (gb1, full((1, FF))),
            (gb2, full((1, D))),
        ]
        + piece_ins(set_a),
        [
            (pair_spec(length, D), (pairs, length, D), F32),
            (full((16, D)), (16, D), F32),
        ],
        [pltpu.VMEM((D, 3 * D), BF16), sems],
        spent(15),
        "grad_in",
    )

    vec_gens = [1, 2] + plan.batch
    vec_got = plan.exchange(vec_sum, vec_gens[0])

    last = plan.bbits
    sum_3.add()
    sum_1.add()
    while sum_2.count > 1:
        sum_2.add()
    moved_2, (new_m2, new_v2) = finish(sum_2, (3,), (w_fc2,), ((m_fc2, v_fc2),))

    (layer_out,) = call(
        functools.partial(out_kernel, rows_f),
        (pairs,),
        [place],
        [
            (z, pair_spec(length, FF)),
            (h1, pair_spec(length, D)),
            vec_in,
            (perm, pair_spec(length, length)),
        ]
        + piece_ins(set_c),
        [(pair_spec(length, D), (pairs, length, D), BF16)],
        [pltpu.VMEM((FF, D), BF16), sems],
        spent(13),
        "out",
    )

    vec_place = 1

    def vec_step():
        nonlocal vec_sum, vec_got, vec_place
        if vec_place > len(vec_gens):
            return
        one, two = call.pin([vec_sum, vec_got])
        vec_sum = one + two
        if vec_place < len(vec_gens):
            vec_got = plan.exchange(vec_sum, vec_gens[vec_place])
        vec_place += 1

    moved_1 = moved_3 = None
    while moved_3 is None or moved_3.place < last:
        token = None
        if sum_3.count > 1:
            sum_3.add()
            token = sum_3.sent
        elif moved_3 is None:
            moved_3, (new_mq, new_vq) = finish(sum_3, (0,), (w_qkv,), ((m_qkv, v_qkv),))
            token = moved_3.blocks
        else:
            moved_3.join()
            token = moved_3.blocks
        if sum_1.count > 1:
            sum_1.add()
        elif moved_1 is None:
            moved_1, (new_m1, new_v1, new_mo, new_vo) = finish(
                sum_1, (2, 1), (w_fc1, w_out), ((m_fc1, v_fc1), (m_out, v_out))
            )
        elif moved_1.place < last:
            moved_1.join()
        if moved_2.place < last:
            moved_2.join()
        vec_step()
        call.last = token
    while len(vec_gens) >= vec_place:
        vec_step()
    while moved_1.place < last:
        moved_1.join()
    while moved_2.place < last:
        moved_2.join()
    call.waiting = []
    (new_2,) = put(moved_2, (D,))
    new_1, new_o = put(moved_1, (FF, D))
    (new_q,) = put(moved_3, (3 * D,))

    states = jnp.concatenate([m_vec, v_vec], axis=0)[None]
    for rank in range(plan.bbits):
        got = plan.exchange(states, *(order[rank] for order in plan.gather))
        states = jnp.concatenate([states, got], axis=0)
    order = jnp.zeros(nb, jnp.int32).at[tab[places:]].set(jnp.arange(nb, dtype=jnp.int32))
    own_cols = D // nd
    states = jnp.transpose(jnp.take(states, order, axis=0), (1, 0, 2)).reshape(2 * NVEC, nb * own_cols)
    grad_vec = lax.dynamic_slice_in_dim(vec_sum[:NVEC], fi * nb * own_cols, nb * own_cols, 1)
    vec_new, all_m, all_v = adamw(
        vectors, grad_vec, states[:NVEC], states[NVEC:], STEP_RATES[4], DECAY_RATES[4]
    )
    new_mv = lax.dynamic_slice_in_dim(all_m, bi * own_cols, own_cols, 1)
    new_vv = lax.dynamic_slice_in_dim(all_v, bi * own_cols, own_cols, 1)

    return (
        layer_out,
        grad_tokens,
        new_q,
        new_mq,
        new_vq,
        new_o,
        new_mo,
        new_vo,
        new_1,
        new_m1,
        new_v1,
        new_2,
        new_m2,
        new_v2,
        vec_new,
        new_mv,
        new_vv,
    )


def solution(mesh):
    pairs = P(("batch", "fsdp"), None, None)
    weight = P("fsdp", None)
    state = P(("fsdp", "batch"), None)
    vec_state = P(None, ("fsdp", "batch"))
    matrix = (weight, state, state)
    return jax.shard_map(
        functools.partial(shards, Plan(mesh)),
        mesh=mesh,
        in_specs=(pairs, pairs, P(("batch", "fsdp"), None), P(("batch", "fsdp")))
        + matrix * 4
        + (P(None, "fsdp"), vec_state, vec_state),
        out_specs=(pairs, pairs) + matrix * 4 + (P(None, "fsdp"), vec_state, vec_state),
        check_vma=False,
    )
```

```python
import functools
import math

import jax
import jax.numpy as jnp
import numpy as np
from jax import lax
from jax.experimental import pallas as pl
from jax.experimental.pallas import tpu as pltpu
from jax.sharding import PartitionSpec as P

D = 768
HEADS = 12
HDIM = 64
FF = 3072
TEXT = 40
STEP = 3
MAXM = 128
NVEC = 14
PARTS = FF // D
LANES = 128
SLABS = D // LANES

BETA_ONE = 0.5
BETA_TWO = 0.5
EPS_ADAM = 1e-08
STEP_RATES = (0.03, 0.1, 0.03, 0.015, 0.3)
DECAY_RATES = (0.01, 0.01, 0.01, 0.01, 0.0)
INV_ROOT_TWO = 1.0 / math.sqrt(2.0)
INV_ROOT_TWOPI = 1.0 / math.sqrt(2.0 * math.pi)

KERNEL_VMEM = 20 * 2**20
FLOPS_SCALE = 3e9
BYTES_SCALE = 1e7
F32 = jnp.float32
BF16 = jnp.bfloat16


def dot(a, b):
    return lax.dot_general(a, b, (((1,), (0,)), ((), ())), preferred_element_type=F32)


def dot_first(a, b):
    return lax.dot_general(a, b, (((0,), (0,)), ((), ())), preferred_element_type=F32)


def dot_last(a, b):
    return lax.dot_general(a, b, (((1,), (1,)), ((), ())), preferred_element_type=F32)


def normalize(hidden):
    row_mean = jnp.mean(hidden, axis=-1, keepdims=True)
    centred = hidden - row_mean
    inv_scale = lax.rsqrt(jnp.mean(centred * centred, axis=-1, keepdims=True) + 1e-06)
    return centred * inv_scale, inv_scale


def norm_back(gradient, normed, inv_scale, gain_row):
    scaled = gradient * gain_row
    return inv_scale * (
        scaled
        - jnp.mean(scaled, axis=-1, keepdims=True)
        - normed * jnp.mean(scaled * normed, axis=-1, keepdims=True)
    )


def adamw(weight, gradient, moment_one, moment_two, step_rate, decay_rate):
    new_first = BETA_ONE * moment_one + (1.0 - BETA_ONE) * gradient
    new_second = BETA_TWO * moment_two + (1.0 - BETA_TWO) * gradient * gradient
    correct_one = 1.0 - BETA_ONE**STEP
    correct_two = 1.0 - BETA_TWO**STEP
    update = (
        new_first / correct_one / (jnp.sqrt(new_second / correct_two) + EPS_ADAM)
        + decay_rate * weight
    )
    return (weight - step_rate * update, new_first, new_second)


def spent(micros):
    return pl.CostEstimate(
        flops=int(micros * FLOPS_SCALE), bytes_accessed=int(micros * BYTES_SCALE), transcendentals=0
    )


def full(shape):
    zeros = (0,) * len(shape)
    return pl.BlockSpec(shape, lambda *_: zeros)


ANYWHERE = pl.BlockSpec(memory_space=pl.ANY)


class Plan:
    def __init__(self, mesh):
        self.nf = mesh.shape["fsdp"]
        self.nb = mesh.shape["batch"]
        self.nd = self.nf * self.nb
        self.fbits = self.nf.bit_length() - 1
        self.bbits = self.nb.bit_length() - 1
        assert self.nf == 1 << self.fbits and self.nb == 1 << self.bbits
        assert self.fbits == 2 and self.bbits >= 2
        near = [1, 2, 6] if self.bbits == 3 else [1 << k for k in range(self.bbits)]
        self.batch = [mask * self.nf for mask in near]
        first, second, *rest = self.batch
        self.scatter = ([1, 2, second, first] + rest, [1, first, 2, second] + rest)
        self.gather = (rest[::-1] + [second, first], rest[::-1] + [first, second])
        self.helper = (first, second)

    def exchange(self, value, even, odd=None):
        odd = even if odd is None else odd
        pairs = [(i, i ^ (odd if i & 1 else even)) for i in range(self.nd)]
        return lax.ppermute(value, ("batch", "fsdp"), pairs)

    def spans(self, gens):
        masks = np.zeros(1, np.int32)
        for mask in reversed(gens):
            masks = np.concatenate([masks, masks ^ mask])
        return masks

    def table(self):
        rows = []
        for index in range(self.nd):
            core, fi, bi = index & 1, index & (self.nf - 1), index >> self.fbits
            halves = (bi & 1, (bi >> 1) & 1)
            keep = index ^ self.spans(self.scatter[core][1:])
            send = (index ^ 1) ^ self.spans(self.scatter[1 - core][1:])
            order = np.concatenate([keep, send])
            owners = (order & (self.nf - 1)) * self.nb + (order >> self.fbits)
            places = bi ^ (self.spans(self.gather[core][::-1]) >> self.fbits)
            own = np.asarray([fi, halves[core], halves[1 - core], bi])
            rows.append(np.concatenate([own, owners, places, np.argsort(places)]))
        return np.stack(rows).astype(np.int32)


OWN = 4


PIECES = ((0, None), (1, None), (2, 0), (2, 1), (3, 2), (3, 3))


def piece_copies(refs, target, sems, place_ref, rows, start=0):
    copies = []
    cols = target.shape[1]
    for number, ((mask, kind), ref) in enumerate(zip(PIECES, refs)):
        row = (place_ref[0] ^ mask) * rows
        length = rows
        if kind is not None:
            length = rows // 2
            low = place_ref[1 + kind // 2]
            row = row + (low if kind % 2 == 0 else 1 - low) * length
        copies.append(
            pltpu.make_async_copy(
                ref.at[:, pl.ds(start, cols)],
                target.at[pl.ds(pl.multiple_of(row, 8), length)],
                sems.at[number],
            )
        )
    return copies


def start_all(copies):
    for copy in copies:
        copy.start()


def wait_all(copies):
    for copy in copies:
        copy.wait()


def cast_kernel(place_ref, *refs):
    parts, (shard_ref, mine_ref) = refs[:-2], refs[-2:]
    start = 0
    for part in parts:
        cols = slice(start, start + part.shape[1])
        low = part[...].astype(BF16)
        shard_ref[:, cols] = low

        @pl.when(pl.program_id(0) == 0)
        def _(low=low, cols=cols):
            mine_ref[:, cols] = low

        start += part.shape[1]


def order_kernel(count_ref, pos_ref, tok_ref, cot_ref, perm_ref, tokp_ref, img_ref, dy_ref):
    pair = pl.program_id(0)
    length = tok_ref.shape[1]
    slots = pos_ref.shape[2]
    token = lax.broadcasted_iota(jnp.int32, (length, slots), 0)
    slot = lax.broadcasted_iota(jnp.int32, (length, slots), 1)
    hit = jnp.where(token == pos_ref[0], 1.0, 0.0)
    free = 1.0 - jnp.sum(hit, axis=1, keepdims=True)
    below = lax.broadcasted_iota(jnp.int32, (length, length), 1) < lax.broadcasted_iota(
        jnp.int32, (length, length), 0
    )
    rank = dot(
        jnp.where(below, 1.0, 0.0).astype(BF16),
        jnp.broadcast_to(free, (length, slots)).astype(BF16),
    )
    rest = jnp.where(rank == slot.astype(F32), jnp.broadcast_to(free, (length, slots)), 0.0)
    perm = jnp.concatenate([hit, rest], axis=1).astype(BF16)
    perm_ref[0] = perm
    tokp_ref[0] = dot_first(perm, tok_ref[0]).astype(BF16)
    image = jnp.where(lax.broadcasted_iota(jnp.int32, (length, LANES), 0) >= TEXT, 1.0, 0.0)
    img_ref[0] = dot_first(perm, image.astype(BF16)).astype(BF16)
    chosen = dot_first(perm[:, :slots], cot_ref[0])
    live = lax.broadcasted_iota(jnp.int32, (slots, 1), 0) < count_ref[pair]
    dy_ref[0] = jnp.where(live, chosen, 0.0).astype(BF16)


def start_row(tok_ref, img_ref, vec_ref):
    return tok_ref[0].astype(F32) + jnp.where(
        img_ref[0][:, :1].astype(F32) > 0.5, vec_ref[1:2, :], vec_ref[0:1, :]
    )


def qkv_kernel(rows, place_ref, tok_ref, img_ref, vec_ref, *refs):
    pieces = refs[: len(PIECES)]
    n1_ref, qkv_ref, w_ref, sems = refs[len(PIECES) :]
    first = pl.program_id(0) == 0
    copies = piece_copies(pieces, w_ref, sems, place_ref, rows)

    @pl.when(first)
    def _():
        start_all(copies)

    normed, _ = normalize(start_row(tok_ref, img_ref, vec_ref))
    n1 = (normed * vec_ref[2:3, :] + vec_ref[3:4, :]).astype(BF16)
    n1_ref[0] = n1

    @pl.when(first)
    def _():
        wait_all(copies)

    qkv_ref[0, :, :D] = (dot(n1, w_ref[:, :D]) + vec_ref[4:5, :]).astype(BF16)
    qkv_ref[0, :, D : 2 * D] = dot(n1, w_ref[:, D : 2 * D]).astype(BF16)
    qkv_ref[0, :, 2 * D :] = (dot(n1, w_ref[:, 2 * D :]) + vec_ref[5:6, :]).astype(BF16)


def mix_kernel(qkv_ref, a_ref):
    low = lax.broadcasted_iota(jnp.int32, (1, LANES), 1) < HDIM
    for slab in range(SLABS):
        cols = slice(slab * LANES, (slab + 1) * LANES)
        q = qkv_ref[0, :, cols] * jnp.asarray(HDIM**-0.5, BF16)
        k = qkv_ref[0, :, D + slab * LANES : D + (slab + 1) * LANES]
        v = qkv_ref[0, :, 2 * D + slab * LANES : 2 * D + (slab + 1) * LANES]
        outs = []
        for head in range(2):
            mine = low if head == 0 else jnp.logical_not(low)
            scores = dot_last(jnp.where(mine, q, jnp.zeros_like(q)), k)
            e = jnp.exp(scores - jnp.max(scores, axis=-1, keepdims=True))
            p = (e * (1.0 / jnp.sum(e, axis=-1, keepdims=True))).astype(BF16)
            outs.append(dot(p, v))
        a_ref[0, :, cols] = jnp.where(low, outs[0], outs[1]).astype(BF16)


def fc1_kernel(rows, place_ref, tok_ref, img_ref, a_ref, vec_ref, *refs):
    pieces = refs[: len(PIECES)]
    h1_ref, n2_ref, z_ref, slope_ref, wo_ref, w1_ref, sem_o, sem_1 = refs[len(PIECES) :]
    first = pl.program_id(0) == 0
    copies_o = piece_copies(pieces, wo_ref, sem_o, place_ref, rows)
    copies_1 = piece_copies(pieces, w1_ref, sem_1, place_ref, rows, D)

    @pl.when(first)
    def _():
        start_all(copies_o)
        start_all(copies_1)
        wait_all(copies_o)

    h1 = start_row(tok_ref, img_ref, vec_ref) + dot(a_ref[0], wo_ref[...]) + vec_ref[6:7, :]
    h1_ref[0] = h1
    normed, _ = normalize(h1)
    n2 = (normed * vec_ref[7:8, :] + vec_ref[8:9, :]).astype(BF16)
    n2_ref[0] = n2

    @pl.when(first)
    def _():
        wait_all(copies_1)

    slots = slope_ref.shape[1]
    for part in range(PARTS):
        cols = slice(part * D, (part + 1) * D)
        f = dot(n2, w1_ref[:, cols]) + vec_ref[9 + part : 10 + part, :]
        phi = 0.5 * (1.0 + lax.erf(f * INV_ROOT_TWO))
        z_ref[0, :, cols] = (f * phi).astype(BF16)
        fs = f[:slots]
        slope = phi[:slots] + fs * jnp.exp(-0.5 * fs * fs) * INV_ROOT_TWOPI
        slope_ref[0, :, cols] = slope.astype(BF16)


def spread(acc_ref, owners_ref, outs):
    if len(outs) == 1:
        outs[0][...] = acc_ref[...].astype(BF16)
        return
    keep_ref, send_ref = outs
    half, block, _ = send_ref.shape

    def one(spot, _):
        for out_ref, base in ((send_ref, half), (keep_ref, 0)):
            start = pl.multiple_of(owners_ref[OWN + base + spot] * block, 8)
            out_ref[spot] = acc_ref[pl.ds(start, block), :].astype(BF16)
        return 0

    lax.fori_loop(0, half, one, 0)


def gw2_kernel(owners_ref, z_ref, dy_ref, *refs):
    outs, (sum_ref, zt_ref, acc_ref) = refs[:-3], refs[-3:]
    pairs, slots, width = z_ref.shape

    @pl.when(pl.program_id(0) == 0)
    def _():
        zt_ref[...] = z_ref[...].reshape(pairs * slots, width).T

    dy = dy_ref[...].reshape(pairs * slots, -1)
    acc_ref[...] = dot(zt_ref[...], dy)
    sum_ref[...] = jnp.sum(dy.astype(F32), axis=0, keepdims=True)
    spread(acc_ref, owners_ref, outs)


def df_kernel(rows, place_ref, dy_ref, slope_ref, *refs):
    pieces = refs[: len(PIECES)]
    df_ref, gb1_ref, w2_ref, sems = refs[len(PIECES) :]
    step = pl.program_id(0)
    pairs, slots, width = slope_ref.shape
    total = pairs * slots
    copies = piece_copies(pieces, w2_ref, sems, place_ref, rows)

    @pl.when(step == 0)
    def _():
        start_all(copies)
        wait_all(copies)

    dz = dot_last(
        dy_ref[...].reshape(total, D), w2_ref[pl.ds(pl.multiple_of(step * width, 8), width), :]
    )
    df = dz * slope_ref[...].reshape(total, width).astype(F32)
    gb1_ref[...] = jnp.sum(df, axis=0, keepdims=True)
    df_ref[...] = df.astype(BF16)


def mlp_back_kernel(rows, place_ref, df_ref, dy_ref, h1_ref, vec_ref, *refs):
    pieces = refs[: len(PIECES)]
    dh_ref, dhr_ref, da_ref, sum_ref, w1_ref, wo_ref, sem_1, sem_o = refs[len(PIECES) :]
    first = pl.program_id(0) == 0
    copies_1 = piece_copies(pieces, w1_ref, sem_1, place_ref, rows, D)
    copies_o = piece_copies(pieces, wo_ref, sem_o, place_ref, rows)

    @pl.when(first)
    def _():
        start_all(copies_1)
        start_all(copies_o)
        sum_ref[...] = jnp.zeros_like(sum_ref)
        wait_all(copies_1)
        wait_all(copies_o)

    some, slots, _ = dy_ref.shape
    total = some * slots
    dn2 = dot_last(df_ref[...], w1_ref[...])
    normed, scale = normalize(h1_ref[...].reshape(total, D))
    dh = dy_ref[...].reshape(total, D).astype(F32) + norm_back(dn2, normed, scale, vec_ref[7:8, :])
    dh_ref[...] = dh.reshape(some, slots, D)
    sum_ref[0:1, :] += jnp.sum(dh, axis=0, keepdims=True)
    sum_ref[1:2, :] += jnp.sum(dn2 * normed, axis=0, keepdims=True)
    sum_ref[2:3, :] += jnp.sum(dn2, axis=0, keepdims=True)
    low = dh.astype(BF16)
    dhr_ref[...] = low.reshape(some, slots, D)
    da_ref[...] = dot_last(low, wo_ref[...]).astype(BF16).reshape(some, slots, D)


def gw1o_kernel(owners_ref, n2_ref, df_ref, a_ref, dhr_ref, *refs):
    outs, (n2t_ref, acc_ref) = refs[:-2], refs[-2:]
    step = pl.program_id(0)
    pairs, slots, _ = n2_ref.shape
    total = pairs * slots

    @pl.when(step == 0)
    def _():
        n2t_ref[...] = n2_ref[...].reshape(total, D).T

    @pl.when(step < PARTS)
    def _():
        acc_ref[...] = dot(n2t_ref[...], df_ref[...])

    @pl.when(step == PARTS)
    def _():
        acc_ref[...] = dot_first(a_ref[...].reshape(total, D), dhr_ref[...].reshape(total, D))

    spread(acc_ref, owners_ref, outs)


def attn_back_kernel(more, qkv_ref, da_ref, *refs):
    if more:
        _, _, before_ref, dq_ref, dkv_ref, sum_ref = refs
    else:
        dq_ref, dkv_ref, sum_ref = refs
    slots = da_ref.shape[1]

    @pl.when(pl.program_id(0) == 0)
    def _():
        sum_ref[...] = before_ref[...] if more else jnp.zeros_like(sum_ref)

    low = lax.broadcasted_iota(jnp.int32, (1, LANES), 1) < HDIM
    scale = jnp.asarray(HDIM**-0.5, BF16)
    for slab in range(SLABS):
        cols = slice(slab * LANES, (slab + 1) * LANES)
        q = qkv_ref[0, :slots, cols] * scale
        k = qkv_ref[0, :, D + slab * LANES : D + (slab + 1) * LANES]
        v = qkv_ref[0, :, 2 * D + slab * LANES : 2 * D + (slab + 1) * LANES]
        da = da_ref[0, :, cols]
        gqs, gks, gvs = [], [], []
        for head in range(2):
            mine = low if head == 0 else jnp.logical_not(low)
            zero = jnp.zeros_like(q)
            scores = dot_last(jnp.where(mine, q, zero), k)
            e = jnp.exp(scores - jnp.max(scores, axis=-1, keepdims=True))
            p = e * (1.0 / jnp.sum(e, axis=-1, keepdims=True))
            gvs.append(dot_first(p.astype(BF16), da))
            dp = dot_last(jnp.where(mine, da, zero), v)
            ds = (p * (dp - jnp.sum(p * dp, axis=-1, keepdims=True))).astype(BF16)
            gqs.append(dot(ds, k))
            gks.append(dot_first(ds, q))
        gq = jnp.where(low, gqs[0], gqs[1]) * (HDIM**-0.5)
        gk = jnp.where(low, gks[0], gks[1])
        gv = jnp.where(low, gvs[0], gvs[1])
        dq_ref[0, :, cols] = gq.astype(BF16)
        dkv_ref[0, :, cols] = gk.astype(BF16)
        dkv_ref[0, :, D + slab * LANES : D + (slab + 1) * LANES] = gv.astype(BF16)
        sum_ref[0:1, cols] += jnp.sum(gq, axis=0, keepdims=True)
        sum_ref[1:2, cols] += jnp.sum(gv, axis=0, keepdims=True)


def gqkv_kernel(owners_ref, n1_ref, dq_ref, dkv_ref, *refs):
    outs, (n1t_ref, acc_ref) = refs[:-2], refs[-2:]
    step = pl.program_id(0)
    pairs, length, _ = n1_ref.shape
    slots = dq_ref.shape[1]

    @pl.when(step == 0)
    def _():
        n1t_ref[...] = n1_ref[...].reshape(pairs * length, D).T
        total = dot(n1t_ref[:, :slots], dq_ref[0])
        for pair in range(1, pairs):
            total += dot(n1t_ref[:, pair * length : pair * length + slots], dq_ref[pair])
        acc_ref[...] = total

    @pl.when(step > 0)
    def _():
        acc_ref[...] = dot(n1t_ref[...], dkv_ref[...].reshape(pairs * length, D))

    spread(acc_ref, owners_ref, outs)


def split_two(value):
    one = value.astype(BF16)
    return one, (value - one.astype(F32)).astype(BF16)


def grad_in_kernel(
    rows,
    place_ref,
    tok_ref,
    img_ref,
    vec_ref,
    dq_ref,
    dkv_ref,
    dh_ref,
    perm_ref,
    attn_sum_ref,
    mlp_sum_ref,
    gb1_ref,
    gb2_ref,
    *refs,
):
    pieces = refs[: len(PIECES)]
    out_ref, sum_ref, w_ref, sems = refs[len(PIECES) :]
    first = pl.program_id(0) == 0
    slots = dq_ref.shape[1]
    copies = piece_copies(pieces, w_ref, sems, place_ref, rows)

    @pl.when(first)
    def _():
        start_all(copies)
        sum_ref[...] = jnp.zeros_like(sum_ref)
        sum_ref[4:6, :] = attn_sum_ref[0:2, :]
        sum_ref[6:9, :] = mlp_sum_ref[0:3, :]
        for part in range(PARTS):
            sum_ref[9 + part : 10 + part, :] = gb1_ref[:, part * D : (part + 1) * D]
        sum_ref[9 + PARTS : 10 + PARTS, :] = gb2_ref[...]
        wait_all(copies)

    dn_all = dot_last(dkv_ref[0], w_ref[:, D:])
    dn_top = dn_all[:slots] + dot_last(dq_ref[0], w_ref[:, :D])
    dn = jnp.concatenate([dn_top, dn_all[slots:]], axis=0)
    normed, scale = normalize(start_row(tok_ref, img_ref, vec_ref))
    grad = norm_back(dn, normed, scale, vec_ref[2:3, :])
    grad = jnp.concatenate([grad[:slots] + dh_ref[0], grad[slots:]], axis=0)
    image = img_ref[0][:, :1].astype(F32) > 0.5
    sum_ref[0:1, :] += jnp.sum(jnp.where(image, 0.0, grad), axis=0, keepdims=True)
    sum_ref[1:2, :] += jnp.sum(jnp.where(image, grad, 0.0), axis=0, keepdims=True)
    sum_ref[2:3, :] += jnp.sum(dn * normed, axis=0, keepdims=True)
    sum_ref[3:4, :] += jnp.sum(dn, axis=0, keepdims=True)
    one, two = split_two(grad)
    perm = perm_ref[0]
    out_ref[0] = dot(perm, one) + dot(perm, two)


def out_kernel(rows, place_ref, z_ref, h1_ref, vec_ref, perm_ref, *refs):
    pieces = refs[: len(PIECES)]
    out_ref, w_ref, sems = refs[len(PIECES) :]
    first = pl.program_id(0) == 0
    copies = piece_copies(pieces, w_ref, sems, place_ref, rows)

    @pl.when(first)
    def _():
        start_all(copies)
        wait_all(copies)

    y = h1_ref[0] + dot(z_ref[0], w_ref[...]) + vec_ref[9 + PARTS : 10 + PARTS, :]
    out_ref[0] = dot(perm_ref[0], y.astype(BF16)).astype(BF16)


def place_kernel(number, base, rows, spots_ref, one_ref, two_ref, *refs):
    step = pl.program_id(0)
    count = one_ref.shape[0]

    def put(out_ref):
        def one(spot, _):
            for source, first in ((one_ref, base), (two_ref, base + count)):
                at = pl.ds(pl.multiple_of(spots_ref[first + spot] * rows, 8), rows)
                out_ref[at, :] = source[spot, :rows].astype(F32)
            return 0

        lax.fori_loop(0, count, one, 0)

    if number == 1:
        put(refs[0])
        return
    last = pl.num_programs(0) - 1

    @pl.when(step < last)
    def _():
        put(refs[0])

    @pl.when(step == last)
    def _():
        put(refs[1])


def later(value, dep):
    return lax.optimization_barrier((value, dep))[0]


class Chain:
    def __init__(self):
        self.last, self.waiting = None, []

    def pin(self, values):
        return lax.optimization_barrier((list(values), self.last))[0]

    def hold(self, value):
        self.waiting.append(value)
        return value

    def __call__(
        self, kernel, grid, scalars, ins, outs, scratch, estimate, name, after=(), aliases=None
    ):
        deps = list(after) + self.waiting
        self.waiting = []
        if self.last is not None:
            deps.append(self.last)
        fixed = len(scalars) + len(ins)
        extra = len(deps)

        def body(*refs):
            kernel(*refs[:fixed], *refs[fixed + extra :])

        got = pl.pallas_call(
            body,
            grid_spec=pltpu.PrefetchScalarGridSpec(
                num_scalar_prefetch=len(scalars),
                grid=grid,
                in_specs=[spec for _, spec in ins] + [ANYWHERE] * extra,
                out_specs=[spec for spec, _, _ in outs],
                scratch_shapes=scratch,
            ),
            out_shape=[jax.ShapeDtypeStruct(dims, kind) for _, dims, kind in outs],
            input_output_aliases={
                len(scalars) + k: v for k, v in (aliases or {}).items()
            },
            cost_estimate=estimate,
            compiler_params=pltpu.CompilerParams(vmem_limit_bytes=KERNEL_VMEM),
            name=name,
        )(*scalars, *[value for value, _ in ins], *deps)
        self.last = got[-1]
        return got


class Sum:
    def __init__(self, plan, call, keep, send):
        self.plan, self.call = plan, call
        self.parts, self.count, self.place = [keep], keep.shape[0], 0
        self.move(send)

    def move(self, send):
        got = self.plan.exchange(send, *(order[self.place] for order in self.plan.scatter))
        self.parts.append(got)
        self.place += 1

    def total(self, low, high):
        parts = self.call.pin(self.parts)
        total = parts[0][low:high].astype(F32)
        for part in parts[1:]:
            total = total + part[low:high].astype(F32)
        return total

    def add(self):
        self.count //= 2
        total = self.total(self.count, 2 * self.count)
        self.sent = self.call.hold(total.astype(BF16))
        self.move(self.sent)


class Spread:
    def __init__(self, plan, call, block):
        self.plan, self.call, self.place = plan, call, 0
        self.move(block)

    def move(self, blocks):
        self.blocks = self.call.hold(blocks)
        self.got = self.plan.exchange(blocks, *(order[self.place] for order in self.plan.gather))
        self.place += 1

    def join(self):
        self.move(jnp.concatenate(self.call.pin([self.blocks, self.got]), axis=0))

    def put(self, base, tab, widths, rows):
        count, whole, cols = self.blocks.shape
        step = D if len(widths) > 1 or cols > D else D // 3
        last = widths[0] // step - 1
        ins = [
            (value, pl.BlockSpec((count, whole, step), lambda i, *_: (0, 0, i)))
            for value in (self.blocks, self.got)
        ]
        maps = [lambda i, *_: (0, jnp.minimum(i, last)), lambda i, *_: (0, 0)]
        return self.call(
            functools.partial(place_kernel, len(widths), base, rows),
            (cols // step,),
            [tab],
            ins,
            [
                (pl.BlockSpec((2 * count * rows, step), idx), (2 * count * rows, width), F32)
                for idx, width in zip(maps, widths)
            ],
            [],
            spent(1),
            "place",
        )


def shards(
    plan,
    tokens,
    cotangent,
    mask_pos,
    mask_count,
    w_qkv,
    m_qkv,
    v_qkv,
    w_out,
    m_out,
    v_out,
    w_fc1,
    m_fc1,
    v_fc1,
    w_fc2,
    m_fc2,
    v_fc2,
    vectors,
    m_vec,
    v_vec,
):
    pairs, length, _ = tokens.shape
    slots = mask_pos.shape[1]
    nf, nb, nd = plan.nf, plan.nb, plan.nd
    fi = lax.axis_index("fsdp").astype(jnp.int32)
    bi = lax.axis_index("batch").astype(jnp.int32)
    tab = lax.dynamic_index_in_dim(jnp.asarray(plan.table()), bi * nf + fi, 0, keepdims=False)
    place = owners = tab
    call = Chain()


    def pair_spec(rows, cols):
        return pl.BlockSpec((1, rows, cols), lambda i, *_: (i, 0, 0))

    def piece_ins(pieces):
        return [(value, pl.BlockSpec(memory_space=pltpu.HBM)) for value in pieces]

    sems = pltpu.SemaphoreType.DMA((len(PIECES),))
    rows_d, rows_f = D // nf, FF // nf

    low_vec = vectors.astype(BF16)
    vec_parts = [low_vec, plan.exchange(low_vec, 1)]
    vec_parts += [plan.exchange(part, 2) for part in vec_parts]
    columns = []
    for spot in range(nf):
        chosen = vec_parts[0]
        for mask in range(1, nf):
            chosen = jnp.where((fi ^ mask) == spot, vec_parts[mask], chosen)
        columns.append(chosen)
    vec = jnp.concatenate(columns, axis=1).astype(F32)
    vec = jnp.pad(vec, ((0, 16 - NVEC), (0, 0)))
    vec_in = (vec, full(vec.shape))

    def cast(shard_list, after=()):
        rows = shard_list[0].shape[0]
        half = rows // 2
        cols = sum(value.shape[1] for value in shard_list)
        row = lambda i, place_ref: (i ^ place_ref[1], 0)
        shard, mine = call(
            cast_kernel,
            (2,),
            [place],
            [(value, pl.BlockSpec((half, value.shape[1]), row)) for value in shard_list],
            [
                (pl.BlockSpec((half, cols), row), (rows, cols), BF16),
                (pl.BlockSpec((half, cols), lambda i, *_: (0, 0)), (half, cols), BF16),
            ],
            [],
            spent(rows * cols / 2e5),
            "cast",
            after,
        )
        return [shard, plan.exchange(shard, 1), plan.exchange(mine, 2)]

    def spread_pieces(pieces, dep=None):
        near = pieces[2]
        ready = near if dep is None else later(near, dep)
        other = plan.exchange(ready, *plan.helper)
        return pieces[:2] + [near, other, plan.exchange(ready, 1)]

    def last_piece(pieces, dep=None):
        other = pieces[3]
        return pieces + [plan.exchange(other if dep is None else later(other, dep), 1)]

    set_a = cast([w_qkv])

    perm, tokp, img, dy = call(
        order_kernel,
        (pairs,),
        [mask_count],
        [
            (mask_pos.reshape(pairs, 1, slots), pl.BlockSpec((1, 1, slots), lambda i, *_: (i, 0, 0))),
            (tokens, pair_spec(length, D)),
            (cotangent, pair_spec(length, D)),
        ],
        [
            (pair_spec(length, length), (pairs, length, length), BF16),
            (pair_spec(length, D), (pairs, length, D), BF16),
            (pair_spec(length, LANES), (pairs, length, LANES), BF16),
            (pair_spec(slots, D), (pairs, slots, D), BF16),
        ],
        [],
        spent(6),
        "order",
    )

    set_b = cast([w_out, w_fc1])
    set_a = last_piece(spread_pieces(set_a, [set_b[0]] + vec_parts))

    n1, qkv = call(
        functools.partial(qkv_kernel, rows_d),
        (pairs,),
        [place],
        [(tokp, pair_spec(length, D)), (img, pair_spec(length, LANES)), vec_in] + piece_ins(set_a),
        [
            (pair_spec(length, D), (pairs, length, D), BF16),
            (pair_spec(length, 3 * D), (pairs, length, 3 * D), BF16),
        ],
        [pltpu.VMEM((D, 3 * D), BF16), sems],
        spent(1),
        "qkv",
    )

    set_c = cast([w_fc2])
    near_b = set_b[2]
    set_b = spread_pieces(set_b, set_c[0])
    (mixed,) = call(
        mix_kernel,
        (pairs,),
        [],
        [(qkv, pair_spec(length, 3 * D))],
        [(pair_spec(length, D), (pairs, length, D), BF16)],
        [],
        spent(1),
        "mix",
        [near_b],
    )

    set_b = last_piece(set_b, mixed)
    h1, n2, z, slope = call(
        functools.partial(fc1_kernel, rows_d),
        (pairs,),
        [place],
        [
            (tokp, pair_spec(length, D)),
            (img, pair_spec(length, LANES)),
            (mixed, pair_spec(length, D)),
            vec_in,
        ]
        + piece_ins(set_b),
        [
            (pair_spec(length, D), (pairs, length, D), F32),
            (pair_spec(length, D), (pairs, length, D), BF16),
            (pair_spec(length, FF), (pairs, length, FF), BF16),
            (pair_spec(slots, FF), (pairs, slots, FF), BF16),
        ],
        [pltpu.VMEM((D, D), BF16), pltpu.VMEM((D, FF), BF16), sems, sems],
        spent(18),
        "fc1",
    )

    def top_rows(cols, idx=lambda i, *_: (0, 0, 0)):
        return pl.BlockSpec((pairs, slots, cols), idx)

    def grad_outs(rows, cols, chunk):
        block = rows // nd
        if block % 8:
            return [(pl.BlockSpec((rows, chunk), lambda i, *_: (0, i)), (rows, cols), BF16)]
        spec = pl.BlockSpec((nd // 2, block, chunk), lambda i, *_: (0, 0, i))
        return [(spec, (nd // 2, block, cols), BF16)] * 2

    def grad_sum(outs):
        if len(outs) == 1:
            rows, cols = outs[0].shape
            blocks = jnp.take(outs[0].reshape(nd, rows // nd, cols), tab[OWN : OWN + nd], axis=0)
            outs = [blocks[: nd // 2], blocks[nd // 2 :]]
        return Sum(plan, call, *outs)

    set_c = spread_pieces(set_c, n2)

    chunk = 2 * LANES
    *got, gb2 = call(
        gw2_kernel,
        (D // chunk,),
        [owners],
        [
            (z, top_rows(FF)),
            (dy, top_rows(chunk, lambda i, *_: (0, 0, i))),
        ],
        grad_outs(FF, D, chunk) + [(pl.BlockSpec((1, chunk), lambda i, *_: (0, i)), (1, D), F32)],
        [pltpu.VMEM((FF, pairs * slots), BF16), pltpu.VMEM((FF, chunk), F32)],
        spent(8),
        "gw2",
    )
    sum_2 = grad_sum(got)
    set_c = last_piece(set_c, gb2)

    df, gb1 = call(
        functools.partial(df_kernel, rows_f),
        (PARTS,),
        [place],
        [(dy, top_rows(D)), (slope, top_rows(D, lambda i, *_: (0, 0, i)))] + piece_ins(set_c),
        [
            (pl.BlockSpec((pairs * slots, D), lambda i, *_: (0, i)), (pairs * slots, FF), BF16),
            (pl.BlockSpec((1, D), lambda i, *_: (0, i)), (1, FF), F32),
        ],
        [pltpu.VMEM((FF, D), BF16), sems],
        spent(7),
        "df",
    )
    sum_2.add()

    some = 2 if pairs % 2 == 0 else 1
    some_spec = pl.BlockSpec((some, slots, D), lambda i, *_: (i, 0, 0))
    dh, dhr, da, mlp_sum = call(
        functools.partial(mlp_back_kernel, rows_d),
        (pairs // some,),
        [place],
        [
            (df, pl.BlockSpec((some * slots, FF), lambda i, *_: (i, 0))),
            (dy, some_spec),
            (h1, some_spec),
            vec_in,
        ]
        + piece_ins(set_b),
        [
            (some_spec, (pairs, slots, D), F32),
            (some_spec, (pairs, slots, D), BF16),
            (some_spec, (pairs, slots, D), BF16),
            (full((8, D)), (8, D), F32),
        ],
        [pltpu.VMEM((D, FF), BF16), pltpu.VMEM((D, D), BF16), sems, sems],
        spent(10),
        "mlp_back",
    )

    got = call(
        gw1o_kernel,
        (PARTS + 1,),
        [owners],
        [
            (n2, top_rows(D)),
            (
                df,
                pl.BlockSpec((pairs * slots, D), lambda i, *_: (0, jnp.minimum(i, PARTS - 1))),
            ),
            (mixed, top_rows(D)),
            (dhr, top_rows(D)),
        ],
        grad_outs(D, FF + D, D),
        [pltpu.VMEM((D, pairs * slots), BF16), pltpu.VMEM((D, D), F32)],
        spent(9),
        "gw1o",
    )
    sum_1 = grad_sum(got)
    sum_2.add()

    part_pairs = pairs // 2 if pairs % 2 == 0 else pairs
    back = None
    for number in range(pairs // part_pairs):
        base = number * part_pairs
        at = lambda rows, cols, base=base: pl.BlockSpec(
            (1, rows, cols), lambda i, *_: (base + i, 0, 0)
        )
        ins = [(qkv, at(length, 3 * D)), (da, at(slots, D))]
        if back is not None:
            ins += [(back[0], ANYWHERE), (back[1], ANYWHERE), (back[2], full((8, D)))]
        back = call(
            functools.partial(attn_back_kernel, back is not None),
            (part_pairs,),
            [],
            ins,
            [
                (at(slots, D), (pairs, slots, D), BF16),
                (at(length, 2 * D), (pairs, length, 2 * D), BF16),
                (full((8, D)), (8, D), F32),
            ],
            [],
            spent(12),
            "attn_back",
            aliases=None if back is None else {2: 0, 3: 1},
        )
        if number == 0:
            sum_1.add()
        sum_2.add()
    dq, dkv, attn_sum = back

    got = call(
        gqkv_kernel,
        (3,),
        [owners],
        [
            (n1, full((pairs, length, D))),
            (dq, full((pairs, slots, D))),
            (
                dkv,
                pl.BlockSpec((pairs, length, D), lambda i, *_: (0, 0, jnp.where(i == 2, 1, 0))),
            ),
        ],
        grad_outs(D, 3 * D, D),
        [pltpu.VMEM((D, pairs * length), BF16), pltpu.VMEM((D, D), F32)],
        spent(9),
        "gqkv",
    )
    sum_3 = grad_sum(got)
    sum_1.add()

    fallback = (D // nd) % 8 != 0 or (FF // nd) % 8 != 0
    places = OWN + nd
    order = tab[places + nb :]

    held = jnp.concatenate([m_vec, v_vec], axis=0).reshape(-1)
    held = jnp.pad(held, (0, -held.size % 8)).reshape(8, -1)
    riders = jnp.concatenate(split_two(held), axis=1)
    rider_cols = riders.shape[1]
    riders = jnp.pad(riders, ((0, 0), (0, D - rider_cols)))

    def finish(total, which, masters, moments, extra=None):
        _, rows, cols = total.parts[0].shape
        grad = total.total(0, 1)[0]
        start, news, made = 0, [], []
        for kind, master, (first, second) in zip(which, masters, moments):
            width = master.shape[1]
            own = lax.dynamic_slice_in_dim(master, bi * rows, rows, 0)
            new_w, new_m, new_v = adamw(
                own,
                grad[:, start : start + width],
                first,
                second,
                STEP_RATES[kind],
                DECAY_RATES[kind],
            )
            news.append(new_w.astype(BF16))
            made += [new_m, new_v]
            start += width
        block = jnp.concatenate(news, axis=1)
        if extra is not None:
            block = jnp.concatenate([block, extra], axis=0)
        return Spread(plan, call, block[None]), made

    def put(moved, widths, rows):
        if not fallback:
            return moved.put(places, tab, widths, rows)
        blocks = jnp.concatenate([moved.blocks, moved.got], axis=0)[:, :rows]
        cols = blocks.shape[2]
        blocks = jnp.take(blocks, order, axis=0).reshape(nb * rows, cols).astype(F32)
        cuts = np.cumsum([0] + list(widths))
        return [blocks[:, a:b] for a, b in zip(cuts[:-1], cuts[1:])]

    sum_3.add()

    grad_tokens, vec_sum = call(
        functools.partial(grad_in_kernel, rows_d),
        (pairs,),
        [place],
        [
            (tokp, pair_spec(length, D)),
            (img, pair_spec(length, LANES)),
            vec_in,
            (dq, pair_spec(slots, D)),
            (dkv, pair_spec(length, 2 * D)),
            (dh, pair_spec(slots, D)),
            (perm, pair_spec(length, length)),
            (attn_sum, full((8, D))),
            (mlp_sum, full((8, D))),
            (gb1, full((1, FF))),
            (gb2, full((1, D))),
        ]
        + piece_ins(set_a),
        [
            (pair_spec(length, D), (pairs, length, D), F32),
            (full((16, D)), (16, D), F32),
        ],
        [pltpu.VMEM((D, 3 * D), BF16), sems],
        spent(15),
        "grad_in",
    )

    vec_gens = [1, 2] + plan.batch
    vec_got = plan.exchange(vec_sum, vec_gens[0])

    last = plan.bbits
    sum_3.add()
    sum_1.add()
    while sum_2.count > 1:
        sum_2.add()
    moved_2, (new_m2, new_v2) = finish(sum_2, (3,), (w_fc2,), ((m_fc2, v_fc2),), riders)

    (layer_out,) = call(
        functools.partial(out_kernel, rows_f),
        (pairs,),
        [place],
        [
            (z, pair_spec(length, FF)),
            (h1, pair_spec(length, D)),
            vec_in,
            (perm, pair_spec(length, length)),
        ]
        + piece_ins(set_c),
        [(pair_spec(length, D), (pairs, length, D), BF16)],
        [pltpu.VMEM((FF, D), BF16), sems],
        spent(13),
        "out",
    )

    vec_place = 1

    def vec_step():
        nonlocal vec_sum, vec_got, vec_place
        if vec_place > len(vec_gens):
            return
        one, two = call.pin([vec_sum, vec_got])
        vec_sum = one + two
        if vec_place < len(vec_gens):
            vec_got = plan.exchange(vec_sum, vec_gens[vec_place])
        vec_place += 1

    moved_1 = moved_3 = None
    while moved_3 is None or moved_3.place < last:
        token = None
        if sum_3.count > 1:
            sum_3.add()
            token = sum_3.sent
        elif moved_3 is None:
            moved_3, (new_mq, new_vq) = finish(sum_3, (0,), (w_qkv,), ((m_qkv, v_qkv),))
            token = moved_3.blocks
        else:
            moved_3.join()
            token = moved_3.blocks
        if sum_1.count > 1:
            sum_1.add()
        elif moved_1 is None:
            moved_1, (new_m1, new_v1, new_mo, new_vo) = finish(
                sum_1, (2, 1), (w_fc1, w_out), ((m_fc1, v_fc1), (m_out, v_out))
            )
        elif moved_1.place < last:
            moved_1.join()
        if moved_2.place < last:
            moved_2.join()
        vec_step()
        call.last = token
    while len(vec_gens) >= vec_place:
        vec_step()
    while moved_1.place < last:
        moved_1.join()
    while moved_2.place < last:
        moved_2.join()
    call.waiting = []
    (new_2,) = put(moved_2, (D,), FF // nd)
    new_1, new_o = put(moved_1, (FF, D), D // nd)
    (new_q,) = put(moved_3, (3 * D,), D // nd)

    own_cols = D // nd
    got = jnp.concatenate([moved_2.blocks[:, FF // nd :], moved_2.got[:, FF // nd :]], axis=0)
    half = rider_cols // 2
    held = got[:, :, :half].astype(F32) + got[:, :, half:rider_cols].astype(F32)
    held = held.reshape(nb, -1)[:, : 2 * NVEC * own_cols].reshape(nb, 2 * NVEC, own_cols)
    held = jnp.take(held, order, axis=0)
    states = jnp.transpose(held, (1, 0, 2)).reshape(2 * NVEC, nb * own_cols)
    grad_vec = lax.dynamic_slice_in_dim(vec_sum[:NVEC], fi * nb * own_cols, nb * own_cols, 1)
    vec_new, _, _ = adamw(
        vectors, grad_vec, states[:NVEC], states[NVEC:], STEP_RATES[4], DECAY_RATES[4]
    )
    own_grad = lax.dynamic_slice_in_dim(grad_vec, bi * own_cols, own_cols, 1)
    _, new_mv, new_vv = adamw(0.0, own_grad, m_vec, v_vec, STEP_RATES[4], DECAY_RATES[4])

    return (
        layer_out,
        grad_tokens,
        new_q,
        new_mq,
        new_vq,
        new_o,
        new_mo,
        new_vo,
        new_1,
        new_m1,
        new_v1,
        new_2,
        new_m2,
        new_v2,
        vec_new,
        new_mv,
        new_vv,
    )


def solution(mesh):
    pairs = P(("batch", "fsdp"), None, None)
    weight = P("fsdp", None)
    state = P(("fsdp", "batch"), None)
    vec_state = P(None, ("fsdp", "batch"))
    matrix = (weight, state, state)
    return jax.shard_map(
        functools.partial(shards, Plan(mesh)),
        mesh=mesh,
        in_specs=(pairs, pairs, P(("batch", "fsdp"), None), P(("batch", "fsdp")))
        + matrix * 4
        + (P(None, "fsdp"), vec_state, vec_state),
        out_specs=(pairs, pairs) + matrix * 4 + (P(None, "fsdp"), vec_state, vec_state),
        check_vma=False,
    )
```

```python
import functools
import math

import jax
import jax.numpy as jnp
import numpy as np
from jax import lax
from jax.experimental import pallas as pl
from jax.experimental.pallas import tpu as pltpu
from jax.sharding import PartitionSpec as P

D = 768
HEADS = 12
HDIM = 64
FF = 3072
TEXT = 40
STEP = 3
MAXM = 128
NVEC = 14
PARTS = FF // D
LANES = 128
SLABS = D // LANES

BETA_ONE = 0.5
BETA_TWO = 0.5
EPS_ADAM = 1e-08
STEP_RATES = (0.03, 0.1, 0.03, 0.015, 0.3)
DECAY_RATES = (0.01, 0.01, 0.01, 0.01, 0.0)
INV_ROOT_TWO = 1.0 / math.sqrt(2.0)
INV_ROOT_TWOPI = 1.0 / math.sqrt(2.0 * math.pi)

KERNEL_VMEM = 20 * 2**20
FLOPS_SCALE = 3e9
BYTES_SCALE = 1e7
F32 = jnp.float32
BF16 = jnp.bfloat16


def dot(a, b):
    return lax.dot_general(a, b, (((1,), (0,)), ((), ())), preferred_element_type=F32)


def dot_first(a, b):
    return lax.dot_general(a, b, (((0,), (0,)), ((), ())), preferred_element_type=F32)


def dot_last(a, b):
    return lax.dot_general(a, b, (((1,), (1,)), ((), ())), preferred_element_type=F32)


def normalize(hidden):
    row_mean = jnp.mean(hidden, axis=-1, keepdims=True)
    centred = hidden - row_mean
    inv_scale = lax.rsqrt(jnp.mean(centred * centred, axis=-1, keepdims=True) + 1e-06)
    return centred * inv_scale, inv_scale


def norm_back(gradient, normed, inv_scale, gain_row):
    scaled = gradient * gain_row
    return inv_scale * (
        scaled
        - jnp.mean(scaled, axis=-1, keepdims=True)
        - normed * jnp.mean(scaled * normed, axis=-1, keepdims=True)
    )


def adamw(weight, gradient, moment_one, moment_two, step_rate, decay_rate):
    new_first = BETA_ONE * moment_one + (1.0 - BETA_ONE) * gradient
    new_second = BETA_TWO * moment_two + (1.0 - BETA_TWO) * gradient * gradient
    correct_one = 1.0 - BETA_ONE**STEP
    correct_two = 1.0 - BETA_TWO**STEP
    update = (
        new_first / correct_one / (jnp.sqrt(new_second / correct_two) + EPS_ADAM)
        + decay_rate * weight
    )
    return (weight - step_rate * update, new_first, new_second)


def spent(micros):
    return pl.CostEstimate(
        flops=int(micros * FLOPS_SCALE), bytes_accessed=int(micros * BYTES_SCALE), transcendentals=0
    )


def full(shape):
    zeros = (0,) * len(shape)
    return pl.BlockSpec(shape, lambda *_: zeros)


ANYWHERE = pl.BlockSpec(memory_space=pl.ANY)


class Plan:
    def __init__(self, mesh):
        self.nf = mesh.shape["fsdp"]
        self.nb = mesh.shape["batch"]
        self.nd = self.nf * self.nb
        self.fbits = self.nf.bit_length() - 1
        self.bbits = self.nb.bit_length() - 1
        assert self.nf == 1 << self.fbits and self.nb == 1 << self.bbits
        assert self.fbits == 2 and self.bbits >= 2
        near = [1, 2, 6] if self.bbits == 3 else [1 << k for k in range(self.bbits)]
        self.batch = [mask * self.nf for mask in near]
        first, second, *rest = self.batch
        self.scatter = ([1, first, second] + rest + [2], [1, second, first, 2] + rest)
        self.gather = (rest[::-1] + [second, first], rest[::-1] + [first, second])
        self.helper = (first, second)

    def exchange(self, value, even, odd=None):
        odd = even if odd is None else odd
        pairs = [(i, i ^ (odd if i & 1 else even)) for i in range(self.nd)]
        return lax.ppermute(value, ("batch", "fsdp"), pairs)

    def spans(self, gens):
        masks = np.zeros(1, np.int32)
        for mask in reversed(gens):
            masks = np.concatenate([masks, masks ^ mask])
        return masks

    def table(self):
        rows = []
        for index in range(self.nd):
            core, fi, bi = index & 1, index & (self.nf - 1), index >> self.fbits
            halves = (bi & 1, (bi >> 1) & 1)
            keep = index ^ self.spans(self.scatter[core][1:])
            send = (index ^ 1) ^ self.spans(self.scatter[1 - core][1:])
            order = np.concatenate([keep, send])
            owners = (order & (self.nf - 1)) * self.nb + (order >> self.fbits)
            places = bi ^ (self.spans(self.gather[core][::-1]) >> self.fbits)
            own = np.asarray([fi, halves[core], halves[1 - core], bi])
            rows.append(np.concatenate([own, owners, places, np.argsort(places)]))
        return np.stack(rows).astype(np.int32)


OWN = 4


PIECES = ((0, None), (1, None), (2, 0), (2, 1), (3, 2), (3, 3))


def piece_copies(refs, target, sems, place_ref, rows, start=0):
    copies = []
    cols = target.shape[1]
    for number, ((mask, kind), ref) in enumerate(zip(PIECES, refs)):
        row = (place_ref[0] ^ mask) * rows
        length = rows
        if kind is not None:
            length = rows // 2
            low = place_ref[1 + kind // 2]
            row = row + (low if kind % 2 == 0 else 1 - low) * length
        copies.append(
            pltpu.make_async_copy(
                ref.at[:, pl.ds(start, cols)],
                target.at[pl.ds(pl.multiple_of(row, 8), length)],
                sems.at[number],
            )
        )
    return copies


def start_all(copies):
    for copy in copies:
        copy.start()


def wait_all(copies):
    for copy in copies:
        copy.wait()


def cast_kernel(place_ref, *refs):
    parts, (shard_ref, mine_ref) = refs[:-2], refs[-2:]
    start = 0
    for part in parts:
        cols = slice(start, start + part.shape[1])
        low = part[...].astype(BF16)
        shard_ref[:, cols] = low

        @pl.when(pl.program_id(0) == 0)
        def _(low=low, cols=cols):
            mine_ref[:, cols] = low

        start += part.shape[1]


def order_kernel(count_ref, pos_ref, tok_ref, cot_ref, perm_ref, tokp_ref, img_ref, dy_ref):
    pair = pl.program_id(0)
    length = tok_ref.shape[1]
    slots = pos_ref.shape[2]
    token = lax.broadcasted_iota(jnp.int32, (length, slots), 0)
    slot = lax.broadcasted_iota(jnp.int32, (length, slots), 1)
    hit = jnp.where(token == pos_ref[0], 1.0, 0.0)
    free = 1.0 - jnp.sum(hit, axis=1, keepdims=True)
    below = lax.broadcasted_iota(jnp.int32, (length, length), 1) < lax.broadcasted_iota(
        jnp.int32, (length, length), 0
    )
    rank = dot(
        jnp.where(below, 1.0, 0.0).astype(BF16),
        jnp.broadcast_to(free, (length, slots)).astype(BF16),
    )
    rest = jnp.where(rank == slot.astype(F32), jnp.broadcast_to(free, (length, slots)), 0.0)
    perm = jnp.concatenate([hit, rest], axis=1).astype(BF16)
    perm_ref[0] = perm
    tokp_ref[0] = dot_first(perm, tok_ref[0]).astype(BF16)
    image = jnp.where(lax.broadcasted_iota(jnp.int32, (length, LANES), 0) >= TEXT, 1.0, 0.0)
    img_ref[0] = dot_first(perm, image.astype(BF16)).astype(BF16)
    chosen = dot_first(perm[:, :slots], cot_ref[0])
    live = lax.broadcasted_iota(jnp.int32, (slots, 1), 0) < count_ref[pair]
    dy_ref[0] = jnp.where(live, chosen, 0.0).astype(BF16)


def start_row(tok_ref, img_ref, vec_ref):
    return tok_ref[0].astype(F32) + jnp.where(
        img_ref[0][:, :1].astype(F32) > 0.5, vec_ref[1:2, :], vec_ref[0:1, :]
    )


def qkv_kernel(rows, place_ref, tok_ref, img_ref, vec_ref, *refs):
    pieces = refs[: len(PIECES)]
    n1_ref, qkv_ref, w_ref, sems = refs[len(PIECES) :]
    first = pl.program_id(0) == 0
    copies = piece_copies(pieces, w_ref, sems, place_ref, rows)

    @pl.when(first)
    def _():
        start_all(copies)

    normed, _ = normalize(start_row(tok_ref, img_ref, vec_ref))
    n1 = (normed * vec_ref[2:3, :] + vec_ref[3:4, :]).astype(BF16)
    n1_ref[0] = n1

    @pl.when(first)
    def _():
        wait_all(copies)

    qkv_ref[0, :, :D] = (dot(n1, w_ref[:, :D]) + vec_ref[4:5, :]).astype(BF16)
    qkv_ref[0, :, D : 2 * D] = dot(n1, w_ref[:, D : 2 * D]).astype(BF16)
    qkv_ref[0, :, 2 * D :] = (dot(n1, w_ref[:, 2 * D :]) + vec_ref[5:6, :]).astype(BF16)


def lane_slab(slab):
    return pl.ds(pl.multiple_of(slab * LANES, LANES), LANES)


def mix_kernel(qkv_ref, a_ref):
    low = lax.broadcasted_iota(jnp.int32, (1, LANES), 1) < HDIM

    def some_slabs(turn, _):
        for slab in [3 * turn + k for k in range(3)]:
            cols = lane_slab(slab)
            q = qkv_ref[0, :, cols] * jnp.asarray(HDIM**-0.5, BF16)
            k = qkv_ref[0, :, lane_slab(slab + SLABS)]
            v = qkv_ref[0, :, lane_slab(slab + 2 * SLABS)]
            outs = []
            for head in range(2):
                mine = low if head == 0 else jnp.logical_not(low)
                scores = dot_last(jnp.where(mine, q, jnp.zeros_like(q)), k)
                e = jnp.exp(scores - jnp.max(scores, axis=-1, keepdims=True))
                p = (e * (1.0 / jnp.sum(e, axis=-1, keepdims=True))).astype(BF16)
                outs.append(dot(p, v))
            a_ref[0, :, cols] = jnp.where(low, outs[0], outs[1]).astype(BF16)
        return 0

    lax.fori_loop(0, SLABS // 3, some_slabs, 0)


def fc1_kernel(rows, place_ref, tok_ref, img_ref, a_ref, vec_ref, *refs):
    pieces = refs[: len(PIECES)]
    h1_ref, n2_ref, z_ref, slope_ref, wo_ref, w1_ref, sem_o, sem_1 = refs[len(PIECES) :]
    first = pl.program_id(0) == 0
    copies_o = piece_copies(pieces, wo_ref, sem_o, place_ref, rows)
    copies_1 = piece_copies(pieces, w1_ref, sem_1, place_ref, rows, D)

    @pl.when(first)
    def _():
        start_all(copies_o)
        start_all(copies_1)
        wait_all(copies_o)

    h1 = start_row(tok_ref, img_ref, vec_ref) + dot(a_ref[0], wo_ref[...]) + vec_ref[6:7, :]
    h1_ref[0] = h1
    normed, _ = normalize(h1)
    n2 = (normed * vec_ref[7:8, :] + vec_ref[8:9, :]).astype(BF16)
    n2_ref[0] = n2

    @pl.when(first)
    def _():
        wait_all(copies_1)

    slots = slope_ref.shape[1]
    for part in range(PARTS):
        cols = slice(part * D, (part + 1) * D)
        f = dot(n2, w1_ref[:, cols]) + vec_ref[9 + part : 10 + part, :]
        phi = 0.5 * (1.0 + lax.erf(f * INV_ROOT_TWO))
        z_ref[0, :, cols] = (f * phi).astype(BF16)
        fs = f[:slots]
        slope = phi[:slots] + fs * jnp.exp(-0.5 * fs * fs) * INV_ROOT_TWOPI
        slope_ref[0, :, cols] = slope.astype(BF16)


def spread(acc_ref, owners_ref, outs):
    if len(outs) == 1:
        outs[0][...] = acc_ref[...].astype(BF16)
        return
    keep_ref, send_ref = outs
    half, block, _ = send_ref.shape

    def one(spot, _):
        for out_ref, base in ((send_ref, half), (keep_ref, 0)):
            start = pl.multiple_of(owners_ref[OWN + base + spot] * block, 8)
            out_ref[spot] = acc_ref[pl.ds(start, block), :].astype(BF16)
        return 0

    lax.fori_loop(0, half, one, 0)


def gw2_kernel(owners_ref, z_ref, dy_ref, *refs):
    outs, (sum_ref, zt_ref, acc_ref) = refs[:-3], refs[-3:]
    pairs, slots, width = z_ref.shape

    @pl.when(pl.program_id(0) == 0)
    def _():
        zt_ref[...] = z_ref[...].reshape(pairs * slots, width).T

    dy = dy_ref[...].reshape(pairs * slots, -1)
    acc_ref[...] = dot(zt_ref[...], dy)
    sum_ref[...] = jnp.sum(dy.astype(F32), axis=0, keepdims=True)
    spread(acc_ref, owners_ref, outs)


def df_kernel(rows, place_ref, dy_ref, slope_ref, *refs):
    pieces = refs[: len(PIECES)]
    df_ref, gb1_ref, w2_ref, sems = refs[len(PIECES) :]
    step = pl.program_id(0)
    pairs, slots, width = slope_ref.shape
    total = pairs * slots
    copies = piece_copies(pieces, w2_ref, sems, place_ref, rows)

    @pl.when(step == 0)
    def _():
        start_all(copies)
        wait_all(copies)

    dz = dot_last(
        dy_ref[...].reshape(total, D), w2_ref[pl.ds(pl.multiple_of(step * width, 8), width), :]
    )
    df = dz * slope_ref[...].reshape(total, width).astype(F32)
    gb1_ref[...] = jnp.sum(df, axis=0, keepdims=True)
    df_ref[...] = df.astype(BF16)


def mlp_back_kernel(rows, place_ref, df_ref, dy_ref, h1_ref, vec_ref, *refs):
    pieces = refs[: len(PIECES)]
    dh_ref, dhr_ref, da_ref, sum_ref, w1_ref, wo_ref, sem_1, sem_o = refs[len(PIECES) :]
    first = pl.program_id(0) == 0
    copies_1 = piece_copies(pieces, w1_ref, sem_1, place_ref, rows, D)
    copies_o = piece_copies(pieces, wo_ref, sem_o, place_ref, rows)

    @pl.when(first)
    def _():
        start_all(copies_1)
        start_all(copies_o)
        sum_ref[...] = jnp.zeros_like(sum_ref)
        wait_all(copies_1)
        wait_all(copies_o)

    some, slots, _ = dy_ref.shape
    total = some * slots
    dn2 = dot_last(df_ref[...], w1_ref[...])
    normed, scale = normalize(h1_ref[...].reshape(total, D))
    dh = dy_ref[...].reshape(total, D).astype(F32) + norm_back(dn2, normed, scale, vec_ref[7:8, :])
    dh_ref[...] = dh.reshape(some, slots, D)
    sum_ref[0:1, :] += jnp.sum(dh, axis=0, keepdims=True)
    sum_ref[1:2, :] += jnp.sum(dn2 * normed, axis=0, keepdims=True)
    sum_ref[2:3, :] += jnp.sum(dn2, axis=0, keepdims=True)
    low = dh.astype(BF16)
    dhr_ref[...] = low.reshape(some, slots, D)
    da_ref[...] = dot_last(low, wo_ref[...]).astype(BF16).reshape(some, slots, D)


def gw1o_kernel(owners_ref, n2_ref, df_ref, a_ref, dhr_ref, *refs):
    outs, (n2t_ref, acc_ref) = refs[:-2], refs[-2:]
    step = pl.program_id(0)
    pairs, slots, _ = n2_ref.shape
    total = pairs * slots

    @pl.when(step == 0)
    def _():
        n2t_ref[...] = n2_ref[...].reshape(total, D).T

    @pl.when(step < PARTS)
    def _():
        acc_ref[...] = dot(n2t_ref[...], df_ref[...])

    @pl.when(step == PARTS)
    def _():
        acc_ref[...] = dot_first(a_ref[...].reshape(total, D), dhr_ref[...].reshape(total, D))

    spread(acc_ref, owners_ref, outs)


def attn_back_kernel(more, qkv_ref, da_ref, *refs):
    if more:
        _, _, before_ref, dq_ref, dkv_ref, sum_ref = refs
    else:
        dq_ref, dkv_ref, sum_ref = refs
    slots = da_ref.shape[1]

    @pl.when(pl.program_id(0) == 0)
    def _():
        sum_ref[...] = before_ref[...] if more else jnp.zeros_like(sum_ref)

    low = lax.broadcasted_iota(jnp.int32, (1, LANES), 1) < HDIM
    scale = jnp.asarray(HDIM**-0.5, BF16)
    for slab in range(SLABS):
        cols = slice(slab * LANES, (slab + 1) * LANES)
        q = qkv_ref[0, :slots, cols] * scale
        k = qkv_ref[0, :, D + slab * LANES : D + (slab + 1) * LANES]
        v = qkv_ref[0, :, 2 * D + slab * LANES : 2 * D + (slab + 1) * LANES]
        da = da_ref[0, :, cols]
        gqs, gks, gvs = [], [], []
        for head in range(2):
            mine = low if head == 0 else jnp.logical_not(low)
            zero = jnp.zeros_like(q)
            scores = dot_last(jnp.where(mine, q, zero), k)
            e = jnp.exp(scores - jnp.max(scores, axis=-1, keepdims=True))
            p = e * (1.0 / jnp.sum(e, axis=-1, keepdims=True))
            gvs.append(dot_first(p.astype(BF16), da))
            dp = dot_last(jnp.where(mine, da, zero), v)
            ds = (p * (dp - jnp.sum(p * dp, axis=-1, keepdims=True))).astype(BF16)
            gqs.append(dot(ds, k))
            gks.append(dot_first(ds, q))
        gq = jnp.where(low, gqs[0], gqs[1]) * (HDIM**-0.5)
        gk = jnp.where(low, gks[0], gks[1])
        gv = jnp.where(low, gvs[0], gvs[1])
        dq_ref[0, :, cols] = gq.astype(BF16)
        dkv_ref[0, :, cols] = gk.astype(BF16)
        dkv_ref[0, :, D + slab * LANES : D + (slab + 1) * LANES] = gv.astype(BF16)
        sum_ref[0:1, cols] += jnp.sum(gq, axis=0, keepdims=True)
        sum_ref[1:2, cols] += jnp.sum(gv, axis=0, keepdims=True)


def gqkv_kernel(owners_ref, n1_ref, dq_ref, dkv_ref, *refs):
    outs, (n1t_ref, acc_ref) = refs[:-2], refs[-2:]
    step = pl.program_id(0)
    pairs, length, _ = n1_ref.shape
    slots = dq_ref.shape[1]

    @pl.when(step == 0)
    def _():
        n1t_ref[...] = n1_ref[...].reshape(pairs * length, D).T
        total = dot(n1t_ref[:, :slots], dq_ref[0])
        for pair in range(1, pairs):
            total += dot(n1t_ref[:, pair * length : pair * length + slots], dq_ref[pair])
        acc_ref[...] = total

    @pl.when(step > 0)
    def _():
        acc_ref[...] = dot(n1t_ref[...], dkv_ref[...].reshape(pairs * length, D))

    spread(acc_ref, owners_ref, outs)


def split_two(value):
    one = value.astype(BF16)
    return one, (value - one.astype(F32)).astype(BF16)


def grad_in_kernel(
    rows,
    place_ref,
    tok_ref,
    img_ref,
    vec_ref,
    dq_ref,
    dkv_ref,
    dh_ref,
    perm_ref,
    attn_sum_ref,
    mlp_sum_ref,
    gb1_ref,
    gb2_ref,
    *refs,
):
    pieces = refs[: len(PIECES)]
    out_ref, sum_ref, w_ref, sems = refs[len(PIECES) :]
    first = pl.program_id(0) == 0
    slots = dq_ref.shape[1]
    copies = piece_copies(pieces, w_ref, sems, place_ref, rows)

    @pl.when(first)
    def _():
        start_all(copies)
        sum_ref[...] = jnp.zeros_like(sum_ref)
        sum_ref[4:6, :] = attn_sum_ref[0:2, :]
        sum_ref[6:9, :] = mlp_sum_ref[0:3, :]
        for part in range(PARTS):
            sum_ref[9 + part : 10 + part, :] = gb1_ref[:, part * D : (part + 1) * D]
        sum_ref[9 + PARTS : 10 + PARTS, :] = gb2_ref[...]
        wait_all(copies)

    dn_all = dot_last(dkv_ref[0], w_ref[:, D:])
    dn_top = dn_all[:slots] + dot_last(dq_ref[0], w_ref[:, :D])
    dn = jnp.concatenate([dn_top, dn_all[slots:]], axis=0)
    normed, scale = normalize(start_row(tok_ref, img_ref, vec_ref))
    grad = norm_back(dn, normed, scale, vec_ref[2:3, :])
    grad = jnp.concatenate([grad[:slots] + dh_ref[0], grad[slots:]], axis=0)
    image = img_ref[0][:, :1].astype(F32) > 0.5
    sum_ref[0:1, :] += jnp.sum(jnp.where(image, 0.0, grad), axis=0, keepdims=True)
    sum_ref[1:2, :] += jnp.sum(jnp.where(image, grad, 0.0), axis=0, keepdims=True)
    sum_ref[2:3, :] += jnp.sum(dn * normed, axis=0, keepdims=True)
    sum_ref[3:4, :] += jnp.sum(dn, axis=0, keepdims=True)
    one, two = split_two(grad)
    perm = perm_ref[0]
    out_ref[0] = dot(perm, one) + dot(perm, two)


def out_kernel(rows, place_ref, z_ref, h1_ref, vec_ref, perm_ref, *refs):
    pieces = refs[: len(PIECES)]
    out_ref, w_ref, sems = refs[len(PIECES) :]
    first = pl.program_id(0) == 0
    copies = piece_copies(pieces, w_ref, sems, place_ref, rows)

    @pl.when(first)
    def _():
        start_all(copies)
        wait_all(copies)

    y = h1_ref[0] + dot(z_ref[0], w_ref[...]) + vec_ref[9 + PARTS : 10 + PARTS, :]
    out_ref[0] = dot(perm_ref[0], y.astype(BF16)).astype(BF16)


def place_kernel(number, base, rows, spots_ref, one_ref, two_ref, *refs):
    step = pl.program_id(0)
    count = one_ref.shape[0]

    def put(out_ref):
        def one(spot, _):
            for source, first in ((one_ref, base), (two_ref, base + count)):
                at = pl.ds(pl.multiple_of(spots_ref[first + spot] * rows, 8), rows)
                out_ref[at, :] = source[spot, :rows].astype(F32)
            return 0

        lax.fori_loop(0, count, one, 0)

    if number == 1:
        put(refs[0])
        return
    last = pl.num_programs(0) - 1

    @pl.when(step < last)
    def _():
        put(refs[0])

    @pl.when(step == last)
    def _():
        put(refs[1])


def later(value, dep):
    return lax.optimization_barrier((value, dep))[0]


class Chain:
    def __init__(self):
        self.last, self.waiting = None, []

    def pin(self, values):
        return lax.optimization_barrier((list(values), self.last))[0]

    def hold(self, value):
        self.waiting.append(value)
        return value

    def __call__(
        self, kernel, grid, scalars, ins, outs, scratch, estimate, name, after=(), aliases=None
    ):
        deps = list(after) + self.waiting
        self.waiting = []
        if self.last is not None:
            deps.append(self.last)
        fixed = len(scalars) + len(ins)
        extra = len(deps)

        def body(*refs):
            kernel(*refs[:fixed], *refs[fixed + extra :])

        got = pl.pallas_call(
            body,
            grid_spec=pltpu.PrefetchScalarGridSpec(
                num_scalar_prefetch=len(scalars),
                grid=grid,
                in_specs=[spec for _, spec in ins] + [ANYWHERE] * extra,
                out_specs=[spec for spec, _, _ in outs],
                scratch_shapes=scratch,
            ),
            out_shape=[jax.ShapeDtypeStruct(dims, kind) for _, dims, kind in outs],
            input_output_aliases={
                len(scalars) + k: v for k, v in (aliases or {}).items()
            },
            cost_estimate=estimate,
            compiler_params=pltpu.CompilerParams(vmem_limit_bytes=KERNEL_VMEM),
            name=name,
        )(*scalars, *[value for value, _ in ins], *deps)
        self.last = got[-1]
        return got


class Sum:
    def __init__(self, plan, call, keep, send):
        self.plan, self.call = plan, call
        self.parts, self.count, self.place = [keep], keep.shape[0], 0
        self.move(send)

    def move(self, send):
        got = self.plan.exchange(send, *(order[self.place] for order in self.plan.scatter))
        self.parts.append(got)
        self.place += 1

    def total(self, low, high):
        parts = self.call.pin(self.parts)
        total = parts[0][low:high].astype(F32)
        for part in parts[1:]:
            total = total + part[low:high].astype(F32)
        return total

    def add(self):
        self.count //= 2
        total = self.total(self.count, 2 * self.count)
        self.sent = self.call.hold(total.astype(BF16))
        self.move(self.sent)


class Spread:
    def __init__(self, plan, call, block):
        self.plan, self.call, self.place = plan, call, 0
        self.move(block)

    def move(self, blocks):
        self.blocks = self.call.hold(blocks)
        self.got = self.plan.exchange(blocks, *(order[self.place] for order in self.plan.gather))
        self.place += 1

    def join(self):
        self.move(jnp.concatenate(self.call.pin([self.blocks, self.got]), axis=0))

    def put(self, base, tab, widths, rows):
        count, whole, cols = self.blocks.shape
        step = D if len(widths) > 1 or cols > D else D // 3
        last = widths[0] // step - 1
        ins = [
            (value, pl.BlockSpec((count, whole, step), lambda i, *_: (0, 0, i)))
            for value in (self.blocks, self.got)
        ]
        maps = [lambda i, *_: (0, jnp.minimum(i, last)), lambda i, *_: (0, 0)]
        return self.call(
            functools.partial(place_kernel, len(widths), base, rows),
            (cols // step,),
            [tab],
            ins,
            [
                (pl.BlockSpec((2 * count * rows, step), idx), (2 * count * rows, width), F32)
                for idx, width in zip(maps, widths)
            ],
            [],
            spent(1),
            "place",
        )


def shards(
    plan,
    tokens,
    cotangent,
    mask_pos,
    mask_count,
    w_qkv,
    m_qkv,
    v_qkv,
    w_out,
    m_out,
    v_out,
    w_fc1,
    m_fc1,
    v_fc1,
    w_fc2,
    m_fc2,
    v_fc2,
    vectors,
    m_vec,
    v_vec,
):
    pairs, length, _ = tokens.shape
    slots = mask_pos.shape[1]
    nf, nb, nd = plan.nf, plan.nb, plan.nd
    fi = lax.axis_index("fsdp").astype(jnp.int32)
    bi = lax.axis_index("batch").astype(jnp.int32)
    tab = lax.dynamic_index_in_dim(jnp.asarray(plan.table()), bi * nf + fi, 0, keepdims=False)
    place = owners = tab
    call = Chain()


    def pair_spec(rows, cols):
        return pl.BlockSpec((1, rows, cols), lambda i, *_: (i, 0, 0))

    def piece_ins(pieces):
        return [(value, pl.BlockSpec(memory_space=pltpu.HBM)) for value in pieces]

    sems = pltpu.SemaphoreType.DMA((len(PIECES),))
    rows_d, rows_f = D // nf, FF // nf

    low_vec = vectors.astype(BF16)
    vec_far = plan.exchange(low_vec, 2)
    vec_parts = [low_vec, plan.exchange(low_vec, 1), vec_far, plan.exchange(vec_far, 1)]
    columns = []
    for spot in range(nf):
        chosen = vec_parts[0]
        for mask in range(1, nf):
            chosen = jnp.where((fi ^ mask) == spot, vec_parts[mask], chosen)
        columns.append(chosen)
    vec = jnp.concatenate(columns, axis=1).astype(F32)
    vec = jnp.pad(vec, ((0, 16 - NVEC), (0, 0)))
    vec_in = (vec, full(vec.shape))

    def cast(shard_list, after=()):
        rows = shard_list[0].shape[0]
        half = rows // 2
        cols = sum(value.shape[1] for value in shard_list)
        row = lambda i, place_ref: (i ^ place_ref[1], 0)
        shard, mine = call(
            cast_kernel,
            (2,),
            [place],
            [(value, pl.BlockSpec((half, value.shape[1]), row)) for value in shard_list],
            [
                (pl.BlockSpec((half, cols), row), (rows, cols), BF16),
                (pl.BlockSpec((half, cols), lambda i, *_: (0, 0)), (half, cols), BF16),
            ],
            [],
            spent(0.1),
            "cast",
            after,
        )
        return [shard, plan.exchange(shard, 1), plan.exchange(mine, 2)]

    def spread_pieces(pieces, dep=None):
        near = pieces[2]
        ready = near if dep is None else later(near, dep)
        other = plan.exchange(ready, *plan.helper)
        return pieces[:2] + [near, other, plan.exchange(ready, 1)]

    def last_piece(pieces, dep=None):
        other = pieces[3]
        return pieces + [plan.exchange(other if dep is None else later(other, dep), 1)]

    set_a = cast([w_qkv])

    perm, tokp, img, dy = call(
        order_kernel,
        (pairs,),
        [mask_count],
        [
            (mask_pos.reshape(pairs, 1, slots), pl.BlockSpec((1, 1, slots), lambda i, *_: (i, 0, 0))),
            (tokens, pair_spec(length, D)),
            (cotangent, pair_spec(length, D)),
        ],
        [
            (pair_spec(length, length), (pairs, length, length), BF16),
            (pair_spec(length, D), (pairs, length, D), BF16),
            (pair_spec(length, LANES), (pairs, length, LANES), BF16),
            (pair_spec(slots, D), (pairs, slots, D), BF16),
        ],
        [],
        spent(6),
        "order",
    )

    set_b = cast([w_out, w_fc1])
    set_a = last_piece(spread_pieces(set_a, [set_b[0]] + vec_parts))

    n1, qkv = call(
        functools.partial(qkv_kernel, rows_d),
        (pairs,),
        [place],
        [(tokp, pair_spec(length, D)), (img, pair_spec(length, LANES)), vec_in] + piece_ins(set_a),
        [
            (pair_spec(length, D), (pairs, length, D), BF16),
            (pair_spec(length, 3 * D), (pairs, length, 3 * D), BF16),
        ],
        [pltpu.VMEM((D, 3 * D), BF16), sems],
        spent(0.1),
        "qkv",
    )

    set_c = cast([w_fc2])
    near_b = set_b[2]
    set_b = spread_pieces(set_b, set_c[0])
    (mixed,) = call(
        mix_kernel,
        (pairs,),
        [],
        [(qkv, pair_spec(length, 3 * D))],
        [(pair_spec(length, D), (pairs, length, D), BF16)],
        [],
        spent(1),
        "mix",
        [near_b],
    )

    set_b = last_piece(set_b, mixed)
    h1, n2, z, slope = call(
        functools.partial(fc1_kernel, rows_d),
        (pairs,),
        [place],
        [
            (tokp, pair_spec(length, D)),
            (img, pair_spec(length, LANES)),
            (mixed, pair_spec(length, D)),
            vec_in,
        ]
        + piece_ins(set_b),
        [
            (pair_spec(length, D), (pairs, length, D), F32),
            (pair_spec(length, D), (pairs, length, D), BF16),
            (pair_spec(length, FF), (pairs, length, FF), BF16),
            (pair_spec(slots, FF), (pairs, slots, FF), BF16),
        ],
        [pltpu.VMEM((D, D), BF16), pltpu.VMEM((D, FF), BF16), sems, sems],
        spent(18),
        "fc1",
    )

    def top_rows(cols, idx=lambda i, *_: (0, 0, 0)):
        return pl.BlockSpec((pairs, slots, cols), idx)

    def grad_outs(rows, cols, chunk):
        block = rows // nd
        if block % 8:
            return [(pl.BlockSpec((rows, chunk), lambda i, *_: (0, i)), (rows, cols), BF16)]
        spec = pl.BlockSpec((nd // 2, block, chunk), lambda i, *_: (0, 0, i))
        return [(spec, (nd // 2, block, cols), BF16)] * 2

    def grad_sum(outs):
        if len(outs) == 1:
            rows, cols = outs[0].shape
            blocks = jnp.take(outs[0].reshape(nd, rows // nd, cols), tab[OWN : OWN + nd], axis=0)
            outs = [blocks[: nd // 2], blocks[nd // 2 :]]
        return Sum(plan, call, *outs)

    set_c = spread_pieces(set_c, n2)

    chunk = 2 * LANES
    *got, gb2 = call(
        gw2_kernel,
        (D // chunk,),
        [owners],
        [
            (z, top_rows(FF)),
            (dy, top_rows(chunk, lambda i, *_: (0, 0, i))),
        ],
        grad_outs(FF, D, chunk) + [(pl.BlockSpec((1, chunk), lambda i, *_: (0, i)), (1, D), F32)],
        [pltpu.VMEM((FF, pairs * slots), BF16), pltpu.VMEM((FF, chunk), F32)],
        spent(8),
        "gw2",
    )
    sum_2 = grad_sum(got)
    set_c = last_piece(set_c, gb2)

    df, gb1 = call(
        functools.partial(df_kernel, rows_f),
        (PARTS,),
        [place],
        [(dy, top_rows(D)), (slope, top_rows(D, lambda i, *_: (0, 0, i)))] + piece_ins(set_c),
        [
            (pl.BlockSpec((pairs * slots, D), lambda i, *_: (0, i)), (pairs * slots, FF), BF16),
            (pl.BlockSpec((1, D), lambda i, *_: (0, i)), (1, FF), F32),
        ],
        [pltpu.VMEM((FF, D), BF16), sems],
        spent(7),
        "df",
    )
    sum_2.add()

    some = 2 if pairs % 2 == 0 else 1
    some_spec = pl.BlockSpec((some, slots, D), lambda i, *_: (i, 0, 0))
    dh, dhr, da, mlp_sum = call(
        functools.partial(mlp_back_kernel, rows_d),
        (pairs // some,),
        [place],
        [
            (df, pl.BlockSpec((some * slots, FF), lambda i, *_: (i, 0))),
            (dy, some_spec),
            (h1, some_spec),
            vec_in,
        ]
        + piece_ins(set_b),
        [
            (some_spec, (pairs, slots, D), F32),
            (some_spec, (pairs, slots, D), BF16),
            (some_spec, (pairs, slots, D), BF16),
            (full((8, D)), (8, D), F32),
        ],
        [pltpu.VMEM((D, FF), BF16), pltpu.VMEM((D, D), BF16), sems, sems],
        spent(10),
        "mlp_back",
    )

    got = call(
        gw1o_kernel,
        (PARTS + 1,),
        [owners],
        [
            (n2, top_rows(D)),
            (
                df,
                pl.BlockSpec((pairs * slots, D), lambda i, *_: (0, jnp.minimum(i, PARTS - 1))),
            ),
            (mixed, top_rows(D)),
            (dhr, top_rows(D)),
        ],
        grad_outs(D, FF + D, D),
        [pltpu.VMEM((D, pairs * slots), BF16), pltpu.VMEM((D, D), F32)],
        spent(9),
        "gw1o",
    )
    sum_1 = grad_sum(got)
    sum_2.add()

    part_pairs = pairs // 2 if pairs % 2 == 0 else pairs
    back = None
    for number in range(pairs // part_pairs):
        base = number * part_pairs
        at = lambda rows, cols, base=base: pl.BlockSpec(
            (1, rows, cols), lambda i, *_: (base + i, 0, 0)
        )
        ins = [(qkv, at(length, 3 * D)), (da, at(slots, D))]
        if back is not None:
            ins += [(back[0], ANYWHERE), (back[1], ANYWHERE), (back[2], full((8, D)))]
        back = call(
            functools.partial(attn_back_kernel, back is not None),
            (part_pairs,),
            [],
            ins,
            [
                (at(slots, D), (pairs, slots, D), BF16),
                (at(length, 2 * D), (pairs, length, 2 * D), BF16),
                (full((8, D)), (8, D), F32),
            ],
            [],
            spent(12),
            "attn_back",
            aliases=None if back is None else {2: 0, 3: 1},
        )
        if number == 0:
            sum_1.add()
        sum_2.add()
    dq, dkv, attn_sum = back

    got = call(
        gqkv_kernel,
        (3,),
        [owners],
        [
            (n1, full((pairs, length, D))),
            (dq, full((pairs, slots, D))),
            (
                dkv,
                pl.BlockSpec((pairs, length, D), lambda i, *_: (0, 0, jnp.where(i == 2, 1, 0))),
            ),
        ],
        grad_outs(D, 3 * D, D),
        [pltpu.VMEM((D, pairs * length), BF16), pltpu.VMEM((D, D), F32)],
        spent(9),
        "gqkv",
    )
    sum_3 = grad_sum(got)
    sum_1.add()

    fallback = (D // nd) % 8 != 0 or (FF // nd) % 8 != 0
    places = OWN + nd
    order = tab[places + nb :]

    held = jnp.concatenate([m_vec, v_vec], axis=0).reshape(-1)
    held = jnp.pad(held, (0, -held.size % 8)).reshape(8, -1)
    riders = jnp.concatenate(split_two(held), axis=1)
    rider_cols = riders.shape[1]
    riders = jnp.pad(riders, ((0, 0), (0, D - rider_cols)))

    def finish(total, which, masters, moments, extra=None):
        _, rows, cols = total.parts[0].shape
        grad = total.total(0, 1)[0]
        start, news, made = 0, [], []
        for kind, master, (first, second) in zip(which, masters, moments):
            width = master.shape[1]
            own = lax.dynamic_slice_in_dim(master, bi * rows, rows, 0)
            new_w, new_m, new_v = adamw(
                own,
                grad[:, start : start + width],
                first,
                second,
                STEP_RATES[kind],
                DECAY_RATES[kind],
            )
            news.append(new_w.astype(BF16))
            made += [new_m, new_v]
            start += width
        block = jnp.concatenate(news, axis=1)
        if extra is not None:
            block = jnp.concatenate([block, extra], axis=0)
        return Spread(plan, call, block[None]), made

    def put(moved, widths, rows):
        if not fallback:
            return moved.put(places, tab, widths, rows)
        blocks = jnp.concatenate([moved.blocks, moved.got], axis=0)[:, :rows]
        cols = blocks.shape[2]
        blocks = jnp.take(blocks, order, axis=0).reshape(nb * rows, cols).astype(F32)
        cuts = np.cumsum([0] + list(widths))
        return [blocks[:, a:b] for a, b in zip(cuts[:-1], cuts[1:])]

    sum_3.add()

    paced, call.last = call.last, sum_3.sent
    moved_2, (new_m2, new_v2) = finish(sum_2, (3,), (w_fc2,), ((m_fc2, v_fc2),), riders)
    call.last = paced

    grad_tokens, vec_sum = call(
        functools.partial(grad_in_kernel, rows_d),
        (pairs,),
        [place],
        [
            (tokp, pair_spec(length, D)),
            (img, pair_spec(length, LANES)),
            vec_in,
            (dq, pair_spec(slots, D)),
            (dkv, pair_spec(length, 2 * D)),
            (dh, pair_spec(slots, D)),
            (perm, pair_spec(length, length)),
            (attn_sum, full((8, D))),
            (mlp_sum, full((8, D))),
            (gb1, full((1, FF))),
            (gb2, full((1, D))),
        ]
        + piece_ins(set_a),
        [
            (pair_spec(length, D), (pairs, length, D), F32),
            (full((16, D)), (16, D), F32),
        ],
        [pltpu.VMEM((D, 3 * D), BF16), sems],
        spent(15),
        "grad_in",
    )

    vec_gens = [1] + plan.batch[1:] + plan.batch[:1] + [2]
    vec_got = plan.exchange(vec_sum, vec_gens[0])

    vec_place = 1

    def vec_step():
        nonlocal vec_sum, vec_got, vec_place
        if vec_place > len(vec_gens):
            return
        one, two = call.pin([vec_sum, vec_got])
        vec_sum = one + two
        if vec_place < len(vec_gens):
            vec_got = plan.exchange(vec_sum, vec_gens[vec_place])
        vec_place += 1

    last = plan.bbits
    sum_3.add()
    sum_1.add()
    moved_2.join()

    (layer_out,) = call(
        functools.partial(out_kernel, rows_f),
        (pairs,),
        [place],
        [
            (z, pair_spec(length, FF)),
            (h1, pair_spec(length, D)),
            vec_in,
            (perm, pair_spec(length, length)),
        ]
        + piece_ins(set_c),
        [(pair_spec(length, D), (pairs, length, D), BF16)],
        [pltpu.VMEM((FF, D), BF16), sems],
        spent(13),
        "out",
    )

    moved_1 = moved_3 = None
    while moved_3 is None or moved_3.place < last:
        token = None
        if sum_3.count > 1:
            sum_3.add()
            token = sum_3.sent
        elif moved_3 is None:
            moved_3, (new_mq, new_vq) = finish(sum_3, (0,), (w_qkv,), ((m_qkv, v_qkv),))
            token = moved_3.blocks
        else:
            moved_3.join()
            token = moved_3.blocks
        if sum_1.count > 1:
            sum_1.add()
        elif moved_1 is None:
            moved_1, (new_m1, new_v1, new_mo, new_vo) = finish(
                sum_1, (2, 1), (w_fc1, w_out), ((m_fc1, v_fc1), (m_out, v_out))
            )
        elif moved_1.place < last:
            moved_1.join()
        if moved_2.place < last:
            moved_2.join()
        vec_step()
        call.last = token
    while len(vec_gens) >= vec_place:
        vec_step()
    while moved_1.place < last:
        moved_1.join()
    while moved_2.place < last:
        moved_2.join()
    call.waiting = []
    tail = call.pin([moved_2.blocks, moved_2.got])
    (new_2,) = put(moved_2, (D,), FF // nd)
    new_1, new_o = put(moved_1, (FF, D), D // nd)
    (new_q,) = put(moved_3, (3 * D,), D // nd)

    own_cols = D // nd
    got = jnp.concatenate([part[:, FF // nd :] for part in tail], axis=0)
    half = rider_cols // 2
    held = got[:, :, :half].astype(F32) + got[:, :, half:rider_cols].astype(F32)
    held = held.reshape(nb, -1)[:, : 2 * NVEC * own_cols].reshape(nb, 2 * NVEC, own_cols)
    held = jnp.take(held, order, axis=0)
    states = jnp.transpose(held, (1, 0, 2)).reshape(2 * NVEC, nb * own_cols)
    grad_vec = lax.dynamic_slice_in_dim(vec_sum[:NVEC], fi * nb * own_cols, nb * own_cols, 1)
    vec_new, _, _ = adamw(
        vectors, grad_vec, states[:NVEC], states[NVEC:], STEP_RATES[4], DECAY_RATES[4]
    )
    own_grad = lax.dynamic_slice_in_dim(grad_vec, bi * own_cols, own_cols, 1)
    _, new_mv, new_vv = adamw(0.0, own_grad, m_vec, v_vec, STEP_RATES[4], DECAY_RATES[4])

    return (
        layer_out,
        grad_tokens,
        new_q,
        new_mq,
        new_vq,
        new_o,
        new_mo,
        new_vo,
        new_1,
        new_m1,
        new_v1,
        new_2,
        new_m2,
        new_v2,
        vec_new,
        new_mv,
        new_vv,
    )


def solution(mesh):
    pairs = P(("batch", "fsdp"), None, None)
    weight = P("fsdp", None)
    state = P(("fsdp", "batch"), None)
    vec_state = P(None, ("fsdp", "batch"))
    matrix = (weight, state, state)
    return jax.shard_map(
        functools.partial(shards, Plan(mesh)),
        mesh=mesh,
        in_specs=(pairs, pairs, P(("batch", "fsdp"), None), P(("batch", "fsdp")))
        + matrix * 4
        + (P(None, "fsdp"), vec_state, vec_state),
        out_specs=(pairs, pairs) + matrix * 4 + (P(None, "fsdp"), vec_state, vec_state),
        check_vma=False,
    )
```

```python
import functools
import math

import jax
import jax.numpy as jnp
import numpy as np
from jax import lax
from jax.experimental import pallas as pl
from jax.experimental.pallas import tpu as pltpu
from jax.sharding import PartitionSpec as P

D = 768
HEADS = 12
HDIM = 64
FF = 3072
TEXT = 40
STEP = 3
MAXM = 128
NVEC = 14
PARTS = FF // D
LANES = 128
SLABS = D // LANES

BETA_ONE = 0.5
BETA_TWO = 0.5
EPS_ADAM = 1e-08
STEP_RATES = (0.03, 0.1, 0.03, 0.015, 0.3)
DECAY_RATES = (0.01, 0.01, 0.01, 0.01, 0.0)
INV_ROOT_TWO = 1.0 / math.sqrt(2.0)
INV_ROOT_TWOPI = 1.0 / math.sqrt(2.0 * math.pi)

KERNEL_VMEM = 20 * 2**20
FLOPS_SCALE = 3e9
BYTES_SCALE = 1e7
F32 = jnp.float32
BF16 = jnp.bfloat16


def dot(a, b):
    return lax.dot_general(a, b, (((1,), (0,)), ((), ())), preferred_element_type=F32)


def dot_first(a, b):
    return lax.dot_general(a, b, (((0,), (0,)), ((), ())), preferred_element_type=F32)


def dot_last(a, b):
    return lax.dot_general(a, b, (((1,), (1,)), ((), ())), preferred_element_type=F32)


def normalize(hidden):
    row_mean = jnp.mean(hidden, axis=-1, keepdims=True)
    centred = hidden - row_mean
    inv_scale = lax.rsqrt(jnp.mean(centred * centred, axis=-1, keepdims=True) + 1e-06)
    return centred * inv_scale, inv_scale


def norm_back(gradient, normed, inv_scale, gain_row):
    scaled = gradient * gain_row
    return inv_scale * (
        scaled
        - jnp.mean(scaled, axis=-1, keepdims=True)
        - normed * jnp.mean(scaled * normed, axis=-1, keepdims=True)
    )


def adamw(weight, gradient, moment_one, moment_two, step_rate, decay_rate):
    new_first = BETA_ONE * moment_one + (1.0 - BETA_ONE) * gradient
    new_second = BETA_TWO * moment_two + (1.0 - BETA_TWO) * gradient * gradient
    correct_one = 1.0 - BETA_ONE**STEP
    correct_two = 1.0 - BETA_TWO**STEP
    update = (
        new_first / correct_one / (jnp.sqrt(new_second / correct_two) + EPS_ADAM)
        + decay_rate * weight
    )
    return (weight - step_rate * update, new_first, new_second)


def spent(micros):
    return pl.CostEstimate(
        flops=int(micros * FLOPS_SCALE), bytes_accessed=int(micros * BYTES_SCALE), transcendentals=0
    )


def full(shape):
    zeros = (0,) * len(shape)
    return pl.BlockSpec(shape, lambda *_: zeros)


ANYWHERE = pl.BlockSpec(memory_space=pl.ANY)


class Plan:
    def __init__(self, mesh):
        self.nf = mesh.shape["fsdp"]
        self.nb = mesh.shape["batch"]
        self.nd = self.nf * self.nb
        self.fbits = self.nf.bit_length() - 1
        self.bbits = self.nb.bit_length() - 1
        assert self.nf == 1 << self.fbits and self.nb == 1 << self.bbits
        assert self.fbits == 2 and self.bbits >= 2
        near = [1, 2, 6] if self.bbits == 3 else [1 << k for k in range(self.bbits)]
        self.batch = [mask * self.nf for mask in near]
        first, second, *rest = self.batch
        self.scatter = ([1, first, second] + rest + [2], [1, second, first, 2] + rest)
        self.gather = (rest[::-1] + [second, first], rest[::-1] + [first, second])
        self.helper = (first, second)

    def exchange(self, value, even, odd=None):
        odd = even if odd is None else odd
        pairs = [(i, i ^ (odd if i & 1 else even)) for i in range(self.nd)]
        return lax.ppermute(value, ("batch", "fsdp"), pairs)

    def spans(self, gens):
        masks = np.zeros(1, np.int32)
        for mask in reversed(gens):
            masks = np.concatenate([masks, masks ^ mask])
        return masks

    def table(self):
        rows = []
        for index in range(self.nd):
            core, fi, bi = index & 1, index & (self.nf - 1), index >> self.fbits
            halves = (bi & 1, (bi >> 1) & 1)
            keep = index ^ self.spans(self.scatter[core][1:])
            send = (index ^ 1) ^ self.spans(self.scatter[1 - core][1:])
            order = np.concatenate([keep, send])
            owners = (order & (self.nf - 1)) * self.nb + (order >> self.fbits)
            places = bi ^ (self.spans(self.gather[core][::-1]) >> self.fbits)
            own = np.asarray([fi, halves[core], halves[1 - core], bi])
            rows.append(np.concatenate([own, owners, places, np.argsort(places)]))
        return np.stack(rows).astype(np.int32)


OWN = 4


PIECES = ((0, None), (1, None), (2, 0), (2, 1), (3, 2), (3, 3))


def piece_copies(refs, target, sems, place_ref, rows, start=0):
    copies = []
    cols = target.shape[1]
    for number, ((mask, kind), ref) in enumerate(zip(PIECES, refs)):
        row = (place_ref[0] ^ mask) * rows
        length = rows
        if kind is not None:
            length = rows // 2
            low = place_ref[1 + kind // 2]
            row = row + (low if kind % 2 == 0 else 1 - low) * length
        copies.append(
            pltpu.make_async_copy(
                ref.at[:, pl.ds(start, cols)],
                target.at[pl.ds(pl.multiple_of(row, 8), length)],
                sems.at[number],
            )
        )
    return copies


def start_all(copies):
    for copy in copies:
        copy.start()


def wait_all(copies):
    for copy in copies:
        copy.wait()


def cast_kernel(place_ref, *refs):
    parts, (shard_ref, mine_ref) = refs[:-2], refs[-2:]
    start = 0
    for part in parts:
        cols = slice(start, start + part.shape[1])
        low = part[...].astype(BF16)
        shard_ref[:, cols] = low

        @pl.when(pl.program_id(0) == 0)
        def _(low=low, cols=cols):
            mine_ref[:, cols] = low

        start += part.shape[1]


def order_kernel(count_ref, pos_ref, tok_ref, cot_ref, perm_ref, tokp_ref, img_ref, dy_ref):
    pair = pl.program_id(0)
    length = tok_ref.shape[1]
    slots = pos_ref.shape[2]
    token = lax.broadcasted_iota(jnp.int32, (length, slots), 0)
    slot = lax.broadcasted_iota(jnp.int32, (length, slots), 1)
    hit = jnp.where(token == pos_ref[0], 1.0, 0.0)
    free = 1.0 - jnp.sum(hit, axis=1, keepdims=True)
    below = lax.broadcasted_iota(jnp.int32, (length, length), 1) < lax.broadcasted_iota(
        jnp.int32, (length, length), 0
    )
    rank = dot(
        jnp.where(below, 1.0, 0.0).astype(BF16),
        jnp.broadcast_to(free, (length, slots)).astype(BF16),
    )
    rest = jnp.where(rank == slot.astype(F32), jnp.broadcast_to(free, (length, slots)), 0.0)
    perm = jnp.concatenate([hit, rest], axis=1).astype(BF16)
    perm_ref[0] = perm
    tokp_ref[0] = dot_first(perm, tok_ref[0]).astype(BF16)
    image = jnp.where(lax.broadcasted_iota(jnp.int32, (length, LANES), 0) >= TEXT, 1.0, 0.0)
    img_ref[0] = dot_first(perm, image.astype(BF16)).astype(BF16)
    chosen = dot_first(perm[:, :slots], cot_ref[0])
    live = lax.broadcasted_iota(jnp.int32, (slots, 1), 0) < count_ref[pair]
    dy_ref[0] = jnp.where(live, chosen, 0.0).astype(BF16)


def start_row(tok_ref, img_ref, vec_ref):
    return tok_ref[0].astype(F32) + jnp.where(
        img_ref[0][:, :1].astype(F32) > 0.5, vec_ref[1:2, :], vec_ref[0:1, :]
    )


def qkv_kernel(rows, place_ref, tok_ref, img_ref, vec_ref, *refs):
    pieces = refs[: len(PIECES)]
    n1_ref, qkv_ref, w_ref, sems = refs[len(PIECES) :]
    first = pl.program_id(0) == 0
    copies = piece_copies(pieces, w_ref, sems, place_ref, rows)

    @pl.when(first)
    def _():
        start_all(copies)

    normed, _ = normalize(start_row(tok_ref, img_ref, vec_ref))
    n1 = (normed * vec_ref[2:3, :] + vec_ref[3:4, :]).astype(BF16)
    n1_ref[0] = n1

    @pl.when(first)
    def _():
        wait_all(copies)

    qkv_ref[0, :, :D] = (dot(n1, w_ref[:, :D]) + vec_ref[4:5, :]).astype(BF16)
    qkv_ref[0, :, D : 2 * D] = dot(n1, w_ref[:, D : 2 * D]).astype(BF16)
    qkv_ref[0, :, 2 * D :] = (dot(n1, w_ref[:, 2 * D :]) + vec_ref[5:6, :]).astype(BF16)


def mix_kernel(qkv_ref, a_ref):
    low = lax.broadcasted_iota(jnp.int32, (1, LANES), 1) < HDIM
    for slab in range(SLABS):
        cols = slice(slab * LANES, (slab + 1) * LANES)
        q = qkv_ref[0, :, cols] * jnp.asarray(HDIM**-0.5, BF16)
        k = qkv_ref[0, :, D + slab * LANES : D + (slab + 1) * LANES]
        v = qkv_ref[0, :, 2 * D + slab * LANES : 2 * D + (slab + 1) * LANES]
        outs = []
        for head in range(2):
            mine = low if head == 0 else jnp.logical_not(low)
            scores = dot_last(jnp.where(mine, q, jnp.zeros_like(q)), k)
            e = jnp.exp(scores - jnp.max(scores, axis=-1, keepdims=True))
            inverse = 1.0 / jnp.sum(e, axis=-1, keepdims=True)
            outs.append(dot(e.astype(BF16), v) * inverse)
        a_ref[0, :, cols] = jnp.where(low, outs[0], outs[1]).astype(BF16)


def fc1_kernel(rows, place_ref, tok_ref, img_ref, a_ref, vec_ref, *refs):
    pieces = refs[: len(PIECES)]
    h1_ref, n2_ref, z_ref, slope_ref, wo_ref, w1_ref, sem_o, sem_1 = refs[len(PIECES) :]
    first = pl.program_id(0) == 0
    copies_o = piece_copies(pieces, wo_ref, sem_o, place_ref, rows)
    copies_1 = piece_copies(pieces, w1_ref, sem_1, place_ref, rows, D)

    @pl.when(first)
    def _():
        start_all(copies_o)
        start_all(copies_1)
        wait_all(copies_o)

    h1 = start_row(tok_ref, img_ref, vec_ref) + dot(a_ref[0], wo_ref[...]) + vec_ref[6:7, :]
    h1_ref[0] = h1
    normed, _ = normalize(h1)
    n2 = (normed * vec_ref[7:8, :] + vec_ref[8:9, :]).astype(BF16)
    n2_ref[0] = n2

    @pl.when(first)
    def _():
        wait_all(copies_1)

    slots = slope_ref.shape[1]
    for part in range(PARTS):
        cols = slice(part * D, (part + 1) * D)
        f = dot(n2, w1_ref[:, cols]) + vec_ref[9 + part : 10 + part, :]
        phi = 0.5 * (1.0 + lax.erf(f * INV_ROOT_TWO))
        z_ref[0, :, cols] = (f * phi).astype(BF16)
        fs = f[:slots]
        slope = phi[:slots] + fs * jnp.exp(-0.5 * fs * fs) * INV_ROOT_TWOPI
        slope_ref[0, :, cols] = slope.astype(BF16)


def spread(acc_ref, owners_ref, outs):
    if len(outs) == 1:
        outs[0][...] = acc_ref[...].astype(BF16)
        return
    keep_ref, send_ref = outs
    half, block, _ = send_ref.shape

    def one(spot, _):
        for out_ref, base in ((send_ref, half), (keep_ref, 0)):
            start = pl.multiple_of(owners_ref[OWN + base + spot] * block, 8)
            out_ref[spot] = acc_ref[pl.ds(start, block), :].astype(BF16)
        return 0

    lax.fori_loop(0, half, one, 0)


def gw2_kernel(owners_ref, z_ref, dy_ref, *refs):
    outs, (sum_ref, zt_ref, acc_ref) = refs[:-3], refs[-3:]
    pairs, slots, width = z_ref.shape

    @pl.when(pl.program_id(0) == 0)
    def _():
        zt_ref[...] = z_ref[...].reshape(pairs * slots, width).T

    dy = dy_ref[...].reshape(pairs * slots, -1)
    acc_ref[...] = dot(zt_ref[...], dy)
    sum_ref[...] = jnp.sum(dy.astype(F32), axis=0, keepdims=True)
    spread(acc_ref, owners_ref, outs)


def df_kernel(rows, place_ref, dy_ref, slope_ref, *refs):
    pieces = refs[: len(PIECES)]
    df_ref, gb1_ref, w2_ref, sems = refs[len(PIECES) :]
    step = pl.program_id(0)
    pairs, slots, width = slope_ref.shape
    total = pairs * slots
    copies = piece_copies(pieces, w2_ref, sems, place_ref, rows)

    @pl.when(step == 0)
    def _():
        start_all(copies)
        wait_all(copies)

    dz = dot_last(
        dy_ref[...].reshape(total, D), w2_ref[pl.ds(pl.multiple_of(step * width, 8), width), :]
    )
    df = dz * slope_ref[...].reshape(total, width).astype(F32)
    gb1_ref[...] = jnp.sum(df, axis=0, keepdims=True)
    df_ref[...] = df.astype(BF16)


def mlp_back_kernel(rows, place_ref, df_ref, dy_ref, h1_ref, vec_ref, *refs):
    pieces = refs[: len(PIECES)]
    dh_ref, dhr_ref, da_ref, sum_ref, w1_ref, wo_ref, sem_1, sem_o = refs[len(PIECES) :]
    first = pl.program_id(0) == 0
    copies_1 = piece_copies(pieces, w1_ref, sem_1, place_ref, rows, D)
    copies_o = piece_copies(pieces, wo_ref, sem_o, place_ref, rows)

    @pl.when(first)
    def _():
        start_all(copies_1)
        start_all(copies_o)
        sum_ref[...] = jnp.zeros_like(sum_ref)
        wait_all(copies_1)
        wait_all(copies_o)

    some, slots, _ = dy_ref.shape
    total = some * slots
    dn2 = dot_last(df_ref[...], w1_ref[...])
    normed, scale = normalize(h1_ref[...].reshape(total, D))
    dh = dy_ref[...].reshape(total, D).astype(F32) + norm_back(dn2, normed, scale, vec_ref[7:8, :])
    dh_ref[...] = dh.reshape(some, slots, D)
    sum_ref[0:1, :] += jnp.sum(dh, axis=0, keepdims=True)
    sum_ref[1:2, :] += jnp.sum(dn2 * normed, axis=0, keepdims=True)
    sum_ref[2:3, :] += jnp.sum(dn2, axis=0, keepdims=True)
    low = dh.astype(BF16)
    dhr_ref[...] = low.reshape(some, slots, D)
    da_ref[...] = dot_last(low, wo_ref[...]).astype(BF16).reshape(some, slots, D)


def gw1o_kernel(owners_ref, n2_ref, df_ref, a_ref, dhr_ref, *refs):
    outs, (n2t_ref, acc_ref) = refs[:-2], refs[-2:]
    step = pl.program_id(0)
    pairs, slots, _ = n2_ref.shape
    total = pairs * slots

    @pl.when(step == 0)
    def _():
        n2t_ref[...] = n2_ref[...].reshape(total, D).T

    @pl.when(step < PARTS)
    def _():
        acc_ref[...] = dot(n2t_ref[...], df_ref[...])

    @pl.when(step == PARTS)
    def _():
        acc_ref[...] = dot_first(a_ref[...].reshape(total, D), dhr_ref[...].reshape(total, D))

    spread(acc_ref, owners_ref, outs)


def attn_back_kernel(more, qkv_ref, da_ref, *refs):
    if more:
        _, _, before_ref, dq_ref, dkv_ref, sum_ref = refs
    else:
        dq_ref, dkv_ref, sum_ref = refs
    slots = da_ref.shape[1]

    @pl.when(pl.program_id(0) == 0)
    def _():
        sum_ref[...] = before_ref[...] if more else jnp.zeros_like(sum_ref)

    low = lax.broadcasted_iota(jnp.int32, (1, LANES), 1) < HDIM
    scale = jnp.asarray(HDIM**-0.5, BF16)
    for slab in range(SLABS):
        cols = slice(slab * LANES, (slab + 1) * LANES)
        q = qkv_ref[0, :slots, cols] * scale
        k = qkv_ref[0, :, D + slab * LANES : D + (slab + 1) * LANES]
        v = qkv_ref[0, :, 2 * D + slab * LANES : 2 * D + (slab + 1) * LANES]
        da = da_ref[0, :, cols]
        gqs, gks, gvs = [], [], []
        for head in range(2):
            mine = low if head == 0 else jnp.logical_not(low)
            zero = jnp.zeros_like(q)
            scores = dot_last(k, jnp.where(mine, q, zero))
            e = jnp.exp(scores - jnp.max(scores, axis=0, keepdims=True))
            p = e * (1.0 / jnp.sum(e, axis=0, keepdims=True))
            gvs.append(dot(p.astype(BF16), da))
            dp = dot_last(v, jnp.where(mine, da, zero))
            ds = (p * (dp - jnp.sum(p * dp, axis=0, keepdims=True))).astype(BF16)
            gqs.append(dot_first(ds, k))
            gks.append(dot(ds, q))
        gq = jnp.where(low, gqs[0], gqs[1]) * (HDIM**-0.5)
        gk = jnp.where(low, gks[0], gks[1])
        gv = jnp.where(low, gvs[0], gvs[1])
        dq_ref[0, :, cols] = gq.astype(BF16)
        dkv_ref[0, :, cols] = gk.astype(BF16)
        dkv_ref[0, :, D + slab * LANES : D + (slab + 1) * LANES] = gv.astype(BF16)
        sum_ref[0:1, cols] += jnp.sum(gq, axis=0, keepdims=True)
        sum_ref[1:2, cols] += jnp.sum(gv, axis=0, keepdims=True)


def gqkv_kernel(owners_ref, n1_ref, dq_ref, dkv_ref, *refs):
    outs, (n1t_ref, acc_ref) = refs[:-2], refs[-2:]
    step = pl.program_id(0)
    pairs, length, _ = n1_ref.shape
    slots = dq_ref.shape[1]

    @pl.when(step == 0)
    def _():
        n1t_ref[...] = n1_ref[...].reshape(pairs * length, D).T
        total = dot(n1t_ref[:, :slots], dq_ref[0])
        for pair in range(1, pairs):
            total += dot(n1t_ref[:, pair * length : pair * length + slots], dq_ref[pair])
        acc_ref[...] = total

    @pl.when(step > 0)
    def _():
        acc_ref[...] = dot(n1t_ref[...], dkv_ref[...].reshape(pairs * length, D))

    spread(acc_ref, owners_ref, outs)


def split_two(value):
    one = value.astype(BF16)
    return one, (value - one.astype(F32)).astype(BF16)


def grad_in_kernel(
    rows,
    place_ref,
    tok_ref,
    img_ref,
    vec_ref,
    dq_ref,
    dkv_ref,
    dh_ref,
    perm_ref,
    attn_sum_ref,
    mlp_sum_ref,
    gb1_ref,
    gb2_ref,
    *refs,
):
    pieces = refs[: len(PIECES)]
    out_ref, sum_ref, w_ref, sems = refs[len(PIECES) :]
    first = pl.program_id(0) == 0
    slots = dq_ref.shape[1]
    copies = piece_copies(pieces, w_ref, sems, place_ref, rows)

    @pl.when(first)
    def _():
        start_all(copies)
        sum_ref[...] = jnp.zeros_like(sum_ref)
        sum_ref[4:6, :] = attn_sum_ref[0:2, :]
        sum_ref[6:9, :] = mlp_sum_ref[0:3, :]
        for part in range(PARTS):
            sum_ref[9 + part : 10 + part, :] = gb1_ref[:, part * D : (part + 1) * D]
        sum_ref[9 + PARTS : 10 + PARTS, :] = gb2_ref[...]
        wait_all(copies)

    dn_all = dot_last(dkv_ref[0], w_ref[:, D:])
    dn_top = dn_all[:slots] + dot_last(dq_ref[0], w_ref[:, :D])
    dn = jnp.concatenate([dn_top, dn_all[slots:]], axis=0)
    normed, scale = normalize(start_row(tok_ref, img_ref, vec_ref))
    grad = norm_back(dn, normed, scale, vec_ref[2:3, :])
    grad = jnp.concatenate([grad[:slots] + dh_ref[0], grad[slots:]], axis=0)
    image = img_ref[0][:, :1].astype(F32) > 0.5
    sum_ref[0:1, :] += jnp.sum(jnp.where(image, 0.0, grad), axis=0, keepdims=True)
    sum_ref[1:2, :] += jnp.sum(jnp.where(image, grad, 0.0), axis=0, keepdims=True)
    sum_ref[2:3, :] += jnp.sum(dn * normed, axis=0, keepdims=True)
    sum_ref[3:4, :] += jnp.sum(dn, axis=0, keepdims=True)
    one, two = split_two(grad)
    perm = perm_ref[0]
    out_ref[0] = dot(perm, one) + dot(perm, two)


def out_kernel(rows, place_ref, z_ref, h1_ref, vec_ref, perm_ref, *refs):
    pieces = refs[: len(PIECES)]
    out_ref, w_ref, sems = refs[len(PIECES) :]
    first = pl.program_id(0) == 0
    copies = piece_copies(pieces, w_ref, sems, place_ref, rows)

    @pl.when(first)
    def _():
        start_all(copies)
        wait_all(copies)

    y = h1_ref[0] + dot(z_ref[0], w_ref[...]) + vec_ref[9 + PARTS : 10 + PARTS, :]
    out_ref[0] = dot(perm_ref[0], y.astype(BF16)).astype(BF16)


def place_kernel(number, base, rows, spots_ref, one_ref, two_ref, *refs):
    step = pl.program_id(0)
    count = one_ref.shape[0]

    def put(out_ref):
        def one(spot, _):
            for source, first in ((one_ref, base), (two_ref, base + count)):
                at = pl.ds(pl.multiple_of(spots_ref[first + spot] * rows, 8), rows)
                out_ref[at, :] = source[spot, :rows].astype(F32)
            return 0

        lax.fori_loop(0, count, one, 0)

    if number == 1:
        put(refs[0])
        return
    last = pl.num_programs(0) - 1

    @pl.when(step < last)
    def _():
        put(refs[0])

    @pl.when(step == last)
    def _():
        put(refs[1])


def later(value, dep):
    return lax.optimization_barrier((value, dep))[0]


class Chain:
    def __init__(self):
        self.last, self.waiting = None, []

    def pin(self, values):
        return lax.optimization_barrier((list(values), self.last))[0]

    def hold(self, value):
        self.waiting.append(value)
        return value

    def __call__(
        self, kernel, grid, scalars, ins, outs, scratch, estimate, name, after=(), aliases=None
    ):
        deps = list(after) + self.waiting
        self.waiting = []
        if self.last is not None:
            deps.append(self.last)
        fixed = len(scalars) + len(ins)
        extra = len(deps)

        def body(*refs):
            kernel(*refs[:fixed], *refs[fixed + extra :])

        got = pl.pallas_call(
            body,
            grid_spec=pltpu.PrefetchScalarGridSpec(
                num_scalar_prefetch=len(scalars),
                grid=grid,
                in_specs=[spec for _, spec in ins] + [ANYWHERE] * extra,
                out_specs=[spec for spec, _, _ in outs],
                scratch_shapes=scratch,
            ),
            out_shape=[jax.ShapeDtypeStruct(dims, kind) for _, dims, kind in outs],
            input_output_aliases={
                len(scalars) + k: v for k, v in (aliases or {}).items()
            },
            cost_estimate=estimate,
            compiler_params=pltpu.CompilerParams(vmem_limit_bytes=KERNEL_VMEM),
            name=name,
        )(*scalars, *[value for value, _ in ins], *deps)
        self.last = got[-1]
        return got


class Sum:
    def __init__(self, plan, call, keep, send):
        self.plan, self.call = plan, call
        self.parts, self.count, self.place = [keep], keep.shape[0], 0
        self.move(send)

    def move(self, send):
        got = self.plan.exchange(send, *(order[self.place] for order in self.plan.scatter))
        self.parts.append(got)
        self.place += 1

    def total(self, low, high):
        parts = self.call.pin(self.parts)
        total = parts[0][low:high].astype(F32)
        for part in parts[1:]:
            total = total + part[low:high].astype(F32)
        return total

    def last_moves(self, sends):
        pairs = list(zip(*(order[self.place :] for order in self.plan.scatter)))
        (far, far_odd), (near, near_odd) = pairs
        moves = [(near, near_odd), (far, far_odd), (far ^ near, far_odd ^ near_odd)]
        for spot, masks in enumerate(moves):
            self.parts.append(self.plan.exchange(sends[spot : spot + 1], *masks))
        self.count, self.place = 1, self.place + 2

    def add(self):
        if self.count == 4:
            self.sent = self.call.hold(self.total(1, 4).astype(BF16))
            self.last_moves(self.sent)
            return
        self.count //= 2
        total = self.total(self.count, 2 * self.count)
        self.sent = self.call.hold(total.astype(BF16))
        self.move(self.sent)


class Spread:
    def __init__(self, plan, call, block):
        self.plan, self.call, self.place = plan, call, 0
        self.move(block)

    def move(self, blocks):
        self.blocks = self.call.hold(blocks)
        self.got = self.plan.exchange(blocks, *(order[self.place] for order in self.plan.gather))
        self.place += 1

    def join(self):
        self.move(jnp.concatenate(self.call.pin([self.blocks, self.got]), axis=0))

    def put(self, base, tab, widths, rows):
        count, whole, cols = self.blocks.shape
        step = D if len(widths) > 1 or cols > D else D // 3
        last = widths[0] // step - 1
        ins = [
            (value, pl.BlockSpec((count, whole, step), lambda i, *_: (0, 0, i)))
            for value in (self.blocks, self.got)
        ]
        maps = [lambda i, *_: (0, jnp.minimum(i, last)), lambda i, *_: (0, 0)]
        return self.call(
            functools.partial(place_kernel, len(widths), base, rows),
            (cols // step,),
            [tab],
            ins,
            [
                (pl.BlockSpec((2 * count * rows, step), idx), (2 * count * rows, width), F32)
                for idx, width in zip(maps, widths)
            ],
            [],
            spent(1),
            "place",
        )


def shards(
    plan,
    tokens,
    cotangent,
    mask_pos,
    mask_count,
    w_qkv,
    m_qkv,
    v_qkv,
    w_out,
    m_out,
    v_out,
    w_fc1,
    m_fc1,
    v_fc1,
    w_fc2,
    m_fc2,
    v_fc2,
    vectors,
    m_vec,
    v_vec,
):
    pairs, length, _ = tokens.shape
    slots = mask_pos.shape[1]
    nf, nb, nd = plan.nf, plan.nb, plan.nd
    fi = lax.axis_index("fsdp").astype(jnp.int32)
    bi = lax.axis_index("batch").astype(jnp.int32)
    tab = lax.dynamic_index_in_dim(jnp.asarray(plan.table()), bi * nf + fi, 0, keepdims=False)
    place = owners = tab
    call = Chain()


    def pair_spec(rows, cols):
        return pl.BlockSpec((1, rows, cols), lambda i, *_: (i, 0, 0))

    def piece_ins(pieces):
        return [(value, pl.BlockSpec(memory_space=pltpu.HBM)) for value in pieces]

    sems = pltpu.SemaphoreType.DMA((len(PIECES),))
    rows_d, rows_f = D // nf, FF // nf

    low_vec = vectors.astype(BF16)
    vec_far = plan.exchange(low_vec, 2)
    vec_parts = [low_vec, plan.exchange(low_vec, 1), vec_far, plan.exchange(vec_far, 1)]
    columns = []
    for spot in range(nf):
        chosen = vec_parts[0]
        for mask in range(1, nf):
            chosen = jnp.where((fi ^ mask) == spot, vec_parts[mask], chosen)
        columns.append(chosen)
    vec = jnp.concatenate(columns, axis=1).astype(F32)
    vec = jnp.pad(vec, ((0, 16 - NVEC), (0, 0)))
    vec_in = (vec, full(vec.shape))

    def cast(shard_list, after=()):
        rows = shard_list[0].shape[0]
        half = rows // 2
        cols = sum(value.shape[1] for value in shard_list)
        row = lambda i, place_ref: (i ^ place_ref[1], 0)
        shard, mine = call(
            cast_kernel,
            (2,),
            [place],
            [(value, pl.BlockSpec((half, value.shape[1]), row)) for value in shard_list],
            [
                (pl.BlockSpec((half, cols), row), (rows, cols), BF16),
                (pl.BlockSpec((half, cols), lambda i, *_: (0, 0)), (half, cols), BF16),
            ],
            [],
            spent(0.1),
            "cast",
            after,
        )
        return [shard, plan.exchange(shard, 1), plan.exchange(mine, 2)]

    def spread_pieces(pieces, dep=None):
        near = pieces[2]
        ready = near if dep is None else later(near, dep)
        other = plan.exchange(ready, *plan.helper)
        return pieces[:2] + [near, other, plan.exchange(ready, 1)]

    def last_piece(pieces, dep=None):
        other = pieces[3]
        return pieces + [plan.exchange(other if dep is None else later(other, dep), 1)]

    set_a = cast([w_qkv])

    perm, tokp, img, dy = call(
        order_kernel,
        (pairs,),
        [mask_count],
        [
            (mask_pos.reshape(pairs, 1, slots), pl.BlockSpec((1, 1, slots), lambda i, *_: (i, 0, 0))),
            (tokens, pair_spec(length, D)),
            (cotangent, pair_spec(length, D)),
        ],
        [
            (pair_spec(length, length), (pairs, length, length), BF16),
            (pair_spec(length, D), (pairs, length, D), BF16),
            (pair_spec(length, LANES), (pairs, length, LANES), BF16),
            (pair_spec(slots, D), (pairs, slots, D), BF16),
        ],
        [],
        spent(6),
        "order",
    )

    set_b = cast([w_out, w_fc1])
    near_a = set_a[2]
    set_a = last_piece(spread_pieces(set_a, [set_b[0]] + vec_parts))
    set_c = cast([w_fc2], [near_a])

    n1, qkv = call(
        functools.partial(qkv_kernel, rows_d),
        (pairs,),
        [place],
        [(tokp, pair_spec(length, D)), (img, pair_spec(length, LANES)), vec_in] + piece_ins(set_a),
        [
            (pair_spec(length, D), (pairs, length, D), BF16),
            (pair_spec(length, 3 * D), (pairs, length, 3 * D), BF16),
        ],
        [pltpu.VMEM((D, 3 * D), BF16), sems],
        spent(0.1),
        "qkv",
    )

    near_b = set_b[2]
    set_b = spread_pieces(set_b, n1)
    (mixed,) = call(
        mix_kernel,
        (pairs,),
        [],
        [(qkv, pair_spec(length, 3 * D))],
        [(pair_spec(length, D), (pairs, length, D), BF16)],
        [],
        spent(1),
        "mix",
        [near_b],
    )

    set_b = last_piece(set_b, mixed)
    h1, n2, z, slope = call(
        functools.partial(fc1_kernel, rows_d),
        (pairs,),
        [place],
        [
            (tokp, pair_spec(length, D)),
            (img, pair_spec(length, LANES)),
            (mixed, pair_spec(length, D)),
            vec_in,
        ]
        + piece_ins(set_b),
        [
            (pair_spec(length, D), (pairs, length, D), F32),
            (pair_spec(length, D), (pairs, length, D), BF16),
            (pair_spec(length, FF), (pairs, length, FF), BF16),
            (pair_spec(slots, FF), (pairs, slots, FF), BF16),
        ],
        [pltpu.VMEM((D, D), BF16), pltpu.VMEM((D, FF), BF16), sems, sems],
        spent(18),
        "fc1",
    )

    def top_rows(cols, idx=lambda i, *_: (0, 0, 0)):
        return pl.BlockSpec((pairs, slots, cols), idx)

    def grad_outs(rows, cols, chunk):
        block = rows // nd
        if block % 8:
            return [(pl.BlockSpec((rows, chunk), lambda i, *_: (0, i)), (rows, cols), BF16)]
        spec = pl.BlockSpec((nd // 2, block, chunk), lambda i, *_: (0, 0, i))
        return [(spec, (nd // 2, block, cols), BF16)] * 2

    def grad_sum(outs):
        if len(outs) == 1:
            rows, cols = outs[0].shape
            blocks = jnp.take(outs[0].reshape(nd, rows // nd, cols), tab[OWN : OWN + nd], axis=0)
            outs = [blocks[: nd // 2], blocks[nd // 2 :]]
        return Sum(plan, call, *outs)

    set_c = spread_pieces(set_c, n2)

    chunk = 2 * LANES
    *got, gb2 = call(
        gw2_kernel,
        (D // chunk,),
        [owners],
        [
            (z, top_rows(FF)),
            (dy, top_rows(chunk, lambda i, *_: (0, 0, i))),
        ],
        grad_outs(FF, D, chunk) + [(pl.BlockSpec((1, chunk), lambda i, *_: (0, i)), (1, D), F32)],
        [pltpu.VMEM((FF, pairs * slots), BF16), pltpu.VMEM((FF, chunk), F32)],
        spent(8),
        "gw2",
    )
    sum_2 = grad_sum(got)
    set_c = last_piece(set_c, gb2)

    df, gb1 = call(
        functools.partial(df_kernel, rows_f),
        (PARTS,),
        [place],
        [(dy, top_rows(D)), (slope, top_rows(D, lambda i, *_: (0, 0, i)))] + piece_ins(set_c),
        [
            (pl.BlockSpec((pairs * slots, D), lambda i, *_: (0, i)), (pairs * slots, FF), BF16),
            (pl.BlockSpec((1, D), lambda i, *_: (0, i)), (1, FF), F32),
        ],
        [pltpu.VMEM((FF, D), BF16), sems],
        spent(7),
        "df",
    )
    sum_2.add()

    some = 2 if pairs % 2 == 0 else 1
    some_spec = pl.BlockSpec((some, slots, D), lambda i, *_: (i, 0, 0))
    dh, dhr, da, mlp_sum = call(
        functools.partial(mlp_back_kernel, rows_d),
        (pairs // some,),
        [place],
        [
            (df, pl.BlockSpec((some * slots, FF), lambda i, *_: (i, 0))),
            (dy, some_spec),
            (h1, some_spec),
            vec_in,
        ]
        + piece_ins(set_b),
        [
            (some_spec, (pairs, slots, D), F32),
            (some_spec, (pairs, slots, D), BF16),
            (some_spec, (pairs, slots, D), BF16),
            (full((8, D)), (8, D), F32),
        ],
        [pltpu.VMEM((D, FF), BF16), pltpu.VMEM((D, D), BF16), sems, sems],
        spent(10),
        "mlp_back",
    )

    got = call(
        gw1o_kernel,
        (PARTS + 1,),
        [owners],
        [
            (n2, top_rows(D)),
            (
                df,
                pl.BlockSpec((pairs * slots, D), lambda i, *_: (0, jnp.minimum(i, PARTS - 1))),
            ),
            (mixed, top_rows(D)),
            (dhr, top_rows(D)),
        ],
        grad_outs(D, FF + D, D),
        [pltpu.VMEM((D, pairs * slots), BF16), pltpu.VMEM((D, D), F32)],
        spent(9),
        "gw1o",
    )
    sum_1 = grad_sum(got)
    sum_2.add()

    part_pairs = pairs // 2 if pairs % 2 == 0 else pairs
    back = None
    for number in range(pairs // part_pairs):
        base = number * part_pairs
        at = lambda rows, cols, base=base: pl.BlockSpec(
            (1, rows, cols), lambda i, *_: (base + i, 0, 0)
        )
        ins = [(qkv, at(length, 3 * D)), (da, at(slots, D))]
        if back is not None:
            ins += [(back[0], ANYWHERE), (back[1], ANYWHERE), (back[2], full((8, D)))]
        back = call(
            functools.partial(attn_back_kernel, back is not None),
            (part_pairs,),
            [],
            ins,
            [
                (at(slots, D), (pairs, slots, D), BF16),
                (at(length, 2 * D), (pairs, length, 2 * D), BF16),
                (full((8, D)), (8, D), F32),
            ],
            [],
            spent(12),
            "attn_back",
            aliases=None if back is None else {2: 0, 3: 1},
        )
        if number == 0:
            sum_1.add()
            sum_2.add()
    dq, dkv, attn_sum = back

    fallback = (D // nd) % 8 != 0 or (FF // nd) % 8 != 0
    places = OWN + nd
    order = tab[places + nb :]

    held = jnp.concatenate([m_vec, v_vec], axis=0).reshape(-1)
    held = jnp.pad(held, (0, -held.size % 8)).reshape(8, -1)
    riders = jnp.concatenate(split_two(held), axis=1)
    rider_cols = riders.shape[1]
    riders = jnp.pad(riders, ((0, 0), (0, D - rider_cols)))

    def finish(total, which, masters, moments, extra=None):
        _, rows, cols = total.parts[0].shape
        grad = total.total(0, 1)[0]
        start, news, made = 0, [], []
        for kind, master, (first, second) in zip(which, masters, moments):
            width = master.shape[1]
            own = lax.dynamic_slice_in_dim(master, bi * rows, rows, 0)
            new_w, new_m, new_v = adamw(
                own,
                grad[:, start : start + width],
                first,
                second,
                STEP_RATES[kind],
                DECAY_RATES[kind],
            )
            news.append(new_w.astype(BF16))
            made += [new_m, new_v]
            start += width
        block = jnp.concatenate(news, axis=1)
        if extra is not None:
            block = jnp.concatenate([block, extra], axis=0)
        return Spread(plan, call, block[None]), made

    def put(moved, widths, rows):
        if not fallback:
            return moved.put(places, tab, widths, rows)
        blocks = jnp.concatenate([moved.blocks, moved.got], axis=0)[:, :rows]
        cols = blocks.shape[2]
        blocks = jnp.take(blocks, order, axis=0).reshape(nb * rows, cols).astype(F32)
        cuts = np.cumsum([0] + list(widths))
        return [blocks[:, a:b] for a, b in zip(cuts[:-1], cuts[1:])]

    while sum_2.count > 1:
        sum_2.add()
    moved_2, (new_m2, new_v2) = finish(sum_2, (3,), (w_fc2,), ((m_fc2, v_fc2),), riders)

    got = call(
        gqkv_kernel,
        (3,),
        [owners],
        [
            (n1, full((pairs, length, D))),
            (dq, full((pairs, slots, D))),
            (
                dkv,
                pl.BlockSpec((pairs, length, D), lambda i, *_: (0, 0, jnp.where(i == 2, 1, 0))),
            ),
        ],
        grad_outs(D, 3 * D, D),
        [pltpu.VMEM((D, pairs * length), BF16), pltpu.VMEM((D, D), F32)],
        spent(9),
        "gqkv",
    )
    sum_3 = grad_sum(got)
    sum_1.add()

    sum_3.add()
    paced, call.last = call.last, sum_3.sent
    moved_2.join()
    call.last = paced

    grad_tokens, vec_sum = call(
        functools.partial(grad_in_kernel, rows_d),
        (pairs,),
        [place],
        [
            (tokp, pair_spec(length, D)),
            (img, pair_spec(length, LANES)),
            vec_in,
            (dq, pair_spec(slots, D)),
            (dkv, pair_spec(length, 2 * D)),
            (dh, pair_spec(slots, D)),
            (perm, pair_spec(length, length)),
            (attn_sum, full((8, D))),
            (mlp_sum, full((8, D))),
            (gb1, full((1, FF))),
            (gb2, full((1, D))),
        ]
        + piece_ins(set_a),
        [
            (pair_spec(length, D), (pairs, length, D), F32),
            (full((16, D)), (16, D), F32),
        ],
        [pltpu.VMEM((D, 3 * D), BF16), sems],
        spent(15),
        "grad_in",
    )

    vec_gens = [1] + plan.batch[1:] + plan.batch[:1] + [2]
    vec_got = plan.exchange(vec_sum, vec_gens[0])

    vec_place = 1

    def vec_step():
        nonlocal vec_sum, vec_got, vec_place
        if vec_place > len(vec_gens):
            return
        one, two = call.pin([vec_sum, vec_got])
        vec_sum = one + two
        if vec_place < len(vec_gens):
            vec_got = plan.exchange(vec_sum, vec_gens[vec_place])
        vec_place += 1

    last = plan.bbits
    sum_3.add()
    sum_1.add()
    moved_2.join()

    (layer_out,) = call(
        functools.partial(out_kernel, rows_f),
        (pairs,),
        [place],
        [
            (z, pair_spec(length, FF)),
            (h1, pair_spec(length, D)),
            vec_in,
            (perm, pair_spec(length, length)),
        ]
        + piece_ins(set_c),
        [(pair_spec(length, D), (pairs, length, D), BF16)],
        [pltpu.VMEM((FF, D), BF16), sems],
        spent(13),
        "out",
    )

    moved_1 = moved_3 = put_2 = None
    while moved_3 is None or moved_3.place < last:
        token = None
        if sum_3.count > 1:
            sum_3.add()
            token = sum_3.sent
            call.last = token
        elif moved_3 is None:
            moved_3, (new_mq, new_vq) = finish(sum_3, (0,), (w_qkv,), ((m_qkv, v_qkv),))
            token = moved_3.blocks
        else:
            moved_3.join()
            token = moved_3.blocks
        if sum_1.count > 1:
            sum_1.add()
        elif moved_1 is None:
            moved_1, (new_m1, new_v1, new_mo, new_vo) = finish(
                sum_1, (2, 1), (w_fc1, w_out), ((m_fc1, v_fc1), (m_out, v_out))
            )
        elif moved_1.place < last:
            moved_1.join()
        if moved_2.place < last:
            moved_2.join()
        vec_step()
        call.last = token
        if put_2 is None and moved_2.place == last:
            tail = call.pin([moved_2.blocks, moved_2.got])
            (put_2,) = put(moved_2, (D,), FF // nd)
    while len(vec_gens) >= vec_place:
        vec_step()
    while moved_1.place < last:
        moved_1.join()
    call.waiting = []
    if put_2 is None:
        while moved_2.place < last:
            moved_2.join()
        tail = call.pin([moved_2.blocks, moved_2.got])
        (put_2,) = put(moved_2, (D,), FF // nd)
    new_2 = put_2
    new_1, new_o = put(moved_1, (FF, D), D // nd)
    (new_q,) = put(moved_3, (3 * D,), D // nd)

    own_cols = D // nd
    got = jnp.concatenate([part[:, FF // nd :] for part in tail], axis=0)
    half = rider_cols // 2
    held = got[:, :, :half].astype(F32) + got[:, :, half:rider_cols].astype(F32)
    held = held.reshape(nb, -1)[:, : 2 * NVEC * own_cols].reshape(nb, 2 * NVEC, own_cols)
    held = jnp.take(held, order, axis=0)
    states = jnp.transpose(held, (1, 0, 2)).reshape(2 * NVEC, nb * own_cols)
    grad_vec = lax.dynamic_slice_in_dim(vec_sum[:NVEC], fi * nb * own_cols, nb * own_cols, 1)
    vec_new, _, _ = adamw(
        vectors, grad_vec, states[:NVEC], states[NVEC:], STEP_RATES[4], DECAY_RATES[4]
    )
    own_grad = lax.dynamic_slice_in_dim(grad_vec, bi * own_cols, own_cols, 1)
    _, new_mv, new_vv = adamw(0.0, own_grad, m_vec, v_vec, STEP_RATES[4], DECAY_RATES[4])

    return (
        layer_out,
        grad_tokens,
        new_q,
        new_mq,
        new_vq,
        new_o,
        new_mo,
        new_vo,
        new_1,
        new_m1,
        new_v1,
        new_2,
        new_m2,
        new_v2,
        vec_new,
        new_mv,
        new_vv,
    )


def solution(mesh):
    pairs = P(("batch", "fsdp"), None, None)
    weight = P("fsdp", None)
    state = P(("fsdp", "batch"), None)
    vec_state = P(None, ("fsdp", "batch"))
    matrix = (weight, state, state)
    return jax.shard_map(
        functools.partial(shards, Plan(mesh)),
        mesh=mesh,
        in_specs=(pairs, pairs, P(("batch", "fsdp"), None), P(("batch", "fsdp")))
        + matrix * 4
        + (P(None, "fsdp"), vec_state, vec_state),
        out_specs=(pairs, pairs) + matrix * 4 + (P(None, "fsdp"), vec_state, vec_state),
        check_vma=False,
    )
```

```python
import functools
import math

import jax
import jax.numpy as jnp
import numpy as np
from jax import lax
from jax.experimental import pallas as pl
from jax.experimental.pallas import tpu as pltpu
from jax.sharding import PartitionSpec as P

D = 768
HEADS = 12
HDIM = 64
FF = 3072
TEXT = 40
STEP = 3
MAXM = 128
NVEC = 14
PARTS = FF // D
LANES = 128
SLABS = D // LANES

BETA_ONE = 0.5
BETA_TWO = 0.5
EPS_ADAM = 1e-08
STEP_RATES = (0.03, 0.1, 0.03, 0.015, 0.3)
DECAY_RATES = (0.01, 0.01, 0.01, 0.01, 0.0)
INV_ROOT_TWO = 1.0 / math.sqrt(2.0)
INV_ROOT_TWOPI = 1.0 / math.sqrt(2.0 * math.pi)

KERNEL_VMEM = 20 * 2**20
FLOPS_SCALE = 3e9
BYTES_SCALE = 1e7
F32 = jnp.float32
BF16 = jnp.bfloat16


def dot(a, b):
    return lax.dot_general(a, b, (((1,), (0,)), ((), ())), preferred_element_type=F32)


def dot_first(a, b):
    return lax.dot_general(a, b, (((0,), (0,)), ((), ())), preferred_element_type=F32)


def dot_last(a, b):
    return lax.dot_general(a, b, (((1,), (1,)), ((), ())), preferred_element_type=F32)


def normalize(hidden):
    row_mean = jnp.mean(hidden, axis=-1, keepdims=True)
    centred = hidden - row_mean
    inv_scale = lax.rsqrt(jnp.mean(centred * centred, axis=-1, keepdims=True) + 1e-06)
    return centred * inv_scale, inv_scale


def norm_back(gradient, normed, inv_scale, gain_row):
    scaled = gradient * gain_row
    return inv_scale * (
        scaled
        - jnp.mean(scaled, axis=-1, keepdims=True)
        - normed * jnp.mean(scaled * normed, axis=-1, keepdims=True)
    )


def adamw(weight, gradient, moment_one, moment_two, step_rate, decay_rate):
    new_first = BETA_ONE * moment_one + (1.0 - BETA_ONE) * gradient
    new_second = BETA_TWO * moment_two + (1.0 - BETA_TWO) * gradient * gradient
    correct_one = 1.0 - BETA_ONE**STEP
    correct_two = 1.0 - BETA_TWO**STEP
    update = (
        new_first / correct_one / (jnp.sqrt(new_second / correct_two) + EPS_ADAM)
        + decay_rate * weight
    )
    return (weight - step_rate * update, new_first, new_second)


def spent(micros):
    return pl.CostEstimate(
        flops=int(micros * FLOPS_SCALE), bytes_accessed=int(micros * BYTES_SCALE), transcendentals=0
    )


def full(shape):
    zeros = (0,) * len(shape)
    return pl.BlockSpec(shape, lambda *_: zeros)


ANYWHERE = pl.BlockSpec(memory_space=pl.ANY)


class Plan:
    def __init__(self, mesh):
        self.nf = mesh.shape["fsdp"]
        self.nb = mesh.shape["batch"]
        self.nd = self.nf * self.nb
        self.fbits = self.nf.bit_length() - 1
        self.bbits = self.nb.bit_length() - 1
        assert self.nf == 1 << self.fbits and self.nb == 1 << self.bbits
        assert self.fbits == 2 and self.bbits >= 2
        near = [1, 2, 6] if self.bbits == 3 else [1 << k for k in range(self.bbits)]
        self.batch = [mask * self.nf for mask in near]
        first, second, *rest = self.batch
        self.scatter = ([1, first, second] + rest + [2], [1, second, first, 2] + rest)
        self.gather = (rest[::-1] + [second, first], rest[::-1] + [first, second])
        self.helper = (first, second)

    def exchange(self, value, even, odd=None):
        odd = even if odd is None else odd
        pairs = [(i, i ^ (odd if i & 1 else even)) for i in range(self.nd)]
        return lax.ppermute(value, ("batch", "fsdp"), pairs)

    def spans(self, gens):
        masks = np.zeros(1, np.int32)
        for mask in reversed(gens):
            masks = np.concatenate([masks, masks ^ mask])
        return masks

    def table(self):
        rows = []
        for index in range(self.nd):
            core, fi, bi = index & 1, index & (self.nf - 1), index >> self.fbits
            halves = (bi & 1, (bi >> 1) & 1)
            keep = index ^ self.spans(self.scatter[core][1:])
            send = (index ^ 1) ^ self.spans(self.scatter[1 - core][1:])
            order = np.concatenate([keep, send])
            owners = (order & (self.nf - 1)) * self.nb + (order >> self.fbits)
            places = bi ^ (self.spans(self.gather[core][::-1]) >> self.fbits)
            own = np.asarray([fi, halves[core], halves[1 - core], bi])
            rows.append(np.concatenate([own, owners, places, np.argsort(places)]))
        return np.stack(rows).astype(np.int32)


OWN = 4


PIECES = ((0, None), (1, None), (2, 0), (2, 1), (3, 2), (3, 3))


def piece_copies(refs, target, sems, place_ref, rows, start=0):
    copies = []
    cols = target.shape[1]
    for number, ((mask, kind), ref) in enumerate(zip(PIECES, refs)):
        row = (place_ref[0] ^ mask) * rows
        length = rows
        if kind is not None:
            length = rows // 2
            low = place_ref[1 + kind // 2]
            row = row + (low if kind % 2 == 0 else 1 - low) * length
        copies.append(
            pltpu.make_async_copy(
                ref.at[:, pl.ds(start, cols)],
                target.at[pl.ds(pl.multiple_of(row, 8), length)],
                sems.at[number],
            )
        )
    return copies


def start_all(copies):
    for copy in copies:
        copy.start()


def wait_all(copies):
    for copy in copies:
        copy.wait()


def cast_kernel(place_ref, *refs):
    parts, (shard_ref, mine_ref) = refs[:-2], refs[-2:]
    start = 0
    for part in parts:
        cols = slice(start, start + part.shape[1])
        low = part[...].astype(BF16)
        shard_ref[:, cols] = low

        @pl.when(pl.program_id(0) == 0)
        def _(low=low, cols=cols):
            mine_ref[:, cols] = low

        start += part.shape[1]


def order_kernel(count_ref, pos_ref, tok_ref, cot_ref, perm_ref, tokp_ref, img_ref, dy_ref):
    pair = pl.program_id(0)
    length = tok_ref.shape[1]
    slots = pos_ref.shape[2]
    token = lax.broadcasted_iota(jnp.int32, (length, slots), 0)
    slot = lax.broadcasted_iota(jnp.int32, (length, slots), 1)
    hit = jnp.where(token == pos_ref[0], 1.0, 0.0)
    free = 1.0 - jnp.sum(hit, axis=1, keepdims=True)
    below = lax.broadcasted_iota(jnp.int32, (length, length), 1) < lax.broadcasted_iota(
        jnp.int32, (length, length), 0
    )
    rank = dot(
        jnp.where(below, 1.0, 0.0).astype(BF16),
        jnp.broadcast_to(free, (length, slots)).astype(BF16),
    )
    rest = jnp.where(rank == slot.astype(F32), jnp.broadcast_to(free, (length, slots)), 0.0)
    perm = jnp.concatenate([hit, rest], axis=1).astype(BF16)
    perm_ref[0] = perm
    tokp_ref[0] = dot_first(perm, tok_ref[0]).astype(BF16)
    image = jnp.where(lax.broadcasted_iota(jnp.int32, (length, LANES), 0) >= TEXT, 1.0, 0.0)
    img_ref[0] = dot_first(perm, image.astype(BF16)).astype(BF16)
    chosen = dot_first(perm[:, :slots], cot_ref[0])
    live = lax.broadcasted_iota(jnp.int32, (slots, 1), 0) < count_ref[pair]
    dy_ref[0] = jnp.where(live, chosen, 0.0).astype(BF16)


def start_row(tok_ref, img_ref, vec_ref):
    return tok_ref[0].astype(F32) + jnp.where(
        img_ref[0][:, :1].astype(F32) > 0.5, vec_ref[1:2, :], vec_ref[0:1, :]
    )


def qkv_kernel(rows, place_ref, tok_ref, img_ref, vec_ref, *refs):
    pieces = refs[: len(PIECES)]
    n1_ref, qkv_ref, w_ref, sems = refs[len(PIECES) :]
    first = pl.program_id(0) == 0
    copies = piece_copies(pieces, w_ref, sems, place_ref, rows)

    @pl.when(first)
    def _():
        start_all(copies)

    normed, _ = normalize(start_row(tok_ref, img_ref, vec_ref))
    n1 = (normed * vec_ref[2:3, :] + vec_ref[3:4, :]).astype(BF16)
    n1_ref[0] = n1

    @pl.when(first)
    def _():
        wait_all(copies)

    qkv_ref[0, :, :D] = (dot(n1, w_ref[:, :D]) + vec_ref[4:5, :]).astype(BF16)
    qkv_ref[0, :, D : 2 * D] = dot(n1, w_ref[:, D : 2 * D]).astype(BF16)
    qkv_ref[0, :, 2 * D :] = (dot(n1, w_ref[:, 2 * D :]) + vec_ref[5:6, :]).astype(BF16)


def mix_kernel(qkv_ref, a_ref):
    low = lax.broadcasted_iota(jnp.int32, (1, LANES), 1) < HDIM
    for slab in range(SLABS):
        cols = slice(slab * LANES, (slab + 1) * LANES)
        q = qkv_ref[0, :, cols] * jnp.asarray(HDIM**-0.5, BF16)
        k = qkv_ref[0, :, D + slab * LANES : D + (slab + 1) * LANES]
        v = qkv_ref[0, :, 2 * D + slab * LANES : 2 * D + (slab + 1) * LANES]
        outs = []
        for head in range(2):
            mine = low if head == 0 else jnp.logical_not(low)
            scores = dot_last(jnp.where(mine, q, jnp.zeros_like(q)), k)
            e = jnp.exp(scores - jnp.max(scores, axis=-1, keepdims=True))
            inverse = 1.0 / jnp.sum(e, axis=-1, keepdims=True)
            outs.append(dot(e.astype(BF16), v) * inverse)
        a_ref[0, :, cols] = jnp.where(low, outs[0], outs[1]).astype(BF16)


def fc1_kernel(rows, place_ref, tok_ref, img_ref, a_ref, vec_ref, *refs):
    pieces = refs[: len(PIECES)]
    h1_ref, n2_ref, z_ref, slope_ref, wo_ref, w1_ref, sem_o, sem_1 = refs[len(PIECES) :]
    first = pl.program_id(0) == 0
    copies_o = piece_copies(pieces, wo_ref, sem_o, place_ref, rows)
    copies_1 = piece_copies(pieces, w1_ref, sem_1, place_ref, rows, D)

    @pl.when(first)
    def _():
        start_all(copies_o)
        start_all(copies_1)
        wait_all(copies_o)

    h1 = start_row(tok_ref, img_ref, vec_ref) + dot(a_ref[0], wo_ref[...]) + vec_ref[6:7, :]
    h1_ref[0] = h1
    normed, _ = normalize(h1)
    n2 = (normed * vec_ref[7:8, :] + vec_ref[8:9, :]).astype(BF16)
    n2_ref[0] = n2

    @pl.when(first)
    def _():
        wait_all(copies_1)

    slots = slope_ref.shape[1]
    for part in range(PARTS):
        cols = slice(part * D, (part + 1) * D)
        f = dot(n2, w1_ref[:, cols]) + vec_ref[9 + part : 10 + part, :]
        phi = 0.5 * (1.0 + lax.erf(f * INV_ROOT_TWO))
        z_ref[0, :, cols] = (f * phi).astype(BF16)
        fs = f[:slots]
        slope = phi[:slots] + fs * jnp.exp(-0.5 * fs * fs) * INV_ROOT_TWOPI
        slope_ref[0, :, cols] = slope.astype(BF16)


def spread(acc_ref, owners_ref, outs):
    if len(outs) == 1:
        outs[0][...] = acc_ref[...].astype(BF16)
        return
    keep_ref, send_ref = outs
    half, block, _ = send_ref.shape

    def one(spot, _):
        for out_ref, base in ((send_ref, half), (keep_ref, 0)):
            start = pl.multiple_of(owners_ref[OWN + base + spot] * block, 8)
            out_ref[spot] = acc_ref[pl.ds(start, block), :].astype(BF16)
        return 0

    lax.fori_loop(0, half, one, 0)


def gw2_kernel(owners_ref, z_ref, dy_ref, *refs):
    outs, (sum_ref, zt_ref, acc_ref) = refs[:-3], refs[-3:]
    pairs, slots, width = z_ref.shape

    @pl.when(pl.program_id(0) == 0)
    def _():
        zt_ref[...] = z_ref[...].reshape(pairs * slots, width).T

    dy = dy_ref[...].reshape(pairs * slots, -1)
    acc_ref[...] = dot(zt_ref[...], dy)
    sum_ref[...] = jnp.sum(dy.astype(F32), axis=0, keepdims=True)
    spread(acc_ref, owners_ref, outs)


def df_kernel(rows, place_ref, dy_ref, slope_ref, *refs):
    pieces = refs[: len(PIECES)]
    df_ref, gb1_ref, w2_ref, sems = refs[len(PIECES) :]
    step = pl.program_id(0)
    pairs, slots, width = slope_ref.shape
    total = pairs * slots
    copies = piece_copies(pieces, w2_ref, sems, place_ref, rows)

    @pl.when(step == 0)
    def _():
        start_all(copies)
        wait_all(copies)

    dz = dot_last(
        dy_ref[...].reshape(total, D), w2_ref[pl.ds(pl.multiple_of(step * width, 8), width), :]
    )
    df = dz * slope_ref[...].reshape(total, width).astype(F32)
    gb1_ref[...] = jnp.sum(df, axis=0, keepdims=True)
    df_ref[...] = df.astype(BF16)


def mlp_back_kernel(rows, place_ref, df_ref, dy_ref, h1_ref, vec_ref, *refs):
    pieces = refs[: len(PIECES)]
    dh_ref, dhr_ref, da_ref, sum_ref, w1_ref, wo_ref, sem_1, sem_o = refs[len(PIECES) :]
    first = pl.program_id(0) == 0
    copies_1 = piece_copies(pieces, w1_ref, sem_1, place_ref, rows, D)
    copies_o = piece_copies(pieces, wo_ref, sem_o, place_ref, rows)

    @pl.when(first)
    def _():
        start_all(copies_1)
        start_all(copies_o)
        sum_ref[...] = jnp.zeros_like(sum_ref)
        wait_all(copies_1)
        wait_all(copies_o)

    some, slots, _ = dy_ref.shape
    total = some * slots
    dn2 = dot_last(df_ref[...], w1_ref[...])
    normed, scale = normalize(h1_ref[...].reshape(total, D))
    dh = dy_ref[...].reshape(total, D).astype(F32) + norm_back(dn2, normed, scale, vec_ref[7:8, :])
    dh_ref[...] = dh.reshape(some, slots, D)
    sum_ref[0:1, :] += jnp.sum(dh, axis=0, keepdims=True)
    sum_ref[1:2, :] += jnp.sum(dn2 * normed, axis=0, keepdims=True)
    sum_ref[2:3, :] += jnp.sum(dn2, axis=0, keepdims=True)
    low = dh.astype(BF16)
    dhr_ref[...] = low.reshape(some, slots, D)
    da_ref[...] = dot_last(low, wo_ref[...]).astype(BF16).reshape(some, slots, D)


def gw1o_kernel(owners_ref, n2_ref, df_ref, a_ref, dhr_ref, *refs):
    outs, (n2t_ref, acc_ref) = refs[:-2], refs[-2:]
    step = pl.program_id(0)
    pairs, slots, _ = n2_ref.shape
    total = pairs * slots

    @pl.when(step == 0)
    def _():
        n2t_ref[...] = n2_ref[...].reshape(total, D).T

    @pl.when(step < PARTS)
    def _():
        acc_ref[...] = dot(n2t_ref[...], df_ref[...])

    @pl.when(step == PARTS)
    def _():
        acc_ref[...] = dot_first(a_ref[...].reshape(total, D), dhr_ref[...].reshape(total, D))

    spread(acc_ref, owners_ref, outs)


def attn_back_kernel(more, qkv_ref, da_ref, *refs):
    if more:
        _, _, before_ref, dq_ref, dkv_ref, sum_ref = refs
    else:
        dq_ref, dkv_ref, sum_ref = refs
    slots = da_ref.shape[1]

    @pl.when(pl.program_id(0) == 0)
    def _():
        sum_ref[...] = before_ref[...] if more else jnp.zeros_like(sum_ref)

    low = lax.broadcasted_iota(jnp.int32, (1, LANES), 1) < HDIM
    scale = jnp.asarray(HDIM**-0.5, BF16)
    for slab in range(SLABS):
        cols = slice(slab * LANES, (slab + 1) * LANES)
        q = qkv_ref[0, :slots, cols] * scale
        k = qkv_ref[0, :, D + slab * LANES : D + (slab + 1) * LANES]
        v = qkv_ref[0, :, 2 * D + slab * LANES : 2 * D + (slab + 1) * LANES]
        da = da_ref[0, :, cols]
        gqs, gks, gvs = [], [], []
        for head in range(2):
            mine = low if head == 0 else jnp.logical_not(low)
            zero = jnp.zeros_like(q)
            scores = dot_last(k, jnp.where(mine, q, zero))
            e = jnp.exp(scores - jnp.max(scores, axis=0, keepdims=True))
            p = e * (1.0 / jnp.sum(e, axis=0, keepdims=True))
            gvs.append(dot(p.astype(BF16), da))
            dp = dot_last(v, jnp.where(mine, da, zero))
            ds = (p * (dp - jnp.sum(p * dp, axis=0, keepdims=True))).astype(BF16)
            gqs.append(dot_first(ds, k))
            gks.append(dot(ds, q))
        gq = jnp.where(low, gqs[0], gqs[1]) * (HDIM**-0.5)
        gk = jnp.where(low, gks[0], gks[1])
        gv = jnp.where(low, gvs[0], gvs[1])
        dq_ref[0, :, cols] = gq.astype(BF16)
        dkv_ref[0, :, cols] = gk.astype(BF16)
        dkv_ref[0, :, D + slab * LANES : D + (slab + 1) * LANES] = gv.astype(BF16)
        sum_ref[0:1, cols] += jnp.sum(gq, axis=0, keepdims=True)
        sum_ref[1:2, cols] += jnp.sum(gv, axis=0, keepdims=True)


def gqkv_kernel(owners_ref, n1_ref, dq_ref, dkv_ref, *refs):
    outs, (n1t_ref, acc_ref) = refs[:-2], refs[-2:]
    step = pl.program_id(0)
    pairs, length, _ = n1_ref.shape
    slots = dq_ref.shape[1]

    @pl.when(step == 0)
    def _():
        n1t_ref[...] = n1_ref[...].reshape(pairs * length, D).T
        total = dot(n1t_ref[:, :slots], dq_ref[0])
        for pair in range(1, pairs):
            total += dot(n1t_ref[:, pair * length : pair * length + slots], dq_ref[pair])
        acc_ref[...] = total

    @pl.when(step > 0)
    def _():
        acc_ref[...] = dot(n1t_ref[...], dkv_ref[...].reshape(pairs * length, D))

    spread(acc_ref, owners_ref, outs)


def split_two(value):
    one = value.astype(BF16)
    return one, (value - one.astype(F32)).astype(BF16)


def grad_in_kernel(
    rows,
    place_ref,
    tok_ref,
    img_ref,
    vec_ref,
    dq_ref,
    dkv_ref,
    dh_ref,
    perm_ref,
    attn_sum_ref,
    mlp_sum_ref,
    gb1_ref,
    gb2_ref,
    *refs,
):
    pieces = refs[: len(PIECES)]
    out_ref, sum_ref, w_ref, sems = refs[len(PIECES) :]
    first = pl.program_id(0) == 0
    slots = dq_ref.shape[1]
    copies = piece_copies(pieces, w_ref, sems, place_ref, rows)

    @pl.when(first)
    def _():
        start_all(copies)
        sum_ref[...] = jnp.zeros_like(sum_ref)
        sum_ref[4:6, :] = attn_sum_ref[0:2, :]
        sum_ref[6:9, :] = mlp_sum_ref[0:3, :]
        for part in range(PARTS):
            sum_ref[9 + part : 10 + part, :] = gb1_ref[:, part * D : (part + 1) * D]
        sum_ref[9 + PARTS : 10 + PARTS, :] = gb2_ref[...]
        wait_all(copies)

    dn_all = dot_last(dkv_ref[0], w_ref[:, D:])
    dn_top = dn_all[:slots] + dot_last(dq_ref[0], w_ref[:, :D])
    dn = jnp.concatenate([dn_top, dn_all[slots:]], axis=0)
    normed, scale = normalize(start_row(tok_ref, img_ref, vec_ref))
    grad = norm_back(dn, normed, scale, vec_ref[2:3, :])
    grad = jnp.concatenate([grad[:slots] + dh_ref[0], grad[slots:]], axis=0)
    image = img_ref[0][:, :1].astype(F32) > 0.5
    sum_ref[0:1, :] += jnp.sum(jnp.where(image, 0.0, grad), axis=0, keepdims=True)
    sum_ref[1:2, :] += jnp.sum(jnp.where(image, grad, 0.0), axis=0, keepdims=True)
    sum_ref[2:3, :] += jnp.sum(dn * normed, axis=0, keepdims=True)
    sum_ref[3:4, :] += jnp.sum(dn, axis=0, keepdims=True)
    one, two = split_two(grad)
    perm = perm_ref[0]
    out_ref[0] = dot(perm, one) + dot(perm, two)


def out_kernel(rows, place_ref, z_ref, h1_ref, vec_ref, perm_ref, *refs):
    pieces = refs[: len(PIECES)]
    out_ref, w_ref, sems = refs[len(PIECES) :]
    first = pl.program_id(0) == 0
    copies = piece_copies(pieces, w_ref, sems, place_ref, rows)

    @pl.when(first)
    def _():
        start_all(copies)
        wait_all(copies)

    y = h1_ref[0] + dot(z_ref[0], w_ref[...]) + vec_ref[9 + PARTS : 10 + PARTS, :]
    out_ref[0] = dot(perm_ref[0], y.astype(BF16)).astype(BF16)


def place_kernel(number, base, rows, spots_ref, one_ref, two_ref, *refs):
    step = pl.program_id(0)
    count = one_ref.shape[0]

    def put(out_ref):
        def one(spot, _):
            for source, first in ((one_ref, base), (two_ref, base + count)):
                at = pl.ds(pl.multiple_of(spots_ref[first + spot] * rows, 8), rows)
                out_ref[at, :] = source[spot, :rows].astype(F32)
            return 0

        lax.fori_loop(0, count, one, 0)

    if number == 1:
        put(refs[0])
        return
    last = pl.num_programs(0) - 1

    @pl.when(step < last)
    def _():
        put(refs[0])

    @pl.when(step == last)
    def _():
        put(refs[1])


def later(value, dep):
    return lax.optimization_barrier((value, dep))[0]


class Chain:
    def __init__(self):
        self.last, self.waiting = None, []

    def pin(self, values):
        return lax.optimization_barrier((list(values), self.last))[0]

    def hold(self, value):
        self.waiting.append(value)
        return value

    def __call__(
        self, kernel, grid, scalars, ins, outs, scratch, estimate, name, after=(), aliases=None
    ):
        deps = list(after) + self.waiting
        self.waiting = []
        if self.last is not None:
            deps.append(self.last)
        fixed = len(scalars) + len(ins)
        extra = len(deps)

        def body(*refs):
            kernel(*refs[:fixed], *refs[fixed + extra :])

        got = pl.pallas_call(
            body,
            grid_spec=pltpu.PrefetchScalarGridSpec(
                num_scalar_prefetch=len(scalars),
                grid=grid,
                in_specs=[spec for _, spec in ins] + [ANYWHERE] * extra,
                out_specs=[spec for spec, _, _ in outs],
                scratch_shapes=scratch,
            ),
            out_shape=[jax.ShapeDtypeStruct(dims, kind) for _, dims, kind in outs],
            input_output_aliases={
                len(scalars) + k: v for k, v in (aliases or {}).items()
            },
            cost_estimate=estimate,
            compiler_params=pltpu.CompilerParams(vmem_limit_bytes=KERNEL_VMEM),
            name=name,
        )(*scalars, *[value for value, _ in ins], *deps)
        self.last = got[-1]
        return got


class Sum:
    def __init__(self, plan, call, keep, send):
        self.plan, self.call = plan, call
        self.parts, self.count, self.place = [keep], keep.shape[0], 0
        self.move(send)

    def move(self, send):
        got = self.plan.exchange(send, *(order[self.place] for order in self.plan.scatter))
        self.parts.append(got)
        self.place += 1

    def total(self, low, high):
        parts = self.call.pin(self.parts)
        total = parts[0][low:high].astype(F32)
        for part in parts[1:]:
            total = total + part[low:high].astype(F32)
        return total

    def add(self):
        self.count //= 2
        total = self.total(self.count, 2 * self.count)
        self.sent = self.call.hold(total.astype(BF16))
        self.move(self.sent)


class Spread:
    def __init__(self, plan, call, block):
        self.plan, self.call, self.place = plan, call, 0
        self.move(block)

    def move(self, blocks):
        self.blocks = self.call.hold(blocks)
        self.got = self.plan.exchange(blocks, *(order[self.place] for order in self.plan.gather))
        self.place += 1

    def join(self):
        self.move(jnp.concatenate(self.call.pin([self.blocks, self.got]), axis=0))

    def put(self, base, tab, widths, rows):
        count, whole, cols = self.blocks.shape
        step = D if len(widths) > 1 or cols > D else D // 3
        last = widths[0] // step - 1
        ins = [
            (value, pl.BlockSpec((count, whole, step), lambda i, *_: (0, 0, i)))
            for value in (self.blocks, self.got)
        ]
        maps = [lambda i, *_: (0, jnp.minimum(i, last)), lambda i, *_: (0, 0)]
        return self.call(
            functools.partial(place_kernel, len(widths), base, rows),
            (cols // step,),
            [tab],
            ins,
            [
                (pl.BlockSpec((2 * count * rows, step), idx), (2 * count * rows, width), F32)
                for idx, width in zip(maps, widths)
            ],
            [],
            spent(1),
            "place",
        )


def shards(
    plan,
    tokens,
    cotangent,
    mask_pos,
    mask_count,
    w_qkv,
    m_qkv,
    v_qkv,
    w_out,
    m_out,
    v_out,
    w_fc1,
    m_fc1,
    v_fc1,
    w_fc2,
    m_fc2,
    v_fc2,
    vectors,
    m_vec,
    v_vec,
):
    pairs, length, _ = tokens.shape
    slots = mask_pos.shape[1]
    nf, nb, nd = plan.nf, plan.nb, plan.nd
    fi = lax.axis_index("fsdp").astype(jnp.int32)
    bi = lax.axis_index("batch").astype(jnp.int32)
    tab = lax.dynamic_index_in_dim(jnp.asarray(plan.table()), bi * nf + fi, 0, keepdims=False)
    place = owners = tab
    call = Chain()


    def pair_spec(rows, cols):
        return pl.BlockSpec((1, rows, cols), lambda i, *_: (i, 0, 0))

    def piece_ins(pieces):
        return [(value, pl.BlockSpec(memory_space=pltpu.HBM)) for value in pieces]

    sems = pltpu.SemaphoreType.DMA((len(PIECES),))
    rows_d, rows_f = D // nf, FF // nf

    low_vec = vectors.astype(BF16)
    vec_far = plan.exchange(low_vec, 2)
    vec_parts = [low_vec, plan.exchange(low_vec, 1), vec_far, plan.exchange(vec_far, 1)]
    columns = []
    for spot in range(nf):
        chosen = vec_parts[0]
        for mask in range(1, nf):
            chosen = jnp.where((fi ^ mask) == spot, vec_parts[mask], chosen)
        columns.append(chosen)
    vec = jnp.concatenate(columns, axis=1).astype(F32)
    vec = jnp.pad(vec, ((0, 16 - NVEC), (0, 0)))
    vec_in = (vec, full(vec.shape))

    def cast(shard_list, after=()):
        rows = shard_list[0].shape[0]
        half = rows // 2
        cols = sum(value.shape[1] for value in shard_list)
        row = lambda i, place_ref: (i ^ place_ref[1], 0)
        shard, mine = call(
            cast_kernel,
            (2,),
            [place],
            [(value, pl.BlockSpec((half, value.shape[1]), row)) for value in shard_list],
            [
                (pl.BlockSpec((half, cols), row), (rows, cols), BF16),
                (pl.BlockSpec((half, cols), lambda i, *_: (0, 0)), (half, cols), BF16),
            ],
            [],
            spent(0.1),
            "cast",
            after,
        )
        return [shard, plan.exchange(shard, 1), plan.exchange(mine, 2)]

    def spread_pieces(pieces, dep=None):
        near = pieces[2]
        ready = near if dep is None else later(near, dep)
        other = plan.exchange(ready, *plan.helper)
        return pieces[:2] + [near, other, plan.exchange(ready, 1)]

    def last_piece(pieces, dep=None):
        other = pieces[3]
        return pieces + [plan.exchange(other if dep is None else later(other, dep), 1)]

    set_a = cast([w_qkv])

    perm, tokp, img, dy = call(
        order_kernel,
        (pairs,),
        [mask_count],
        [
            (mask_pos.reshape(pairs, 1, slots), pl.BlockSpec((1, 1, slots), lambda i, *_: (i, 0, 0))),
            (tokens, pair_spec(length, D)),
            (cotangent, pair_spec(length, D)),
        ],
        [
            (pair_spec(length, length), (pairs, length, length), BF16),
            (pair_spec(length, D), (pairs, length, D), BF16),
            (pair_spec(length, LANES), (pairs, length, LANES), BF16),
            (pair_spec(slots, D), (pairs, slots, D), BF16),
        ],
        [],
        spent(6),
        "order",
    )

    set_b = cast([w_out, w_fc1])
    near_a = set_a[2]
    set_a = last_piece(spread_pieces(set_a, [set_b[0]] + vec_parts))
    set_c = cast([w_fc2], [near_a])

    n1, qkv = call(
        functools.partial(qkv_kernel, rows_d),
        (pairs,),
        [place],
        [(tokp, pair_spec(length, D)), (img, pair_spec(length, LANES)), vec_in] + piece_ins(set_a),
        [
            (pair_spec(length, D), (pairs, length, D), BF16),
            (pair_spec(length, 3 * D), (pairs, length, 3 * D), BF16),
        ],
        [pltpu.VMEM((D, 3 * D), BF16), sems],
        spent(0.1),
        "qkv",
    )

    near_b = set_b[2]
    set_b = spread_pieces(set_b, n1)
    (mixed,) = call(
        mix_kernel,
        (pairs,),
        [],
        [(qkv, pair_spec(length, 3 * D))],
        [(pair_spec(length, D), (pairs, length, D), BF16)],
        [],
        spent(1),
        "mix",
        [near_b],
    )

    set_b = last_piece(set_b, mixed)
    h1, n2, z, slope = call(
        functools.partial(fc1_kernel, rows_d),
        (pairs,),
        [place],
        [
            (tokp, pair_spec(length, D)),
            (img, pair_spec(length, LANES)),
            (mixed, pair_spec(length, D)),
            vec_in,
        ]
        + piece_ins(set_b),
        [
            (pair_spec(length, D), (pairs, length, D), F32),
            (pair_spec(length, D), (pairs, length, D), BF16),
            (pair_spec(length, FF), (pairs, length, FF), BF16),
            (pair_spec(slots, FF), (pairs, slots, FF), BF16),
        ],
        [pltpu.VMEM((D, D), BF16), pltpu.VMEM((D, FF), BF16), sems, sems],
        spent(18),
        "fc1",
    )

    def top_rows(cols, idx=lambda i, *_: (0, 0, 0)):
        return pl.BlockSpec((pairs, slots, cols), idx)

    def grad_outs(rows, cols, chunk):
        block = rows // nd
        if block % 8:
            return [(pl.BlockSpec((rows, chunk), lambda i, *_: (0, i)), (rows, cols), BF16)]
        spec = pl.BlockSpec((nd // 2, block, chunk), lambda i, *_: (0, 0, i))
        return [(spec, (nd // 2, block, cols), BF16)] * 2

    def grad_sum(outs):
        if len(outs) == 1:
            rows, cols = outs[0].shape
            blocks = jnp.take(outs[0].reshape(nd, rows // nd, cols), tab[OWN : OWN + nd], axis=0)
            outs = [blocks[: nd // 2], blocks[nd // 2 :]]
        return Sum(plan, call, *outs)

    set_c = spread_pieces(set_c, n2)

    chunk = 2 * LANES
    *got, gb2 = call(
        gw2_kernel,
        (D // chunk,),
        [owners],
        [
            (z, top_rows(FF)),
            (dy, top_rows(chunk, lambda i, *_: (0, 0, i))),
        ],
        grad_outs(FF, D, chunk) + [(pl.BlockSpec((1, chunk), lambda i, *_: (0, i)), (1, D), F32)],
        [pltpu.VMEM((FF, pairs * slots), BF16), pltpu.VMEM((FF, chunk), F32)],
        spent(8),
        "gw2",
    )
    sum_2 = grad_sum(got)
    set_c = last_piece(set_c, gb2)

    df, gb1 = call(
        functools.partial(df_kernel, rows_f),
        (PARTS,),
        [place],
        [(dy, top_rows(D)), (slope, top_rows(D, lambda i, *_: (0, 0, i)))] + piece_ins(set_c),
        [
            (pl.BlockSpec((pairs * slots, D), lambda i, *_: (0, i)), (pairs * slots, FF), BF16),
            (pl.BlockSpec((1, D), lambda i, *_: (0, i)), (1, FF), F32),
        ],
        [pltpu.VMEM((FF, D), BF16), sems],
        spent(7),
        "df",
    )
    sum_2.add()

    some = 2 if pairs % 2 == 0 else 1
    some_spec = pl.BlockSpec((some, slots, D), lambda i, *_: (i, 0, 0))
    dh, dhr, da, mlp_sum = call(
        functools.partial(mlp_back_kernel, rows_d),
        (pairs // some,),
        [place],
        [
            (df, pl.BlockSpec((some * slots, FF), lambda i, *_: (i, 0))),
            (dy, some_spec),
            (h1, some_spec),
            vec_in,
        ]
        + piece_ins(set_b),
        [
            (some_spec, (pairs, slots, D), F32),
            (some_spec, (pairs, slots, D), BF16),
            (some_spec, (pairs, slots, D), BF16),
            (full((8, D)), (8, D), F32),
        ],
        [pltpu.VMEM((D, FF), BF16), pltpu.VMEM((D, D), BF16), sems, sems],
        spent(10),
        "mlp_back",
    )

    got = call(
        gw1o_kernel,
        (PARTS + 1,),
        [owners],
        [
            (n2, top_rows(D)),
            (
                df,
                pl.BlockSpec((pairs * slots, D), lambda i, *_: (0, jnp.minimum(i, PARTS - 1))),
            ),
            (mixed, top_rows(D)),
            (dhr, top_rows(D)),
        ],
        grad_outs(D, FF + D, D),
        [pltpu.VMEM((D, pairs * slots), BF16), pltpu.VMEM((D, D), F32)],
        spent(9),
        "gw1o",
    )
    sum_1 = grad_sum(got)
    sum_2.add()

    part_pairs = pairs // 2 if pairs % 2 == 0 else pairs
    back = None
    for number in range(pairs // part_pairs):
        base = number * part_pairs
        at = lambda rows, cols, base=base: pl.BlockSpec(
            (1, rows, cols), lambda i, *_: (base + i, 0, 0)
        )
        ins = [(qkv, at(length, 3 * D)), (da, at(slots, D))]
        if back is not None:
            ins += [(back[0], ANYWHERE), (back[1], ANYWHERE), (back[2], full((8, D)))]
        back = call(
            functools.partial(attn_back_kernel, back is not None),
            (part_pairs,),
            [],
            ins,
            [
                (at(slots, D), (pairs, slots, D), BF16),
                (at(length, 2 * D), (pairs, length, 2 * D), BF16),
                (full((8, D)), (8, D), F32),
            ],
            [],
            spent(12),
            "attn_back",
            aliases=None if back is None else {2: 0, 3: 1},
        )
        if number == 0:
            sum_1.add()
        sum_2.add()
    dq, dkv, attn_sum = back

    got = call(
        gqkv_kernel,
        (3,),
        [owners],
        [
            (n1, full((pairs, length, D))),
            (dq, full((pairs, slots, D))),
            (
                dkv,
                pl.BlockSpec((pairs, length, D), lambda i, *_: (0, 0, jnp.where(i == 2, 1, 0))),
            ),
        ],
        grad_outs(D, 3 * D, D),
        [pltpu.VMEM((D, pairs * length), BF16), pltpu.VMEM((D, D), F32)],
        spent(9),
        "gqkv",
    )
    sum_3 = grad_sum(got)
    sum_1.add()

    fallback = (D // nd) % 8 != 0 or (FF // nd) % 8 != 0
    places = OWN + nd
    order = tab[places + nb :]

    held = jnp.concatenate([m_vec, v_vec], axis=0).reshape(-1)
    held = jnp.pad(held, (0, -held.size % 8)).reshape(8, -1)
    riders = jnp.concatenate(split_two(held), axis=1)
    rider_cols = riders.shape[1]
    riders = jnp.pad(riders, ((0, 0), (0, D - rider_cols)))

    def finish(total, which, masters, moments, extra=None):
        _, rows, cols = total.parts[0].shape
        grad = total.total(0, 1)[0]
        start, news, made = 0, [], []
        for kind, master, (first, second) in zip(which, masters, moments):
            width = master.shape[1]
            own = lax.dynamic_slice_in_dim(master, bi * rows, rows, 0)
            new_w, new_m, new_v = adamw(
                own,
                grad[:, start : start + width],
                first,
                second,
                STEP_RATES[kind],
                DECAY_RATES[kind],
            )
            news.append(new_w.astype(BF16))
            made += [new_m, new_v]
            start += width
        block = jnp.concatenate(news, axis=1)
        if extra is not None:
            block = jnp.concatenate([block, extra], axis=0)
        return Spread(plan, call, block[None]), made

    def put(moved, widths, rows):
        if not fallback:
            return moved.put(places, tab, widths, rows)
        blocks = jnp.concatenate([moved.blocks, moved.got], axis=0)[:, :rows]
        cols = blocks.shape[2]
        blocks = jnp.take(blocks, order, axis=0).reshape(nb * rows, cols).astype(F32)
        cuts = np.cumsum([0] + list(widths))
        return [blocks[:, a:b] for a, b in zip(cuts[:-1], cuts[1:])]

    sum_3.add()

    paced, call.last = call.last, sum_3.sent
    moved_2, (new_m2, new_v2) = finish(sum_2, (3,), (w_fc2,), ((m_fc2, v_fc2),), riders)
    call.last = paced

    grad_tokens, vec_sum = call(
        functools.partial(grad_in_kernel, rows_d),
        (pairs,),
        [place],
        [
            (tokp, pair_spec(length, D)),
            (img, pair_spec(length, LANES)),
            vec_in,
            (dq, pair_spec(slots, D)),
            (dkv, pair_spec(length, 2 * D)),
            (dh, pair_spec(slots, D)),
            (perm, pair_spec(length, length)),
            (attn_sum, full((8, D))),
            (mlp_sum, full((8, D))),
            (gb1, full((1, FF))),
            (gb2, full((1, D))),
        ]
        + piece_ins(set_a),
        [
            (pair_spec(length, D), (pairs, length, D), F32),
            (full((16, D)), (16, D), F32),
        ],
        [pltpu.VMEM((D, 3 * D), BF16), sems],
        spent(15),
        "grad_in",
    )

    vec_gens = [1] + plan.batch[1:] + plan.batch[:1] + [2]
    vec_got = plan.exchange(vec_sum, vec_gens[0])

    vec_place = 1

    def vec_step():
        nonlocal vec_sum, vec_got, vec_place
        if vec_place > len(vec_gens):
            return
        one, two = call.pin([vec_sum, vec_got])
        vec_sum = one + two
        if vec_place < len(vec_gens):
            vec_got = plan.exchange(vec_sum, vec_gens[vec_place])
        vec_place += 1

    last = plan.bbits
    sum_3.add()
    sum_1.add()
    moved_2.join()

    (layer_out,) = call(
        functools.partial(out_kernel, rows_f),
        (pairs,),
        [place],
        [
            (z, pair_spec(length, FF)),
            (h1, pair_spec(length, D)),
            vec_in,
            (perm, pair_spec(length, length)),
        ]
        + piece_ins(set_c),
        [(pair_spec(length, D), (pairs, length, D), BF16)],
        [pltpu.VMEM((FF, D), BF16), sems],
        spent(13),
        "out",
    )

    moved_1 = moved_3 = None
    while moved_3 is None or moved_3.place < last:
        token = None
        if sum_3.count > 1:
            sum_3.add()
            token = sum_3.sent
        elif moved_3 is None:
            moved_3, (new_mq, new_vq) = finish(sum_3, (0,), (w_qkv,), ((m_qkv, v_qkv),))
            token = moved_3.blocks
        else:
            moved_3.join()
            token = moved_3.blocks
        if sum_1.count > 1:
            sum_1.add()
        elif moved_1 is None:
            moved_1, (new_m1, new_v1, new_mo, new_vo) = finish(
                sum_1, (2, 1), (w_fc1, w_out), ((m_fc1, v_fc1), (m_out, v_out))
            )
        elif moved_1.place < last:
            moved_1.join()
        if moved_2.place < last:
            moved_2.join()
        vec_step()
        call.last = token
    while len(vec_gens) >= vec_place:
        vec_step()
    while moved_1.place < last:
        moved_1.join()
    while moved_2.place < last:
        moved_2.join()
    call.waiting = []
    tail = call.pin([moved_2.blocks, moved_2.got])
    (new_2,) = put(moved_2, (D,), FF // nd)
    new_1, new_o = put(moved_1, (FF, D), D // nd)
    (new_q,) = put(moved_3, (3 * D,), D // nd)

    own_cols = D // nd
    got = jnp.concatenate([part[:, FF // nd :] for part in tail], axis=0)
    half = rider_cols // 2
    held = got[:, :, :half].astype(F32) + got[:, :, half:rider_cols].astype(F32)
    held = held.reshape(nb, -1)[:, : 2 * NVEC * own_cols].reshape(nb, 2 * NVEC, own_cols)
    held = jnp.take(held, order, axis=0)
    states = jnp.transpose(held, (1, 0, 2)).reshape(2 * NVEC, nb * own_cols)
    grad_vec = lax.dynamic_slice_in_dim(vec_sum[:NVEC], fi * nb * own_cols, nb * own_cols, 1)
    vec_new, _, _ = adamw(
        vectors, grad_vec, states[:NVEC], states[NVEC:], STEP_RATES[4], DECAY_RATES[4]
    )
    own_grad = lax.dynamic_slice_in_dim(grad_vec, bi * own_cols, own_cols, 1)
    _, new_mv, new_vv = adamw(0.0, own_grad, m_vec, v_vec, STEP_RATES[4], DECAY_RATES[4])

    return (
        layer_out,
        grad_tokens,
        new_q,
        new_mq,
        new_vq,
        new_o,
        new_mo,
        new_vo,
        new_1,
        new_m1,
        new_v1,
        new_2,
        new_m2,
        new_v2,
        vec_new,
        new_mv,
        new_vv,
    )


def solution(mesh):
    pairs = P(("batch", "fsdp"), None, None)
    weight = P("fsdp", None)
    state = P(("fsdp", "batch"), None)
    vec_state = P(None, ("fsdp", "batch"))
    matrix = (weight, state, state)
    return jax.shard_map(
        functools.partial(shards, Plan(mesh)),
        mesh=mesh,
        in_specs=(pairs, pairs, P(("batch", "fsdp"), None), P(("batch", "fsdp")))
        + matrix * 4
        + (P(None, "fsdp"), vec_state, vec_state),
        out_specs=(pairs, pairs) + matrix * 4 + (P(None, "fsdp"), vec_state, vec_state),
        check_vma=False,
    )
```

```python
import functools
import math

import jax
import jax.numpy as jnp
import numpy as np
from jax import lax
from jax.experimental import pallas as pl
from jax.experimental.pallas import tpu as pltpu
from jax.sharding import PartitionSpec as P

D = 768
HEADS = 12
HDIM = 64
FF = 3072
TEXT = 40
STEP = 3
MAXM = 128
NVEC = 14
PARTS = FF // D
LANES = 128
SLABS = D // LANES

BETA_ONE = 0.5
BETA_TWO = 0.5
EPS_ADAM = 1e-08
STEP_RATES = (0.03, 0.1, 0.03, 0.015, 0.3)
DECAY_RATES = (0.01, 0.01, 0.01, 0.01, 0.0)
INV_ROOT_TWO = 1.0 / math.sqrt(2.0)
INV_ROOT_TWOPI = 1.0 / math.sqrt(2.0 * math.pi)

KERNEL_VMEM = 20 * 2**20
FLOPS_SCALE = 3e9
BYTES_SCALE = 1e7
F32 = jnp.float32
BF16 = jnp.bfloat16


def dot(a, b):
    return lax.dot_general(a, b, (((1,), (0,)), ((), ())), preferred_element_type=F32)


def dot_first(a, b):
    return lax.dot_general(a, b, (((0,), (0,)), ((), ())), preferred_element_type=F32)


def dot_last(a, b):
    return lax.dot_general(a, b, (((1,), (1,)), ((), ())), preferred_element_type=F32)


def normalize(hidden):
    row_mean = jnp.mean(hidden, axis=-1, keepdims=True)
    centred = hidden - row_mean
    inv_scale = lax.rsqrt(jnp.mean(centred * centred, axis=-1, keepdims=True) + 1e-06)
    return centred * inv_scale, inv_scale


def norm_back(gradient, normed, inv_scale, gain_row):
    scaled = gradient * gain_row
    return inv_scale * (
        scaled
        - jnp.mean(scaled, axis=-1, keepdims=True)
        - normed * jnp.mean(scaled * normed, axis=-1, keepdims=True)
    )


def adamw(weight, gradient, moment_one, moment_two, step_rate, decay_rate):
    new_first = BETA_ONE * moment_one + (1.0 - BETA_ONE) * gradient
    new_second = BETA_TWO * moment_two + (1.0 - BETA_TWO) * gradient * gradient
    correct_one = 1.0 - BETA_ONE**STEP
    correct_two = 1.0 - BETA_TWO**STEP
    update = (
        new_first / correct_one / (jnp.sqrt(new_second / correct_two) + EPS_ADAM)
        + decay_rate * weight
    )
    return (weight - step_rate * update, new_first, new_second)


def spent(micros):
    return pl.CostEstimate(
        flops=int(micros * FLOPS_SCALE), bytes_accessed=int(micros * BYTES_SCALE), transcendentals=0
    )


def full(shape):
    zeros = (0,) * len(shape)
    return pl.BlockSpec(shape, lambda *_: zeros)


ANYWHERE = pl.BlockSpec(memory_space=pl.ANY)


class Plan:
    def __init__(self, mesh):
        self.nf = mesh.shape["fsdp"]
        self.nb = mesh.shape["batch"]
        self.nd = self.nf * self.nb
        self.fbits = self.nf.bit_length() - 1
        self.bbits = self.nb.bit_length() - 1
        assert self.nf == 1 << self.fbits and self.nb == 1 << self.bbits
        assert self.fbits == 2 and self.bbits >= 2
        near = [1, 2, 6] if self.bbits == 3 else [1 << k for k in range(self.bbits)]
        self.batch = [mask * self.nf for mask in near]
        first, second, *rest = self.batch
        self.scatter = ([1, first, second] + rest + [2], [1, second, first, 2] + rest)
        self.gather = (rest[::-1] + [second, first], rest[::-1] + [first, second])
        self.helper = (first, second)

    def exchange(self, value, even, odd=None):
        odd = even if odd is None else odd
        pairs = [(i, i ^ (odd if i & 1 else even)) for i in range(self.nd)]
        return lax.ppermute(value, ("batch", "fsdp"), pairs)

    def spans(self, gens):
        masks = np.zeros(1, np.int32)
        for mask in reversed(gens):
            masks = np.concatenate([masks, masks ^ mask])
        return masks

    def table(self):
        rows = []
        for index in range(self.nd):
            core, fi, bi = index & 1, index & (self.nf - 1), index >> self.fbits
            halves = (bi & 1, (bi >> 1) & 1)
            keep = index ^ self.spans(self.scatter[core][1:])
            send = (index ^ 1) ^ self.spans(self.scatter[1 - core][1:])
            order = np.concatenate([keep, send])
            owners = (order & (self.nf - 1)) * self.nb + (order >> self.fbits)
            places = bi ^ (self.spans(self.gather[core][::-1]) >> self.fbits)
            own = np.asarray([fi, halves[core], halves[1 - core], bi])
            rows.append(np.concatenate([own, owners, places, np.argsort(places)]))
        return np.stack(rows).astype(np.int32)


OWN = 4


PIECES = ((0, None), (1, None), (2, 0), (2, 1), (3, 2), (3, 3))


def piece_copies(refs, target, sems, place_ref, rows, start=0):
    copies = []
    cols = target.shape[1]
    for number, ((mask, kind), ref) in enumerate(zip(PIECES, refs)):
        row = (place_ref[0] ^ mask) * rows
        length = rows
        if kind is not None:
            length = rows // 2
            low = place_ref[1 + kind // 2]
            row = row + (low if kind % 2 == 0 else 1 - low) * length
        copies.append(
            pltpu.make_async_copy(
                ref.at[:, pl.ds(start, cols)],
                target.at[pl.ds(pl.multiple_of(row, 8), length)],
                sems.at[number],
            )
        )
    return copies


def start_all(copies):
    for copy in copies:
        copy.start()


def wait_all(copies):
    for copy in copies:
        copy.wait()


def cast_kernel(place_ref, *refs):
    parts, (shard_ref, mine_ref) = refs[:-2], refs[-2:]
    start = 0
    for part in parts:
        cols = slice(start, start + part.shape[1])
        low = part[...].astype(BF16)
        shard_ref[:, cols] = low

        @pl.when(pl.program_id(0) == 0)
        def _(low=low, cols=cols):
            mine_ref[:, cols] = low

        start += part.shape[1]


def order_kernel(count_ref, pos_ref, tok_ref, cot_ref, perm_ref, tokp_ref, img_ref, dy_ref):
    pair = pl.program_id(0)
    length = tok_ref.shape[1]
    slots = pos_ref.shape[2]
    token = lax.broadcasted_iota(jnp.int32, (length, slots), 0)
    slot = lax.broadcasted_iota(jnp.int32, (length, slots), 1)
    hit = jnp.where(token == pos_ref[0], 1.0, 0.0)
    free = 1.0 - jnp.sum(hit, axis=1, keepdims=True)
    below = lax.broadcasted_iota(jnp.int32, (length, length), 1) < lax.broadcasted_iota(
        jnp.int32, (length, length), 0
    )
    rank = dot(
        jnp.where(below, 1.0, 0.0).astype(BF16),
        jnp.broadcast_to(free, (length, slots)).astype(BF16),
    )
    rest = jnp.where(rank == slot.astype(F32), jnp.broadcast_to(free, (length, slots)), 0.0)
    perm = jnp.concatenate([hit, rest], axis=1).astype(BF16)
    perm_ref[0] = perm
    tokp_ref[0] = dot_first(perm, tok_ref[0]).astype(BF16)
    image = jnp.where(lax.broadcasted_iota(jnp.int32, (length, LANES), 0) >= TEXT, 1.0, 0.0)
    img_ref[0] = dot_first(perm, image.astype(BF16)).astype(BF16)
    chosen = dot_first(perm[:, :slots], cot_ref[0])
    live = lax.broadcasted_iota(jnp.int32, (slots, 1), 0) < count_ref[pair]
    dy_ref[0] = jnp.where(live, chosen, 0.0).astype(BF16)


def start_row(tok_ref, img_ref, vec_ref):
    return tok_ref[0].astype(F32) + jnp.where(
        img_ref[0][:, :1].astype(F32) > 0.5, vec_ref[1:2, :], vec_ref[0:1, :]
    )


def qkv_kernel(rows, place_ref, tok_ref, img_ref, vec_ref, *refs):
    pieces = refs[: len(PIECES)]
    n1_ref, qkv_ref, w_ref, sems = refs[len(PIECES) :]
    first = pl.program_id(0) == 0
    copies = piece_copies(pieces, w_ref, sems, place_ref, rows)

    @pl.when(first)
    def _():
        start_all(copies)

    normed, _ = normalize(start_row(tok_ref, img_ref, vec_ref))
    n1 = (normed * vec_ref[2:3, :] + vec_ref[3:4, :]).astype(BF16)
    n1_ref[0] = n1

    @pl.when(first)
    def _():
        wait_all(copies)

    qkv_ref[0, :, :D] = (dot(n1, w_ref[:, :D]) + vec_ref[4:5, :]).astype(BF16)
    qkv_ref[0, :, D : 2 * D] = dot(n1, w_ref[:, D : 2 * D]).astype(BF16)
    qkv_ref[0, :, 2 * D :] = (dot(n1, w_ref[:, 2 * D :]) + vec_ref[5:6, :]).astype(BF16)


def mix_kernel(qkv_ref, a_ref):
    low = lax.broadcasted_iota(jnp.int32, (1, LANES), 1) < HDIM
    for slab in range(SLABS):
        cols = slice(slab * LANES, (slab + 1) * LANES)
        q = qkv_ref[0, :, cols] * jnp.asarray(HDIM**-0.5, BF16)
        k = qkv_ref[0, :, D + slab * LANES : D + (slab + 1) * LANES]
        v = qkv_ref[0, :, 2 * D + slab * LANES : 2 * D + (slab + 1) * LANES]
        outs = []
        for head in range(2):
            mine = low if head == 0 else jnp.logical_not(low)
            scores = dot_last(jnp.where(mine, q, jnp.zeros_like(q)), k)
            e = jnp.exp(scores - jnp.max(scores, axis=-1, keepdims=True))
            inverse = 1.0 / jnp.sum(e, axis=-1, keepdims=True)
            outs.append(dot(e.astype(BF16), v) * inverse)
        a_ref[0, :, cols] = jnp.where(low, outs[0], outs[1]).astype(BF16)


def fc1_kernel(rows, place_ref, tok_ref, img_ref, a_ref, vec_ref, *refs):
    pieces = refs[: len(PIECES)]
    h1_ref, n2_ref, z_ref, slope_ref, wo_ref, w1_ref, sem_o, sem_1 = refs[len(PIECES) :]
    first = pl.program_id(0) == 0
    copies_o = piece_copies(pieces, wo_ref, sem_o, place_ref, rows)
    copies_1 = piece_copies(pieces, w1_ref, sem_1, place_ref, rows, D)

    @pl.when(first)
    def _():
        start_all(copies_o)
        start_all(copies_1)
        wait_all(copies_o)

    h1 = start_row(tok_ref, img_ref, vec_ref) + dot(a_ref[0], wo_ref[...]) + vec_ref[6:7, :]
    h1_ref[0] = h1
    normed, _ = normalize(h1)
    n2 = (normed * vec_ref[7:8, :] + vec_ref[8:9, :]).astype(BF16)
    n2_ref[0] = n2

    @pl.when(first)
    def _():
        wait_all(copies_1)

    slots = slope_ref.shape[1]
    for part in range(PARTS):
        cols = slice(part * D, (part + 1) * D)
        f = dot(n2, w1_ref[:, cols]) + vec_ref[9 + part : 10 + part, :]
        phi = 0.5 * (1.0 + lax.erf(f * INV_ROOT_TWO))
        z_ref[0, :, cols] = (f * phi).astype(BF16)
        fs = f[:slots]
        slope = phi[:slots] + fs * jnp.exp(-0.5 * fs * fs) * INV_ROOT_TWOPI
        slope_ref[0, :, cols] = slope.astype(BF16)


def spread(acc_ref, owners_ref, outs):
    if len(outs) == 1:
        outs[0][...] = acc_ref[...].astype(BF16)
        return
    keep_ref, send_ref = outs
    half, block, _ = send_ref.shape

    def one(spot, _):
        for out_ref, base in ((send_ref, half), (keep_ref, 0)):
            start = pl.multiple_of(owners_ref[OWN + base + spot] * block, 8)
            out_ref[spot] = acc_ref[pl.ds(start, block), :].astype(BF16)
        return 0

    lax.fori_loop(0, half, one, 0)


def gw2_kernel(owners_ref, z_ref, dy_ref, *refs):
    outs, (sum_ref, zt_ref, acc_ref) = refs[:-3], refs[-3:]
    pairs, slots, width = z_ref.shape

    @pl.when(pl.program_id(0) == 0)
    def _():
        zt_ref[...] = z_ref[...].reshape(pairs * slots, width).T

    dy = dy_ref[...].reshape(pairs * slots, -1)
    acc_ref[...] = dot(zt_ref[...], dy)
    sum_ref[...] = jnp.sum(dy.astype(F32), axis=0, keepdims=True)
    spread(acc_ref, owners_ref, outs)


def df_kernel(rows, place_ref, dy_ref, slope_ref, *refs):
    pieces = refs[: len(PIECES)]
    df_ref, gb1_ref, w2_ref, sems = refs[len(PIECES) :]
    step = pl.program_id(0)
    pairs, slots, width = slope_ref.shape
    total = pairs * slots
    copies = piece_copies(pieces, w2_ref, sems, place_ref, rows)

    @pl.when(step == 0)
    def _():
        start_all(copies)
        wait_all(copies)

    dz = dot_last(
        dy_ref[...].reshape(total, D), w2_ref[pl.ds(pl.multiple_of(step * width, 8), width), :]
    )
    df = dz * slope_ref[...].reshape(total, width).astype(F32)
    gb1_ref[...] = jnp.sum(df, axis=0, keepdims=True)
    df_ref[...] = df.astype(BF16)


def mlp_back_kernel(rows, place_ref, df_ref, dy_ref, h1_ref, vec_ref, *refs):
    pieces = refs[: len(PIECES)]
    dh_ref, dhr_ref, da_ref, sum_ref, w1_ref, wo_ref, sem_1, sem_o = refs[len(PIECES) :]
    first = pl.program_id(0) == 0
    copies_1 = piece_copies(pieces, w1_ref, sem_1, place_ref, rows, D)
    copies_o = piece_copies(pieces, wo_ref, sem_o, place_ref, rows)

    @pl.when(first)
    def _():
        start_all(copies_1)
        start_all(copies_o)
        sum_ref[...] = jnp.zeros_like(sum_ref)
        wait_all(copies_1)
        wait_all(copies_o)

    some, slots, _ = dy_ref.shape
    total = some * slots
    dn2 = dot_last(df_ref[...], w1_ref[...])
    normed, scale = normalize(h1_ref[...].reshape(total, D))
    dh = dy_ref[...].reshape(total, D).astype(F32) + norm_back(dn2, normed, scale, vec_ref[7:8, :])
    dh_ref[...] = dh.reshape(some, slots, D)
    sum_ref[0:1, :] += jnp.sum(dh, axis=0, keepdims=True)
    sum_ref[1:2, :] += jnp.sum(dn2 * normed, axis=0, keepdims=True)
    sum_ref[2:3, :] += jnp.sum(dn2, axis=0, keepdims=True)
    low = dh.astype(BF16)
    dhr_ref[...] = low.reshape(some, slots, D)
    da_ref[...] = dot_last(low, wo_ref[...]).astype(BF16).reshape(some, slots, D)


def gw1o_kernel(owners_ref, n2_ref, df_ref, a_ref, dhr_ref, *refs):
    outs, (n2t_ref, acc_ref) = refs[:-2], refs[-2:]
    step = pl.program_id(0)
    pairs, slots, _ = n2_ref.shape
    total = pairs * slots

    @pl.when(step == 0)
    def _():
        n2t_ref[...] = n2_ref[...].reshape(total, D).T

    @pl.when(step < PARTS)
    def _():
        acc_ref[...] = dot(n2t_ref[...], df_ref[...])

    @pl.when(step == PARTS)
    def _():
        acc_ref[...] = dot_first(a_ref[...].reshape(total, D), dhr_ref[...].reshape(total, D))

    spread(acc_ref, owners_ref, outs)


def attn_back_kernel(more, qkv_ref, da_ref, *refs):
    if more:
        _, _, before_ref, dq_ref, dkv_ref, sum_ref = refs
    else:
        dq_ref, dkv_ref, sum_ref = refs
    slots = da_ref.shape[1]

    @pl.when(pl.program_id(0) == 0)
    def _():
        sum_ref[...] = before_ref[...] if more else jnp.zeros_like(sum_ref)

    low = lax.broadcasted_iota(jnp.int32, (1, LANES), 1) < HDIM
    scale = jnp.asarray(HDIM**-0.5, BF16)
    for slab in range(SLABS):
        cols = slice(slab * LANES, (slab + 1) * LANES)
        q = qkv_ref[0, :slots, cols] * scale
        k = qkv_ref[0, :, D + slab * LANES : D + (slab + 1) * LANES]
        v = qkv_ref[0, :, 2 * D + slab * LANES : 2 * D + (slab + 1) * LANES]
        da = da_ref[0, :, cols]
        gqs, gks, gvs = [], [], []
        for head in range(2):
            mine = low if head == 0 else jnp.logical_not(low)
            zero = jnp.zeros_like(q)
            scores = dot_last(k, jnp.where(mine, q, zero))
            e = jnp.exp(scores - jnp.max(scores, axis=0, keepdims=True))
            p = e * (1.0 / jnp.sum(e, axis=0, keepdims=True))
            gvs.append(dot(p.astype(BF16), da))
            dp = dot_last(v, jnp.where(mine, da, zero))
            ds = (p * (dp - jnp.sum(p * dp, axis=0, keepdims=True))).astype(BF16)
            gqs.append(dot_first(ds, k))
            gks.append(dot(ds, q))
        gq = jnp.where(low, gqs[0], gqs[1]) * (HDIM**-0.5)
        gk = jnp.where(low, gks[0], gks[1])
        gv = jnp.where(low, gvs[0], gvs[1])
        dq_ref[0, :, cols] = gq.astype(BF16)
        dkv_ref[0, :, cols] = gk.astype(BF16)
        dkv_ref[0, :, D + slab * LANES : D + (slab + 1) * LANES] = gv.astype(BF16)
        sum_ref[0:1, cols] += jnp.sum(gq, axis=0, keepdims=True)
        sum_ref[1:2, cols] += jnp.sum(gv, axis=0, keepdims=True)


def gqkv_kernel(owners_ref, n1_ref, dq_ref, dkv_ref, *refs):
    outs, (n1t_ref, acc_ref) = refs[:-2], refs[-2:]
    step = pl.program_id(0)
    pairs, length, _ = n1_ref.shape
    slots = dq_ref.shape[1]

    @pl.when(step == 0)
    def _():
        n1t_ref[...] = n1_ref[...].reshape(pairs * length, D).T
        total = dot(n1t_ref[:, :slots], dq_ref[0])
        for pair in range(1, pairs):
            total += dot(n1t_ref[:, pair * length : pair * length + slots], dq_ref[pair])
        acc_ref[...] = total

    @pl.when(step > 0)
    def _():
        acc_ref[...] = dot(n1t_ref[...], dkv_ref[...].reshape(pairs * length, D))

    spread(acc_ref, owners_ref, outs)


def split_two(value):
    one = value.astype(BF16)
    return one, (value - one.astype(F32)).astype(BF16)


def grad_in_kernel(
    rows,
    place_ref,
    tok_ref,
    img_ref,
    vec_ref,
    dq_ref,
    dkv_ref,
    dh_ref,
    perm_ref,
    attn_sum_ref,
    mlp_sum_ref,
    gb1_ref,
    gb2_ref,
    *refs,
):
    pieces = refs[: len(PIECES)]
    out_ref, sum_ref, w_ref, sems = refs[len(PIECES) :]
    first = pl.program_id(0) == 0
    slots = dq_ref.shape[1]
    copies = piece_copies(pieces, w_ref, sems, place_ref, rows)

    @pl.when(first)
    def _():
        start_all(copies)
        sum_ref[...] = jnp.zeros_like(sum_ref)
        sum_ref[4:6, :] = attn_sum_ref[0:2, :]
        sum_ref[6:9, :] = mlp_sum_ref[0:3, :]
        for part in range(PARTS):
            sum_ref[9 + part : 10 + part, :] = gb1_ref[:, part * D : (part + 1) * D]
        sum_ref[9 + PARTS : 10 + PARTS, :] = gb2_ref[...]
        wait_all(copies)

    dn_all = dot_last(dkv_ref[0], w_ref[:, D:])
    dn_top = dn_all[:slots] + dot_last(dq_ref[0], w_ref[:, :D])
    dn = jnp.concatenate([dn_top, dn_all[slots:]], axis=0)
    normed, scale = normalize(start_row(tok_ref, img_ref, vec_ref))
    grad = norm_back(dn, normed, scale, vec_ref[2:3, :])
    grad = jnp.concatenate([grad[:slots] + dh_ref[0], grad[slots:]], axis=0)
    image = img_ref[0][:, :1].astype(F32) > 0.5
    sum_ref[0:1, :] += jnp.sum(jnp.where(image, 0.0, grad), axis=0, keepdims=True)
    sum_ref[1:2, :] += jnp.sum(jnp.where(image, grad, 0.0), axis=0, keepdims=True)
    sum_ref[2:3, :] += jnp.sum(dn * normed, axis=0, keepdims=True)
    sum_ref[3:4, :] += jnp.sum(dn, axis=0, keepdims=True)
    one, two = split_two(grad)
    perm = perm_ref[0]
    out_ref[0] = dot(perm, one) + dot(perm, two)


def out_kernel(rows, place_ref, z_ref, h1_ref, vec_ref, perm_ref, *refs):
    pieces = refs[: len(PIECES)]
    out_ref, w_ref, sems = refs[len(PIECES) :]
    first = pl.program_id(0) == 0
    copies = piece_copies(pieces, w_ref, sems, place_ref, rows)

    @pl.when(first)
    def _():
        start_all(copies)
        wait_all(copies)

    y = h1_ref[0] + dot(z_ref[0], w_ref[...]) + vec_ref[9 + PARTS : 10 + PARTS, :]
    out_ref[0] = dot(perm_ref[0], y.astype(BF16)).astype(BF16)


def place_kernel(number, base, rows, spots_ref, one_ref, two_ref, *refs):
    step = pl.program_id(0)
    count = one_ref.shape[0]

    def put(out_ref):
        def one(spot, _):
            for source, first in ((one_ref, base), (two_ref, base + count)):
                at = pl.ds(pl.multiple_of(spots_ref[first + spot] * rows, 8), rows)
                out_ref[at, :] = source[spot, :rows].astype(F32)
            return 0

        lax.fori_loop(0, count, one, 0)

    if number == 1:
        put(refs[0])
        return
    last = pl.num_programs(0) - 1

    @pl.when(step < last)
    def _():
        put(refs[0])

    @pl.when(step == last)
    def _():
        put(refs[1])


def later(value, dep):
    return lax.optimization_barrier((value, dep))[0]


class Chain:
    def __init__(self):
        self.last, self.waiting = None, []

    def pin(self, values):
        return lax.optimization_barrier((list(values), self.last))[0]

    def hold(self, value):
        self.waiting.append(value)
        return value

    def __call__(
        self, kernel, grid, scalars, ins, outs, scratch, estimate, name, after=(), aliases=None
    ):
        deps = list(after) + self.waiting
        self.waiting = []
        if self.last is not None:
            deps.append(self.last)
        fixed = len(scalars) + len(ins)
        extra = len(deps)

        def body(*refs):
            kernel(*refs[:fixed], *refs[fixed + extra :])

        got = pl.pallas_call(
            body,
            grid_spec=pltpu.PrefetchScalarGridSpec(
                num_scalar_prefetch=len(scalars),
                grid=grid,
                in_specs=[spec for _, spec in ins] + [ANYWHERE] * extra,
                out_specs=[spec for spec, _, _ in outs],
                scratch_shapes=scratch,
            ),
            out_shape=[jax.ShapeDtypeStruct(dims, kind) for _, dims, kind in outs],
            input_output_aliases={
                len(scalars) + k: v for k, v in (aliases or {}).items()
            },
            cost_estimate=estimate,
            compiler_params=pltpu.CompilerParams(vmem_limit_bytes=KERNEL_VMEM),
            name=name,
        )(*scalars, *[value for value, _ in ins], *deps)
        self.last = got[-1]
        return got


class Sum:
    def __init__(self, plan, call, keep, send):
        self.plan, self.call = plan, call
        self.parts, self.count, self.place = [keep], keep.shape[0], 0
        self.move(send)

    def move(self, send):
        got = self.plan.exchange(send, *(order[self.place] for order in self.plan.scatter))
        self.parts.append(got)
        self.place += 1

    def total(self, low, high):
        parts = self.call.pin(self.parts)
        total = parts[0][low:high].astype(F32)
        for part in parts[1:]:
            total = total + part[low:high].astype(F32)
        return total

    def add(self):
        self.count //= 2
        total = self.total(self.count, 2 * self.count)
        self.sent = self.call.hold(total.astype(BF16))
        self.move(self.sent)


class Spread:
    def __init__(self, plan, call, block):
        self.plan, self.call, self.place = plan, call, 0
        self.move(block)

    def move(self, blocks):
        self.blocks = self.call.hold(blocks)
        self.got = self.plan.exchange(blocks, *(order[self.place] for order in self.plan.gather))
        self.place += 1

    def join(self):
        self.move(jnp.concatenate(self.call.pin([self.blocks, self.got]), axis=0))

    def put(self, base, tab, widths, rows):
        count, whole, cols = self.blocks.shape
        step = D if len(widths) > 1 or cols > D else D // 3
        last = widths[0] // step - 1
        ins = [
            (value, pl.BlockSpec((count, whole, step), lambda i, *_: (0, 0, i)))
            for value in (self.blocks, self.got)
        ]
        maps = [lambda i, *_: (0, jnp.minimum(i, last)), lambda i, *_: (0, 0)]
        return self.call(
            functools.partial(place_kernel, len(widths), base, rows),
            (cols // step,),
            [tab],
            ins,
            [
                (pl.BlockSpec((2 * count * rows, step), idx), (2 * count * rows, width), F32)
                for idx, width in zip(maps, widths)
            ],
            [],
            spent(1),
            "place",
        )


def shards(
    plan,
    tokens,
    cotangent,
    mask_pos,
    mask_count,
    w_qkv,
    m_qkv,
    v_qkv,
    w_out,
    m_out,
    v_out,
    w_fc1,
    m_fc1,
    v_fc1,
    w_fc2,
    m_fc2,
    v_fc2,
    vectors,
    m_vec,
    v_vec,
):
    pairs, length, _ = tokens.shape
    slots = mask_pos.shape[1]
    nf, nb, nd = plan.nf, plan.nb, plan.nd
    fi = lax.axis_index("fsdp").astype(jnp.int32)
    bi = lax.axis_index("batch").astype(jnp.int32)
    tab = lax.dynamic_index_in_dim(jnp.asarray(plan.table()), bi * nf + fi, 0, keepdims=False)
    place = owners = tab
    call = Chain()


    def pair_spec(rows, cols):
        return pl.BlockSpec((1, rows, cols), lambda i, *_: (i, 0, 0))

    def piece_ins(pieces):
        return [(value, pl.BlockSpec(memory_space=pltpu.HBM)) for value in pieces]

    sems = pltpu.SemaphoreType.DMA((len(PIECES),))
    rows_d, rows_f = D // nf, FF // nf

    low_vec = vectors.astype(BF16)
    vec_far = plan.exchange(low_vec, 2)
    vec_parts = [low_vec, plan.exchange(low_vec, 1), vec_far, plan.exchange(vec_far, 1)]
    columns = []
    for spot in range(nf):
        chosen = vec_parts[0]
        for mask in range(1, nf):
            chosen = jnp.where((fi ^ mask) == spot, vec_parts[mask], chosen)
        columns.append(chosen)
    vec = jnp.concatenate(columns, axis=1).astype(F32)
    vec = jnp.pad(vec, ((0, 16 - NVEC), (0, 0)))
    vec_in = (vec, full(vec.shape))

    def cast(shard_list, after=()):
        rows = shard_list[0].shape[0]
        half = rows // 2
        cols = sum(value.shape[1] for value in shard_list)
        row = lambda i, place_ref: (i ^ place_ref[1], 0)
        shard, mine = call(
            cast_kernel,
            (2,),
            [place],
            [(value, pl.BlockSpec((half, value.shape[1]), row)) for value in shard_list],
            [
                (pl.BlockSpec((half, cols), row), (rows, cols), BF16),
                (pl.BlockSpec((half, cols), lambda i, *_: (0, 0)), (half, cols), BF16),
            ],
            [],
            spent(0.1),
            "cast",
            after,
        )
        return [shard, plan.exchange(shard, 1), plan.exchange(mine, 2)]

    def spread_pieces(pieces, dep=None):
        near = pieces[2]
        ready = near if dep is None else later(near, dep)
        other = plan.exchange(ready, *plan.helper)
        return pieces[:2] + [near, other, plan.exchange(ready, 1)]

    def last_piece(pieces, dep=None):
        other = pieces[3]
        return pieces + [plan.exchange(other if dep is None else later(other, dep), 1)]

    set_a = cast([w_qkv])

    perm, tokp, img, dy = call(
        order_kernel,
        (pairs,),
        [mask_count],
        [
            (mask_pos.reshape(pairs, 1, slots), pl.BlockSpec((1, 1, slots), lambda i, *_: (i, 0, 0))),
            (tokens, pair_spec(length, D)),
            (cotangent, pair_spec(length, D)),
        ],
        [
            (pair_spec(length, length), (pairs, length, length), BF16),
            (pair_spec(length, D), (pairs, length, D), BF16),
            (pair_spec(length, LANES), (pairs, length, LANES), BF16),
            (pair_spec(slots, D), (pairs, slots, D), BF16),
        ],
        [],
        spent(6),
        "order",
    )

    set_b = cast([w_out, w_fc1])
    near_a = set_a[2]
    set_a = last_piece(spread_pieces(set_a, [set_b[0]] + vec_parts))
    held = jnp.concatenate([m_vec, v_vec], axis=0).reshape(-1)
    held = jnp.pad(held, (0, -held.size % 8)).reshape(8, -1)
    riders = jnp.concatenate(split_two(held), axis=1)
    rider_cols = riders.shape[1]
    riders = jnp.pad(riders, ((0, 0), (0, D - rider_cols)))
    call.hold(riders)
    set_c = cast([w_fc2], [near_a])

    n1, qkv = call(
        functools.partial(qkv_kernel, rows_d),
        (pairs,),
        [place],
        [(tokp, pair_spec(length, D)), (img, pair_spec(length, LANES)), vec_in] + piece_ins(set_a),
        [
            (pair_spec(length, D), (pairs, length, D), BF16),
            (pair_spec(length, 3 * D), (pairs, length, 3 * D), BF16),
        ],
        [pltpu.VMEM((D, 3 * D), BF16), sems],
        spent(0.1),
        "qkv",
    )

    near_b = set_b[2]
    set_b = spread_pieces(set_b, n1)
    (mixed,) = call(
        mix_kernel,
        (pairs,),
        [],
        [(qkv, pair_spec(length, 3 * D))],
        [(pair_spec(length, D), (pairs, length, D), BF16)],
        [],
        spent(1),
        "mix",
        [near_b],
    )

    set_b = last_piece(set_b, mixed)
    h1, n2, z, slope = call(
        functools.partial(fc1_kernel, rows_d),
        (pairs,),
        [place],
        [
            (tokp, pair_spec(length, D)),
            (img, pair_spec(length, LANES)),
            (mixed, pair_spec(length, D)),
            vec_in,
        ]
        + piece_ins(set_b),
        [
            (pair_spec(length, D), (pairs, length, D), F32),
            (pair_spec(length, D), (pairs, length, D), BF16),
            (pair_spec(length, FF), (pairs, length, FF), BF16),
            (pair_spec(slots, FF), (pairs, slots, FF), BF16),
        ],
        [pltpu.VMEM((D, D), BF16), pltpu.VMEM((D, FF), BF16), sems, sems],
        spent(18),
        "fc1",
    )

    def top_rows(cols, idx=lambda i, *_: (0, 0, 0)):
        return pl.BlockSpec((pairs, slots, cols), idx)

    def grad_outs(rows, cols, chunk):
        block = rows // nd
        if block % 8:
            return [(pl.BlockSpec((rows, chunk), lambda i, *_: (0, i)), (rows, cols), BF16)]
        spec = pl.BlockSpec((nd // 2, block, chunk), lambda i, *_: (0, 0, i))
        return [(spec, (nd // 2, block, cols), BF16)] * 2

    def grad_sum(outs):
        if len(outs) == 1:
            rows, cols = outs[0].shape
            blocks = jnp.take(outs[0].reshape(nd, rows // nd, cols), tab[OWN : OWN + nd], axis=0)
            outs = [blocks[: nd // 2], blocks[nd // 2 :]]
        return Sum(plan, call, *outs)

    set_c = spread_pieces(set_c, n2)

    chunk = 2 * LANES
    *got, gb2 = call(
        gw2_kernel,
        (D // chunk,),
        [owners],
        [
            (z, top_rows(FF)),
            (dy, top_rows(chunk, lambda i, *_: (0, 0, i))),
        ],
        grad_outs(FF, D, chunk) + [(pl.BlockSpec((1, chunk), lambda i, *_: (0, i)), (1, D), F32)],
        [pltpu.VMEM((FF, pairs * slots), BF16), pltpu.VMEM((FF, chunk), F32)],
        spent(8),
        "gw2",
    )
    sum_2 = grad_sum(got)
    set_c = last_piece(set_c, gb2)

    df, gb1 = call(
        functools.partial(df_kernel, rows_f),
        (PARTS,),
        [place],
        [(dy, top_rows(D)), (slope, top_rows(D, lambda i, *_: (0, 0, i)))] + piece_ins(set_c),
        [
            (pl.BlockSpec((pairs * slots, D), lambda i, *_: (0, i)), (pairs * slots, FF), BF16),
            (pl.BlockSpec((1, D), lambda i, *_: (0, i)), (1, FF), F32),
        ],
        [pltpu.VMEM((FF, D), BF16), sems],
        spent(7),
        "df",
    )
    sum_2.add()

    some = 2 if pairs % 2 == 0 else 1
    some_spec = pl.BlockSpec((some, slots, D), lambda i, *_: (i, 0, 0))
    dh, dhr, da, mlp_sum = call(
        functools.partial(mlp_back_kernel, rows_d),
        (pairs // some,),
        [place],
        [
            (df, pl.BlockSpec((some * slots, FF), lambda i, *_: (i, 0))),
            (dy, some_spec),
            (h1, some_spec),
            vec_in,
        ]
        + piece_ins(set_b),
        [
            (some_spec, (pairs, slots, D), F32),
            (some_spec, (pairs, slots, D), BF16),
            (some_spec, (pairs, slots, D), BF16),
            (full((8, D)), (8, D), F32),
        ],
        [pltpu.VMEM((D, FF), BF16), pltpu.VMEM((D, D), BF16), sems, sems],
        spent(10),
        "mlp_back",
    )

    got = call(
        gw1o_kernel,
        (PARTS + 1,),
        [owners],
        [
            (n2, top_rows(D)),
            (
                df,
                pl.BlockSpec((pairs * slots, D), lambda i, *_: (0, jnp.minimum(i, PARTS - 1))),
            ),
            (mixed, top_rows(D)),
            (dhr, top_rows(D)),
        ],
        grad_outs(D, FF + D, D),
        [pltpu.VMEM((D, pairs * slots), BF16), pltpu.VMEM((D, D), F32)],
        spent(9),
        "gw1o",
    )
    sum_1 = grad_sum(got)
    sum_2.add()

    part_pairs = pairs // 2 if pairs % 2 == 0 else pairs
    back = None
    for number in range(pairs // part_pairs):
        base = number * part_pairs
        at = lambda rows, cols, base=base: pl.BlockSpec(
            (1, rows, cols), lambda i, *_: (base + i, 0, 0)
        )
        ins = [(qkv, at(length, 3 * D)), (da, at(slots, D))]
        if back is not None:
            ins += [(back[0], ANYWHERE), (back[1], ANYWHERE), (back[2], full((8, D)))]
        back = call(
            functools.partial(attn_back_kernel, back is not None),
            (part_pairs,),
            [],
            ins,
            [
                (at(slots, D), (pairs, slots, D), BF16),
                (at(length, 2 * D), (pairs, length, 2 * D), BF16),
                (full((8, D)), (8, D), F32),
            ],
            [],
            spent(12),
            "attn_back",
            aliases=None if back is None else {2: 0, 3: 1},
        )
        if number == 0:
            sum_1.add()
        sum_2.add()
    dq, dkv, attn_sum = back

    got = call(
        gqkv_kernel,
        (3,),
        [owners],
        [
            (n1, full((pairs, length, D))),
            (dq, full((pairs, slots, D))),
            (
                dkv,
                pl.BlockSpec((pairs, length, D), lambda i, *_: (0, 0, jnp.where(i == 2, 1, 0))),
            ),
        ],
        grad_outs(D, 3 * D, D),
        [pltpu.VMEM((D, pairs * length), BF16), pltpu.VMEM((D, D), F32)],
        spent(9),
        "gqkv",
    )
    sum_3 = grad_sum(got)
    sum_1.add()

    fallback = (D // nd) % 8 != 0 or (FF // nd) % 8 != 0
    places = OWN + nd
    order = tab[places + nb :]

    def finish(total, which, masters, moments, extra=None):
        _, rows, cols = total.parts[0].shape
        grad = total.total(0, 1)[0]
        start, news, made = 0, [], []
        for kind, master, (first, second) in zip(which, masters, moments):
            width = master.shape[1]
            own = lax.dynamic_slice_in_dim(master, bi * rows, rows, 0)
            new_w, new_m, new_v = adamw(
                own,
                grad[:, start : start + width],
                first,
                second,
                STEP_RATES[kind],
                DECAY_RATES[kind],
            )
            news.append(new_w.astype(BF16))
            made += [new_m, new_v]
            start += width
        block = jnp.concatenate(news, axis=1)
        if extra is not None:
            block = jnp.concatenate([block, extra], axis=0)
        return Spread(plan, call, block[None]), made

    def put(moved, widths, rows):
        if not fallback:
            return moved.put(places, tab, widths, rows)
        blocks = jnp.concatenate([moved.blocks, moved.got], axis=0)[:, :rows]
        cols = blocks.shape[2]
        blocks = jnp.take(blocks, order, axis=0).reshape(nb * rows, cols).astype(F32)
        cuts = np.cumsum([0] + list(widths))
        return [blocks[:, a:b] for a, b in zip(cuts[:-1], cuts[1:])]

    sum_3.add()

    paced, call.last = call.last, sum_3.sent
    moved_2, (new_m2, new_v2) = finish(sum_2, (3,), (w_fc2,), ((m_fc2, v_fc2),), riders)
    call.last = paced

    grad_tokens, vec_sum = call(
        functools.partial(grad_in_kernel, rows_d),
        (pairs,),
        [place],
        [
            (tokp, pair_spec(length, D)),
            (img, pair_spec(length, LANES)),
            vec_in,
            (dq, pair_spec(slots, D)),
            (dkv, pair_spec(length, 2 * D)),
            (dh, pair_spec(slots, D)),
            (perm, pair_spec(length, length)),
            (attn_sum, full((8, D))),
            (mlp_sum, full((8, D))),
            (gb1, full((1, FF))),
            (gb2, full((1, D))),
        ]
        + piece_ins(set_a),
        [
            (pair_spec(length, D), (pairs, length, D), F32),
            (full((16, D)), (16, D), F32),
        ],
        [pltpu.VMEM((D, 3 * D), BF16), sems],
        spent(15),
        "grad_in",
    )

    vec_gens = [1] + plan.batch[1:] + plan.batch[:1] + [2]
    vec_got = plan.exchange(vec_sum, vec_gens[0])

    vec_place = 1

    def vec_step():
        nonlocal vec_sum, vec_got, vec_place
        if vec_place > len(vec_gens):
            return
        one, two = call.pin([vec_sum, vec_got])
        vec_sum = one + two
        if vec_place < len(vec_gens):
            vec_got = plan.exchange(vec_sum, vec_gens[vec_place])
        vec_place += 1

    last = plan.bbits
    sum_3.add()
    sum_1.add()
    moved_2.join()

    (layer_out,) = call(
        functools.partial(out_kernel, rows_f),
        (pairs,),
        [place],
        [
            (z, pair_spec(length, FF)),
            (h1, pair_spec(length, D)),
            vec_in,
            (perm, pair_spec(length, length)),
        ]
        + piece_ins(set_c),
        [(pair_spec(length, D), (pairs, length, D), BF16)],
        [pltpu.VMEM((FF, D), BF16), sems],
        spent(13),
        "out",
    )

    moved_1 = moved_3 = None
    while moved_3 is None or moved_3.place < last:
        token = None
        if sum_3.count > 1:
            sum_3.add()
            token = sum_3.sent
        elif moved_3 is None:
            moved_3, (new_mq, new_vq) = finish(sum_3, (0,), (w_qkv,), ((m_qkv, v_qkv),))
            token = moved_3.blocks
        else:
            moved_3.join()
            token = moved_3.blocks
        if sum_1.count > 1:
            sum_1.add()
        elif moved_1 is None:
            moved_1, (new_m1, new_v1, new_mo, new_vo) = finish(
                sum_1, (2, 1), (w_fc1, w_out), ((m_fc1, v_fc1), (m_out, v_out))
            )
        elif moved_1.place < last:
            moved_1.join()
        if moved_2.place < last:
            moved_2.join()
        vec_step()
        call.last = token
    while len(vec_gens) >= vec_place:
        vec_step()
    while moved_1.place < last:
        moved_1.join()
    while moved_2.place < last:
        moved_2.join()
    call.waiting = []
    tail = call.pin([moved_2.blocks, moved_2.got])
    (new_2,) = put(moved_2, (D,), FF // nd)
    call.last = None
    (new_q,) = put(moved_3, (3 * D,), D // nd)
    call.last = None
    new_1, new_o = put(moved_1, (FF, D), D // nd)

    own_cols = D // nd
    got = jnp.concatenate([part[:, FF // nd :] for part in tail], axis=0)
    half = rider_cols // 2
    held = got[:, :, :half].astype(F32) + got[:, :, half:rider_cols].astype(F32)
    held = held.reshape(nb, -1)[:, : 2 * NVEC * own_cols].reshape(nb, 2 * NVEC, own_cols)
    held = jnp.take(held, order, axis=0)
    states = jnp.transpose(held, (1, 0, 2)).reshape(2 * NVEC, nb * own_cols)
    grad_vec = lax.dynamic_slice_in_dim(vec_sum[:NVEC], fi * nb * own_cols, nb * own_cols, 1)
    vec_new, _, _ = adamw(
        vectors, grad_vec, states[:NVEC], states[NVEC:], STEP_RATES[4], DECAY_RATES[4]
    )
    own_grad = lax.dynamic_slice_in_dim(grad_vec, bi * own_cols, own_cols, 1)
    _, new_mv, new_vv = adamw(0.0, own_grad, m_vec, v_vec, STEP_RATES[4], DECAY_RATES[4])

    return (
        layer_out,
        grad_tokens,
        new_q,
        new_mq,
        new_vq,
        new_o,
        new_mo,
        new_vo,
        new_1,
        new_m1,
        new_v1,
        new_2,
        new_m2,
        new_v2,
        vec_new,
        new_mv,
        new_vv,
    )


def solution(mesh):
    pairs = P(("batch", "fsdp"), None, None)
    weight = P("fsdp", None)
    state = P(("fsdp", "batch"), None)
    vec_state = P(None, ("fsdp", "batch"))
    matrix = (weight, state, state)
    return jax.shard_map(
        functools.partial(shards, Plan(mesh)),
        mesh=mesh,
        in_specs=(pairs, pairs, P(("batch", "fsdp"), None), P(("batch", "fsdp")))
        + matrix * 4
        + (P(None, "fsdp"), vec_state, vec_state),
        out_specs=(pairs, pairs) + matrix * 4 + (P(None, "fsdp"), vec_state, vec_state),
        check_vma=False,
    )
```

```python
import functools
import math

import jax
import jax.numpy as jnp
import numpy as np
from jax import lax
from jax.experimental import pallas as pl
from jax.experimental.pallas import tpu as pltpu
from jax.sharding import PartitionSpec as P

D = 768
HEADS = 12
HDIM = 64
FF = 3072
TEXT = 40
STEP = 3
MAXM = 128
NVEC = 14
PARTS = FF // D
LANES = 128
SLABS = D // LANES

BETA_ONE = 0.5
BETA_TWO = 0.5
EPS_ADAM = 1e-08
STEP_RATES = (0.03, 0.1, 0.03, 0.015, 0.3)
DECAY_RATES = (0.01, 0.01, 0.01, 0.01, 0.0)
INV_ROOT_TWO = 1.0 / math.sqrt(2.0)
INV_ROOT_TWOPI = 1.0 / math.sqrt(2.0 * math.pi)

KERNEL_VMEM = 20 * 2**20
FLOPS_SCALE = 3e9
BYTES_SCALE = 1e7
F32 = jnp.float32
BF16 = jnp.bfloat16


def dot(a, b):
    return lax.dot_general(a, b, (((1,), (0,)), ((), ())), preferred_element_type=F32)


def dot_first(a, b):
    return lax.dot_general(a, b, (((0,), (0,)), ((), ())), preferred_element_type=F32)


def dot_last(a, b):
    return lax.dot_general(a, b, (((1,), (1,)), ((), ())), preferred_element_type=F32)


def normalize(hidden):
    row_mean = jnp.mean(hidden, axis=-1, keepdims=True)
    centred = hidden - row_mean
    inv_scale = lax.rsqrt(jnp.mean(centred * centred, axis=-1, keepdims=True) + 1e-06)
    return centred * inv_scale, inv_scale


def norm_back(gradient, normed, inv_scale, gain_row):
    scaled = gradient * gain_row
    return inv_scale * (
        scaled
        - jnp.mean(scaled, axis=-1, keepdims=True)
        - normed * jnp.mean(scaled * normed, axis=-1, keepdims=True)
    )


def adamw(weight, gradient, moment_one, moment_two, step_rate, decay_rate):
    new_first = BETA_ONE * moment_one + (1.0 - BETA_ONE) * gradient
    new_second = BETA_TWO * moment_two + (1.0 - BETA_TWO) * gradient * gradient
    correct_one = 1.0 - BETA_ONE**STEP
    correct_two = 1.0 - BETA_TWO**STEP
    update = (
        new_first / correct_one / (jnp.sqrt(new_second / correct_two) + EPS_ADAM)
        + decay_rate * weight
    )
    return (weight - step_rate * update, new_first, new_second)


def spent(micros):
    return pl.CostEstimate(
        flops=int(micros * FLOPS_SCALE), bytes_accessed=int(micros * BYTES_SCALE), transcendentals=0
    )


def full(shape):
    zeros = (0,) * len(shape)
    return pl.BlockSpec(shape, lambda *_: zeros)


ANYWHERE = pl.BlockSpec(memory_space=pl.ANY)


class Plan:
    def __init__(self, mesh):
        self.nf = mesh.shape["fsdp"]
        self.nb = mesh.shape["batch"]
        self.nd = self.nf * self.nb
        self.fbits = self.nf.bit_length() - 1
        self.bbits = self.nb.bit_length() - 1
        assert self.nf == 1 << self.fbits and self.nb == 1 << self.bbits
        assert self.fbits == 2 and self.bbits >= 2
        near = [1, 2, 6] if self.bbits == 3 else [1 << k for k in range(self.bbits)]
        self.batch = [mask * self.nf for mask in near]
        first, second, *rest = self.batch
        self.scatter = ([1, first, second] + rest + [2], [1, second, first, 2] + rest)
        self.gather = (rest[::-1] + [second, first], rest[::-1] + [first, second])
        self.helper = (first, second)

    def exchange(self, value, even, odd=None):
        odd = even if odd is None else odd
        pairs = [(i, i ^ (odd if i & 1 else even)) for i in range(self.nd)]
        return lax.ppermute(value, ("batch", "fsdp"), pairs)

    def spans(self, gens):
        masks = np.zeros(1, np.int32)
        for mask in reversed(gens):
            masks = np.concatenate([masks, masks ^ mask])
        return masks

    def table(self):
        rows = []
        for index in range(self.nd):
            core, fi, bi = index & 1, index & (self.nf - 1), index >> self.fbits
            halves = (bi & 1, (bi >> 1) & 1)
            keep = index ^ self.spans(self.scatter[core][1:])
            send = (index ^ 1) ^ self.spans(self.scatter[1 - core][1:])
            order = np.concatenate([keep, send])
            owners = (order & (self.nf - 1)) * self.nb + (order >> self.fbits)
            places = bi ^ (self.spans(self.gather[core][::-1]) >> self.fbits)
            own = np.asarray([fi, halves[core], halves[1 - core], bi])
            rows.append(np.concatenate([own, owners, places, np.argsort(places)]))
        return np.stack(rows).astype(np.int32)


OWN = 4


PIECES = ((0, None), (1, None), (2, 0), (2, 1), (3, 2), (3, 3))


def piece_copies(refs, target, sems, place_ref, rows, start=0):
    copies = []
    cols = target.shape[1]
    for number, ((mask, kind), ref) in enumerate(zip(PIECES, refs)):
        row = (place_ref[0] ^ mask) * rows
        length = rows
        if kind is not None:
            length = rows // 2
            low = place_ref[1 + kind // 2]
            row = row + (low if kind % 2 == 0 else 1 - low) * length
        copies.append(
            pltpu.make_async_copy(
                ref.at[:, pl.ds(start, cols)],
                target.at[pl.ds(pl.multiple_of(row, 8), length)],
                sems.at[number],
            )
        )
    return copies


def start_all(copies):
    for copy in copies:
        copy.start()


def wait_all(copies):
    for copy in copies:
        copy.wait()


def cast_kernel(place_ref, *refs):
    parts, (shard_ref, mine_ref) = refs[:-2], refs[-2:]
    start = 0
    for part in parts:
        cols = slice(start, start + part.shape[1])
        low = part[...].astype(BF16)
        shard_ref[:, cols] = low

        @pl.when(pl.program_id(0) == 0)
        def _(low=low, cols=cols):
            mine_ref[:, cols] = low

        start += part.shape[1]


def order_kernel(count_ref, pos_ref, tok_ref, cot_ref, perm_ref, tokp_ref, img_ref, dy_ref):
    pair = pl.program_id(0)
    length = tok_ref.shape[1]
    slots = pos_ref.shape[2]
    token = lax.broadcasted_iota(jnp.int32, (length, slots), 0)
    slot = lax.broadcasted_iota(jnp.int32, (length, slots), 1)
    hit = jnp.where(token == pos_ref[0], 1.0, 0.0)
    free = 1.0 - jnp.sum(hit, axis=1, keepdims=True)
    below = lax.broadcasted_iota(jnp.int32, (length, length), 1) < lax.broadcasted_iota(
        jnp.int32, (length, length), 0
    )
    rank = dot(
        jnp.where(below, 1.0, 0.0).astype(BF16),
        jnp.broadcast_to(free, (length, slots)).astype(BF16),
    )
    rest = jnp.where(rank == slot.astype(F32), jnp.broadcast_to(free, (length, slots)), 0.0)
    perm = jnp.concatenate([hit, rest], axis=1).astype(BF16)
    perm_ref[0] = perm
    tokp_ref[0] = dot_first(perm, tok_ref[0]).astype(BF16)
    image = jnp.where(lax.broadcasted_iota(jnp.int32, (length, LANES), 0) >= TEXT, 1.0, 0.0)
    img_ref[0] = dot_first(perm, image.astype(BF16)).astype(BF16)
    chosen = dot_first(perm[:, :slots], cot_ref[0])
    live = lax.broadcasted_iota(jnp.int32, (slots, 1), 0) < count_ref[pair]
    dy_ref[0] = jnp.where(live, chosen, 0.0).astype(BF16)


def start_row(tok_ref, img_ref, vec_ref):
    return tok_ref[0].astype(F32) + jnp.where(
        img_ref[0][:, :1].astype(F32) > 0.5, vec_ref[1:2, :], vec_ref[0:1, :]
    )


def qkv_kernel(rows, place_ref, tok_ref, img_ref, vec_ref, *refs):
    pieces = refs[: len(PIECES)]
    n1_ref, qkv_ref, w_ref, sems = refs[len(PIECES) :]
    first = pl.program_id(0) == 0
    copies = piece_copies(pieces, w_ref, sems, place_ref, rows)

    @pl.when(first)
    def _():
        start_all(copies)

    normed, _ = normalize(start_row(tok_ref, img_ref, vec_ref))
    n1 = (normed * vec_ref[2:3, :] + vec_ref[3:4, :]).astype(BF16)
    n1_ref[0] = n1

    @pl.when(first)
    def _():
        wait_all(copies)

    qkv_ref[0, :, :D] = (dot(n1, w_ref[:, :D]) + vec_ref[4:5, :]).astype(BF16)
    qkv_ref[0, :, D : 2 * D] = dot(n1, w_ref[:, D : 2 * D]).astype(BF16)
    qkv_ref[0, :, 2 * D :] = (dot(n1, w_ref[:, 2 * D :]) + vec_ref[5:6, :]).astype(BF16)


def mix_kernel(qkv_ref, a_ref):
    low = lax.broadcasted_iota(jnp.int32, (1, LANES), 1) < HDIM
    for slab in range(SLABS):
        cols = slice(slab * LANES, (slab + 1) * LANES)
        q = qkv_ref[0, :, cols] * jnp.asarray(HDIM**-0.5, BF16)
        k = qkv_ref[0, :, D + slab * LANES : D + (slab + 1) * LANES]
        v = qkv_ref[0, :, 2 * D + slab * LANES : 2 * D + (slab + 1) * LANES]
        outs = []
        for head in range(2):
            mine = low if head == 0 else jnp.logical_not(low)
            scores = dot_last(jnp.where(mine, q, jnp.zeros_like(q)), k)
            e = jnp.exp(scores - jnp.max(scores, axis=-1, keepdims=True))
            inverse = 1.0 / jnp.sum(e, axis=-1, keepdims=True)
            outs.append(dot(e.astype(BF16), v) * inverse)
        a_ref[0, :, cols] = jnp.where(low, outs[0], outs[1]).astype(BF16)


def fc1_kernel(rows, place_ref, tok_ref, img_ref, a_ref, vec_ref, *refs):
    pieces = refs[: len(PIECES)]
    h1_ref, n2_ref, z_ref, slope_ref, wo_ref, w1_ref, sem_o, sem_1 = refs[len(PIECES) :]
    first = pl.program_id(0) == 0
    copies_o = piece_copies(pieces, wo_ref, sem_o, place_ref, rows)
    copies_1 = piece_copies(pieces, w1_ref, sem_1, place_ref, rows, D)

    @pl.when(first)
    def _():
        start_all(copies_o)
        start_all(copies_1)
        wait_all(copies_o)

    h1 = start_row(tok_ref, img_ref, vec_ref) + dot(a_ref[0], wo_ref[...]) + vec_ref[6:7, :]
    h1_ref[0] = h1
    normed, _ = normalize(h1)
    n2 = (normed * vec_ref[7:8, :] + vec_ref[8:9, :]).astype(BF16)
    n2_ref[0] = n2

    @pl.when(first)
    def _():
        wait_all(copies_1)

    slots = slope_ref.shape[1]
    for part in range(PARTS):
        cols = slice(part * D, (part + 1) * D)
        f = dot(n2, w1_ref[:, cols]) + vec_ref[9 + part : 10 + part, :]
        phi = 0.5 * (1.0 + lax.erf(f * INV_ROOT_TWO))
        z_ref[0, :, cols] = (f * phi).astype(BF16)
        fs = f[:slots]
        slope = phi[:slots] + fs * jnp.exp(-0.5 * fs * fs) * INV_ROOT_TWOPI
        slope_ref[0, :, cols] = slope.astype(BF16)


def spread(acc_ref, owners_ref, outs):
    if len(outs) == 1:
        outs[0][...] = acc_ref[...].astype(BF16)
        return
    keep_ref, send_ref = outs
    half, block, _ = send_ref.shape

    def one(spot, _):
        for out_ref, base in ((send_ref, half), (keep_ref, 0)):
            start = pl.multiple_of(owners_ref[OWN + base + spot] * block, 8)
            out_ref[spot] = acc_ref[pl.ds(start, block), :].astype(BF16)
        return 0

    lax.fori_loop(0, half, one, 0)


def gw2_kernel(owners_ref, z_ref, dy_ref, *refs):
    outs, (sum_ref, zt_ref, acc_ref) = refs[:-3], refs[-3:]
    pairs, slots, width = z_ref.shape

    @pl.when(pl.program_id(0) == 0)
    def _():
        zt_ref[...] = z_ref[...].reshape(pairs * slots, width).T

    dy = dy_ref[...].reshape(pairs * slots, -1)
    acc_ref[...] = dot(zt_ref[...], dy)
    sum_ref[...] = jnp.sum(dy.astype(F32), axis=0, keepdims=True)
    spread(acc_ref, owners_ref, outs)


def df_kernel(rows, place_ref, dy_ref, slope_ref, *refs):
    pieces = refs[: len(PIECES)]
    df_ref, gb1_ref, w2_ref, sems = refs[len(PIECES) :]
    step = pl.program_id(0)
    pairs, slots, width = slope_ref.shape
    total = pairs * slots
    copies = piece_copies(pieces, w2_ref, sems, place_ref, rows)

    @pl.when(step == 0)
    def _():
        start_all(copies)
        wait_all(copies)

    dz = dot_last(
        dy_ref[...].reshape(total, D), w2_ref[pl.ds(pl.multiple_of(step * width, 8), width), :]
    )
    df = dz * slope_ref[...].reshape(total, width).astype(F32)
    gb1_ref[...] = jnp.sum(df, axis=0, keepdims=True)
    df_ref[...] = df.astype(BF16)


def mlp_back_kernel(rows, place_ref, df_ref, dy_ref, h1_ref, vec_ref, *refs):
    pieces = refs[: len(PIECES)]
    dh_ref, dhr_ref, da_ref, sum_ref, w1_ref, wo_ref, sem_1, sem_o = refs[len(PIECES) :]
    first = pl.program_id(0) == 0
    copies_1 = piece_copies(pieces, w1_ref, sem_1, place_ref, rows, D)
    copies_o = piece_copies(pieces, wo_ref, sem_o, place_ref, rows)

    @pl.when(first)
    def _():
        start_all(copies_1)
        start_all(copies_o)
        sum_ref[...] = jnp.zeros_like(sum_ref)
        wait_all(copies_1)
        wait_all(copies_o)

    some, slots, _ = dy_ref.shape
    total = some * slots
    dn2 = dot_last(df_ref[...], w1_ref[...])
    normed, scale = normalize(h1_ref[...].reshape(total, D))
    dh = dy_ref[...].reshape(total, D).astype(F32) + norm_back(dn2, normed, scale, vec_ref[7:8, :])
    dh_ref[...] = dh.reshape(some, slots, D)
    sum_ref[0:1, :] += jnp.sum(dh, axis=0, keepdims=True)
    sum_ref[1:2, :] += jnp.sum(dn2 * normed, axis=0, keepdims=True)
    sum_ref[2:3, :] += jnp.sum(dn2, axis=0, keepdims=True)
    low = dh.astype(BF16)
    dhr_ref[...] = low.reshape(some, slots, D)
    da_ref[...] = dot_last(low, wo_ref[...]).astype(BF16).reshape(some, slots, D)


def gw1o_kernel(owners_ref, n2_ref, df_ref, a_ref, dhr_ref, *refs):
    outs, (n2t_ref, acc_ref) = refs[:-2], refs[-2:]
    step = pl.program_id(0)
    pairs, slots, _ = n2_ref.shape
    total = pairs * slots

    @pl.when(step == 0)
    def _():
        n2t_ref[...] = n2_ref[...].reshape(total, D).T

    @pl.when(step < PARTS)
    def _():
        acc_ref[...] = dot(n2t_ref[...], df_ref[...])

    @pl.when(step == PARTS)
    def _():
        acc_ref[...] = dot_first(a_ref[...].reshape(total, D), dhr_ref[...].reshape(total, D))

    spread(acc_ref, owners_ref, outs)


def attn_back_kernel(more, qkv_ref, da_ref, *refs):
    if more:
        _, _, before_ref, dq_ref, dkv_ref, sum_ref = refs
    else:
        dq_ref, dkv_ref, sum_ref = refs
    slots = da_ref.shape[1]

    @pl.when(pl.program_id(0) == 0)
    def _():
        sum_ref[...] = before_ref[...] if more else jnp.zeros_like(sum_ref)

    low = lax.broadcasted_iota(jnp.int32, (1, LANES), 1) < HDIM
    scale = jnp.asarray(HDIM**-0.5, BF16)
    for slab in range(SLABS):
        cols = slice(slab * LANES, (slab + 1) * LANES)
        q = qkv_ref[0, :slots, cols] * scale
        k = qkv_ref[0, :, D + slab * LANES : D + (slab + 1) * LANES]
        v = qkv_ref[0, :, 2 * D + slab * LANES : 2 * D + (slab + 1) * LANES]
        da = da_ref[0, :, cols]
        gqs, gks, gvs = [], [], []
        for head in range(2):
            mine = low if head == 0 else jnp.logical_not(low)
            zero = jnp.zeros_like(q)
            scores = dot_last(k, jnp.where(mine, q, zero))
            e = jnp.exp(scores - jnp.max(scores, axis=0, keepdims=True))
            p = e * (1.0 / jnp.sum(e, axis=0, keepdims=True))
            gvs.append(dot(p.astype(BF16), da))
            dp = dot_last(v, jnp.where(mine, da, zero))
            ds = (p * (dp - jnp.sum(p * dp, axis=0, keepdims=True))).astype(BF16)
            gqs.append(dot_first(ds, k))
            gks.append(dot(ds, q))
        gq = jnp.where(low, gqs[0], gqs[1]) * (HDIM**-0.5)
        gk = jnp.where(low, gks[0], gks[1])
        gv = jnp.where(low, gvs[0], gvs[1])
        dq_ref[0, :, cols] = gq.astype(BF16)
        dkv_ref[0, :, cols] = gk.astype(BF16)
        dkv_ref[0, :, D + slab * LANES : D + (slab + 1) * LANES] = gv.astype(BF16)
        sum_ref[0:1, cols] += jnp.sum(gq, axis=0, keepdims=True)
        sum_ref[1:2, cols] += jnp.sum(gv, axis=0, keepdims=True)


def gqkv_kernel(owners_ref, n1_ref, dq_ref, dkv_ref, *refs):
    outs, (n1t_ref, acc_ref) = refs[:-2], refs[-2:]
    step = pl.program_id(0)
    pairs, length, _ = n1_ref.shape
    slots = dq_ref.shape[1]

    @pl.when(step == 0)
    def _():
        n1t_ref[...] = n1_ref[...].reshape(pairs * length, D).T
        total = dot(n1t_ref[:, :slots], dq_ref[0])
        for pair in range(1, pairs):
            total += dot(n1t_ref[:, pair * length : pair * length + slots], dq_ref[pair])
        acc_ref[...] = total

    @pl.when(step > 0)
    def _():
        acc_ref[...] = dot(n1t_ref[...], dkv_ref[...].reshape(pairs * length, D))

    spread(acc_ref, owners_ref, outs)


def split_two(value):
    one = value.astype(BF16)
    return one, (value - one.astype(F32)).astype(BF16)


def grad_in_kernel(
    rows,
    place_ref,
    tok_ref,
    img_ref,
    vec_ref,
    dq_ref,
    dkv_ref,
    dh_ref,
    perm_ref,
    attn_sum_ref,
    mlp_sum_ref,
    gb1_ref,
    gb2_ref,
    *refs,
):
    pieces = refs[: len(PIECES)]
    out_ref, sum_ref, w_ref, sems = refs[len(PIECES) :]
    first = pl.program_id(0) == 0
    slots = dq_ref.shape[1]
    copies = piece_copies(pieces, w_ref, sems, place_ref, rows)

    @pl.when(first)
    def _():
        start_all(copies)
        sum_ref[...] = jnp.zeros_like(sum_ref)
        sum_ref[4:6, :] = attn_sum_ref[0:2, :]
        sum_ref[6:9, :] = mlp_sum_ref[0:3, :]
        for part in range(PARTS):
            sum_ref[9 + part : 10 + part, :] = gb1_ref[:, part * D : (part + 1) * D]
        sum_ref[9 + PARTS : 10 + PARTS, :] = gb2_ref[...]
        wait_all(copies)

    dn_all = dot_last(dkv_ref[0], w_ref[:, D:])
    dn_top = dn_all[:slots] + dot_last(dq_ref[0], w_ref[:, :D])
    dn = jnp.concatenate([dn_top, dn_all[slots:]], axis=0)
    normed, scale = normalize(start_row(tok_ref, img_ref, vec_ref))
    grad = norm_back(dn, normed, scale, vec_ref[2:3, :])
    grad = jnp.concatenate([grad[:slots] + dh_ref[0], grad[slots:]], axis=0)
    image = img_ref[0][:, :1].astype(F32) > 0.5
    sum_ref[0:1, :] += jnp.sum(jnp.where(image, 0.0, grad), axis=0, keepdims=True)
    sum_ref[1:2, :] += jnp.sum(jnp.where(image, grad, 0.0), axis=0, keepdims=True)
    sum_ref[2:3, :] += jnp.sum(dn * normed, axis=0, keepdims=True)
    sum_ref[3:4, :] += jnp.sum(dn, axis=0, keepdims=True)
    one, two = split_two(grad)
    perm = perm_ref[0]
    out_ref[0] = dot(perm, one) + dot(perm, two)


def out_kernel(rows, place_ref, z_ref, h1_ref, vec_ref, perm_ref, *refs):
    pieces = refs[: len(PIECES)]
    out_ref, w_ref, sems = refs[len(PIECES) :]
    first = pl.program_id(0) == 0
    copies = piece_copies(pieces, w_ref, sems, place_ref, rows)

    @pl.when(first)
    def _():
        start_all(copies)
        wait_all(copies)

    y = h1_ref[0] + dot(z_ref[0], w_ref[...]) + vec_ref[9 + PARTS : 10 + PARTS, :]
    out_ref[0] = dot(perm_ref[0], y.astype(BF16)).astype(BF16)


def place_kernel(number, base, rows, spots_ref, one_ref, two_ref, *refs):
    step = pl.program_id(0)
    count = one_ref.shape[0]

    def put(out_ref):
        def one(spot, _):
            for source, first in ((one_ref, base), (two_ref, base + count)):
                at = pl.ds(pl.multiple_of(spots_ref[first + spot] * rows, 8), rows)
                out_ref[at, :] = source[spot, :rows].astype(F32)
            return 0

        lax.fori_loop(0, count, one, 0)

    if number == 1:
        put(refs[0])
        return
    last = pl.num_programs(0) - 1

    @pl.when(step < last)
    def _():
        put(refs[0])

    @pl.when(step == last)
    def _():
        put(refs[1])


def later(value, dep):
    return lax.optimization_barrier((value, dep))[0]


class Chain:
    def __init__(self):
        self.last, self.waiting = None, []

    def pin(self, values):
        return lax.optimization_barrier((list(values), self.last))[0]

    def hold(self, value):
        self.waiting.append(value)
        return value

    def __call__(
        self, kernel, grid, scalars, ins, outs, scratch, estimate, name, after=(), aliases=None
    ):
        deps = list(after) + self.waiting
        self.waiting = []
        if self.last is not None:
            deps.append(self.last)
        fixed = len(scalars) + len(ins)
        extra = len(deps)

        def body(*refs):
            kernel(*refs[:fixed], *refs[fixed + extra :])

        got = pl.pallas_call(
            body,
            grid_spec=pltpu.PrefetchScalarGridSpec(
                num_scalar_prefetch=len(scalars),
                grid=grid,
                in_specs=[spec for _, spec in ins] + [ANYWHERE] * extra,
                out_specs=[spec for spec, _, _ in outs],
                scratch_shapes=scratch,
            ),
            out_shape=[jax.ShapeDtypeStruct(dims, kind) for _, dims, kind in outs],
            input_output_aliases={
                len(scalars) + k: v for k, v in (aliases or {}).items()
            },
            cost_estimate=estimate,
            compiler_params=pltpu.CompilerParams(vmem_limit_bytes=KERNEL_VMEM),
            name=name,
        )(*scalars, *[value for value, _ in ins], *deps)
        self.last = got[-1]
        return got


class Sum:
    def __init__(self, plan, call, keep, send):
        self.plan, self.call = plan, call
        self.parts, self.count, self.place = [keep], keep.shape[0], 0
        self.move(send)

    def move(self, send):
        got = self.plan.exchange(send, *(order[self.place] for order in self.plan.scatter))
        self.parts.append(got)
        self.place += 1

    def total(self, low, high):
        parts = self.call.pin(self.parts)
        total = parts[0][low:high].astype(F32)
        for part in parts[1:]:
            total = total + part[low:high].astype(F32)
        return total

    def add(self):
        self.count //= 2
        total = self.total(self.count, 2 * self.count)
        self.sent = self.call.hold(total.astype(BF16))
        self.move(self.sent)


class Spread:
    def __init__(self, plan, call, block):
        self.plan, self.call, self.place = plan, call, 0
        self.move(block)

    def move(self, blocks):
        self.blocks = self.call.hold(blocks)
        self.got = self.plan.exchange(blocks, *(order[self.place] for order in self.plan.gather))
        self.place += 1

    def join(self):
        self.move(jnp.concatenate(self.call.pin([self.blocks, self.got]), axis=0))

    def put(self, base, tab, widths, rows):
        count, whole, cols = self.blocks.shape
        step = D if len(widths) > 1 or cols > D else D // 3
        last = widths[0] // step - 1
        ins = [
            (value, pl.BlockSpec((count, whole, step), lambda i, *_: (0, 0, i)))
            for value in (self.blocks, self.got)
        ]
        maps = [lambda i, *_: (0, jnp.minimum(i, last)), lambda i, *_: (0, 0)]
        return self.call(
            functools.partial(place_kernel, len(widths), base, rows),
            (cols // step,),
            [tab],
            ins,
            [
                (pl.BlockSpec((2 * count * rows, step), idx), (2 * count * rows, width), F32)
                for idx, width in zip(maps, widths)
            ],
            [],
            spent(1),
            "place",
        )


def shards(
    plan,
    tokens,
    cotangent,
    mask_pos,
    mask_count,
    w_qkv,
    m_qkv,
    v_qkv,
    w_out,
    m_out,
    v_out,
    w_fc1,
    m_fc1,
    v_fc1,
    w_fc2,
    m_fc2,
    v_fc2,
    vectors,
    m_vec,
    v_vec,
):
    pairs, length, _ = tokens.shape
    slots = mask_pos.shape[1]
    nf, nb, nd = plan.nf, plan.nb, plan.nd
    fi = lax.axis_index("fsdp").astype(jnp.int32)
    bi = lax.axis_index("batch").astype(jnp.int32)
    tab = lax.dynamic_index_in_dim(jnp.asarray(plan.table()), bi * nf + fi, 0, keepdims=False)
    place = owners = tab
    call = Chain()


    def pair_spec(rows, cols):
        return pl.BlockSpec((1, rows, cols), lambda i, *_: (i, 0, 0))

    def piece_ins(pieces):
        return [(value, pl.BlockSpec(memory_space=pltpu.HBM)) for value in pieces]

    sems = pltpu.SemaphoreType.DMA((len(PIECES),))
    rows_d, rows_f = D // nf, FF // nf

    low_vec = vectors.astype(BF16)
    vec_far = plan.exchange(low_vec, 2)
    vec_parts = [low_vec, plan.exchange(low_vec, 1), vec_far, plan.exchange(vec_far, 1)]
    columns = []
    for spot in range(nf):
        chosen = vec_parts[0]
        for mask in range(1, nf):
            chosen = jnp.where((fi ^ mask) == spot, vec_parts[mask], chosen)
        columns.append(chosen)
    vec = jnp.concatenate(columns, axis=1).astype(F32)
    vec = jnp.pad(vec, ((0, 16 - NVEC), (0, 0)))
    vec_in = (vec, full(vec.shape))

    def cast(shard_list, after=()):
        rows = shard_list[0].shape[0]
        half = rows // 2
        cols = sum(value.shape[1] for value in shard_list)
        row = lambda i, place_ref: (i ^ place_ref[1], 0)
        shard, mine = call(
            cast_kernel,
            (2,),
            [place],
            [(value, pl.BlockSpec((half, value.shape[1]), row)) for value in shard_list],
            [
                (pl.BlockSpec((half, cols), row), (rows, cols), BF16),
                (pl.BlockSpec((half, cols), lambda i, *_: (0, 0)), (half, cols), BF16),
            ],
            [],
            spent(0.1),
            "cast",
            after,
        )
        return [shard, plan.exchange(shard, 1), plan.exchange(mine, 2)]

    def spread_pieces(pieces, dep=None):
        near = pieces[2]
        ready = near if dep is None else later(near, dep)
        other = plan.exchange(ready, *plan.helper)
        return pieces[:2] + [near, other, plan.exchange(ready, 1)]

    def last_piece(pieces, dep=None):
        other = pieces[3]
        return pieces + [plan.exchange(other if dep is None else later(other, dep), 1)]

    set_a = cast([w_qkv])

    perm, tokp, img, dy = call(
        order_kernel,
        (pairs,),
        [mask_count],
        [
            (mask_pos.reshape(pairs, 1, slots), pl.BlockSpec((1, 1, slots), lambda i, *_: (i, 0, 0))),
            (tokens, pair_spec(length, D)),
            (cotangent, pair_spec(length, D)),
        ],
        [
            (pair_spec(length, length), (pairs, length, length), BF16),
            (pair_spec(length, D), (pairs, length, D), BF16),
            (pair_spec(length, LANES), (pairs, length, LANES), BF16),
            (pair_spec(slots, D), (pairs, slots, D), BF16),
        ],
        [],
        spent(6),
        "order",
    )

    set_b = cast([w_out, w_fc1])
    set_a = last_piece(spread_pieces(set_a, [set_b[0]] + vec_parts))

    n1, qkv = call(
        functools.partial(qkv_kernel, rows_d),
        (pairs,),
        [place],
        [(tokp, pair_spec(length, D)), (img, pair_spec(length, LANES)), vec_in] + piece_ins(set_a),
        [
            (pair_spec(length, D), (pairs, length, D), BF16),
            (pair_spec(length, 3 * D), (pairs, length, 3 * D), BF16),
        ],
        [pltpu.VMEM((D, 3 * D), BF16), sems],
        spent(0.1),
        "qkv",
    )

    near_b = set_b[2]
    set_b = spread_pieces(set_b, n1)
    (mixed,) = call(
        mix_kernel,
        (pairs,),
        [],
        [(qkv, pair_spec(length, 3 * D))],
        [(pair_spec(length, D), (pairs, length, D), BF16)],
        [],
        spent(1),
        "mix",
        [near_b],
    )

    set_b = last_piece(set_b, mixed)
    set_c = cast([w_fc2])
    h1, n2, z, slope = call(
        functools.partial(fc1_kernel, rows_d),
        (pairs,),
        [place],
        [
            (tokp, pair_spec(length, D)),
            (img, pair_spec(length, LANES)),
            (mixed, pair_spec(length, D)),
            vec_in,
        ]
        + piece_ins(set_b),
        [
            (pair_spec(length, D), (pairs, length, D), F32),
            (pair_spec(length, D), (pairs, length, D), BF16),
            (pair_spec(length, FF), (pairs, length, FF), BF16),
            (pair_spec(slots, FF), (pairs, slots, FF), BF16),
        ],
        [pltpu.VMEM((D, D), BF16), pltpu.VMEM((D, FF), BF16), sems, sems],
        spent(18),
        "fc1",
    )

    def top_rows(cols, idx=lambda i, *_: (0, 0, 0)):
        return pl.BlockSpec((pairs, slots, cols), idx)

    def grad_outs(rows, cols, chunk):
        block = rows // nd
        if block % 8:
            return [(pl.BlockSpec((rows, chunk), lambda i, *_: (0, i)), (rows, cols), BF16)]
        spec = pl.BlockSpec((nd // 2, block, chunk), lambda i, *_: (0, 0, i))
        return [(spec, (nd // 2, block, cols), BF16)] * 2

    def grad_sum(outs):
        if len(outs) == 1:
            rows, cols = outs[0].shape
            blocks = jnp.take(outs[0].reshape(nd, rows // nd, cols), tab[OWN : OWN + nd], axis=0)
            outs = [blocks[: nd // 2], blocks[nd // 2 :]]
        return Sum(plan, call, *outs)

    set_c = spread_pieces(set_c, n2)

    chunk = 2 * LANES
    *got, gb2 = call(
        gw2_kernel,
        (D // chunk,),
        [owners],
        [
            (z, top_rows(FF)),
            (dy, top_rows(chunk, lambda i, *_: (0, 0, i))),
        ],
        grad_outs(FF, D, chunk) + [(pl.BlockSpec((1, chunk), lambda i, *_: (0, i)), (1, D), F32)],
        [pltpu.VMEM((FF, pairs * slots), BF16), pltpu.VMEM((FF, chunk), F32)],
        spent(8),
        "gw2",
    )
    sum_2 = grad_sum(got)
    set_c = last_piece(set_c, gb2)

    df, gb1 = call(
        functools.partial(df_kernel, rows_f),
        (PARTS,),
        [place],
        [(dy, top_rows(D)), (slope, top_rows(D, lambda i, *_: (0, 0, i)))] + piece_ins(set_c),
        [
            (pl.BlockSpec((pairs * slots, D), lambda i, *_: (0, i)), (pairs * slots, FF), BF16),
            (pl.BlockSpec((1, D), lambda i, *_: (0, i)), (1, FF), F32),
        ],
        [pltpu.VMEM((FF, D), BF16), sems],
        spent(7),
        "df",
    )
    sum_2.add()

    some = 2 if pairs % 2 == 0 else 1
    some_spec = pl.BlockSpec((some, slots, D), lambda i, *_: (i, 0, 0))
    dh, dhr, da, mlp_sum = call(
        functools.partial(mlp_back_kernel, rows_d),
        (pairs // some,),
        [place],
        [
            (df, pl.BlockSpec((some * slots, FF), lambda i, *_: (i, 0))),
            (dy, some_spec),
            (h1, some_spec),
            vec_in,
        ]
        + piece_ins(set_b),
        [
            (some_spec, (pairs, slots, D), F32),
            (some_spec, (pairs, slots, D), BF16),
            (some_spec, (pairs, slots, D), BF16),
            (full((8, D)), (8, D), F32),
        ],
        [pltpu.VMEM((D, FF), BF16), pltpu.VMEM((D, D), BF16), sems, sems],
        spent(10),
        "mlp_back",
    )

    got = call(
        gw1o_kernel,
        (PARTS + 1,),
        [owners],
        [
            (n2, top_rows(D)),
            (
                df,
                pl.BlockSpec((pairs * slots, D), lambda i, *_: (0, jnp.minimum(i, PARTS - 1))),
            ),
            (mixed, top_rows(D)),
            (dhr, top_rows(D)),
        ],
        grad_outs(D, FF + D, D),
        [pltpu.VMEM((D, pairs * slots), BF16), pltpu.VMEM((D, D), F32)],
        spent(9),
        "gw1o",
    )
    sum_1 = grad_sum(got)
    sum_2.add()

    part_pairs = pairs // 2 if pairs % 2 == 0 else pairs
    back = None
    for number in range(pairs // part_pairs):
        base = number * part_pairs
        at = lambda rows, cols, base=base: pl.BlockSpec(
            (1, rows, cols), lambda i, *_: (base + i, 0, 0)
        )
        ins = [(qkv, at(length, 3 * D)), (da, at(slots, D))]
        if back is not None:
            ins += [(back[0], ANYWHERE), (back[1], ANYWHERE), (back[2], full((8, D)))]
        back = call(
            functools.partial(attn_back_kernel, back is not None),
            (part_pairs,),
            [],
            ins,
            [
                (at(slots, D), (pairs, slots, D), BF16),
                (at(length, 2 * D), (pairs, length, 2 * D), BF16),
                (full((8, D)), (8, D), F32),
            ],
            [],
            spent(12),
            "attn_back",
            aliases=None if back is None else {2: 0, 3: 1},
        )
        if number == 0:
            sum_1.add()
        sum_2.add()
    dq, dkv, attn_sum = back

    got = call(
        gqkv_kernel,
        (3,),
        [owners],
        [
            (n1, full((pairs, length, D))),
            (dq, full((pairs, slots, D))),
            (
                dkv,
                pl.BlockSpec((pairs, length, D), lambda i, *_: (0, 0, jnp.where(i == 2, 1, 0))),
            ),
        ],
        grad_outs(D, 3 * D, D),
        [pltpu.VMEM((D, pairs * length), BF16), pltpu.VMEM((D, D), F32)],
        spent(9),
        "gqkv",
    )
    sum_3 = grad_sum(got)
    sum_1.add()

    fallback = (D // nd) % 8 != 0 or (FF // nd) % 8 != 0
    places = OWN + nd
    order = tab[places + nb :]

    held = jnp.concatenate([m_vec, v_vec], axis=0).reshape(-1)
    held = jnp.pad(held, (0, -held.size % 8)).reshape(8, -1)
    riders = jnp.concatenate(split_two(held), axis=1)
    rider_cols = riders.shape[1]
    riders = jnp.pad(riders, ((0, 0), (0, D - rider_cols)))

    def finish(total, which, masters, moments, extra=None):
        _, rows, cols = total.parts[0].shape
        grad = total.total(0, 1)[0]
        start, news, made = 0, [], []
        for kind, master, (first, second) in zip(which, masters, moments):
            width = master.shape[1]
            own = lax.dynamic_slice_in_dim(master, bi * rows, rows, 0)
            new_w, new_m, new_v = adamw(
                own,
                grad[:, start : start + width],
                first,
                second,
                STEP_RATES[kind],
                DECAY_RATES[kind],
            )
            news.append(new_w.astype(BF16))
            made += [new_m, new_v]
            start += width
        block = jnp.concatenate(news, axis=1)
        if extra is not None:
            block = jnp.concatenate([block, extra], axis=0)
        return Spread(plan, call, block[None]), made

    def put(moved, widths, rows):
        if not fallback:
            return moved.put(places, tab, widths, rows)
        blocks = jnp.concatenate([moved.blocks, moved.got], axis=0)[:, :rows]
        cols = blocks.shape[2]
        blocks = jnp.take(blocks, order, axis=0).reshape(nb * rows, cols).astype(F32)
        cuts = np.cumsum([0] + list(widths))
        return [blocks[:, a:b] for a, b in zip(cuts[:-1], cuts[1:])]

    sum_3.add()

    paced, call.last = call.last, sum_3.sent
    moved_2, (new_m2, new_v2) = finish(sum_2, (3,), (w_fc2,), ((m_fc2, v_fc2),), riders)
    call.last = paced

    grad_tokens, vec_sum = call(
        functools.partial(grad_in_kernel, rows_d),
        (pairs,),
        [place],
        [
            (tokp, pair_spec(length, D)),
            (img, pair_spec(length, LANES)),
            vec_in,
            (dq, pair_spec(slots, D)),
            (dkv, pair_spec(length, 2 * D)),
            (dh, pair_spec(slots, D)),
            (perm, pair_spec(length, length)),
            (attn_sum, full((8, D))),
            (mlp_sum, full((8, D))),
            (gb1, full((1, FF))),
            (gb2, full((1, D))),
        ]
        + piece_ins(set_a),
        [
            (pair_spec(length, D), (pairs, length, D), F32),
            (full((16, D)), (16, D), F32),
        ],
        [pltpu.VMEM((D, 3 * D), BF16), sems],
        spent(15),
        "grad_in",
    )

    vec_gens = [1] + plan.batch[1:] + plan.batch[:1] + [2]
    vec_got = plan.exchange(vec_sum, vec_gens[0])

    vec_place = 1

    def vec_step():
        nonlocal vec_sum, vec_got, vec_place
        if vec_place > len(vec_gens):
            return
        one, two = call.pin([vec_sum, vec_got])
        vec_sum = one + two
        if vec_place < len(vec_gens):
            vec_got = plan.exchange(vec_sum, vec_gens[vec_place])
        vec_place += 1

    last = plan.bbits
    sum_3.add()
    sum_1.add()
    moved_2.join()

    (layer_out,) = call(
        functools.partial(out_kernel, rows_f),
        (pairs,),
        [place],
        [
            (z, pair_spec(length, FF)),
            (h1, pair_spec(length, D)),
            vec_in,
            (perm, pair_spec(length, length)),
        ]
        + piece_ins(set_c),
        [(pair_spec(length, D), (pairs, length, D), BF16)],
        [pltpu.VMEM((FF, D), BF16), sems],
        spent(13),
        "out",
    )

    moved_1 = moved_3 = None
    while moved_3 is None or moved_3.place < last:
        token = None
        if sum_3.count > 1:
            sum_3.add()
            token = sum_3.sent
        elif moved_3 is None:
            moved_3, (new_mq, new_vq) = finish(sum_3, (0,), (w_qkv,), ((m_qkv, v_qkv),))
            token = moved_3.blocks
        else:
            moved_3.join()
            token = moved_3.blocks
        if sum_1.count > 1:
            sum_1.add()
        elif moved_1 is None:
            moved_1, (new_m1, new_v1, new_mo, new_vo) = finish(
                sum_1, (2, 1), (w_fc1, w_out), ((m_fc1, v_fc1), (m_out, v_out))
            )
        elif moved_1.place < last:
            moved_1.join()
        if moved_2.place < last:
            moved_2.join()
        vec_step()
        call.last = token
    while len(vec_gens) >= vec_place:
        vec_step()
    while moved_1.place < last:
        moved_1.join()
    while moved_2.place < last:
        moved_2.join()
    call.waiting = []
    tail = call.pin([moved_2.blocks, moved_2.got])
    (new_2,) = put(moved_2, (D,), FF // nd)
    new_1, new_o = put(moved_1, (FF, D), D // nd)
    (new_q,) = put(moved_3, (3 * D,), D // nd)

    own_cols = D // nd
    got = jnp.concatenate([part[:, FF // nd :] for part in tail], axis=0)
    half = rider_cols // 2
    held = got[:, :, :half].astype(F32) + got[:, :, half:rider_cols].astype(F32)
    held = held.reshape(nb, -1)[:, : 2 * NVEC * own_cols].reshape(nb, 2 * NVEC, own_cols)
    held = jnp.take(held, order, axis=0)
    states = jnp.transpose(held, (1, 0, 2)).reshape(2 * NVEC, nb * own_cols)
    grad_vec = lax.dynamic_slice_in_dim(vec_sum[:NVEC], fi * nb * own_cols, nb * own_cols, 1)
    vec_new, _, _ = adamw(
        vectors, grad_vec, states[:NVEC], states[NVEC:], STEP_RATES[4], DECAY_RATES[4]
    )
    own_grad = lax.dynamic_slice_in_dim(grad_vec, bi * own_cols, own_cols, 1)
    _, new_mv, new_vv = adamw(0.0, own_grad, m_vec, v_vec, STEP_RATES[4], DECAY_RATES[4])

    return (
        layer_out,
        grad_tokens,
        new_q,
        new_mq,
        new_vq,
        new_o,
        new_mo,
        new_vo,
        new_1,
        new_m1,
        new_v1,
        new_2,
        new_m2,
        new_v2,
        vec_new,
        new_mv,
        new_vv,
    )


def solution(mesh):
    pairs = P(("batch", "fsdp"), None, None)
    weight = P("fsdp", None)
    state = P(("fsdp", "batch"), None)
    vec_state = P(None, ("fsdp", "batch"))
    matrix = (weight, state, state)
    return jax.shard_map(
        functools.partial(shards, Plan(mesh)),
        mesh=mesh,
        in_specs=(pairs, pairs, P(("batch", "fsdp"), None), P(("batch", "fsdp")))
        + matrix * 4
        + (P(None, "fsdp"), vec_state, vec_state),
        out_specs=(pairs, pairs) + matrix * 4 + (P(None, "fsdp"), vec_state, vec_state),
        check_vma=False,
    )
```
